32 devices in a mesh: dp: 2 (over x), seq: 4 (over y, core), mp: 4 (over z).
Axes of the slice: x: 2, y: 2, z: 4, core: 2. Of those that a mesh axis runs over, the one named last changes fastest.
Arguments:
- incoming_embeddings: bfloat16 [4, 4, 1024, 512], P(None, 'seq', 'dp'), may hold values from -6 to 6
- output_sensitivity: bfloat16 [4, 4, 1024, 512], P(None, 'seq', 'dp'), may hold values from -6 to 6
- sequence_extents: int32 [4], replicated, may hold values from 512 to 4096, as said below
- asking_projector: bfloat16 [512, 512], P(('dp', 'seq'), 'mp'), may hold values from -0.375 to 0.375
- lookup_projector: bfloat16 [512, 512], P(('dp', 'seq'), 'mp'), may hold values from -0.375 to 0.375
- content_projector: bfloat16 [512, 512], P(('dp', 'seq'), 'mp'), may hold values from -0.25 to 0.25
- attention_combiner: bfloat16 [512, 512], P('mp', ('dp', 'seq')), may hold values from -1.5 to 1.5
- feedforward_expand: bfloat16 [512, 2048], P(('dp', 'seq'), 'mp'), may hold values from -0.25 to 0.25
- feedforward_contract: bfloat16 [2048, 512], P('mp', ('dp', 'seq')), may hold values from -0.125 to 0.125
- attention_norm_scale: bfloat16 [512], P(('dp', 'seq')), may hold values from 0.5 to 1.5
- attention_norm_bias: bfloat16 [512], P(('dp', 'seq')), may hold values from -1.5 to 1.5
- feedforward_norm_scale: bfloat16 [512], P(('dp', 'seq')), may hold values from 0.5 to 1.5
- feedforward_norm_bias: bfloat16 [512], P(('dp', 'seq')), may hold values from -1.5 to 1.5
Outputs:
- output: bfloat16 [4, 4, 1024, 512], P(None, 'seq', ('dp', 'mp'))
- token_grad: bfloat16 [4, 4, 1024, 512], P(None, 'seq', ('dp', 'mp'))
- query_grad: float32 [512, 512], P(('dp', 'seq'), 'mp')
- key_grad: float32 [512, 512], P(('dp', 'seq'), 'mp')
- value_grad: float32 [512, 512], P(('dp', 'seq'), 'mp')
- merge_grad: float32 [512, 512], P('mp', ('dp', 'seq'))
- up_grad: float32 [512, 2048], P(('dp', 'seq'), 'mp')
- down_grad: float32 [2048, 512], P('mp', ('dp', 'seq'))
- pregain_grad: float32 [512], P(('dp', 'seq'))
- preshift_grad: float32 [512], P(('dp', 'seq'))
- midgain_grad: float32 [512], P(('dp', 'seq'))
- midshift_grad: float32 [512], P(('dp', 'seq'))
The draws below stay inside these ranges and needn't reach their ends.
Inputs may be any that keep to these rules, and one draw needn't show every extreme that they name: `sequence_extents`: valid tokens of each sequence in input order; one sequence has exactly 4096 and one exactly 512.
All inputs are finite; a program needn't handle non-finite values.
Results may differ from the reference program's by a relative error of at most 0.015.
Values may be sent and summed in bfloat16 or wider, within the bound.
A program may use at most 256 MiB of HBM per device.

```python
import jax
import jax.numpy as jnp
from jax import lax

EMBED_WIDTH = 512
HEADS = 8
HD = 64
FF = 2048
NR = 16
SEQ_PART = 1024
LEN = 4096
NSEQ = 4
SLICES = 4


def draw_sequence_extents(key, part):
    draw_key, place_key = jax.random.split(jax.random.fold_in(key, 11), 2)
    drawn = jax.random.randint(draw_key, (NSEQ,), LEN // 8, LEN + 1, dtype=jnp.int32)
    placing = jax.random.permutation(place_key, NSEQ)
    drawn = drawn.at[placing[0]].set(LEN)
    drawn = drawn.at[placing[1]].set(LEN // 8)
    return drawn.astype(jnp.int32)


def shard_levels(rng, extent, cuts, low, high):
    loudness, own = 1.0, jax.random.fold_in(rng, 6)
    for axis_at, blocks in cuts:
        draws = jnp.exp(jax.random.uniform(jax.random.fold_in(own, axis_at), (blocks,), jnp.float32, low / len(cuts), high / len(cuts)))
        loudness = loudness * jnp.repeat(draws, extent[axis_at] // blocks).reshape([-1 if axis == axis_at else 1 for axis in range(len(extent))])
    return loudness


def centred(own_key, shape, scale, reach, shards=(), kind=jnp.bfloat16):
    array = jax.random.normal(own_key, shape, jnp.float32) * scale
    if len(shards) > 0:
        array = shard_levels(own_key, shape, shards, -0.22, 0.18) * array
    return jnp.clip(array, min=-reach, max=reach).astype(kind)


def setup_inputs(seed: int = 0) -> dict:
    key_of = jax.random.split(jax.random.key(seed), 14)
    incoming_embeddings = centred(key_of[0], (NSEQ, SLICES, SEQ_PART, EMBED_WIDTH), 1.0, 6.0, ((1, 4), (2, 2)))
    output_sensitivity = centred(key_of[1], (NSEQ, SLICES, SEQ_PART, EMBED_WIDTH), 1.0, 6.0, ((1, 4), (2, 2)))
    sequence_extents = draw_sequence_extents(jax.random.fold_in(key_of[13], 71), 0)
    asking_projector = centred(key_of[3], (EMBED_WIDTH, HEADS * HD), (EMBED_WIDTH // 2) ** -0.5, 0.375, ((0, 8), (1, 4)))
    lookup_projector = centred(key_of[4], (EMBED_WIDTH, HEADS * HD), (EMBED_WIDTH // 2) ** -0.5, 0.375, ((0, 8), (1, 4)))
    content_projector = centred(key_of[5], (EMBED_WIDTH, HEADS * HD), EMBED_WIDTH ** -0.5, 0.25, ((0, 8), (1, 4)))
    attention_combiner = centred(key_of[6], (HEADS * HD, EMBED_WIDTH), (HEADS * HD // 32) ** -0.5, 1.5, ((0, 4), (1, 8)))
    feedforward_expand = centred(key_of[7], (EMBED_WIDTH, FF), EMBED_WIDTH ** -0.5, 0.25, ((0, 8), (1, 4)))
    feedforward_contract = centred(key_of[8], (FF, EMBED_WIDTH), FF ** -0.5, 0.125, ((0, 4), (1, 8)))
    attention_norm_scale = jnp.clip(1.0 + 0.1 * jax.random.normal(key_of[9], (EMBED_WIDTH,), jnp.float32), 0.5, 1.5).astype(jnp.bfloat16)
    attention_norm_bias = centred(key_of[10], (EMBED_WIDTH,), 0.3, 1.5, ((0, 8),))
    feedforward_norm_scale = jnp.clip(1.0 + 0.1 * jax.random.normal(key_of[11], (EMBED_WIDTH,), jnp.float32), 0.5, 1.5).astype(jnp.bfloat16)
    feedforward_norm_bias = centred(key_of[12], (EMBED_WIDTH,), 0.3, 1.5, ((0, 8),))
    return dict(incoming_embeddings=incoming_embeddings, output_sensitivity=output_sensitivity, sequence_extents=sequence_extents, asking_projector=asking_projector, lookup_projector=lookup_projector, content_projector=content_projector, attention_combiner=attention_combiner, feedforward_expand=feedforward_expand, feedforward_contract=feedforward_contract, attention_norm_scale=attention_norm_scale, attention_norm_bias=attention_norm_bias, feedforward_norm_scale=feedforward_norm_scale, feedforward_norm_bias=feedforward_norm_bias)


@jax.custom_vjp
def low(v):
    return lax.optimization_barrier(v.astype(jnp.bfloat16)).astype(jnp.float32)

@jax.custom_vjp
def low_back(v):
    return v

def low_keep(v):
    return (low(v), None)

def low_pass(kept, grad):
    return (grad,)

def back_keep(v):
    return (v, None)

def back_low(kept, grad):
    return (low(grad),)
low.defvjp(low_keep, low_pass)
low_back.defvjp(back_keep, back_low)

def norm_rows(values, gain_row, shift_row):
    center = values - lax.optimization_barrier(jnp.mean(values, axis=-1, keepdims=True))
    spread = lax.optimization_barrier(jnp.mean(center * center, axis=-1, keepdims=True))
    return center * lax.rsqrt(spread + 1e-05) * gain_row + shift_row

def product(left_mat, right_mat):
    return jnp.dot(left_mat, right_mat, precision=lax.Precision.HIGHEST, preferred_element_type=jnp.float32)

def windows(padded, block_count, block_len):
    span_rows = block_count * block_len
    window_parts = [padded[offset * block_len:offset * block_len + span_rows].reshape(block_count, block_len, -1) for offset in range(3)]
    return jnp.concatenate(window_parts, axis=1)

def band_mask(level_at):
    if level_at == 0:
        return jnp.ones((NR, 3 * NR), jnp.float32)
    rows_in = jnp.arange(NR, dtype=jnp.int32)[:, None]
    cols_in = jnp.arange(3 * NR, dtype=jnp.int32)[None, :]
    half_block = NR // 2
    return (jnp.abs(2 + rows_in // half_block - cols_in // half_block) >= 2).astype(jnp.float32)

def level_attend(query_rows, key_rows, value_rows, count_rows, band_rows):
    coarse_rows = query_rows.shape[0]
    blocks = coarse_rows // NR
    highest = lax.Precision.HIGHEST
    key_win = windows(jnp.pad(key_rows, ((NR, NR), (0, 0))), blocks, NR).reshape(blocks, 3 * NR, HEADS, HD)
    value_win = windows(jnp.pad(value_rows, ((NR, NR), (0, 0))), blocks, NR).reshape(blocks, 3 * NR, HEADS, HD)
    count_win = windows(jnp.pad(count_rows, (NR, NR))[:, None], blocks, NR)[:, :, 0]
    query_blocks = query_rows.reshape(blocks, NR, HEADS, HD)
    scores = low_back(jnp.einsum('bqhd,bkhd->bhqk', query_blocks, key_win, precision=highest) * HD ** (-0.5))
    weight = jnp.exp(scores) * count_win[:, None, None, :] * band_rows[None, None]
    totals = lax.optimization_barrier(jnp.sum(weight, axis=-1)).transpose(0, 2, 1).reshape(coarse_rows, HEADS)
    numer_part = jnp.einsum('bhqk,bkhd->bqhd', low(weight), value_win, precision=highest).reshape(coarse_rows, HEADS, HD)
    return (numer_part, totals)

def layer_forward(inputs, length_now, learnable_collection):
    full_query, full_key, full_value, full_merge, full_up, full_down, gain_pre, shift_pre, gain_mid, shift_mid = learnable_collection
    seq_len = inputs.shape[0]
    columns = HEADS * HD
    positions = jnp.arange(seq_len, dtype=jnp.int32)
    valid_rows = (positions < length_now).astype(jnp.float32)
    normed = low(norm_rows(inputs, gain_pre, shift_pre))
    queries = low_back(low(product(normed, full_query)))
    keys_all = low_back(low(product(normed, full_key)))
    values_all = low_back(low(product(normed, full_value)))
    fine_all = jnp.concatenate([queries, keys_all, values_all], axis=1) * valid_rows[:, None]
    numer_all, total_all = level_attend(queries, keys_all, values_all, valid_rows, band_mask(0))
    level_top = (seq_len // (2 * NR)).bit_length() - 1
    for level_at in range(1, level_top + 1):
        group_len = 2 ** level_at
        coarse_rows = seq_len // group_len
        counts = jnp.clip(length_now - group_len * jnp.arange(coarse_rows, dtype=jnp.int32), 0, group_len).astype(jnp.float32)
        coarse_means = low(lax.optimization_barrier(jnp.sum(fine_all.reshape(coarse_rows, group_len, 3 * columns), axis=1)) / jnp.maximum(counts, 1.0)[:, None])
        numer_part, totals = level_attend(coarse_means[:, :columns], coarse_means[:, columns:2 * columns], coarse_means[:, 2 * columns:], counts, band_mask(level_at))
        numer_all = numer_all + jnp.repeat(low_back(numer_part), group_len, axis=0)
        total_all = total_all + jnp.repeat(totals, group_len, axis=0)
    numerator = low_back(numer_all)
    attended = low((numerator / total_all[:, :, None]).reshape(seq_len, columns))
    branch_attn = low_back(product(attended, full_merge))
    after_attn = inputs + branch_attn
    mid_normed = low(norm_rows(after_attn, gain_mid, shift_mid))
    up_proj = low_back(product(mid_normed, full_up))
    activated = low(jax.nn.gelu(up_proj, approximate=False))
    branch_ffn = product(activated, full_down)
    return valid_rows[:, None] * (after_attn + branch_ffn)

def reference(incoming_embeddings, output_sensitivity, sequence_extents, asking_projector, lookup_projector, content_projector, attention_combiner, feedforward_expand, feedforward_contract, attention_norm_scale, attention_norm_bias, feedforward_norm_scale, feedforward_norm_bias):
    learnable_collection = tuple((learnable_tensor.astype(jnp.float32) for learnable_tensor in (asking_projector, lookup_projector, content_projector, attention_combiner, feedforward_expand, feedforward_contract, attention_norm_scale, attention_norm_bias, feedforward_norm_scale, feedforward_norm_bias)))
    seq_count = incoming_embeddings.shape[0]
    inputs = incoming_embeddings.astype(jnp.float32).reshape(seq_count, LEN, EMBED_WIDTH)
    grads_in = output_sensitivity.astype(jnp.float32).reshape(seq_count, LEN, EMBED_WIDTH)

    def one_sequence(running, member):
        inputs_row, grad_row, length_now = member
        output_row, pull_back = jax.vjp(lambda values, params: layer_forward(values, length_now, params), inputs_row, learnable_collection)
        input_grad, weight_grads = pull_back(grad_row)
        return (tuple((older_sum + newer_sum for older_sum, newer_sum in zip(running, weight_grads))), (output_row, input_grad))
    zero_sums = tuple((jnp.zeros_like(learnable_tensor) for learnable_tensor in learnable_collection))
    grad_sums, (outputs, token_grads) = lax.scan(one_sequence, zero_sums, (inputs, grads_in, sequence_extents))
    full_shape = (seq_count, SLICES, SEQ_PART, EMBED_WIDTH)
    return (outputs.reshape(full_shape).astype(jnp.bfloat16), token_grads.reshape(full_shape).astype(jnp.bfloat16), grad_sums[0], grad_sums[1], grad_sums[2], grad_sums[3], grad_sums[4], grad_sums[5], grad_sums[6], grad_sums[7], grad_sums[8], grad_sums[9])
```

```python
import functools

import jax
import jax.numpy as jnp
from jax import lax
from jax.experimental import pallas as pl
from jax.experimental.pallas import tpu as pltpu
from jax.sharding import PartitionSpec as P

HD = 64
NR = 16


def cut_along(x, dim, count):
    before, after = (x.shape[:dim], x.shape[dim + 1 :])
    return jnp.moveaxis(x.reshape(*before, count, -1, *after), dim, 0)


def summed_on_arrival(x, axis, dim):
    count = lax.axis_size(axis)
    blocks = lax.all_to_all(cut_along(x, dim, count), axis, 0, 0, tiled=True)
    return jnp.sum(blocks.astype(jnp.float32), axis=0)


def sent_together(arrays, axis, dim, along):
    ends, at = ([], 0)
    for a in arrays[:-1]:
        at += a.shape[along]
        ends.append(at)
    both = jnp.concatenate(arrays, axis=along)
    return tuple(jnp.split(summed_on_arrival(both, axis, dim), ends, axis=along))


def norm_rows(values, gain_row, shift_row):
    center = values - jnp.mean(values, axis=-1, keepdims=True)
    spread = jnp.mean(center * center, axis=-1, keepdims=True)
    return center * lax.rsqrt(spread + 1e-05) * gain_row + shift_row


def norm_gain_parts(values, grad_rows):
    center = values - jnp.mean(values, axis=-1, keepdims=True)
    spread = jnp.mean(center * center, axis=-1, keepdims=True)
    scaled = center * lax.rsqrt(spread + 1e-05)
    return (jnp.sum(grad_rows * scaled, axis=0), jnp.sum(grad_rows, axis=0))


def gelu_exact(values):
    return jax.nn.gelu(values, approximate=False)


def dot_plain(left_mat, right_mat):
    return jnp.dot(left_mat, right_mat, preferred_element_type=jnp.float32)


def dot_inner(left_mat, right_mat):
    return lax.dot_general(
        left_mat, right_mat, (((0,), (0,)), ((), ())), preferred_element_type=jnp.float32
    )


def dot_outer(left_mat, right_mat):
    return lax.dot_general(
        left_mat, right_mat, (((1,), (1,)), ((), ())), preferred_element_type=jnp.float32
    )


def group_sum(values, group_width):
    return jnp.sum(
        values.reshape((values.shape[0] // group_width, group_width) + values.shape[1:]), axis=1
    )


def block_shape(coarse_rows):
    query_len = min(coarse_rows, 512)
    span_len = query_len + 2 * NR
    window_len = -(-span_len // 128) * 128
    return (query_len, span_len, window_len)


def window_mask(level_at, first_row, query_len, window_len, span_len):
    rows_at = first_row + jnp.arange(query_len, dtype=jnp.int32)[:, None]
    keys_at = first_row + jnp.arange(window_len, dtype=jnp.int32)[None, :]
    inside = keys_at - first_row < span_len
    allowed = jnp.abs(rows_at // NR + 1 - keys_at // NR) <= 1
    if level_at > 0:
        half_block = NR // 2
        allowed = allowed & (jnp.abs(rows_at // half_block + 2 - keys_at // half_block) >= 2)
    return (allowed & inside).astype(jnp.float32)


def level_forward(query_rows, pair_wide, count_wide, level_at):
    coarse_rows = query_rows.shape[0]
    columns = query_rows.shape[1]
    heads_here = columns // HD
    query_len, span_len, window_len = block_shape(coarse_rows)
    tail_pad = window_len - span_len
    pair_padded = jnp.pad(pair_wide, ((0, tail_pad), (0, 0)))
    count_padded = jnp.pad(count_wide, (0, tail_pad))
    weight_list = []
    total_parts = []
    numer_parts = []
    for block_at in range(coarse_rows // query_len):
        first_row = block_at * query_len
        query_block = query_rows[first_row : first_row + query_len]
        pair_block = pair_padded[first_row : first_row + window_len]
        count_block = count_padded[first_row : first_row + window_len]
        keep_mask = (
            window_mask(level_at, first_row, query_len, window_len, span_len) * count_block[None, :]
        )
        head_weights = []
        head_totals = []
        head_numers = []
        for head_at in range(heads_here):
            head_cols = slice(head_at * HD, (head_at + 1) * HD)
            value_cols = slice(columns + head_at * HD, columns + (head_at + 1) * HD)
            scores = dot_outer(query_block[:, head_cols], pair_block[:, head_cols]) * HD ** (-0.5)
            weight = jnp.exp(scores) * keep_mask
            head_weights.append(weight)
            head_totals.append(jnp.sum(weight, axis=-1))
            head_numers.append(dot_plain(weight.astype(jnp.bfloat16), pair_block[:, value_cols]))
        weight_list.append(head_weights)
        total_parts.append(jnp.stack(head_totals, axis=1))
        numer_parts.append(jnp.concatenate(head_numers, axis=1))
    totals = jnp.concatenate(total_parts, axis=0)
    numer_part = jnp.concatenate(numer_parts, axis=0).reshape(coarse_rows, heads_here, HD)
    return ((query_rows, pair_padded, weight_list), totals, numer_part)


def level_backward(level_kept, numer_rows, total_rows):
    query_rows, pair_padded, weight_list = level_kept
    coarse_rows = query_rows.shape[0]
    columns = query_rows.shape[1]
    heads_here = columns // HD
    query_len, span_len, window_len = block_shape(coarse_rows)
    numer_flat = numer_rows.reshape(coarse_rows, columns)
    pair_grad = jnp.zeros(pair_padded.shape, jnp.float32)
    query_parts = []
    for block_at in range(coarse_rows // query_len):
        first_row = block_at * query_len
        query_block = query_rows[first_row : first_row + query_len]
        pair_block = pair_padded[first_row : first_row + window_len]
        numer_block = numer_flat[first_row : first_row + query_len]
        total_block = total_rows[first_row : first_row + query_len]
        query_heads = []
        key_heads = []
        value_heads = []
        for head_at in range(heads_here):
            head_cols = slice(head_at * HD, (head_at + 1) * HD)
            value_cols = slice(columns + head_at * HD, columns + (head_at + 1) * HD)
            weight = head_weights = weight_list[block_at][head_at]
            grad_here = numer_block[:, head_cols]
            score_grad = (
                (dot_outer(grad_here, pair_block[:, value_cols]) + total_block[:, head_at][:, None])
                * weight
            ).astype(jnp.bfloat16)
            query_heads.append(dot_plain(score_grad, pair_block[:, head_cols]) * HD ** (-0.5))
            key_heads.append(dot_inner(score_grad, query_block[:, head_cols]) * HD ** (-0.5))
            value_heads.append(dot_inner(head_weights.astype(jnp.bfloat16), grad_here))
        query_parts.append(jnp.concatenate(query_heads, axis=1))
        block_grad = jnp.concatenate(key_heads + value_heads, axis=1)
        pair_grad = pair_grad + jnp.pad(
            block_grad, ((first_row, pair_padded.shape[0] - first_row - window_len), (0, 0))
        )
    query_grad = jnp.concatenate(query_parts, axis=0)
    return (query_grad, pair_grad[: coarse_rows + 2 * NR])


def general_body(
    incoming_embeddings,
    output_sensitivity,
    sequence_extents,
    asking_projector,
    lookup_projector,
    content_projector,
    attention_combiner,
    feedforward_expand,
    feedforward_contract,
    attention_norm_scale,
    attention_norm_bias,
    feedforward_norm_scale,
    feedforward_norm_bias,
):
    groups = lax.axis_size("dp")
    slices = lax.axis_size("seq")
    models = lax.axis_size("mp")
    group_id = lax.axis_index("dp")
    slice_id = lax.axis_index("seq")
    model_id = lax.axis_index("mp")
    seq_count = incoming_embeddings.shape[0]
    piece_len = incoming_embeddings.shape[2]
    model_width = incoming_embeddings.shape[3]
    part_len = piece_len * groups
    batches = seq_count // groups
    share_len = piece_len // models
    share_rows = groups * share_len
    local_top = (part_len // NR).bit_length() - 1
    upper_start = local_top + 1
    level_top = (part_len * slices // (2 * NR)).bit_length() - 1
    upper_rows = NR // 2
    upper_whole = upper_rows * slices
    send_tok = incoming_embeddings.reshape(
        groups, batches, piece_len, model_width
    )
    send_cot = output_sensitivity.reshape(
        groups, batches, piece_len, model_width
    )
    dealt_tok, dealt_cot = (
        lax.all_to_all(send_tok, "dp", split_axis=0, concat_axis=2, tiled=True),
        lax.all_to_all(send_cot, "dp", split_axis=0, concat_axis=2, tiled=True),
    )
    dealt_tok = dealt_tok.reshape(batches, part_len, model_width)
    dealt_cot = dealt_cot.reshape(batches, part_len, model_width)
    my_lengths = lax.dynamic_slice_in_dim(sequence_extents, group_id * batches, batches, 0)

    def split_rows(rows):
        return rows.reshape((groups, models, share_len) + rows.shape[1:])

    def take_share(rows):
        return lax.dynamic_slice_in_dim(split_rows(rows), model_id, 1, 1).reshape(
            (share_rows,) + rows.shape[1:]
        )

    def neighbour_rims(gathered):
        padded = jnp.pad(gathered, ((2 * NR, 2 * NR), (0, 0)))
        from_left = lax.dynamic_slice_in_dim(padded, slice_id * 2 * NR + NR, NR, 0)
        from_right = lax.dynamic_slice_in_dim(padded, (slice_id + 2) * 2 * NR, NR, 0)
        return (from_left, from_right)

    def one_batch(batch_index, learnable_collection):
        full_query, full_key, full_value, full_merge, full_up, full_down = learnable_collection[:6]
        gain_pre, shift_pre, gain_mid, shift_mid = (
            learnable_tensor.astype(jnp.float32) for learnable_tensor in learnable_collection[6:]
        )
        columns = full_query.shape[1]
        heads_here = columns // HD
        length_now = my_lengths[batch_index]

        def level_counts(level_at, first_id, id_total):
            coarse_ids = first_id + jnp.arange(id_total, dtype=jnp.int32)
            group_len = 2**level_at
            return jnp.where(
                coarse_ids >= 0, jnp.clip(length_now - group_len * coarse_ids, 0, group_len), 0
            ).astype(jnp.float32)

        positions = slice_id * part_len + jnp.arange(part_len, dtype=jnp.int32)
        valid_rows = (positions < length_now).astype(jnp.float32)
        inputs = dealt_tok[batch_index].astype(jnp.float32)
        grad_in = dealt_cot[batch_index].astype(jnp.float32) * valid_rows[:, None]
        valid_share = take_share(valid_rows)
        normed, pull_pre = jax.vjp(norm_rows, inputs, gain_pre, shift_pre)
        normed_low = normed.astype(jnp.bfloat16)
        queries = dot_plain(normed_low, full_query).astype(jnp.bfloat16)
        keys_own = dot_plain(normed_low, full_key).astype(jnp.bfloat16)
        values_own = dot_plain(normed_low, full_value).astype(jnp.bfloat16)
        pair_own = jnp.concatenate([keys_own, values_own], axis=1)
        fine_all = (
            jnp.concatenate([queries, pair_own], axis=1).astype(jnp.float32) * valid_rows[:, None]
        )
        level_sums = [fine_all]
        for level_at in range(1, upper_start + 1):
            level_sums.append(group_sum(level_sums[-1], 2))
        query_levels = [queries]
        pair_levels = [pair_own]
        own_counts = [valid_rows]
        for level_at in range(1, local_top + 1):
            coarse_rows = part_len >> level_at
            counts_here = level_counts(level_at, slice_id * coarse_rows, coarse_rows)
            coarse_means = (level_sums[level_at] / jnp.maximum(counts_here, 1.0)[:, None]).astype(
                jnp.bfloat16
            )
            query_levels.append(coarse_means[:, :columns])
            pair_levels.append(coarse_means[:, columns:])
            own_counts.append(counts_here)
        edge_rows = jnp.concatenate(
            [
                jnp.concatenate([pair_rows[:NR], pair_rows[-NR:]], axis=0)
                for pair_rows in pair_levels
            ],
            axis=1,
        )
        edges_all, upper_all = (
            lax.all_gather(
                edge_rows.astype(jnp.float32).astype(jnp.bfloat16), "seq", axis=0, tiled=True
            ).astype(jnp.float32),
            lax.all_gather(
                level_sums[upper_start].astype(jnp.bfloat16), "seq", axis=0, tiled=True
            ).astype(jnp.float32),
        )
        left_edge, right_edge = neighbour_rims(edges_all)
        left_edge = left_edge.astype(jnp.bfloat16)
        right_edge = right_edge.astype(jnp.bfloat16)
        kept_levels = []
        total_all = jnp.zeros((part_len, heads_here), jnp.float32)
        numer_all = jnp.zeros((part_len, heads_here, HD), jnp.float32)
        for level_at in range(local_top + 1):
            coarse_rows = part_len >> level_at
            col_range = slice(level_at * 2 * columns, (level_at + 1) * 2 * columns)
            pair_wide = jnp.concatenate(
                [left_edge[:, col_range], pair_levels[level_at], right_edge[:, col_range]], axis=0
            )
            count_wide = level_counts(level_at, slice_id * coarse_rows - NR, coarse_rows + 2 * NR)
            level_kept, totals, numer_part = level_forward(
                query_levels[level_at], pair_wide, count_wide, level_at
            )
            kept_levels.append(level_kept)
            total_all = total_all + jnp.repeat(totals, 2**level_at, axis=0)
            numer_all = numer_all + jnp.repeat(numer_part, 2**level_at, axis=0)
        level_at = 7
        repeat_by = 2 ** (level_at - upper_start)
        coarse_rows = upper_whole // repeat_by
        counts_here = level_counts(level_at, 0, coarse_rows)
        coarse_means = (
            group_sum(upper_all, repeat_by) / jnp.maximum(counts_here, 1.0)[:, None]
        ).astype(jnp.bfloat16)
        pair_wide = jnp.pad(coarse_means[:, columns:], ((NR, NR), (0, 0)))
        count_wide = level_counts(level_at, -NR, coarse_rows + 2 * NR)
        level_kept, totals, numer_part = level_forward(
            coarse_means[:, :columns], pair_wide, count_wide, level_at
        )
        upper_kept = [level_kept]
        upper_counts = [counts_here]
        upper_total = jnp.repeat(totals, repeat_by, axis=0)
        upper_numer = jnp.repeat(numer_part, repeat_by, axis=0)
        total_all = total_all + jnp.repeat(
            lax.dynamic_slice_in_dim(upper_total, slice_id * upper_rows, upper_rows, 0),
            2**upper_start,
            axis=0,
        )
        numer_all = numer_all + jnp.repeat(
            lax.dynamic_slice_in_dim(upper_numer, slice_id * upper_rows, upper_rows, 0),
            2**upper_start,
            axis=0,
        )
        attended = (
            (numer_all / total_all[:, :, None]).reshape(part_len, columns).astype(jnp.bfloat16)
        )
        merged_part = dot_plain(attended, full_merge)
        branch_attn = lax.psum(merged_part, "mp")
        after_attn = inputs + branch_attn
        mid_normed, pull_mid = jax.vjp(norm_rows, after_attn, gain_mid, shift_mid)
        mid_low = mid_normed.astype(jnp.bfloat16)
        after_share = take_share(after_attn)
        up_proj = dot_plain(mid_low, full_up)
        activated, pull_gelu = jax.vjp(gelu_exact, up_proj)
        act_low = activated.astype(jnp.bfloat16)
        ffn_share = (
            lax.psum_scatter(
                split_rows(dot_plain(act_low, full_down)).astype(jnp.bfloat16),
                "mp",
                scatter_dimension=1,
                tiled=True,
            )
            .astype(jnp.float32)
            .reshape(share_rows, model_width)
        )
        result_share = (valid_share[:, None] * (after_share + ffn_share)).astype(jnp.bfloat16)
        grad_low = grad_in.astype(jnp.bfloat16)
        act_grad = dot_outer(grad_low, full_down)
        down_acc = dot_inner(act_low, grad_low)
        hidden_grad = pull_gelu(act_grad)[0].astype(jnp.bfloat16)
        up_acc = dot_inner(mid_low, hidden_grad)
        mid_part = dot_outer(hidden_grad, full_up)
        mid_grad = lax.psum(mid_part, "mp")
        back_mid = pull_mid(mid_grad)[0]
        residual_grad = grad_in + back_mid
        branch_grad = residual_grad.astype(jnp.bfloat16)
        residual_share = take_share(residual_grad)
        gain_mid_part, shift_mid_part = norm_gain_parts(after_share, take_share(mid_grad))
        merge_acc = dot_inner(attended, branch_grad)
        attended_grad = dot_outer(branch_grad, full_merge).reshape(part_len, heads_here, HD)
        numer_grad = (attended_grad / total_all[:, :, None]).astype(jnp.bfloat16)
        total_grad = -jnp.sum(attended_grad * numer_all, axis=-1) / (total_all * total_all)
        numer_wide = numer_grad.astype(jnp.float32)
        rim_parts = []
        own_pair_grads = []
        query_coarse = []
        for level_at in range(local_top + 1):
            coarse_rows = part_len >> level_at
            if level_at == 0:
                numer_sum = numer_grad
                total_sum = total_grad
            else:
                numer_sum = group_sum(numer_wide, 2**level_at).astype(jnp.bfloat16)
                total_sum = group_sum(total_grad, 2**level_at)
            query_grad, pair_grad = level_backward(kept_levels[level_at], numer_sum, total_sum)
            rim_parts.append(
                jnp.concatenate([pair_grad[:NR], pair_grad[NR + coarse_rows :]], axis=0)
            )
            own_pair_grads.append(pair_grad[NR : NR + coarse_rows])
            query_coarse.append(query_grad)
        rim_grads = jnp.concatenate(rim_parts, axis=1)
        upper_numer_grad = group_sum(numer_wide, 2**upper_start).reshape(upper_rows, columns)
        upper_total_grad = group_sum(total_grad, 2**upper_start)
        rims_all, numer_sums, total_sums = (
            lax.all_gather(rim_grads.astype(jnp.bfloat16), "seq", axis=0, tiled=True).astype(
                rim_grads.dtype
            ),
            lax.all_gather(upper_numer_grad.astype(jnp.bfloat16), "seq", axis=0, tiled=True).astype(
                upper_numer_grad.dtype
            ),
            lax.all_gather(upper_total_grad.astype(jnp.bfloat16), "seq", axis=0, tiled=True).astype(
                upper_total_grad.dtype
            ),
        )
        from_left, from_right = neighbour_rims(rims_all)
        fine_grad = jnp.zeros((part_len, 3 * columns), jnp.float32)
        for level_at in range(local_top + 1):
            coarse_rows = part_len >> level_at
            col_range = slice(level_at * 2 * columns, (level_at + 1) * 2 * columns)
            pair_here = (
                own_pair_grads[level_at]
                + jnp.pad(from_left[:, col_range], ((0, coarse_rows - NR), (0, 0)))
                + jnp.pad(from_right[:, col_range], ((coarse_rows - NR, 0), (0, 0)))
            )
            coarse_grad = jnp.concatenate([query_coarse[level_at], pair_here], axis=1)
            if level_at == 0:
                fine_grad = coarse_grad
            else:
                coarse_grad = coarse_grad / jnp.maximum(own_counts[level_at], 1.0)[:, None]
                fine_grad = (
                    fine_grad + jnp.repeat(coarse_grad, 2**level_at, axis=0) * valid_rows[:, None]
                )
        upper_grad = jnp.zeros((upper_whole, 3 * columns), jnp.float32)
        for index_at, level_at in enumerate(range(upper_start, level_top + 1)):
            repeat_by = 2 ** (level_at - upper_start)
            coarse_rows = upper_whole // repeat_by
            numer_sum = (
                group_sum(numer_sums, repeat_by)
                .reshape(coarse_rows, heads_here, HD)
                .astype(jnp.bfloat16)
            )
            total_sum = group_sum(total_sums, repeat_by)
            query_grad, pair_grad = level_backward(upper_kept[index_at], numer_sum, total_sum)
            coarse_grad = (
                jnp.concatenate([query_grad, pair_grad[NR : NR + coarse_rows]], axis=1)
                / jnp.maximum(upper_counts[index_at], 1.0)[:, None]
            )
            upper_grad = jnp.repeat(coarse_grad, repeat_by, axis=0)
        own_upper = lax.dynamic_slice_in_dim(upper_grad, slice_id * upper_rows, upper_rows, 0)
        fine_grad = fine_grad + jnp.repeat(own_upper, 2**upper_start, axis=0) * valid_rows[:, None]
        rows_grad = fine_grad.astype(jnp.bfloat16)
        query_rows_grad = rows_grad[:, :columns]
        key_rows_grad = rows_grad[:, columns : 2 * columns]
        value_rows_grad = rows_grad[:, 2 * columns :]
        query_acc = dot_inner(normed_low, query_rows_grad)
        key_acc = dot_inner(normed_low, key_rows_grad)
        value_acc = dot_inner(normed_low, value_rows_grad)
        normed_part = (
            dot_outer(query_rows_grad, full_query)
            + dot_outer(key_rows_grad, full_key)
            + dot_outer(value_rows_grad, full_value)
        )
        normed_grad, gain_mid_sum, shift_mid_sum = (
            lax.psum(normed_part.astype(jnp.bfloat16), "mp").astype(jnp.float32),
            lax.psum(gain_mid_part.astype(jnp.bfloat16), "mp").astype(jnp.float32),
            lax.psum(shift_mid_part.astype(jnp.bfloat16), "mp").astype(jnp.float32),
        )
        back_pre, gain_pre_acc, shift_pre_acc = pull_pre(normed_grad)
        input_share = (residual_share + take_share(back_pre)).astype(jnp.bfloat16)
        grad_terms = (
            query_acc,
            key_acc,
            value_acc,
            merge_acc,
            up_acc,
            down_acc,
            gain_pre_acc,
            shift_pre_acc,
            gain_mid_sum,
            shift_mid_sum,
        )
        return (result_share, input_share, grad_terms)

    result_list = []
    grad_list = []
    running_sum = None
    for batch_index in range(batches):
        learnable_collection = (
            lax.all_gather(asking_projector, ("dp", "seq"), axis=0, tiled=True),
            lax.all_gather(lookup_projector, ("dp", "seq"), axis=0, tiled=True),
            lax.all_gather(content_projector, ("dp", "seq"), axis=0, tiled=True),
            lax.all_gather(attention_combiner, ("dp", "seq"), axis=1, tiled=True),
            lax.all_gather(feedforward_expand, ("dp", "seq"), axis=0, tiled=True),
            lax.all_gather(feedforward_contract, ("dp", "seq"), axis=1, tiled=True),
            lax.all_gather(attention_norm_scale, ("dp", "seq"), axis=0, tiled=True),
            lax.all_gather(attention_norm_bias, ("dp", "seq"), axis=0, tiled=True),
            lax.all_gather(feedforward_norm_scale, ("dp", "seq"), axis=0, tiled=True),
            lax.all_gather(feedforward_norm_bias, ("dp", "seq"), axis=0, tiled=True),
        )
        result_share, input_share, grad_terms = one_batch(batch_index, learnable_collection)
        result_list.append(result_share)
        grad_list.append(input_share)
        if running_sum is None:
            running_sum = grad_terms
        else:
            running_sum = tuple(
                (older_sum + newer_sum for older_sum, newer_sum in zip(running_sum, grad_terms))
            )
    owned_grads = (
        *sent_together(
            (
                running_sum[0].astype(jnp.bfloat16),
                running_sum[1].astype(jnp.bfloat16),
                running_sum[2].astype(jnp.bfloat16),
            ),
            ("dp", "seq"),
            0,
            1,
        ),
        summed_on_arrival(running_sum[3].astype(jnp.bfloat16), ("dp", "seq"), 1),
        summed_on_arrival(running_sum[4].astype(jnp.bfloat16), ("dp", "seq"), 0),
        summed_on_arrival(running_sum[5].astype(jnp.bfloat16), ("dp", "seq"), 1),
        summed_on_arrival(running_sum[6].astype(jnp.bfloat16), ("dp", "seq"), 0),
        summed_on_arrival(running_sum[7].astype(jnp.bfloat16), ("dp", "seq"), 0),
        summed_on_arrival(running_sum[8].astype(jnp.bfloat16), ("dp", "seq"), 0),
        summed_on_arrival(running_sum[9].astype(jnp.bfloat16), ("dp", "seq"), 0),
    )
    result_all = jnp.stack(result_list, axis=0).reshape(batches, groups, share_len, model_width)
    grad_all = jnp.stack(grad_list, axis=0).reshape(batches, groups, share_len, model_width)
    back_out, back_grad = (
        lax.all_to_all(result_all, "dp", split_axis=1, concat_axis=0, tiled=True),
        lax.all_to_all(grad_all, "dp", split_axis=1, concat_axis=0, tiled=True),
    )
    return (
        back_out,
        back_grad,
        owned_grads[0],
        owned_grads[1],
        owned_grads[2],
        owned_grads[3],
        owned_grads[4],
        owned_grads[5],
        owned_grads[6],
        owned_grads[7],
        owned_grads[8],
        owned_grads[9],
    )


MESH = pl.DeviceIdType.MESH
NEG = -1e30


def nn(a, b):
    return lax.dot_general(a, b, (((1,), (0,)), ((), ())), preferred_element_type=jnp.float32)


def nt(a, b):
    return lax.dot_general(a, b, (((1,), (1,)), ((), ())), preferred_element_type=jnp.float32)


def tn(a, b):
    return lax.dot_general(a, b, (((0,), (0,)), ((), ())), preferred_element_type=jnp.float32)


def halves(values):
    high = values.astype(jnp.bfloat16)
    return high, (values - high.astype(jnp.float32)).astype(jnp.bfloat16)


class Plan:
    def __init__(self, part, spots):
        self.part, self.spots = part, spots
        self.levels = (part // NR).bit_length()
        self.top = (part * spots // (2 * NR)).bit_length() - 1
        self.own = [part >> level for level in range(self.levels)]
        self.at, row = [], 0
        for rows in self.own:
            self.at.append(row)
            row += rows + 2 * NR
        self.upper = row
        self.rows = row + spots * NR
        self.pool_at, row = [None], 0
        for rows in self.own[1:]:
            self.pool_at.append(row)
            row += rows
        self.pool_upper = row
        self.pooled = row + NR
        self.slot, row = [], 0
        for level in range(self.levels, self.top + 1):
            self.slot.append((level, row, part >> level))
            row += part >> level
        assert row <= NR and spots * NR == 128 and self.pooled == part
        self.segments = [(self.at[lv], self.own[lv] + 2 * NR, lv) for lv in range(self.levels)]
        self.inner, self.outer = [], []
        level = 0
        while level < self.levels:
            start, total = self.at[level], self.own[level] + 2 * NR
            end = start + total
            if total < 96:
                self.outer.append((start, self.upper - start, self.upper - 128, None))
                break
            row = start
            while row < end:
                count = min(96, end - row)
                window = max(start, min(row - NR, end - 128))
                tile = (row, count, window, level if window + 128 <= end else None)
                inside = window >= start + NR and window + 128 <= end - NR
                (self.inner if inside else self.outer).append(tile)
                row += count
            level += 1
        self.outer.append((self.upper, 128, self.upper, None))
        self.tiles = self.inner + self.outer


def row_places(plan, rows, low, high, spot):
    level = jnp.full(rows.shape, -1, jnp.int32)
    place = jnp.zeros(rows.shape, jnp.int32)
    for start, count, lv in plan.segments:
        if start < high and start + count > low:
            inside = (rows >= start) & (rows < start + count)
            level = jnp.where(inside, lv, level)
            place = jnp.where(inside, spot * plan.own[lv] - NR + rows - start, place)
    if high > plan.upper:
        owner = lax.shift_right_arithmetic(rows - plan.upper, 4)
        within = (rows - plan.upper) & (NR - 1)
        for lv, first, count in plan.slot:
            inside = (rows >= plan.upper) & (within >= first) & (within < first + count)
            level = jnp.where(inside, lv, level)
            place = jnp.where(inside, owner * count + within - first, place)
    return level, place


def log_counts(plan, tile, spot, length):
    first, count, window, level = tile
    row_at = first + lax.broadcasted_iota(jnp.int32, (count, 128), 0)
    key_at = window + lax.broadcasted_iota(jnp.int32, (8, 128), 1)
    row_level, row_place = row_places(plan, row_at, first, first + count, spot)
    key_level, key_place = row_places(plan, key_at, window, window + 128, spot)
    span = lax.shift_left(jnp.ones_like(key_level), jnp.maximum(key_level, 0))
    counts = jnp.clip(length - span * key_place, 0, span)
    usable = (counts > 0) & (key_place >= 0) & (key_level >= 0)
    logs = jnp.where(usable, jnp.log(jnp.maximum(counts, 1).astype(jnp.float32)), NEG)
    coarse = lambda level_at, place_at, by: level_at * 65536 + lax.shift_right_arithmetic(place_at, by)
    key_block = coarse(key_level, key_place, 4)[:1]
    key_half = coarse(key_level, key_place, 3)[:1]
    allowed = jnp.abs(coarse(row_level, row_place, 4) - key_block) <= 1
    if level != 0:
        apart = jnp.abs(coarse(row_level, row_place, 3) - key_half) >= 2
        allowed = allowed & (apart if level is not None else apart | (row_level == 0)) & (row_level >= 0)
    return jnp.where(allowed, logs[:1], NEG)


def pool_bounds(plan, shape, dim):
    row = lax.broadcasted_iota(jnp.int32, shape, dim)
    low = jnp.full(shape, -1, jnp.int32)
    size = jnp.zeros(shape, jnp.int32)
    level = jnp.zeros(shape, jnp.int32)
    parts = [(plan.pool_at[lv], plan.own[lv], lv) for lv in range(1, plan.levels)]
    parts += [(plan.pool_upper + first, count, lv) for lv, first, count in plan.slot]
    for start, count, lv in parts:
        inside = (row >= start) & (row < start + count)
        low = jnp.where(inside, (row - start) << lv, low)
        size = jnp.where(inside, 1 << lv, size)
    return low, size


def whole_layer(plan, dims, net_count, *refs):
    (extents, own_weights, own_norms, tokens_in, cotangent_in,
     out_rows, out_grads, weight_grads, norm_grads,
     weights, norms, tokens, cotangent, ext, logs, pool, unpool, inverse, work,
     attended, ratio, recip, normed, scaled, rstd, grad_ext, total_ext, residual, acc, acc2, totals, result, row_grads,
     grads, got1, got2, got3, got4, norm_got,
     load_sem, send_sem, recv_sem) = refs
    part, width, pair, hidden = dims
    f32, bf16 = jnp.float32, jnp.bfloat16
    models = weights.shape[0]
    ax, sq, az = lax.axis_index("dp"), lax.axis_index("seq"), lax.axis_index("mp")
    ay, ac = sq // 2, sq % 2
    spot = sq * 2 + ax
    spots = plan.spots
    length = extents[az]
    qkv = 3 * pair

    def device(x, y, c, z):
        return (x, y * 2 + c, z)

    def at_spot(place):
        return (place % 2, place // 2, az)

    barrier = pltpu.get_barrier_semaphore()
    for step in range(1, spots):
        pl.semaphore_signal(barrier, inc=1, device_id=at_spot((spot + step) % spots), device_id_type=MESH)
    for step in range(1, models):
        pl.semaphore_signal(barrier, inc=1, device_id=device(ax, ay, ac, (az + step) % models), device_id_type=MESH)
    load_tokens = pltpu.make_async_copy(tokens_in.at[az, 0], tokens, load_sem.at[0])
    load_cotangent = pltpu.make_async_copy(cotangent_in.at[az, 0], cotangent, load_sem.at[1])
    load_tokens.start()
    load_cotangent.start()
    weights[az, ax, ay, ac] = own_weights[...]
    norms[spot] = own_norms[...]
    pl.semaphore_wait(barrier, spots - 1 + models - 1)

    used = [0]
    sent = []

    def copy(src, dst, to):
        i = used[0]
        used[0] += 1
        assert i < net_count
        return pltpu.make_async_remote_copy(
            src_ref=src, dst_ref=dst, send_sem=send_sem.at[i], recv_sem=recv_sem.at[i],
            device_id=to, device_id_type=MESH)

    def send(src, dst, to):
        c = copy(src, dst, to)
        c.start()
        sent.append((c, None))
        return c

    x_peer = device(1 - ax, ay, ac, az)
    y_peer = device(ax, 1 - ay, ac, az)
    c_peer = device(ax, ay, 1 - ac, az)

    chunks = [(0, 2 * pair, True), (2 * pair, 2 * pair, False),
              (4 * pair, hidden, True), (4 * pair + hidden, hidden, False)]

    def gather_z(chunk):
        col, count, _ = chunk
        cols = pl.ds(col, count)
        place = weights.at[az, ax, ay, ac, :, cols]
        return [send(own_weights.at[:, cols], place, device(ax, ay, ac, (az + step) % models))
                for step in range(1, models)]

    def gather_first(chunk):
        col, count, x_first = chunk
        block = weights.at[:, ax, ay, ac, :, pl.ds(col, count)]
        return [send(block, block, x_peer if x_first else y_peer)]

    def gather_second(chunk):
        col, count, x_first = chunk
        cols = pl.ds(col, count)
        block = weights.at[:, :, ay, ac, :, cols] if x_first else weights.at[:, ax, :, ac, :, cols]
        return [send(block, block, y_peer if x_first else x_peer)]

    def gather_core(chunk):
        col, count, _ = chunk
        block = weights.at[:, :, :, ac, :, pl.ds(col, count)]
        return [send(block, block, c_peer)]

    def arrive(copies):
        for c in copies:
            c.wait_recv()

    norm_copies = [send(own_norms, norms.at[spot], at_spot((spot + step) % spots)) for step in range(1, spots)]
    flight = [gather_z(chunk) for chunk in chunks]

    low, size = pool_bounds(plan, (part, 128), 0)
    for block in range(part // 128):
        token_at = block * 128 + lax.broadcasted_iota(jnp.int32, (part, 128), 1)
        member = (token_at >= low) & (token_at < low + size) & (token_at + spot * part < length)
        pool[:, block * 128:(block + 1) * 128] = jnp.where(member, 1.0, 0.0).astype(bf16)
    first_token = spot * part + low
    counts = jnp.clip(length - first_token, 0, size)
    inverse[...] = 1.0 / jnp.maximum(counts, 1).astype(f32)
    low, size = pool_bounds(plan, (8, part), 1)
    token_at = lax.broadcasted_iota(jnp.int32, (part, part), 0)
    member = (token_at >= low[:1]) & (token_at < (low + size)[:1])
    unpool[...] = jnp.where(member, 1.0, 0.0).astype(bf16)
    load_tokens.wait()

    def statistics(values):
        center = values - jnp.mean(values, axis=-1, keepdims=True)
        spread = jnp.mean(center * center, axis=-1, keepdims=True)
        scale = lax.rsqrt(spread + 1e-05)
        return center * scale, scale

    xhat, scale = statistics(tokens[...].astype(f32))
    scaled[...] = xhat
    rstd[...] = jnp.broadcast_to(scale, (part, 128))
    arrive(flight[0])
    flight[0] = gather_first(chunks[0])
    arrive(flight[1])
    flight[1] = gather_first(chunks[1])
    for i, tile in enumerate(plan.tiles):
        logs[i, 0:tile[1]] = log_counts(plan, tile, spot, length)
    arrive(norm_copies)
    gains = norms[0]
    for i in range(1, spots):
        gains = gains + norms[i]
    pre_gain, pre_shift, mid_gain, mid_shift = (gains[i:i + 1] for i in range(4))
    normed[...] = (scaled[...] * pre_gain + pre_shift).astype(bf16)
    for i in (0, 1):
        arrive(flight[i])
        flight[i] = gather_second(chunks[i])
    for i in (0, 1):
        arrive(flight[i])
        flight[i] = gather_core(chunks[i])
    for i in (2, 3):
        arrive(flight[i])
        flight[i] = gather_first(chunks[i])

    def weight_cols(m, col, count):
        return weights[m, :, :, :, :, col:col + count].reshape(width, count)

    arrive(flight[0])
    arrive(flight[1])

    def project(m, carry):
        rows = nn(normed[...], weight_cols(m, 0, qkv)).astype(bf16)
        ext[m, NR:NR + part, :] = rows
        sums = nn(pool[...], rows)
        means = (sums * jnp.concatenate([inverse[...]] * 3, axis=1)).astype(bf16)
        for lv in range(1, plan.levels):
            ext[m, plan.at[lv] + NR:plan.at[lv] + NR + plan.own[lv], :] = means[plan.pool_at[lv]:plan.pool_at[lv] + plan.own[lv]]
        ext[m, pl.ds(plan.upper + spot * NR, NR), :] = means[plan.pool_upper:plan.pool_upper + NR]
        return carry

    lax.fori_loop(0, models, project, 0)

    is_first, is_last = spot == 0, spot == spots - 1

    def exchange(arrays):
        pending = []
        for ref in arrays:
            lead = (slice(None),) * (len(ref.shape) - 2)
            for lv in range(plan.levels):
                start, rows = plan.at[lv], plan.own[lv]
                to_right = copy(ref.at[lead + (pl.ds(start + rows, NR), slice(None))],
                                ref.at[lead + (pl.ds(start, NR), slice(None))], at_spot((spot + 1) % spots))
                to_left = copy(ref.at[lead + (pl.ds(start + NR, NR), slice(None))],
                               ref.at[lead + (pl.ds(start + NR + rows, NR), slice(None))],
                               at_spot((spot + spots - 1) % spots))
                pending.append((to_right, to_left))
        uppers = []
        for ref in arrays:
            lead = (slice(None),) * (len(ref.shape) - 2)
            block = ref.at[lead + (pl.ds(plan.upper + spot * NR, NR), slice(None))]
            for step in range(1, spots):
                uppers.append(copy(block, block, at_spot((spot + step) % spots)))

        @pl.when(jnp.logical_not(is_last))
        def _():
            for to_right, _ in pending:
                to_right.start()

        @pl.when(jnp.logical_not(is_first))
        def _():
            for _, to_left in pending:
                to_left.start()

        for c in uppers:
            c.start()

        @pl.when(is_first)
        def _():
            for ref in arrays:
                lead = (slice(None),) * (len(ref.shape) - 2)
                for lv in range(plan.levels):
                    place = lead + (slice(plan.at[lv], plan.at[lv] + NR), slice(None))
                    ref[place] = jnp.zeros(ref.shape[:-2] + (NR, ref.shape[-1]), ref.dtype)

        @pl.when(is_last)
        def _():
            for ref in arrays:
                lead = (slice(None),) * (len(ref.shape) - 2)
                for lv in range(plan.levels):
                    row = plan.at[lv] + NR + plan.own[lv]
                    ref[lead + (slice(row, row + NR), slice(None))] = jnp.zeros(
                        ref.shape[:-2] + (NR, ref.shape[-1]), ref.dtype)

        def wait():
            @pl.when(jnp.logical_not(is_first))
            def _():
                for to_right, _ in pending:
                    to_right.wait_recv()

            @pl.when(jnp.logical_not(is_last))
            def _():
                for _, to_left in pending:
                    to_left.wait_recv()

            for c in uppers:
                c.wait_recv()

        def done():
            @pl.when(jnp.logical_not(is_last))
            def _():
                for to_right, _ in pending:
                    to_right.wait_send()

            @pl.when(jnp.logical_not(is_first))
            def _():
                for _, to_left in pending:
                    to_left.wait_send()

            for c in uppers:
                c.wait_send()

        return wait, done

    rims_wait, rims_done = exchange([ext])

    lane = lax.broadcasted_iota(jnp.int32, (1, pair), 1)
    left_head = lane < HD

    def both_heads(rows):
        zero = jnp.zeros_like(rows)
        return jnp.concatenate([jnp.where(left_head, rows, zero), jnp.where(left_head, zero, rows)], axis=0)

    def joined(rows):
        half = rows.shape[0] // 2
        return jnp.where(left_head, rows[:half], rows[half:])

    ones = jnp.ones((128, 128), bf16)
    slot_row = pl.multiple_of(spot * NR, NR)

    def tile_weights(m, index, rows_at, count, window, own_slot=False):
        queries = both_heads(ext[m, rows_at, 0:pair])
        keys = ext[m, window:window + 128, pair:2 * pair]
        values = jnp.concatenate([ext[m, window:window + 128, 2 * pair:3 * pair], ones], axis=1)
        mask = logs[index, pl.ds(slot_row, NR)] if own_slot else logs[index, 0:count]
        weight = jnp.exp(nt(queries, keys) + jnp.concatenate([mask, mask], axis=0))
        return queries, keys, values, weight

    def attend(tiles):
        def body(m, carry):
            for tile in tiles:
                first, count, window, _ = tile
                own_slot = first == plan.upper
                if own_slot:
                    rows_at, count = pl.ds(pl.multiple_of(plan.upper + slot_row, NR), NR), NR
                else:
                    rows_at = slice(first, first + count)
                _, _, values, weight = tile_weights(m, plan.tiles.index(tile), rows_at, count, window, own_slot)
                both = nn(weight.astype(bf16), values)
                work[m, first:first + count, 0:pair] = joined(both[:, :128])
                work[m, first:first + count, pair:2 * pair] = joined(both[:, 128:])
            return carry

        lax.fori_loop(0, models, body, 0)

    attend(plan.inner)
    for i in (2, 3):
        arrive(flight[i])
        flight[i] = gather_second(chunks[i])
    rims_wait()
    attend(plan.outer)
    for i in (2, 3):
        arrive(flight[i])
        flight[i] = gather_core(chunks[i])

    def coarse_rows(m, cols, slot_at):
        rows = [work[m, plan.at[lv] + NR:plan.at[lv] + NR + plan.own[lv], 0:cols] for lv in range(1, plan.levels)]
        return jnp.concatenate(rows + [work[m, slot_at, 0:cols]], axis=0)

    def spread_out(rows):
        high, rest = halves(rows)
        return nn(unpool[...], high) + nn(unpool[...], rest)

    def normalise(m, carry):
        both = spread_out(coarse_rows(m, 2 * pair, slice(plan.upper, plan.upper + NR)))
        both = both + work[m, NR:NR + part, 0:2 * pair]
        inv_total = 1.0 / both[:, pair:]
        quotient = both[:, :pair] * inv_total
        ratio[m] = quotient
        recip[m] = inv_total
        attended[m] = quotient.astype(bf16)
        return carry

    lax.fori_loop(0, models, normalise, 0)

    residual[...] = tokens[...].astype(f32)

    def merge(m, carry):
        residual[...] += nt(attended[m], weight_cols(m, qkv, pair))
        return carry

    lax.fori_loop(0, models, merge, 0)
    after = residual[...]
    mid_hat, mid_scale = statistics(after)
    mid = (mid_hat * mid_gain + mid_shift).astype(bf16)
    mid_t = mid.T
    load_cotangent.wait()
    row_at = lax.broadcasted_iota(jnp.int32, (part, 1), 0) + spot * part
    valid = row_at < length
    out_grad = jnp.where(valid, cotangent[...], jnp.zeros((), bf16))
    out_grad_t = out_grad.T
    arrive(flight[2])
    arrive(flight[3])
    acc[...] = jnp.zeros(acc.shape, f32)
    acc2[...] = jnp.zeros(acc.shape, f32)
    block_shape = grads.shape[1:5] + (hidden,)

    def feed(m, carry):
        expand = weight_cols(m, 4 * pair, hidden)
        contract_t = weight_cols(m, 4 * pair + hidden, hidden)
        up = nn(mid, expand)
        phi = 0.5 + 0.5 * lax.erf(up * (0.5 ** 0.5))
        act = (up * phi).astype(bf16)
        slope = phi + up * (jnp.exp(-0.5 * up * up) * 0.3989422804014327)
        acc[...] += nt(act, contract_t)
        hidden_grad = (nn(out_grad, contract_t) * slope).astype(bf16)
        grads[m, :, :, :, :, 4 * pair:4 * pair + hidden] = nn(mid_t, hidden_grad).astype(bf16).reshape(block_shape)
        grads[m, :, :, :, :, 4 * pair + hidden:4 * pair + 2 * hidden] = nn(out_grad_t, act).astype(bf16).reshape(block_shape)
        acc2[...] += nt(hidden_grad, expand)
        return carry

    lax.fori_loop(0, models, feed, 0)
    result[...] = jnp.where(valid, after + acc[...], 0.0).astype(bf16)
    mid_grad = acc2[...]

    def reduce_core(chunk):
        col, count, _ = chunk
        cols = pl.ds(col, count)
        return [send(grads.at[:, :, :, 1 - ac, :, cols], got1.at[:, :, :, :, cols], c_peer)]

    def reduce_first(chunk):
        col, count, x_first = chunk
        cols = pl.ds(col, count)
        got1[:, :, :, :, cols] = got1[:, :, :, :, cols] + grads[:, :, :, ac, :, cols]
        src = got1.at[:, 1 - ax, :, :, cols] if x_first else got1.at[:, :, 1 - ay, :, cols]
        return [send(src, got2.at[:, :, :, cols], x_peer if x_first else y_peer)]

    def reduce_second(chunk):
        col, count, x_first = chunk
        cols = pl.ds(col, count)
        mine = got1[:, ax, :, :, cols] if x_first else got1[:, :, ay, :, cols]
        got2[:, :, :, cols] = got2[:, :, :, cols] + mine
        src = got2.at[:, 1 - ay if x_first else 1 - ax, :, cols]
        return [send(src, got3.at[:, :, cols], y_peer if x_first else x_peer)]

    def reduce_z(chunk):
        col, count, x_first = chunk
        cols = pl.ds(col, count)
        got3[:, :, cols] = got3[:, :, cols] + got2[:, ay if x_first else ax, :, cols]
        return [send(got3.at[(az + step) % models, :, cols], got4.at[step - 1, :, cols],
                     device(ax, ay, ac, (az + step) % models)) for step in range(1, models)]

    def reduce_end(chunk):
        col, count, _ = chunk
        cols = pl.ds(col, count)
        total = got3[az, :, cols].astype(f32)
        for step in range(1, models):
            total = total + got4[step - 1, :, cols].astype(f32)
        weight_grads[:, cols] = total

    back = {i: reduce_core(chunks[i]) for i in (2, 3)}

    def rows_home(source, target):
        share = part // models
        target[az] = source[pl.ds(pl.multiple_of(az * share, share), share), :]
        return [send(source.at[pl.ds(pl.multiple_of(((az + step) % models) * share, share), share), :],
                     target.at[az], device(ax, ay, ac, (az + step) % models)) for step in range(1, models)]

    def norm_back(grad, hat, scale_row, gain):
        scaled_grad = grad * gain
        mean_grad = jnp.mean(scaled_grad, axis=-1, keepdims=True)
        mean_along = jnp.mean(scaled_grad * hat, axis=-1, keepdims=True)
        return scale_row * (scaled_grad - mean_grad - hat * mean_along)

    through = out_grad.astype(f32) + norm_back(mid_grad, mid_hat, mid_scale, mid_gain)
    residual[...] = through
    branch = through.astype(bf16)
    branch_t = branch.T
    norm_sums = [jnp.sum(mid_grad * mid_hat, axis=0, keepdims=True), jnp.sum(mid_grad, axis=0, keepdims=True)]

    merge_shape = grads.shape[1:5] + (pair,)
    select_row = lax.broadcasted_iota(jnp.int32, (pair, 128), 0) // HD
    select_col = lax.broadcasted_iota(jnp.int32, (pair, 128), 1) // 2

    totals[...] = jnp.zeros(totals.shape, f32)

    def unmerge(m, carry):
        grads[m, :, :, :, :, qkv:qkv + pair] = nn(branch_t, attended[m]).astype(bf16).reshape(merge_shape)
        attended_grad = nn(branch, weight_cols(m, qkv, pair)) * recip[m]
        fine = attended_grad.astype(bf16)
        grad_ext[m, NR:NR + part, :] = fine
        sums = nn(pool[...], fine).astype(bf16)
        for lv in range(1, plan.levels):
            grad_ext[m, plan.at[lv] + NR:plan.at[lv] + NR + plan.own[lv], :] = sums[plan.pool_at[lv]:plan.pool_at[lv] + plan.own[lv]]
        grad_ext[m, pl.ds(pl.multiple_of(plan.upper + slot_row, NR), NR), :] = sums[plan.pool_upper:plan.pool_upper + NR]
        high, rest = halves(attended_grad * ratio[m])
        chosen = jnp.where(select_row + 2 * m == select_col, -1.0, 0.0).astype(bf16)
        totals[...] += nn(high, chosen) + nn(rest, chosen)
        return carry

    lax.fori_loop(0, models, unmerge, 0)
    even = lax.broadcasted_iota(jnp.int32, (1, 128), 1) % 2 == 0

    def high_rest(values):
        high, rest = halves(values)
        return jnp.where(even, high, rest)

    high, rest = halves(totals[...])
    total_ext[NR:NR + part, :] = jnp.where(even, high, rest)
    sums = high_rest(nn(pool[...], high) + nn(pool[...], rest))
    for lv in range(1, plan.levels):
        total_ext[plan.at[lv] + NR:plan.at[lv] + NR + plan.own[lv], :] = sums[plan.pool_at[lv]:plan.pool_at[lv] + plan.own[lv]]
    total_ext[pl.ds(pl.multiple_of(plan.upper + slot_row, NR), NR), :] = sums[plan.pool_upper:plan.pool_upper + NR]
    back_wait, back_done = exchange([grad_ext, total_ext])
    rows_out = rows_home(result, out_rows)

    head_of_lane = lax.broadcasted_iota(jnp.int32, (1, 128), 1) // 2

    def clear(m, carry):
        work[m] = jnp.zeros(work.shape[1:], f32)
        return carry

    lax.fori_loop(0, models, clear, 0)

    def attend_back(tiles):
        def body(m, carry):
            for tile in tiles:
                first, count, window, _ = tile
                rows_at = slice(first, first + count)
                queries, keys, values, weight = tile_weights(m, plan.tiles.index(tile), rows_at, count, window)
                numer = both_heads(grad_ext[m, rows_at, :])
                tot = total_ext[rows_at, :]
                zero = jnp.zeros_like(tot)
                tots = jnp.concatenate([jnp.where(head_of_lane == 2 * m, tot, zero),
                                        jnp.where(head_of_lane == 2 * m + 1, tot, zero)], axis=0)
                score_grad = (weight * nt(jnp.concatenate([numer, tots], axis=1), values)).astype(bf16)
                work[m, rows_at, 0:pair] = joined(nn(score_grad, keys))
                key_rows = slice(window, window + 128)
                work[m, key_rows, pair:2 * pair] += tn(score_grad, queries)
                work[m, key_rows, 2 * pair:3 * pair] += tn(weight.astype(bf16), numer)
            return carry

        lax.fori_loop(0, models, body, 0)

    attend_back(plan.inner)
    for i in (2, 3):
        arrive(back[i])
        back[i] = reduce_first(chunks[i])
    back_wait()
    attend_back(plan.outer)
    for i in (2, 3):
        arrive(back[i])
        back[i] = reduce_second(chunks[i])

    normed_t = normed[...].T
    qkv_shape = grads.shape[1:5] + (qkv,)
    query_scale = jnp.where(lax.broadcasted_iota(jnp.int32, (1, qkv), 1) < pair, HD ** -0.5, 1.0)

    acc[...] = jnp.zeros(acc.shape, f32)

    def finish(m, carry):
        coarse = coarse_rows(m, qkv, pl.ds(pl.multiple_of(plan.upper + slot_row, NR), NR))
        spread = spread_out(coarse * jnp.concatenate([inverse[...]] * 3, axis=1))
        rows = (work[m, NR:NR + part, :] + jnp.where(valid, spread, 0.0)).astype(bf16)
        grads[m, :, :, :, :, 0:qkv] = (nn(normed_t, rows) * query_scale).astype(bf16).reshape(qkv_shape)
        acc[...] += nt(rows, weight_cols(m, 0, qkv))
        return carry

    lax.fori_loop(0, models, finish, 0)
    normed_grad = acc[...]
    for i in (0, 1):
        back[i] = reduce_core(chunks[i])
    for i in (2, 3):
        arrive(back[i])
        back[i] = reduce_z(chunks[i])
    hat = scaled[...]
    row_grads[...] = (residual[...] + norm_back(normed_grad, hat, rstd[:, 0:1], pre_gain)).astype(bf16)
    grads_out = rows_home(row_grads, out_grads)
    norm_sums = [jnp.sum(normed_grad * hat, axis=0, keepdims=True), jnp.sum(normed_grad, axis=0, keepdims=True)] + norm_sums
    norm_got[0] = jnp.concatenate(norm_sums + [jnp.zeros((4, width), f32)], axis=0)
    norm_peers = [[c_peer], [y_peer], [x_peer], [device(ax, ay, ac, (az + step) % models) for step in range(1, models)]]

    def norm_send(stage):
        first = 1 + 2 * stage
        return [send(norm_got.at[2 * stage], norm_got.at[first + i], to) for i, to in enumerate(norm_peers[stage])]

    def norm_sum(stage):
        total = norm_got[2 * stage]
        for i in range(len(norm_peers[stage])):
            total = total + norm_got[1 + 2 * stage + i]
        return total

    small = norm_send(0)
    stages = [reduce_first, reduce_second, reduce_z]
    for step, stage in enumerate(stages):
        for i in (0, 1):
            arrive(back[i])
            back[i] = stage(chunks[i])
        arrive(small)
        norm_got[2 * step + 2] = norm_sum(step)
        small = norm_send(step + 1)
    for i in (2, 3, 0, 1):
        arrive(back[i])
        reduce_end(chunks[i])
    arrive(small)
    norm_grads[...] = norm_sum(3)
    arrive(rows_out)
    arrive(grads_out)
    for c, _ in sent:
        c.wait_send()
    rims_done()
    back_done()


def fast_body(plan, incoming_embeddings, output_sensitivity, sequence_extents, asking_projector, lookup_projector,
              content_projector, attention_combiner, feedforward_expand, feedforward_contract,
              attention_norm_scale, attention_norm_bias, feedforward_norm_scale, feedforward_norm_bias):
    bf16, f32 = jnp.bfloat16, jnp.float32
    models = lax.axis_size("mp")
    seqs, _, part, width = incoming_embeddings.shape
    strip, pair = asking_projector.shape
    hidden = feedforward_expand.shape[1]
    owner = lax.axis_index("dp") * lax.axis_size("seq") + lax.axis_index("seq")
    own_weights = jnp.concatenate(
        [asking_projector * jnp.asarray(HD ** -0.5, bf16), lookup_projector, content_projector,
         attention_combiner.T, feedforward_expand, feedforward_contract.T], axis=1)
    columns = own_weights.shape[1]
    norm_parts = jnp.stack([attention_norm_scale, attention_norm_bias, feedforward_norm_scale, feedforward_norm_bias])
    own_norms = lax.dynamic_update_slice(
        jnp.zeros((8, width), f32), norm_parts.astype(f32), (0, owner * strip))
    share = part // models
    spots, rows = plan.spots, plan.rows
    deep = (2, 2, 2, strip, columns)
    net_count = 128
    vmem = pltpu.VMEM
    scratch = [
        vmem((models,) + deep, bf16), vmem((spots, 8, width), f32), vmem((part, width), bf16), vmem((part, width), bf16),
        vmem((models, rows, 3 * pair), bf16), vmem((len(plan.tiles), 128, 128), f32),
        vmem((part, part), bf16), vmem((part, part), bf16), vmem((part, 128), f32), vmem((models, rows, 3 * pair), f32),
        vmem((models, part, pair), bf16), vmem((models, part, pair), f32), vmem((models, part, pair), f32),
        vmem((part, width), bf16), vmem((part, width), f32), vmem((part, 128), f32),
        vmem((models, rows, pair), bf16), vmem((rows, 128), bf16), vmem((part, width), f32), vmem((part, width), f32),
        vmem((part, width), f32), vmem((part, 128), f32), vmem((part, width), bf16), vmem((part, width), bf16),
        vmem((models,) + deep, bf16), vmem((models, 2, 2, strip, columns), bf16), vmem((models, 2, strip, columns), bf16),
        vmem((models, strip, columns), bf16), vmem((models - 1, strip, columns), bf16), vmem((10, 8, width), f32),
        pltpu.SemaphoreType.DMA((2,)), pltpu.SemaphoreType.DMA((net_count,)), pltpu.SemaphoreType.DMA((net_count,)),
    ]
    any_space, in_vmem = pl.BlockSpec(memory_space=pl.ANY), pl.BlockSpec(memory_space=pltpu.VMEM)
    out_rows, out_grads, weight_grads, norm_grads = pl.pallas_call(
        functools.partial(whole_layer, plan, (part, width, pair, hidden), net_count),
        out_shape=(jax.ShapeDtypeStruct((seqs, share, width), bf16), jax.ShapeDtypeStruct((seqs, share, width), bf16),
                   jax.ShapeDtypeStruct((strip, columns), f32), jax.ShapeDtypeStruct((8, width), f32)),
        in_specs=[pl.BlockSpec(memory_space=pltpu.SMEM), in_vmem, in_vmem, any_space, any_space],
        out_specs=(in_vmem,) * 4,
        scratch_shapes=scratch,
        compiler_params=pltpu.CompilerParams(collective_id=0, has_side_effects=True, vmem_limit_bytes=60 * 2 ** 20),
        name="layer",
    )(sequence_extents, own_weights, own_norms, incoming_embeddings, output_sensitivity)
    ends = [0, pair, 2 * pair, 3 * pair, 4 * pair, 4 * pair + hidden, columns]
    query_grad, key_grad, value_grad, merge_t, up_grad, down_t = (
        weight_grads[:, low:high] for low, high in zip(ends, ends[1:]))
    mine = lax.dynamic_slice(norm_grads, (0, owner * strip), (4, strip))
    return (out_rows[:, None], out_grads[:, None], query_grad, key_grad, value_grad, merge_t.T, up_grad, down_t.T,
            mine[0], mine[1], mine[2], mine[3])


def solution(mesh):
    in_specs = (
        P(None, "seq", "dp", None),
        P(None, "seq", "dp", None),
        P(),
        P(("dp", "seq"), "mp"),
        P(("dp", "seq"), "mp"),
        P(("dp", "seq"), "mp"),
        P("mp", ("dp", "seq")),
        P(("dp", "seq"), "mp"),
        P("mp", ("dp", "seq")),
        P(("dp", "seq")),
        P(("dp", "seq")),
        P(("dp", "seq")),
        P(("dp", "seq")),
    )
    out_specs = (
        P(None, "seq", ("dp", "mp"), None),
        P(None, "seq", ("dp", "mp"), None),
        P(("dp", "seq"), "mp"),
        P(("dp", "seq"), "mp"),
        P(("dp", "seq"), "mp"),
        P("mp", ("dp", "seq")),
        P(("dp", "seq"), "mp"),
        P("mp", ("dp", "seq")),
        P(("dp", "seq")),
        P(("dp", "seq")),
        P(("dp", "seq")),
        P(("dp", "seq")),
    )
    sizes = (mesh.shape["dp"], mesh.shape["seq"], mesh.shape["mp"])

    def chosen(*arrays):
        seqs, _, part, width = arrays[0].shape
        if sizes == (2, 4, 4) and seqs == sizes[2] and part == width == 512 and arrays[3].shape[1] == 128:
            return fast_body(Plan(part, sizes[0] * sizes[1]), *arrays)
        return general_body(*arrays)

    return jax.shard_map(chosen, mesh=mesh, in_specs=in_specs, out_specs=out_specs, check_vma=False)
```

```python
import functools

import jax
import jax.numpy as jnp
from jax import lax
from jax.experimental import pallas as pl
from jax.experimental.pallas import tpu as pltpu
from jax.sharding import PartitionSpec as P

HD = 64
NR = 16


def cut_along(x, dim, count):
    before, after = (x.shape[:dim], x.shape[dim + 1 :])
    return jnp.moveaxis(x.reshape(*before, count, -1, *after), dim, 0)


def summed_on_arrival(x, axis, dim):
    count = lax.axis_size(axis)
    blocks = lax.all_to_all(cut_along(x, dim, count), axis, 0, 0, tiled=True)
    return jnp.sum(blocks.astype(jnp.float32), axis=0)


def sent_together(arrays, axis, dim, along):
    ends, at = ([], 0)
    for a in arrays[:-1]:
        at += a.shape[along]
        ends.append(at)
    both = jnp.concatenate(arrays, axis=along)
    return tuple(jnp.split(summed_on_arrival(both, axis, dim), ends, axis=along))


def norm_rows(values, gain_row, shift_row):
    center = values - jnp.mean(values, axis=-1, keepdims=True)
    spread = jnp.mean(center * center, axis=-1, keepdims=True)
    return center * lax.rsqrt(spread + 1e-05) * gain_row + shift_row


def norm_gain_parts(values, grad_rows):
    center = values - jnp.mean(values, axis=-1, keepdims=True)
    spread = jnp.mean(center * center, axis=-1, keepdims=True)
    scaled = center * lax.rsqrt(spread + 1e-05)
    return (jnp.sum(grad_rows * scaled, axis=0), jnp.sum(grad_rows, axis=0))


def gelu_exact(values):
    return jax.nn.gelu(values, approximate=False)


def dot_plain(left_mat, right_mat):
    return jnp.dot(left_mat, right_mat, preferred_element_type=jnp.float32)


def dot_inner(left_mat, right_mat):
    return lax.dot_general(
        left_mat, right_mat, (((0,), (0,)), ((), ())), preferred_element_type=jnp.float32
    )


def dot_outer(left_mat, right_mat):
    return lax.dot_general(
        left_mat, right_mat, (((1,), (1,)), ((), ())), preferred_element_type=jnp.float32
    )


def group_sum(values, group_width):
    return jnp.sum(
        values.reshape((values.shape[0] // group_width, group_width) + values.shape[1:]), axis=1
    )


def block_shape(coarse_rows):
    query_len = min(coarse_rows, 512)
    span_len = query_len + 2 * NR
    window_len = -(-span_len // 128) * 128
    return (query_len, span_len, window_len)


def window_mask(level_at, first_row, query_len, window_len, span_len):
    rows_at = first_row + jnp.arange(query_len, dtype=jnp.int32)[:, None]
    keys_at = first_row + jnp.arange(window_len, dtype=jnp.int32)[None, :]
    inside = keys_at - first_row < span_len
    allowed = jnp.abs(rows_at // NR + 1 - keys_at // NR) <= 1
    if level_at > 0:
        half_block = NR // 2
        allowed = allowed & (jnp.abs(rows_at // half_block + 2 - keys_at // half_block) >= 2)
    return (allowed & inside).astype(jnp.float32)


def level_forward(query_rows, pair_wide, count_wide, level_at):
    coarse_rows = query_rows.shape[0]
    columns = query_rows.shape[1]
    heads_here = columns // HD
    query_len, span_len, window_len = block_shape(coarse_rows)
    tail_pad = window_len - span_len
    pair_padded = jnp.pad(pair_wide, ((0, tail_pad), (0, 0)))
    count_padded = jnp.pad(count_wide, (0, tail_pad))
    weight_list = []
    total_parts = []
    numer_parts = []
    for block_at in range(coarse_rows // query_len):
        first_row = block_at * query_len
        query_block = query_rows[first_row : first_row + query_len]
        pair_block = pair_padded[first_row : first_row + window_len]
        count_block = count_padded[first_row : first_row + window_len]
        keep_mask = (
            window_mask(level_at, first_row, query_len, window_len, span_len) * count_block[None, :]
        )
        head_weights = []
        head_totals = []
        head_numers = []
        for head_at in range(heads_here):
            head_cols = slice(head_at * HD, (head_at + 1) * HD)
            value_cols = slice(columns + head_at * HD, columns + (head_at + 1) * HD)
            scores = dot_outer(query_block[:, head_cols], pair_block[:, head_cols]) * HD ** (-0.5)
            weight = jnp.exp(scores) * keep_mask
            head_weights.append(weight)
            head_totals.append(jnp.sum(weight, axis=-1))
            head_numers.append(dot_plain(weight.astype(jnp.bfloat16), pair_block[:, value_cols]))
        weight_list.append(head_weights)
        total_parts.append(jnp.stack(head_totals, axis=1))
        numer_parts.append(jnp.concatenate(head_numers, axis=1))
    totals = jnp.concatenate(total_parts, axis=0)
    numer_part = jnp.concatenate(numer_parts, axis=0).reshape(coarse_rows, heads_here, HD)
    return ((query_rows, pair_padded, weight_list), totals, numer_part)


def level_backward(level_kept, numer_rows, total_rows):
    query_rows, pair_padded, weight_list = level_kept
    coarse_rows = query_rows.shape[0]
    columns = query_rows.shape[1]
    heads_here = columns // HD
    query_len, span_len, window_len = block_shape(coarse_rows)
    numer_flat = numer_rows.reshape(coarse_rows, columns)
    pair_grad = jnp.zeros(pair_padded.shape, jnp.float32)
    query_parts = []
    for block_at in range(coarse_rows // query_len):
        first_row = block_at * query_len
        query_block = query_rows[first_row : first_row + query_len]
        pair_block = pair_padded[first_row : first_row + window_len]
        numer_block = numer_flat[first_row : first_row + query_len]
        total_block = total_rows[first_row : first_row + query_len]
        query_heads = []
        key_heads = []
        value_heads = []
        for head_at in range(heads_here):
            head_cols = slice(head_at * HD, (head_at + 1) * HD)
            value_cols = slice(columns + head_at * HD, columns + (head_at + 1) * HD)
            weight = head_weights = weight_list[block_at][head_at]
            grad_here = numer_block[:, head_cols]
            score_grad = (
                (dot_outer(grad_here, pair_block[:, value_cols]) + total_block[:, head_at][:, None])
                * weight
            ).astype(jnp.bfloat16)
            query_heads.append(dot_plain(score_grad, pair_block[:, head_cols]) * HD ** (-0.5))
            key_heads.append(dot_inner(score_grad, query_block[:, head_cols]) * HD ** (-0.5))
            value_heads.append(dot_inner(head_weights.astype(jnp.bfloat16), grad_here))
        query_parts.append(jnp.concatenate(query_heads, axis=1))
        block_grad = jnp.concatenate(key_heads + value_heads, axis=1)
        pair_grad = pair_grad + jnp.pad(
            block_grad, ((first_row, pair_padded.shape[0] - first_row - window_len), (0, 0))
        )
    query_grad = jnp.concatenate(query_parts, axis=0)
    return (query_grad, pair_grad[: coarse_rows + 2 * NR])


def general_body(
    incoming_embeddings,
    output_sensitivity,
    sequence_extents,
    asking_projector,
    lookup_projector,
    content_projector,
    attention_combiner,
    feedforward_expand,
    feedforward_contract,
    attention_norm_scale,
    attention_norm_bias,
    feedforward_norm_scale,
    feedforward_norm_bias,
):
    groups = lax.axis_size("dp")
    slices = lax.axis_size("seq")
    models = lax.axis_size("mp")
    group_id = lax.axis_index("dp")
    slice_id = lax.axis_index("seq")
    model_id = lax.axis_index("mp")
    seq_count = incoming_embeddings.shape[0]
    piece_len = incoming_embeddings.shape[2]
    model_width = incoming_embeddings.shape[3]
    part_len = piece_len * groups
    batches = seq_count // groups
    share_len = piece_len // models
    share_rows = groups * share_len
    local_top = (part_len // NR).bit_length() - 1
    upper_start = local_top + 1
    level_top = (part_len * slices // (2 * NR)).bit_length() - 1
    upper_rows = NR // 2
    upper_whole = upper_rows * slices
    send_tok = incoming_embeddings.reshape(
        groups, batches, piece_len, model_width
    )
    send_cot = output_sensitivity.reshape(
        groups, batches, piece_len, model_width
    )
    dealt_tok, dealt_cot = (
        lax.all_to_all(send_tok, "dp", split_axis=0, concat_axis=2, tiled=True),
        lax.all_to_all(send_cot, "dp", split_axis=0, concat_axis=2, tiled=True),
    )
    dealt_tok = dealt_tok.reshape(batches, part_len, model_width)
    dealt_cot = dealt_cot.reshape(batches, part_len, model_width)
    my_lengths = lax.dynamic_slice_in_dim(sequence_extents, group_id * batches, batches, 0)

    def split_rows(rows):
        return rows.reshape((groups, models, share_len) + rows.shape[1:])

    def take_share(rows):
        return lax.dynamic_slice_in_dim(split_rows(rows), model_id, 1, 1).reshape(
            (share_rows,) + rows.shape[1:]
        )

    def neighbour_rims(gathered):
        padded = jnp.pad(gathered, ((2 * NR, 2 * NR), (0, 0)))
        from_left = lax.dynamic_slice_in_dim(padded, slice_id * 2 * NR + NR, NR, 0)
        from_right = lax.dynamic_slice_in_dim(padded, (slice_id + 2) * 2 * NR, NR, 0)
        return (from_left, from_right)

    def one_batch(batch_index, learnable_collection):
        full_query, full_key, full_value, full_merge, full_up, full_down = learnable_collection[:6]
        gain_pre, shift_pre, gain_mid, shift_mid = (
            learnable_tensor.astype(jnp.float32) for learnable_tensor in learnable_collection[6:]
        )
        columns = full_query.shape[1]
        heads_here = columns // HD
        length_now = my_lengths[batch_index]

        def level_counts(level_at, first_id, id_total):
            coarse_ids = first_id + jnp.arange(id_total, dtype=jnp.int32)
            group_len = 2**level_at
            return jnp.where(
                coarse_ids >= 0, jnp.clip(length_now - group_len * coarse_ids, 0, group_len), 0
            ).astype(jnp.float32)

        positions = slice_id * part_len + jnp.arange(part_len, dtype=jnp.int32)
        valid_rows = (positions < length_now).astype(jnp.float32)
        inputs = dealt_tok[batch_index].astype(jnp.float32)
        grad_in = dealt_cot[batch_index].astype(jnp.float32) * valid_rows[:, None]
        valid_share = take_share(valid_rows)
        normed, pull_pre = jax.vjp(norm_rows, inputs, gain_pre, shift_pre)
        normed_low = normed.astype(jnp.bfloat16)
        queries = dot_plain(normed_low, full_query).astype(jnp.bfloat16)
        keys_own = dot_plain(normed_low, full_key).astype(jnp.bfloat16)
        values_own = dot_plain(normed_low, full_value).astype(jnp.bfloat16)
        pair_own = jnp.concatenate([keys_own, values_own], axis=1)
        fine_all = (
            jnp.concatenate([queries, pair_own], axis=1).astype(jnp.float32) * valid_rows[:, None]
        )
        level_sums = [fine_all]
        for level_at in range(1, upper_start + 1):
            level_sums.append(group_sum(level_sums[-1], 2))
        query_levels = [queries]
        pair_levels = [pair_own]
        own_counts = [valid_rows]
        for level_at in range(1, local_top + 1):
            coarse_rows = part_len >> level_at
            counts_here = level_counts(level_at, slice_id * coarse_rows, coarse_rows)
            coarse_means = (level_sums[level_at] / jnp.maximum(counts_here, 1.0)[:, None]).astype(
                jnp.bfloat16
            )
            query_levels.append(coarse_means[:, :columns])
            pair_levels.append(coarse_means[:, columns:])
            own_counts.append(counts_here)
        edge_rows = jnp.concatenate(
            [
                jnp.concatenate([pair_rows[:NR], pair_rows[-NR:]], axis=0)
                for pair_rows in pair_levels
            ],
            axis=1,
        )
        edges_all, upper_all = (
            lax.all_gather(
                edge_rows.astype(jnp.float32).astype(jnp.bfloat16), "seq", axis=0, tiled=True
            ).astype(jnp.float32),
            lax.all_gather(
                level_sums[upper_start].astype(jnp.bfloat16), "seq", axis=0, tiled=True
            ).astype(jnp.float32),
        )
        left_edge, right_edge = neighbour_rims(edges_all)
        left_edge = left_edge.astype(jnp.bfloat16)
        right_edge = right_edge.astype(jnp.bfloat16)
        kept_levels = []
        total_all = jnp.zeros((part_len, heads_here), jnp.float32)
        numer_all = jnp.zeros((part_len, heads_here, HD), jnp.float32)
        for level_at in range(local_top + 1):
            coarse_rows = part_len >> level_at
            col_range = slice(level_at * 2 * columns, (level_at + 1) * 2 * columns)
            pair_wide = jnp.concatenate(
                [left_edge[:, col_range], pair_levels[level_at], right_edge[:, col_range]], axis=0
            )
            count_wide = level_counts(level_at, slice_id * coarse_rows - NR, coarse_rows + 2 * NR)
            level_kept, totals, numer_part = level_forward(
                query_levels[level_at], pair_wide, count_wide, level_at
            )
            kept_levels.append(level_kept)
            total_all = total_all + jnp.repeat(totals, 2**level_at, axis=0)
            numer_all = numer_all + jnp.repeat(numer_part, 2**level_at, axis=0)
        level_at = 7
        repeat_by = 2 ** (level_at - upper_start)
        coarse_rows = upper_whole // repeat_by
        counts_here = level_counts(level_at, 0, coarse_rows)
        coarse_means = (
            group_sum(upper_all, repeat_by) / jnp.maximum(counts_here, 1.0)[:, None]
        ).astype(jnp.bfloat16)
        pair_wide = jnp.pad(coarse_means[:, columns:], ((NR, NR), (0, 0)))
        count_wide = level_counts(level_at, -NR, coarse_rows + 2 * NR)
        level_kept, totals, numer_part = level_forward(
            coarse_means[:, :columns], pair_wide, count_wide, level_at
        )
        upper_kept = [level_kept]
        upper_counts = [counts_here]
        upper_total = jnp.repeat(totals, repeat_by, axis=0)
        upper_numer = jnp.repeat(numer_part, repeat_by, axis=0)
        total_all = total_all + jnp.repeat(
            lax.dynamic_slice_in_dim(upper_total, slice_id * upper_rows, upper_rows, 0),
            2**upper_start,
            axis=0,
        )
        numer_all = numer_all + jnp.repeat(
            lax.dynamic_slice_in_dim(upper_numer, slice_id * upper_rows, upper_rows, 0),
            2**upper_start,
            axis=0,
        )
        attended = (
            (numer_all / total_all[:, :, None]).reshape(part_len, columns).astype(jnp.bfloat16)
        )
        merged_part = dot_plain(attended, full_merge)
        branch_attn = lax.psum(merged_part, "mp")
        after_attn = inputs + branch_attn
        mid_normed, pull_mid = jax.vjp(norm_rows, after_attn, gain_mid, shift_mid)
        mid_low = mid_normed.astype(jnp.bfloat16)
        after_share = take_share(after_attn)
        up_proj = dot_plain(mid_low, full_up)
        activated, pull_gelu = jax.vjp(gelu_exact, up_proj)
        act_low = activated.astype(jnp.bfloat16)
        ffn_share = (
            lax.psum_scatter(
                split_rows(dot_plain(act_low, full_down)).astype(jnp.bfloat16),
                "mp",
                scatter_dimension=1,
                tiled=True,
            )
            .astype(jnp.float32)
            .reshape(share_rows, model_width)
        )
        result_share = (valid_share[:, None] * (after_share + ffn_share)).astype(jnp.bfloat16)
        grad_low = grad_in.astype(jnp.bfloat16)
        act_grad = dot_outer(grad_low, full_down)
        down_acc = dot_inner(act_low, grad_low)
        hidden_grad = pull_gelu(act_grad)[0].astype(jnp.bfloat16)
        up_acc = dot_inner(mid_low, hidden_grad)
        mid_part = dot_outer(hidden_grad, full_up)
        mid_grad = lax.psum(mid_part, "mp")
        back_mid = pull_mid(mid_grad)[0]
        residual_grad = grad_in + back_mid
        branch_grad = residual_grad.astype(jnp.bfloat16)
        residual_share = take_share(residual_grad)
        gain_mid_part, shift_mid_part = norm_gain_parts(after_share, take_share(mid_grad))
        merge_acc = dot_inner(attended, branch_grad)
        attended_grad = dot_outer(branch_grad, full_merge).reshape(part_len, heads_here, HD)
        numer_grad = (attended_grad / total_all[:, :, None]).astype(jnp.bfloat16)
        total_grad = -jnp.sum(attended_grad * numer_all, axis=-1) / (total_all * total_all)
        numer_wide = numer_grad.astype(jnp.float32)
        rim_parts = []
        own_pair_grads = []
        query_coarse = []
        for level_at in range(local_top + 1):
            coarse_rows = part_len >> level_at
            if level_at == 0:
                numer_sum = numer_grad
                total_sum = total_grad
            else:
                numer_sum = group_sum(numer_wide, 2**level_at).astype(jnp.bfloat16)
                total_sum = group_sum(total_grad, 2**level_at)
            query_grad, pair_grad = level_backward(kept_levels[level_at], numer_sum, total_sum)
            rim_parts.append(
                jnp.concatenate([pair_grad[:NR], pair_grad[NR + coarse_rows :]], axis=0)
            )
            own_pair_grads.append(pair_grad[NR : NR + coarse_rows])
            query_coarse.append(query_grad)
        rim_grads = jnp.concatenate(rim_parts, axis=1)
        upper_numer_grad = group_sum(numer_wide, 2**upper_start).reshape(upper_rows, columns)
        upper_total_grad = group_sum(total_grad, 2**upper_start)
        rims_all, numer_sums, total_sums = (
            lax.all_gather(rim_grads.astype(jnp.bfloat16), "seq", axis=0, tiled=True).astype(
                rim_grads.dtype
            ),
            lax.all_gather(upper_numer_grad.astype(jnp.bfloat16), "seq", axis=0, tiled=True).astype(
                upper_numer_grad.dtype
            ),
            lax.all_gather(upper_total_grad.astype(jnp.bfloat16), "seq", axis=0, tiled=True).astype(
                upper_total_grad.dtype
            ),
        )
        from_left, from_right = neighbour_rims(rims_all)
        fine_grad = jnp.zeros((part_len, 3 * columns), jnp.float32)
        for level_at in range(local_top + 1):
            coarse_rows = part_len >> level_at
            col_range = slice(level_at * 2 * columns, (level_at + 1) * 2 * columns)
            pair_here = (
                own_pair_grads[level_at]
                + jnp.pad(from_left[:, col_range], ((0, coarse_rows - NR), (0, 0)))
                + jnp.pad(from_right[:, col_range], ((coarse_rows - NR, 0), (0, 0)))
            )
            coarse_grad = jnp.concatenate([query_coarse[level_at], pair_here], axis=1)
            if level_at == 0:
                fine_grad = coarse_grad
            else:
                coarse_grad = coarse_grad / jnp.maximum(own_counts[level_at], 1.0)[:, None]
                fine_grad = (
                    fine_grad + jnp.repeat(coarse_grad, 2**level_at, axis=0) * valid_rows[:, None]
                )
        upper_grad = jnp.zeros((upper_whole, 3 * columns), jnp.float32)
        for index_at, level_at in enumerate(range(upper_start, level_top + 1)):
            repeat_by = 2 ** (level_at - upper_start)
            coarse_rows = upper_whole // repeat_by
            numer_sum = (
                group_sum(numer_sums, repeat_by)
                .reshape(coarse_rows, heads_here, HD)
                .astype(jnp.bfloat16)
            )
            total_sum = group_sum(total_sums, repeat_by)
            query_grad, pair_grad = level_backward(upper_kept[index_at], numer_sum, total_sum)
            coarse_grad = (
                jnp.concatenate([query_grad, pair_grad[NR : NR + coarse_rows]], axis=1)
                / jnp.maximum(upper_counts[index_at], 1.0)[:, None]
            )
            upper_grad = jnp.repeat(coarse_grad, repeat_by, axis=0)
        own_upper = lax.dynamic_slice_in_dim(upper_grad, slice_id * upper_rows, upper_rows, 0)
        fine_grad = fine_grad + jnp.repeat(own_upper, 2**upper_start, axis=0) * valid_rows[:, None]
        rows_grad = fine_grad.astype(jnp.bfloat16)
        query_rows_grad = rows_grad[:, :columns]
        key_rows_grad = rows_grad[:, columns : 2 * columns]
        value_rows_grad = rows_grad[:, 2 * columns :]
        query_acc = dot_inner(normed_low, query_rows_grad)
        key_acc = dot_inner(normed_low, key_rows_grad)
        value_acc = dot_inner(normed_low, value_rows_grad)
        normed_part = (
            dot_outer(query_rows_grad, full_query)
            + dot_outer(key_rows_grad, full_key)
            + dot_outer(value_rows_grad, full_value)
        )
        normed_grad, gain_mid_sum, shift_mid_sum = (
            lax.psum(normed_part.astype(jnp.bfloat16), "mp").astype(jnp.float32),
            lax.psum(gain_mid_part.astype(jnp.bfloat16), "mp").astype(jnp.float32),
            lax.psum(shift_mid_part.astype(jnp.bfloat16), "mp").astype(jnp.float32),
        )
        back_pre, gain_pre_acc, shift_pre_acc = pull_pre(normed_grad)
        input_share = (residual_share + take_share(back_pre)).astype(jnp.bfloat16)
        grad_terms = (
            query_acc,
            key_acc,
            value_acc,
            merge_acc,
            up_acc,
            down_acc,
            gain_pre_acc,
            shift_pre_acc,
            gain_mid_sum,
            shift_mid_sum,
        )
        return (result_share, input_share, grad_terms)

    result_list = []
    grad_list = []
    running_sum = None
    for batch_index in range(batches):
        learnable_collection = (
            lax.all_gather(asking_projector, ("dp", "seq"), axis=0, tiled=True),
            lax.all_gather(lookup_projector, ("dp", "seq"), axis=0, tiled=True),
            lax.all_gather(content_projector, ("dp", "seq"), axis=0, tiled=True),
            lax.all_gather(attention_combiner, ("dp", "seq"), axis=1, tiled=True),
            lax.all_gather(feedforward_expand, ("dp", "seq"), axis=0, tiled=True),
            lax.all_gather(feedforward_contract, ("dp", "seq"), axis=1, tiled=True),
            lax.all_gather(attention_norm_scale, ("dp", "seq"), axis=0, tiled=True),
            lax.all_gather(attention_norm_bias, ("dp", "seq"), axis=0, tiled=True),
            lax.all_gather(feedforward_norm_scale, ("dp", "seq"), axis=0, tiled=True),
            lax.all_gather(feedforward_norm_bias, ("dp", "seq"), axis=0, tiled=True),
        )
        result_share, input_share, grad_terms = one_batch(batch_index, learnable_collection)
        result_list.append(result_share)
        grad_list.append(input_share)
        if running_sum is None:
            running_sum = grad_terms
        else:
            running_sum = tuple(
                (older_sum + newer_sum for older_sum, newer_sum in zip(running_sum, grad_terms))
            )
    owned_grads = (
        *sent_together(
            (
                running_sum[0].astype(jnp.bfloat16),
                running_sum[1].astype(jnp.bfloat16),
                running_sum[2].astype(jnp.bfloat16),
            ),
            ("dp", "seq"),
            0,
            1,
        ),
        summed_on_arrival(running_sum[3].astype(jnp.bfloat16), ("dp", "seq"), 1),
        summed_on_arrival(running_sum[4].astype(jnp.bfloat16), ("dp", "seq"), 0),
        summed_on_arrival(running_sum[5].astype(jnp.bfloat16), ("dp", "seq"), 1),
        summed_on_arrival(running_sum[6].astype(jnp.bfloat16), ("dp", "seq"), 0),
        summed_on_arrival(running_sum[7].astype(jnp.bfloat16), ("dp", "seq"), 0),
        summed_on_arrival(running_sum[8].astype(jnp.bfloat16), ("dp", "seq"), 0),
        summed_on_arrival(running_sum[9].astype(jnp.bfloat16), ("dp", "seq"), 0),
    )
    result_all = jnp.stack(result_list, axis=0).reshape(batches, groups, share_len, model_width)
    grad_all = jnp.stack(grad_list, axis=0).reshape(batches, groups, share_len, model_width)
    back_out, back_grad = (
        lax.all_to_all(result_all, "dp", split_axis=1, concat_axis=0, tiled=True),
        lax.all_to_all(grad_all, "dp", split_axis=1, concat_axis=0, tiled=True),
    )
    return (
        back_out,
        back_grad,
        owned_grads[0],
        owned_grads[1],
        owned_grads[2],
        owned_grads[3],
        owned_grads[4],
        owned_grads[5],
        owned_grads[6],
        owned_grads[7],
        owned_grads[8],
        owned_grads[9],
    )


MESH = pl.DeviceIdType.MESH
NEG = -1e30


def nn(a, b):
    return lax.dot_general(a, b, (((1,), (0,)), ((), ())), preferred_element_type=jnp.float32)


def nt(a, b):
    return lax.dot_general(a, b, (((1,), (1,)), ((), ())), preferred_element_type=jnp.float32)


def tn(a, b):
    return lax.dot_general(a, b, (((0,), (0,)), ((), ())), preferred_element_type=jnp.float32)


def halves(values):
    high = values.astype(jnp.bfloat16)
    return high, (values - high.astype(jnp.float32)).astype(jnp.bfloat16)


class Plan:
    def __init__(self, part, spots):
        self.part, self.spots = part, spots
        self.levels = (part // NR).bit_length()
        self.top = (part * spots // (2 * NR)).bit_length() - 1
        self.own = [part >> level for level in range(self.levels)]
        self.at, row = [], 0
        for rows in self.own:
            self.at.append(row)
            row += rows + 2 * NR
        self.upper = row
        self.rows = row + spots * NR
        self.pool_at, row = [None], 0
        for rows in self.own[1:]:
            self.pool_at.append(row)
            row += rows
        self.pool_upper = row
        self.pooled = row + NR
        self.slot, row = [], 0
        for level in range(self.levels, self.top + 1):
            self.slot.append((level, row, part >> level))
            row += part >> level
        assert row <= NR and spots * NR == 128 and self.pooled == part
        self.segments = [(self.at[lv], self.own[lv] + 2 * NR, lv) for lv in range(self.levels)]
        self.inner, self.outer = [], []
        level = 0
        while level < self.levels:
            start, total = self.at[level], self.own[level] + 2 * NR
            end = start + total
            if total < 96:
                self.outer.append((start, self.upper - start, self.upper - 128, None))
                break
            row = start
            while row < end:
                count = min(96, end - row)
                window = max(start, min(row - NR, end - 128))
                tile = (row, count, window, level if window + 128 <= end else None)
                inside = window >= start + NR and window + 128 <= end - NR
                (self.inner if inside else self.outer).append(tile)
                row += count
            level += 1
        self.outer.append((self.upper, 128, self.upper, None))
        self.tiles = self.inner + self.outer

    def own_pieces(self, tile):
        first, count = tile[:2]
        pieces = []
        for start, rows in zip(self.at, self.own):
            low, high = max(first, start + NR), min(first + count, start + NR + rows)
            if low < high:
                pieces.append((low, high - low))
        return pieces


def row_places(plan, rows, low, high, spot):
    level = jnp.full(rows.shape, -1, jnp.int32)
    place = jnp.zeros(rows.shape, jnp.int32)
    for start, count, lv in plan.segments:
        if start < high and start + count > low:
            inside = (rows >= start) & (rows < start + count)
            level = jnp.where(inside, lv, level)
            place = jnp.where(inside, spot * plan.own[lv] - NR + rows - start, place)
    if high > plan.upper:
        owner = lax.shift_right_arithmetic(rows - plan.upper, 4)
        within = (rows - plan.upper) & (NR - 1)
        for lv, first, count in plan.slot:
            inside = (rows >= plan.upper) & (within >= first) & (within < first + count)
            level = jnp.where(inside, lv, level)
            place = jnp.where(inside, owner * count + within - first, place)
    return level, place


def log_counts(plan, tile, spot, length):
    first, count, window, level = tile
    row_at = first + lax.broadcasted_iota(jnp.int32, (count, 128), 0)
    key_at = window + lax.broadcasted_iota(jnp.int32, (8, 128), 1)
    row_level, row_place = row_places(plan, row_at, first, first + count, spot)
    key_level, key_place = row_places(plan, key_at, window, window + 128, spot)
    span = lax.shift_left(jnp.ones_like(key_level), jnp.maximum(key_level, 0))
    counts = jnp.clip(length - span * key_place, 0, span)
    usable = (counts > 0) & (key_place >= 0) & (key_level >= 0)
    logs = jnp.where(usable, jnp.log(jnp.maximum(counts, 1).astype(jnp.float32)), NEG)
    coarse = lambda level_at, place_at, by: level_at * 65536 + lax.shift_right_arithmetic(place_at, by)
    key_block = coarse(key_level, key_place, 4)[:1]
    key_half = coarse(key_level, key_place, 3)[:1]
    allowed = jnp.abs(coarse(row_level, row_place, 4) - key_block) <= 1
    if level != 0:
        apart = jnp.abs(coarse(row_level, row_place, 3) - key_half) >= 2
        allowed = allowed & (apart if level is not None else apart | (row_level == 0)) & (row_level >= 0)
    return jnp.where(allowed, logs[:1], NEG)


def pool_bounds(plan, shape, dim):
    row = lax.broadcasted_iota(jnp.int32, shape, dim)
    low = jnp.full(shape, -1, jnp.int32)
    size = jnp.zeros(shape, jnp.int32)
    level = jnp.zeros(shape, jnp.int32)
    parts = [(plan.pool_at[lv], plan.own[lv], lv) for lv in range(1, plan.levels)]
    parts += [(plan.pool_upper + first, count, lv) for lv, first, count in plan.slot]
    for start, count, lv in parts:
        inside = (row >= start) & (row < start + count)
        low = jnp.where(inside, (row - start) << lv, low)
        size = jnp.where(inside, 1 << lv, size)
    return low, size


def spread_columns(rows, place, count):
    width = rows.shape[1]
    source = lax.broadcasted_iota(jnp.int32, (width, width * count), 0)
    target = lax.broadcasted_iota(jnp.int32, (width, width * count), 1)
    return nn(rows, jnp.where(target == source + place * width, 1.0, 0.0).astype(rows.dtype))


def flipped(rows):
    size = rows.shape[1]
    row = lax.broadcasted_iota(jnp.int32, (size, size), 0)
    col = lax.broadcasted_iota(jnp.int32, (size, size), 1)
    return nt(jnp.where(row == col, 1.0, 0.0).astype(rows.dtype), rows).astype(rows.dtype)


def flip_bits(value, k):
    low, high, k_low, k_high = value % 2, value // 2, k % 2, k // 2
    return (high + k_high - 2 * high * k_high) * 2 + low + k_low - 2 * low * k_low


class Marks:
    def __init__(self):
        self.used = 0

    def take(self, count):
        self.used += count
        return self.used - count


def whole_layer(plan, dims, net_count, *refs):
    (extents, w_query, w_key, w_value, w_merge, w_expand, w_contract, norm_parts, tokens_in, cotangent_in,
     out_rows, out_grads, weight_grads, norm_grads,
     weights, norms, tokens, cotangent, ext, logs, pool, unpool, inverse, work,
     attended, ratio, recip, normed, scaled, rstd, grad_ext, total_ext, residual, acc, acc2, totals, result, row_grads,
     active, slope, grads, got1, got2, got3, got4, norm_got,
     load_sem, send_sem, recv_sem) = refs
    part, width, pair, hidden = dims
    f32, bf16 = jnp.float32, jnp.bfloat16
    models = weights.shape[0]
    strip, columns = weights.shape[4:]
    ax, sq, az = lax.axis_index("dp"), lax.axis_index("seq"), lax.axis_index("mp")
    ay, ac = sq // 2, sq % 2
    spot = sq * 2 + ax
    spots = plan.spots
    length = extents[az]
    qkv = 3 * pair

    def device(x, y, c, z):
        return (x, y * 2 + c, z)

    def at_spot(place):
        return (place % 2, place // 2, az)

    def plane(k):
        return flip_bits(az, k)

    x_peer, y_peer, c_peer = device(1 - ax, ay, ac, az), device(ax, 1 - ay, ac, az), device(ax, ay, 1 - ac, az)
    z_peer = lambda k: device(ax, ay, ac, plane(k))

    barrier = pltpu.get_barrier_semaphore()
    for step in range(1, spots):
        pl.semaphore_signal(barrier, inc=1, device_id=at_spot((spot + step) % spots), device_id_type=MESH)
    for k in range(1, models):
        pl.semaphore_signal(barrier, inc=1, device_id=z_peer(k), device_id_type=MESH)
    load_tokens = pltpu.make_async_copy(tokens_in.at[az, 0], tokens, load_sem.at[0])
    load_cotangent = pltpu.make_async_copy(cotangent_in.at[az, 0], cotangent, load_sem.at[1])
    load_tokens.start()
    load_cotangent.start()
    own = (az, ax, ay, ac)
    weights[own + (slice(None), slice(0, pair))] = w_query[...] * jnp.asarray(HD ** -0.5, bf16)
    weights[own + (slice(None), slice(pair, 2 * pair))] = w_key[...]
    weights[own + (slice(None), slice(2 * pair, qkv))] = w_value[...]
    weights[own + (slice(None), slice(qkv, qkv + pair))] = flipped(w_merge[...])
    weights[own + (slice(None), slice(4 * pair, 4 * pair + hidden))] = w_expand[...]
    weights[own + (slice(None), slice(4 * pair + hidden, columns))] = flipped(w_contract[...])
    owner = ax * 4 + sq
    norms[spot] = spread_columns(norm_parts[...], owner, width // strip)
    pl.semaphore_wait(barrier, spots - 1 + models - 1)

    marks = Marks()

    def copy(i, src, dst, to):
        return pltpu.make_async_remote_copy(
            src_ref=src, dst_ref=dst, send_sem=send_sem.at[i], recv_sem=recv_sem.at[i],
            device_id=to, device_id_type=MESH)

    sent = []

    def send(i, src, dst, to):
        c = copy(i, src, dst, to)
        c.start()
        sent.append(c)
        return c

    def arrive(copies):
        for c in copies:
            c.wait_recv()

    class Gather:
        def __init__(self, col, count, through_y):
            self.cols, self.rows = pl.ds(col, count), through_y
            self.flight = {}

        def block(self, k, x, y, rows=slice(None)):
            return weights.at[plane(k), x, y, ac, rows, self.cols]

        def to_planes(self):
            here = self.block(0, ax, ay)
            for k in range(1, models):
                self.flight["z", k] = [send(marks.take(1), here, here, z_peer(k))]

        def to_sides(self, k):
            if k:
                arrive(self.flight["z", k])
            here = self.block(k, ax, ay)
            self.flight["side", k] = [send(marks.take(1), here, here, x_peer), send(marks.take(1), here, here, y_peer)]

        def to_corner(self, k):
            arrive(self.flight["side", k])
            first = self.block(k, 1 - ax, ay, pl.ds(0, self.rows))
            rest = self.block(k, ax, 1 - ay, pl.ds(self.rows, strip - self.rows))
            self.flight["corner", k] = [send(marks.take(1), first, first, y_peer), send(marks.take(1), rest, rest, x_peer)]

        def to_core(self, k):
            arrive(self.flight["corner", k])
            here = weights.at[plane(k), :, :, ac, :, self.cols]
            self.flight["core", k] = [send(marks.take(1), here, here, c_peer)]

        def here(self, k):
            arrive(self.flight["core", k])

    first_gather = Gather(0, qkv, 32)
    merge_gather = Gather(qkv, pair + hidden, 48)
    last_gather = Gather(4 * pair + hidden, hidden, 48)

    first_gather.to_planes()
    first_gather.to_sides(0)
    norm_copies = [send(marks.take(1), norms.at[spot], norms.at[spot], at_spot((spot + step) % spots))
                   for step in range(1, spots)]

    low, size = pool_bounds(plan, (part, 128), 0)
    for block in range(part // 128):
        token_at = block * 128 + lax.broadcasted_iota(jnp.int32, (part, 128), 1)
        member = (token_at >= low) & (token_at < low + size) & (token_at + spot * part < length)
        pool[:, block * 128:(block + 1) * 128] = jnp.where(member, 1.0, 0.0).astype(bf16)
    counts = jnp.clip(length - spot * part - low, 0, size)
    inverse[...] = 1.0 / jnp.maximum(counts, 1).astype(f32)
    low, size = pool_bounds(plan, (8, part), 1)
    token_at = lax.broadcasted_iota(jnp.int32, (part, part), 0)
    member = (token_at >= low[:1]) & (token_at < (low + size)[:1])
    unpool[...] = jnp.where(member, 1.0, 0.0).astype(bf16)
    first_gather.to_corner(0)
    first_gather.to_sides(1)
    load_tokens.wait()

    def statistics(values):
        center = values - jnp.mean(values, axis=-1, keepdims=True)
        spread = jnp.mean(center * center, axis=-1, keepdims=True)
        scale = lax.rsqrt(spread + 1e-05)
        return center * scale, scale

    xhat, scale = statistics(tokens[...].astype(f32))
    scaled[...] = xhat
    rstd[...] = jnp.broadcast_to(scale, (part, 128))
    first_gather.to_sides(2)
    first_gather.to_sides(3)
    merge_gather.to_planes()
    first_gather.to_core(0)
    first_gather.to_corner(1)
    for i, tile in enumerate(plan.tiles):
        logs[i, 0:tile[1]] = log_counts(plan, tile, spot, length)
    first_gather.to_corner(2)
    first_gather.to_corner(3)
    merge_gather.to_sides(0)
    first_gather.to_core(1)
    arrive(norm_copies)
    gains = norms[0]
    for i in range(1, spots):
        gains = gains + norms[i]
    pre_gain, pre_shift, mid_gain, mid_shift = (gains[i:i + 1] for i in range(4))
    normed[...] = (scaled[...] * pre_gain + pre_shift).astype(bf16)
    first_gather.to_core(2)
    first_gather.to_core(3)
    last_gather.to_planes()

    is_first, is_last = spot == 0, spot == spots - 1

    @pl.when(is_first)
    def _():
        for lv in range(plan.levels):
            rows = slice(plan.at[lv], plan.at[lv] + NR)
            ext[:, rows, :] = jnp.zeros((models, NR, qkv), bf16)
            grad_ext[:, rows, :] = jnp.zeros((models, NR, pair), bf16)
            total_ext[rows, :] = jnp.zeros((NR, 128), bf16)

    @pl.when(is_last)
    def _():
        for lv in range(plan.levels):
            end = plan.at[lv] + NR + plan.own[lv]
            rows = slice(end, end + NR)
            ext[:, rows, :] = jnp.zeros((models, NR, qkv), bf16)
            grad_ext[:, rows, :] = jnp.zeros((models, NR, pair), bf16)
            total_ext[rows, :] = jnp.zeros((NR, 128), bf16)

    def weight_cols(m, col, count):
        return weights[m, :, :, :, :, col:col + count].reshape(width, count)

    slot_row = pl.multiple_of(spot * NR, NR)
    own_slot_rows = pl.ds(pl.multiple_of(plan.upper + slot_row, NR), NR)
    per_rim = plan.levels * 2 + spots - 1

    class Rims:
        def __init__(self, view, base):
            right, left = at_spot((spot + 1) % spots), at_spot((spot + spots - 1) % spots)
            self.to_right, self.to_left, self.to_all = [], [], []
            for lv in range(plan.levels):
                start, rows = plan.at[lv], plan.own[lv]
                self.to_right.append(copy(base + 2 * lv, view(pl.ds(start + rows, NR)), view(pl.ds(start, NR)), right))
                self.to_left.append(copy(base + 2 * lv + 1, view(pl.ds(start + NR, NR)), view(pl.ds(start + NR + rows, NR)), left))
            block = view(own_slot_rows)
            for step in range(1, spots):
                self.to_all.append(copy(base + 2 * plan.levels + step - 1, block, block, at_spot((spot + step) % spots)))

        def each(self, verb, not_first, not_last):
            @pl.when(jnp.logical_not(is_last))
            def _():
                for c in not_last:
                    getattr(c, verb)()

            @pl.when(jnp.logical_not(is_first))
            def _():
                for c in not_first:
                    getattr(c, verb)()

            for c in self.to_all:
                getattr(c, verb)()

        def start(self):
            self.each("start", self.to_left, self.to_right)

        def wait(self):
            self.each("wait_recv", self.to_right, self.to_left)

        def done(self):
            self.each("wait_send", self.to_left, self.to_right)

    pair_base = marks.take(models * per_rim)
    query_base = marks.take(per_rim)
    grad_base = marks.take(models * per_rim)
    total_base = marks.take(per_rim)
    pair_rims = lambda k: Rims(lambda rows: ext.at[plane(k), rows, pl.ds(pair, 2 * pair)], pair_base + k * per_rim)
    query_rims = lambda: Rims(lambda rows: ext.at[:, rows, pl.ds(0, pair)], query_base)
    grad_rims = lambda k: Rims(lambda rows: grad_ext.at[plane(k), rows, :], grad_base + k * per_rim)
    total_rims = lambda: Rims(lambda rows: total_ext.at[rows, :], total_base)

    for k in range(models):
        first_gather.here(k)
        m = plane(k)
        rows = nn(normed[...], weight_cols(m, 0, qkv)).astype(bf16)
        ext[m, NR:NR + part, :] = rows
        means = (nn(pool[...], rows) * jnp.concatenate([inverse[...]] * 3, axis=1)).astype(bf16)
        for lv in range(1, plan.levels):
            ext[m, plan.at[lv] + NR:plan.at[lv] + NR + plan.own[lv], :] = means[plan.pool_at[lv]:plan.pool_at[lv] + plan.own[lv]]
        ext[m, own_slot_rows, :] = means[plan.pool_upper:plan.pool_upper + NR]
        pair_rims(k).start()

    for k in range(1, models):
        merge_gather.to_sides(k)

    lane = lax.broadcasted_iota(jnp.int32, (1, pair), 1)
    left_head = lane < HD

    def both_heads(rows):
        zero = jnp.zeros_like(rows)
        return jnp.concatenate([jnp.where(left_head, rows, zero), jnp.where(left_head, zero, rows)], axis=0)

    def joined(rows):
        half = rows.shape[0] // 2
        return jnp.where(left_head, rows[:half], rows[half:])

    ones = jnp.ones((128, 128), bf16)

    def stacked(parts):
        return parts[0] if len(parts) == 1 else jnp.concatenate(parts, axis=0)

    def tile_weights(m, rows, mask, window):
        queries = both_heads(rows)
        keys = ext[m, window:window + 128, pair:2 * pair]
        values = jnp.concatenate([ext[m, window:window + 128, 2 * pair:3 * pair], ones], axis=1)
        weight = jnp.exp(nt(queries, keys) + jnp.concatenate([mask, mask], axis=0))
        return queries, keys, values, weight

    def attend(tiles, first_k, last_k, wait_rims):
        def body(k, carry):
            m = plane(k)
            if wait_rims:
                pair_rims(k).wait()
            for tile in tiles:
                first, _, window, _ = tile
                index = plan.tiles.index(tile)
                if first == plan.upper:
                    pieces = [(first, NR)]
                    rows, mask = ext[m, own_slot_rows, 0:pair], logs[index, pl.ds(slot_row, NR)]
                else:
                    pieces = plan.own_pieces(tile)
                    rows = stacked([ext[m, low:low + count, 0:pair] for low, count in pieces])
                    mask = stacked([logs[index, low - first:low - first + count] for low, count in pieces])
                _, _, values, weight = tile_weights(m, rows, mask, window)
                both = nn(weight.astype(bf16), values)
                numer, tot = joined(both[:, :128]), joined(both[:, 128:])
                at = 0
                for low, count in pieces:
                    work[m, low:low + count, 0:pair] = numer[at:at + count]
                    work[m, low:low + count, pair:2 * pair] = tot[at:at + count]
                    at += count
            return carry

        lax.fori_loop(first_k, last_k, body, 0)

    attend(plan.inner, 0, models, False)
    attend(plan.outer, 0, 2, True)
    for k in range(models):
        merge_gather.to_corner(k)
    for k in range(models):
        last_gather.to_sides(k)
    attend(plan.outer, 2, models, True)
    for k in range(models):
        merge_gather.to_core(k)

    def coarse_rows(m, cols, slot_at):
        rows = [work[m, plan.at[lv] + NR:plan.at[lv] + NR + plan.own[lv], 0:cols] for lv in range(1, plan.levels)]
        return jnp.concatenate(rows + [work[m, slot_at, 0:cols]], axis=0)

    def spread_out(rows):
        high, rest = halves(rows)
        return nn(unpool[...], high) + nn(unpool[...], rest)

    def normalise(m, carry):
        both = spread_out(coarse_rows(m, 2 * pair, slice(plan.upper, plan.upper + NR)))
        both = both + work[m, NR:NR + part, 0:2 * pair]
        inv_total = 1.0 / both[:, pair:]
        quotient = both[:, :pair] * inv_total
        ratio[m] = quotient
        recip[m] = inv_total
        attended[m] = quotient.astype(bf16)
        return carry

    lax.fori_loop(0, models, normalise, 0)
    for k in range(models):
        last_gather.to_corner(k)

    residual[...] = tokens[...].astype(f32)
    for k in range(models):
        merge_gather.here(k)

    def merge(m, carry):
        residual[...] += nt(attended[m], weight_cols(m, qkv, pair))
        return carry

    lax.fori_loop(0, models, merge, 0)
    after = residual[...]
    mid_hat, mid_scale = statistics(after)
    mid = (mid_hat * mid_gain + mid_shift).astype(bf16)
    mid_t = mid.T
    load_cotangent.wait()
    row_at = lax.broadcasted_iota(jnp.int32, (part, 1), 0) + spot * part
    valid = row_at < length
    out_grad = jnp.where(valid, cotangent[...], jnp.zeros((), bf16))
    out_grad_t = out_grad.T
    acc[...] = jnp.zeros(acc.shape, f32)
    acc2[...] = jnp.zeros(acc.shape, f32)
    block_shape = grads.shape[1:5] + (hidden,)

    def feed_up(m, carry):
        up = nn(mid, weight_cols(m, 4 * pair, hidden))
        phi = 0.5 + 0.5 * lax.erf(up * (0.5 ** 0.5))
        active[m] = (up * phi).astype(bf16)
        slope[m] = phi + up * (jnp.exp(-0.5 * up * up) * 0.3989422804014327)
        return carry

    lax.fori_loop(0, models, feed_up, 0)
    for k in range(models):
        last_gather.to_core(k)
    query_rims().start()

    class Reduce:
        def __init__(self, col, count):
            self.cols = pl.ds(col, count)
            self.core = marks.take(models)
            self.side = marks.take(2 * models)
            self.corner = marks.take(2 * models)
            self.z = marks.take(models)

        def core_copy(self, k):
            m = plane(k)
            return copy(self.core + k, grads.at[m, :, :, 1 - ac, :, self.cols], got1.at[m, :, :, :, self.cols], c_peer)

        def side_copies(self, k):
            m = plane(k)
            return [copy(self.side + 2 * k, got1.at[m, 1 - ax, :, pl.ds(0, 32), self.cols],
                         got2.at[m, :, pl.ds(0, 32), self.cols], x_peer),
                    copy(self.side + 2 * k + 1, got1.at[m, :, 1 - ay, pl.ds(32, 32), self.cols],
                         got2.at[m, :, pl.ds(32, 32), self.cols], y_peer)]

        def corner_copies(self, k):
            m = plane(k)
            return [copy(self.corner + 2 * k, got2.at[m, 1 - ay, pl.ds(0, 32), self.cols],
                         got3.at[m, pl.ds(0, 32), self.cols], y_peer),
                    copy(self.corner + 2 * k + 1, got2.at[m, 1 - ax, pl.ds(32, 32), self.cols],
                         got3.at[m, pl.ds(32, 32), self.cols], x_peer)]

        def z_copy(self, k):
            m = plane(k)
            return copy(self.z + k, got3.at[m, :, self.cols], got4.at[k, :, self.cols], z_peer(k))

        def start(self, k):
            self.core_copy(k).start()

        def to_sides(self, k):
            m = plane(k)
            self.core_copy(k).wait_recv()
            got1[m, :, :, :, self.cols] = got1[m, :, :, :, self.cols] + grads[m, :, :, ac, :, self.cols]
            for c in self.side_copies(k):
                c.start()

        def to_corner(self, k):
            m = plane(k)
            arrive(self.side_copies(k))
            top, bottom = pl.ds(0, 32), pl.ds(32, 32)
            got2[m, :, top, self.cols] = got2[m, :, top, self.cols] + got1[m, ax, :, top, self.cols]
            got2[m, :, bottom, self.cols] = got2[m, :, bottom, self.cols] + got1[m, :, ay, bottom, self.cols]
            for c in self.corner_copies(k):
                c.start()

        def to_planes(self, k):
            m = plane(k)
            arrive(self.corner_copies(k))
            top, bottom = pl.ds(0, 32), pl.ds(32, 32)
            got3[m, top, self.cols] = got3[m, top, self.cols] + got2[m, ay, top, self.cols]
            got3[m, bottom, self.cols] = got3[m, bottom, self.cols] + got2[m, ax, bottom, self.cols]

            @pl.when(k > 0)
            def _():
                self.z_copy(k).start()

        def end(self):
            total = got3[az, :, self.cols].astype(f32)
            for k in range(1, models):
                self.z_copy(k).wait_recv()
                total = total + got4[k, :, self.cols].astype(f32)
            weight_grads[:, self.cols] = total

        def done(self, k):
            self.core_copy(k).wait_send()
            for c in self.side_copies(k) + self.corner_copies(k):
                c.wait_send()

            @pl.when(k > 0)
            def _():
                self.z_copy(k).wait_send()

    feed_reduce = Reduce(4 * pair, 2 * hidden)
    attention_reduce = Reduce(0, 4 * pair)
    for k in range(models):
        last_gather.here(k)

    def feed_down(step, carry):
        k = models - 1 - step
        m = plane(k)
        contract_t = weight_cols(m, 4 * pair + hidden, hidden)
        acc[...] += nt(active[m], contract_t)
        hidden_grad = (nn(out_grad, contract_t) * slope[m]).astype(bf16)
        grads[m, :, :, :, :, 4 * pair:4 * pair + hidden] = nn(mid_t, hidden_grad).astype(bf16).reshape(block_shape)
        grads[m, :, :, :, :, 4 * pair + hidden:columns] = nn(out_grad_t, active[m]).astype(bf16).reshape(block_shape)
        feed_reduce.start(k)
        acc2[...] += nt(hidden_grad, weight_cols(m, 4 * pair, hidden))
        return carry

    lax.fori_loop(0, models, feed_down, 0)
    result[...] = jnp.where(valid, after + acc[...], 0.0).astype(bf16)
    mid_grad = acc2[...]

    def rows_home(source, target):
        share = part // models
        target[az] = source[pl.ds(pl.multiple_of(az * share, share), share), :]
        return [send(marks.take(1), source.at[pl.ds(pl.multiple_of(plane(k) * share, share), share), :],
                     target.at[az], z_peer(k)) for k in range(1, models)]

    def norm_back(grad, hat, scale_row, gain):
        scaled_grad = grad * gain
        mean_grad = jnp.mean(scaled_grad, axis=-1, keepdims=True)
        mean_along = jnp.mean(scaled_grad * hat, axis=-1, keepdims=True)
        return scale_row * (scaled_grad - mean_grad - hat * mean_along)

    through = out_grad.astype(f32) + norm_back(mid_grad, mid_hat, mid_scale, mid_gain)
    residual[...] = through
    branch = through.astype(bf16)
    branch_t = branch.T
    norm_sums = [jnp.sum(mid_grad * mid_hat, axis=0, keepdims=True), jnp.sum(mid_grad, axis=0, keepdims=True)]

    merge_shape = grads.shape[1:5] + (pair,)
    select_row = lax.broadcasted_iota(jnp.int32, (pair, 128), 0) // HD
    select_col = lax.broadcasted_iota(jnp.int32, (pair, 128), 1) // 2
    totals[...] = jnp.zeros(totals.shape, f32)

    def unmerge(step, carry):
        k = models - 1 - step
        m = plane(k)
        attended_grad = nn(branch, weight_cols(m, qkv, pair)) * recip[m]
        fine = attended_grad.astype(bf16)
        grad_ext[m, NR:NR + part, :] = fine
        sums = nn(pool[...], fine).astype(bf16)
        for lv in range(1, plan.levels):
            grad_ext[m, plan.at[lv] + NR:plan.at[lv] + NR + plan.own[lv], :] = sums[plan.pool_at[lv]:plan.pool_at[lv] + plan.own[lv]]
        grad_ext[m, own_slot_rows, :] = sums[plan.pool_upper:plan.pool_upper + NR]
        grad_rims(k).start()
        high, rest = halves(attended_grad * ratio[m])
        chosen = jnp.where(select_row + 2 * m == select_col, -1.0, 0.0).astype(bf16)
        totals[...] += nn(high, chosen) + nn(rest, chosen)
        grads[m, :, :, :, :, qkv:qkv + pair] = nn(branch_t, attended[m]).astype(bf16).reshape(merge_shape)
        return carry

    lax.fori_loop(0, models, unmerge, 0)
    even = lax.broadcasted_iota(jnp.int32, (1, 128), 1) % 2 == 0
    high, rest = halves(totals[...])
    total_ext[NR:NR + part, :] = jnp.where(even, high, rest)
    pooled_high, pooled_rest = halves(nn(pool[...], high) + nn(pool[...], rest))
    sums = jnp.where(even, pooled_high, pooled_rest)
    for lv in range(1, plan.levels):
        total_ext[plan.at[lv] + NR:plan.at[lv] + NR + plan.own[lv], :] = sums[plan.pool_at[lv]:plan.pool_at[lv] + plan.own[lv]]
    total_ext[own_slot_rows, :] = sums[plan.pool_upper:plan.pool_upper + NR]
    total_rims().start()
    rows_out = rows_home(result, out_rows)

    def advance(step, carry):
        feed_reduce.to_sides(models - 1 - step)
        return carry

    lax.fori_loop(0, models, advance, 0)

    head_of_lane = lax.broadcasted_iota(jnp.int32, (1, 128), 1) // 2

    def clear(m, carry):
        work[m] = jnp.zeros(work.shape[1:], f32)
        return carry

    lax.fori_loop(0, models, clear, 0)
    normed_t = normed[...].T
    acc[...] = jnp.zeros(acc.shape, f32)
    qkv_shape = grads.shape[1:5] + (qkv,)
    query_scale = jnp.where(lax.broadcasted_iota(jnp.int32, (1, qkv), 1) < pair, HD ** -0.5, 1.0)
    total_rims().wait()
    query_rims().wait()

    def back_tile(m, tile):
        first, count, window, _ = tile
        rows_at = slice(first, first + count)
        mask = logs[plan.tiles.index(tile), 0:count]
        queries, keys, values, weight = tile_weights(m, ext[m, rows_at, 0:pair], mask, window)
        numer = both_heads(grad_ext[m, rows_at, :])
        tot = total_ext[rows_at, :]
        zero = jnp.zeros_like(tot)
        tots = jnp.concatenate([jnp.where(head_of_lane == 2 * m, tot, zero),
                                jnp.where(head_of_lane == 2 * m + 1, tot, zero)], axis=0)
        score_grad = (weight * nt(jnp.concatenate([numer, tots], axis=1), values)).astype(bf16)
        work[m, rows_at, 0:pair] = joined(nn(score_grad, keys))
        key_rows = slice(window, window + 128)
        work[m, key_rows, pair:2 * pair] += tn(score_grad, queries)
        work[m, key_rows, 2 * pair:3 * pair] += tn(weight.astype(bf16), numer)

    def back(step, carry):
        k = models - 1 - step
        m = plane(k)
        grad_rims(k).wait()
        for tile in plan.tiles:
            back_tile(m, tile)
        coarse = coarse_rows(m, qkv, own_slot_rows)
        spread = spread_out(coarse * jnp.concatenate([inverse[...]] * 3, axis=1))
        rows = (work[m, NR:NR + part, :] + jnp.where(valid, spread, 0.0)).astype(bf16)
        grads[m, :, :, :, :, 0:qkv] = (nn(normed_t, rows) * query_scale).astype(bf16).reshape(qkv_shape)
        attention_reduce.start(k)
        acc[...] += nt(rows, weight_cols(m, 0, qkv))

        @pl.when(step >= 1)
        def _():
            attention_reduce.to_sides(k + 1)
            feed_reduce.to_planes(k + 1)

        feed_reduce.to_corner(k)

        @pl.when(step >= 2)
        def _():
            attention_reduce.to_corner(k + 2)

        @pl.when(step >= 3)
        def _():
            attention_reduce.to_planes(k + 3)

        return carry

    lax.fori_loop(0, models, back, 0)
    normed_grad = acc[...]
    hat = scaled[...]
    row_grads[...] = (residual[...] + norm_back(normed_grad, hat, rstd[:, 0:1], pre_gain)).astype(bf16)
    grads_out = rows_home(row_grads, out_grads)
    attention_reduce.to_sides(0)
    attention_reduce.to_corner(1)
    norm_sums = [jnp.sum(normed_grad * hat, axis=0, keepdims=True), jnp.sum(normed_grad, axis=0, keepdims=True)] + norm_sums
    norm_got[0] = jnp.concatenate(norm_sums + [jnp.zeros((4, width), f32)], axis=0)
    small = [send(marks.take(1), norm_got.at[0], norm_got.at[step], at_spot((spot + step) % spots)) for step in range(1, spots)]
    attention_reduce.to_planes(2)
    feed_reduce.to_planes(0)
    arrive(small)
    norm_total = norm_got[0]
    for step in range(1, spots):
        norm_total = norm_total + norm_got[step]
    norm_got[spots] = norm_total
    small = [send(marks.take(1), norm_got.at[spots], norm_got.at[spots + k], z_peer(k)) for k in range(1, models)]
    attention_reduce.to_corner(0)
    attention_reduce.to_planes(1)
    feed_reduce.end()
    attention_reduce.to_planes(0)
    attention_reduce.end()
    arrive(small)
    for k in range(1, models):
        norm_total = norm_total + norm_got[spots + k]
    norm_grads[...] = norm_total
    arrive(rows_out)
    arrive(grads_out)
    assert marks.used <= net_count
    for c in sent:
        c.wait_send()

    def drain(k, carry):
        pair_rims(k).done()
        grad_rims(k).done()
        feed_reduce.done(k)
        attention_reduce.done(k)
        return carry

    lax.fori_loop(0, models, drain, 0)
    query_rims().done()
    total_rims().done()


def finish_outputs(dims, rows_ref, grads_ref, weights_ref, norms_ref,
                   out_rows, out_grads, query, key, value, merge, up, down, *norm_outs):
    part, width, pair, hidden = dims
    out_rows[...] = rows_ref[...].reshape(out_rows.shape)
    out_grads[...] = grads_ref[...].reshape(out_grads.shape)
    strip = query.shape[0]
    query[...] = weights_ref[:, 0:pair]
    key[...] = weights_ref[:, pair:2 * pair]
    value[...] = weights_ref[:, 2 * pair:3 * pair]
    up[...] = weights_ref[:, 4 * pair:4 * pair + hidden]
    padding = lambda block: jnp.concatenate([block, jnp.zeros((128 - strip, block.shape[1]), block.dtype)], axis=0)
    merge[...] = padding(weights_ref[:, 3 * pair:4 * pair]).T[:, :strip]
    down[...] = padding(weights_ref[:, 4 * pair + hidden:4 * pair + 2 * hidden]).T[:, :strip]
    owner = lax.axis_index("dp") * 4 + lax.axis_index("seq")
    strips = width // strip
    mine = norms_ref[:, 0:strip] * (owner == 0).astype(jnp.float32)
    for i in range(1, strips):
        mine = jnp.where(owner == i, norms_ref[:, i * strip:(i + 1) * strip], mine)
    for i, out in enumerate(norm_outs):
        out[...] = mine[i].reshape(out.shape)


def fast_body(plan, incoming_embeddings, output_sensitivity, sequence_extents, asking_projector, lookup_projector,
              content_projector, attention_combiner, feedforward_expand, feedforward_contract,
              attention_norm_scale, attention_norm_bias, feedforward_norm_scale, feedforward_norm_bias):
    bf16, f32 = jnp.bfloat16, jnp.float32
    models = lax.axis_size("mp")
    seqs, _, part, width = incoming_embeddings.shape
    strip, pair = asking_projector.shape
    hidden = feedforward_expand.shape[1]
    columns = 4 * pair + 2 * hidden
    norm_parts = jnp.stack([attention_norm_scale, attention_norm_bias, feedforward_norm_scale, feedforward_norm_bias] * 2)
    share = part // models
    spots, rows = plan.spots, plan.rows
    deep = (2, 2, 2, strip, columns)
    net_count = 400
    vmem = pltpu.VMEM
    scratch = [
        vmem((models,) + deep, bf16), vmem((spots, 8, width), f32), vmem((part, width), bf16), vmem((part, width), bf16),
        vmem((models, rows, 3 * pair), bf16), vmem((len(plan.tiles), 128, 128), f32),
        vmem((part, part), bf16), vmem((part, part), bf16), vmem((part, 128), f32), vmem((models, rows, 3 * pair), f32),
        vmem((models, part, pair), bf16), vmem((models, part, pair), f32), vmem((models, part, pair), f32),
        vmem((part, width), bf16), vmem((part, width), f32), vmem((part, 128), f32),
        vmem((models, rows, pair), bf16), vmem((rows, 128), bf16), vmem((part, width), f32), vmem((part, width), f32),
        vmem((part, width), f32), vmem((part, 128), f32), vmem((part, width), bf16), vmem((part, width), bf16),
        vmem((models, part, hidden), bf16), vmem((models, part, hidden), f32),
        vmem((models,) + deep, bf16), vmem((models, 2, 2, strip, columns), bf16), vmem((models, 2, strip, columns), bf16),
        vmem((models, strip, columns), bf16), vmem((models, strip, columns), bf16), vmem((spots + models, 8, width), f32),
        pltpu.SemaphoreType.DMA((2,)), pltpu.SemaphoreType.DMA((net_count,)), pltpu.SemaphoreType.DMA((net_count,)),
    ]
    any_space, in_vmem = pl.BlockSpec(memory_space=pl.ANY), pl.BlockSpec(memory_space=pltpu.VMEM)
    out_rows, out_grads, weight_grads, norm_grads = pl.pallas_call(
        functools.partial(whole_layer, plan, (part, width, pair, hidden), net_count),
        out_shape=(jax.ShapeDtypeStruct((seqs, share, width), bf16), jax.ShapeDtypeStruct((seqs, share, width), bf16),
                   jax.ShapeDtypeStruct((strip, columns), f32), jax.ShapeDtypeStruct((8, width), f32)),
        in_specs=[pl.BlockSpec(memory_space=pltpu.SMEM)] + [in_vmem] * 7 + [any_space] * 2,
        out_specs=(in_vmem,) * 4,
        scratch_shapes=scratch,
        compiler_params=pltpu.CompilerParams(collective_id=0, has_side_effects=True, vmem_limit_bytes=60 * 2 ** 20),
        name="layer",
    )(sequence_extents, asking_projector, lookup_projector, content_projector, attention_combiner, feedforward_expand,
      feedforward_contract, norm_parts, incoming_embeddings, output_sensitivity)
    flat = lambda *shape: jax.ShapeDtypeStruct(shape, f32)
    rows_type = jax.ShapeDtypeStruct((seqs, 1, share, width), bf16)
    finished = pl.pallas_call(
        functools.partial(finish_outputs, (part, width, pair, hidden)),
        out_shape=(rows_type, rows_type, flat(strip, pair), flat(strip, pair), flat(strip, pair), flat(pair, strip),
                   flat(strip, hidden), flat(hidden, strip)) + (flat(1, strip),) * 4,
        in_specs=[in_vmem] * 4,
        out_specs=(in_vmem,) * 12,
        name="outputs",
    )(out_rows, out_grads, weight_grads, norm_grads)
    return finished[:8] + tuple(row.reshape(strip) for row in finished[8:])


def solution(mesh):
    in_specs = (
        P(None, "seq", "dp", None),
        P(None, "seq", "dp", None),
        P(),
        P(("dp", "seq"), "mp"),
        P(("dp", "seq"), "mp"),
        P(("dp", "seq"), "mp"),
        P("mp", ("dp", "seq")),
        P(("dp", "seq"), "mp"),
        P("mp", ("dp", "seq")),
        P(("dp", "seq")),
        P(("dp", "seq")),
        P(("dp", "seq")),
        P(("dp", "seq")),
    )
    out_specs = (
        P(None, "seq", ("dp", "mp"), None),
        P(None, "seq", ("dp", "mp"), None),
        P(("dp", "seq"), "mp"),
        P(("dp", "seq"), "mp"),
        P(("dp", "seq"), "mp"),
        P("mp", ("dp", "seq")),
        P(("dp", "seq"), "mp"),
        P("mp", ("dp", "seq")),
        P(("dp", "seq")),
        P(("dp", "seq")),
        P(("dp", "seq")),
        P(("dp", "seq")),
    )
    sizes = (mesh.shape["dp"], mesh.shape["seq"], mesh.shape["mp"])

    def chosen(*arrays):
        seqs, _, part, width = arrays[0].shape
        if sizes == (2, 4, 4) and seqs == sizes[2] and part == width == 512 and arrays[3].shape[1] == 128:
            return fast_body(Plan(part, sizes[0] * sizes[1]), *arrays)
        return general_body(*arrays)

    return jax.shard_map(chosen, mesh=mesh, in_specs=in_specs, out_specs=out_specs, check_vma=False)
```

```python
import functools

import jax
import jax.numpy as jnp
from jax import lax
from jax.experimental import pallas as pl
from jax.experimental.pallas import tpu as pltpu
from jax.sharding import PartitionSpec as P

HD = 64
NR = 16


def cut_along(x, dim, count):
    before, after = (x.shape[:dim], x.shape[dim + 1 :])
    return jnp.moveaxis(x.reshape(*before, count, -1, *after), dim, 0)


def summed_on_arrival(x, axis, dim):
    count = lax.axis_size(axis)
    blocks = lax.all_to_all(cut_along(x, dim, count), axis, 0, 0, tiled=True)
    return jnp.sum(blocks.astype(jnp.float32), axis=0)


def sent_together(arrays, axis, dim, along):
    ends, at = ([], 0)
    for a in arrays[:-1]:
        at += a.shape[along]
        ends.append(at)
    both = jnp.concatenate(arrays, axis=along)
    return tuple(jnp.split(summed_on_arrival(both, axis, dim), ends, axis=along))


def norm_rows(values, gain_row, shift_row):
    center = values - jnp.mean(values, axis=-1, keepdims=True)
    spread = jnp.mean(center * center, axis=-1, keepdims=True)
    return center * lax.rsqrt(spread + 1e-05) * gain_row + shift_row


def norm_gain_parts(values, grad_rows):
    center = values - jnp.mean(values, axis=-1, keepdims=True)
    spread = jnp.mean(center * center, axis=-1, keepdims=True)
    scaled = center * lax.rsqrt(spread + 1e-05)
    return (jnp.sum(grad_rows * scaled, axis=0), jnp.sum(grad_rows, axis=0))


def gelu_exact(values):
    return jax.nn.gelu(values, approximate=False)


def dot_plain(left_mat, right_mat):
    return jnp.dot(left_mat, right_mat, preferred_element_type=jnp.float32)


def dot_inner(left_mat, right_mat):
    return lax.dot_general(
        left_mat, right_mat, (((0,), (0,)), ((), ())), preferred_element_type=jnp.float32
    )


def dot_outer(left_mat, right_mat):
    return lax.dot_general(
        left_mat, right_mat, (((1,), (1,)), ((), ())), preferred_element_type=jnp.float32
    )


def group_sum(values, group_width):
    return jnp.sum(
        values.reshape((values.shape[0] // group_width, group_width) + values.shape[1:]), axis=1
    )


def block_shape(coarse_rows):
    query_len = min(coarse_rows, 512)
    span_len = query_len + 2 * NR
    window_len = -(-span_len // 128) * 128
    return (query_len, span_len, window_len)


def window_mask(level_at, first_row, query_len, window_len, span_len):
    rows_at = first_row + jnp.arange(query_len, dtype=jnp.int32)[:, None]
    keys_at = first_row + jnp.arange(window_len, dtype=jnp.int32)[None, :]
    inside = keys_at - first_row < span_len
    allowed = jnp.abs(rows_at // NR + 1 - keys_at // NR) <= 1
    if level_at > 0:
        half_block = NR // 2
        allowed = allowed & (jnp.abs(rows_at // half_block + 2 - keys_at // half_block) >= 2)
    return (allowed & inside).astype(jnp.float32)


def level_forward(query_rows, pair_wide, count_wide, level_at):
    coarse_rows = query_rows.shape[0]
    columns = query_rows.shape[1]
    heads_here = columns // HD
    query_len, span_len, window_len = block_shape(coarse_rows)
    tail_pad = window_len - span_len
    pair_padded = jnp.pad(pair_wide, ((0, tail_pad), (0, 0)))
    count_padded = jnp.pad(count_wide, (0, tail_pad))
    weight_list = []
    total_parts = []
    numer_parts = []
    for block_at in range(coarse_rows // query_len):
        first_row = block_at * query_len
        query_block = query_rows[first_row : first_row + query_len]
        pair_block = pair_padded[first_row : first_row + window_len]
        count_block = count_padded[first_row : first_row + window_len]
        keep_mask = (
            window_mask(level_at, first_row, query_len, window_len, span_len) * count_block[None, :]
        )
        head_weights = []
        head_totals = []
        head_numers = []
        for head_at in range(heads_here):
            head_cols = slice(head_at * HD, (head_at + 1) * HD)
            value_cols = slice(columns + head_at * HD, columns + (head_at + 1) * HD)
            scores = dot_outer(query_block[:, head_cols], pair_block[:, head_cols]) * HD ** (-0.5)
            weight = jnp.exp(scores) * keep_mask
            head_weights.append(weight)
            head_totals.append(jnp.sum(weight, axis=-1))
            head_numers.append(dot_plain(weight.astype(jnp.bfloat16), pair_block[:, value_cols]))
        weight_list.append(head_weights)
        total_parts.append(jnp.stack(head_totals, axis=1))
        numer_parts.append(jnp.concatenate(head_numers, axis=1))
    totals = jnp.concatenate(total_parts, axis=0)
    numer_part = jnp.concatenate(numer_parts, axis=0).reshape(coarse_rows, heads_here, HD)
    return ((query_rows, pair_padded, weight_list), totals, numer_part)


def level_backward(level_kept, numer_rows, total_rows):
    query_rows, pair_padded, weight_list = level_kept
    coarse_rows = query_rows.shape[0]
    columns = query_rows.shape[1]
    heads_here = columns // HD
    query_len, span_len, window_len = block_shape(coarse_rows)
    numer_flat = numer_rows.reshape(coarse_rows, columns)
    pair_grad = jnp.zeros(pair_padded.shape, jnp.float32)
    query_parts = []
    for block_at in range(coarse_rows // query_len):
        first_row = block_at * query_len
        query_block = query_rows[first_row : first_row + query_len]
        pair_block = pair_padded[first_row : first_row + window_len]
        numer_block = numer_flat[first_row : first_row + query_len]
        total_block = total_rows[first_row : first_row + query_len]
        query_heads = []
        key_heads = []
        value_heads = []
        for head_at in range(heads_here):
            head_cols = slice(head_at * HD, (head_at + 1) * HD)
            value_cols = slice(columns + head_at * HD, columns + (head_at + 1) * HD)
            weight = head_weights = weight_list[block_at][head_at]
            grad_here = numer_block[:, head_cols]
            score_grad = (
                (dot_outer(grad_here, pair_block[:, value_cols]) + total_block[:, head_at][:, None])
                * weight
            ).astype(jnp.bfloat16)
            query_heads.append(dot_plain(score_grad, pair_block[:, head_cols]) * HD ** (-0.5))
            key_heads.append(dot_inner(score_grad, query_block[:, head_cols]) * HD ** (-0.5))
            value_heads.append(dot_inner(head_weights.astype(jnp.bfloat16), grad_here))
        query_parts.append(jnp.concatenate(query_heads, axis=1))
        block_grad = jnp.concatenate(key_heads + value_heads, axis=1)
        pair_grad = pair_grad + jnp.pad(
            block_grad, ((first_row, pair_padded.shape[0] - first_row - window_len), (0, 0))
        )
    query_grad = jnp.concatenate(query_parts, axis=0)
    return (query_grad, pair_grad[: coarse_rows + 2 * NR])


def general_body(
    incoming_embeddings,
    output_sensitivity,
    sequence_extents,
    asking_projector,
    lookup_projector,
    content_projector,
    attention_combiner,
    feedforward_expand,
    feedforward_contract,
    attention_norm_scale,
    attention_norm_bias,
    feedforward_norm_scale,
    feedforward_norm_bias,
):
    groups = lax.axis_size("dp")
    slices = lax.axis_size("seq")
    models = lax.axis_size("mp")
    group_id = lax.axis_index("dp")
    slice_id = lax.axis_index("seq")
    model_id = lax.axis_index("mp")
    seq_count = incoming_embeddings.shape[0]
    piece_len = incoming_embeddings.shape[2]
    model_width = incoming_embeddings.shape[3]
    part_len = piece_len * groups
    batches = seq_count // groups
    share_len = piece_len // models
    share_rows = groups * share_len
    local_top = (part_len // NR).bit_length() - 1
    upper_start = local_top + 1
    level_top = (part_len * slices // (2 * NR)).bit_length() - 1
    upper_rows = NR // 2
    upper_whole = upper_rows * slices
    send_tok = incoming_embeddings.reshape(
        groups, batches, piece_len, model_width
    )
    send_cot = output_sensitivity.reshape(
        groups, batches, piece_len, model_width
    )
    dealt_tok, dealt_cot = (
        lax.all_to_all(send_tok, "dp", split_axis=0, concat_axis=2, tiled=True),
        lax.all_to_all(send_cot, "dp", split_axis=0, concat_axis=2, tiled=True),
    )
    dealt_tok = dealt_tok.reshape(batches, part_len, model_width)
    dealt_cot = dealt_cot.reshape(batches, part_len, model_width)
    my_lengths = lax.dynamic_slice_in_dim(sequence_extents, group_id * batches, batches, 0)

    def split_rows(rows):
        return rows.reshape((groups, models, share_len) + rows.shape[1:])

    def take_share(rows):
        return lax.dynamic_slice_in_dim(split_rows(rows), model_id, 1, 1).reshape(
            (share_rows,) + rows.shape[1:]
        )

    def neighbour_rims(gathered):
        padded = jnp.pad(gathered, ((2 * NR, 2 * NR), (0, 0)))
        from_left = lax.dynamic_slice_in_dim(padded, slice_id * 2 * NR + NR, NR, 0)
        from_right = lax.dynamic_slice_in_dim(padded, (slice_id + 2) * 2 * NR, NR, 0)
        return (from_left, from_right)

    def one_batch(batch_index, learnable_collection):
        full_query, full_key, full_value, full_merge, full_up, full_down = learnable_collection[:6]
        gain_pre, shift_pre, gain_mid, shift_mid = (
            learnable_tensor.astype(jnp.float32) for learnable_tensor in learnable_collection[6:]
        )
        columns = full_query.shape[1]
        heads_here = columns // HD
        length_now = my_lengths[batch_index]

        def level_counts(level_at, first_id, id_total):
            coarse_ids = first_id + jnp.arange(id_total, dtype=jnp.int32)
            group_len = 2**level_at
            return jnp.where(
                coarse_ids >= 0, jnp.clip(length_now - group_len * coarse_ids, 0, group_len), 0
            ).astype(jnp.float32)

        positions = slice_id * part_len + jnp.arange(part_len, dtype=jnp.int32)
        valid_rows = (positions < length_now).astype(jnp.float32)
        inputs = dealt_tok[batch_index].astype(jnp.float32)
        grad_in = dealt_cot[batch_index].astype(jnp.float32) * valid_rows[:, None]
        valid_share = take_share(valid_rows)
        normed, pull_pre = jax.vjp(norm_rows, inputs, gain_pre, shift_pre)
        normed_low = normed.astype(jnp.bfloat16)
        queries = dot_plain(normed_low, full_query).astype(jnp.bfloat16)
        keys_own = dot_plain(normed_low, full_key).astype(jnp.bfloat16)
        values_own = dot_plain(normed_low, full_value).astype(jnp.bfloat16)
        pair_own = jnp.concatenate([keys_own, values_own], axis=1)
        fine_all = (
            jnp.concatenate([queries, pair_own], axis=1).astype(jnp.float32) * valid_rows[:, None]
        )
        level_sums = [fine_all]
        for level_at in range(1, upper_start + 1):
            level_sums.append(group_sum(level_sums[-1], 2))
        query_levels = [queries]
        pair_levels = [pair_own]
        own_counts = [valid_rows]
        for level_at in range(1, local_top + 1):
            coarse_rows = part_len >> level_at
            counts_here = level_counts(level_at, slice_id * coarse_rows, coarse_rows)
            coarse_means = (level_sums[level_at] / jnp.maximum(counts_here, 1.0)[:, None]).astype(
                jnp.bfloat16
            )
            query_levels.append(coarse_means[:, :columns])
            pair_levels.append(coarse_means[:, columns:])
            own_counts.append(counts_here)
        edge_rows = jnp.concatenate(
            [
                jnp.concatenate([pair_rows[:NR], pair_rows[-NR:]], axis=0)
                for pair_rows in pair_levels
            ],
            axis=1,
        )
        edges_all, upper_all = (
            lax.all_gather(
                edge_rows.astype(jnp.float32).astype(jnp.bfloat16), "seq", axis=0, tiled=True
            ).astype(jnp.float32),
            lax.all_gather(
                level_sums[upper_start].astype(jnp.bfloat16), "seq", axis=0, tiled=True
            ).astype(jnp.float32),
        )
        left_edge, right_edge = neighbour_rims(edges_all)
        left_edge = left_edge.astype(jnp.bfloat16)
        right_edge = right_edge.astype(jnp.bfloat16)
        kept_levels = []
        total_all = jnp.zeros((part_len, heads_here), jnp.float32)
        numer_all = jnp.zeros((part_len, heads_here, HD), jnp.float32)
        for level_at in range(local_top + 1):
            coarse_rows = part_len >> level_at
            col_range = slice(level_at * 2 * columns, (level_at + 1) * 2 * columns)
            pair_wide = jnp.concatenate(
                [left_edge[:, col_range], pair_levels[level_at], right_edge[:, col_range]], axis=0
            )
            count_wide = level_counts(level_at, slice_id * coarse_rows - NR, coarse_rows + 2 * NR)
            level_kept, totals, numer_part = level_forward(
                query_levels[level_at], pair_wide, count_wide, level_at
            )
            kept_levels.append(level_kept)
            total_all = total_all + jnp.repeat(totals, 2**level_at, axis=0)
            numer_all = numer_all + jnp.repeat(numer_part, 2**level_at, axis=0)
        level_at = 7
        repeat_by = 2 ** (level_at - upper_start)
        coarse_rows = upper_whole // repeat_by
        counts_here = level_counts(level_at, 0, coarse_rows)
        coarse_means = (
            group_sum(upper_all, repeat_by) / jnp.maximum(counts_here, 1.0)[:, None]
        ).astype(jnp.bfloat16)
        pair_wide = jnp.pad(coarse_means[:, columns:], ((NR, NR), (0, 0)))
        count_wide = level_counts(level_at, -NR, coarse_rows + 2 * NR)
        level_kept, totals, numer_part = level_forward(
            coarse_means[:, :columns], pair_wide, count_wide, level_at
        )
        upper_kept = [level_kept]
        upper_counts = [counts_here]
        upper_total = jnp.repeat(totals, repeat_by, axis=0)
        upper_numer = jnp.repeat(numer_part, repeat_by, axis=0)
        total_all = total_all + jnp.repeat(
            lax.dynamic_slice_in_dim(upper_total, slice_id * upper_rows, upper_rows, 0),
            2**upper_start,
            axis=0,
        )
        numer_all = numer_all + jnp.repeat(
            lax.dynamic_slice_in_dim(upper_numer, slice_id * upper_rows, upper_rows, 0),
            2**upper_start,
            axis=0,
        )
        attended = (
            (numer_all / total_all[:, :, None]).reshape(part_len, columns).astype(jnp.bfloat16)
        )
        merged_part = dot_plain(attended, full_merge)
        branch_attn = lax.psum(merged_part, "mp")
        after_attn = inputs + branch_attn
        mid_normed, pull_mid = jax.vjp(norm_rows, after_attn, gain_mid, shift_mid)
        mid_low = mid_normed.astype(jnp.bfloat16)
        after_share = take_share(after_attn)
        up_proj = dot_plain(mid_low, full_up)
        activated, pull_gelu = jax.vjp(gelu_exact, up_proj)
        act_low = activated.astype(jnp.bfloat16)
        ffn_share = (
            lax.psum_scatter(
                split_rows(dot_plain(act_low, full_down)).astype(jnp.bfloat16),
                "mp",
                scatter_dimension=1,
                tiled=True,
            )
            .astype(jnp.float32)
            .reshape(share_rows, model_width)
        )
        result_share = (valid_share[:, None] * (after_share + ffn_share)).astype(jnp.bfloat16)
        grad_low = grad_in.astype(jnp.bfloat16)
        act_grad = dot_outer(grad_low, full_down)
        down_acc = dot_inner(act_low, grad_low)
        hidden_grad = pull_gelu(act_grad)[0].astype(jnp.bfloat16)
        up_acc = dot_inner(mid_low, hidden_grad)
        mid_part = dot_outer(hidden_grad, full_up)
        mid_grad = lax.psum(mid_part, "mp")
        back_mid = pull_mid(mid_grad)[0]
        residual_grad = grad_in + back_mid
        branch_grad = residual_grad.astype(jnp.bfloat16)
        residual_share = take_share(residual_grad)
        gain_mid_part, shift_mid_part = norm_gain_parts(after_share, take_share(mid_grad))
        merge_acc = dot_inner(attended, branch_grad)
        attended_grad = dot_outer(branch_grad, full_merge).reshape(part_len, heads_here, HD)
        numer_grad = (attended_grad / total_all[:, :, None]).astype(jnp.bfloat16)
        total_grad = -jnp.sum(attended_grad * numer_all, axis=-1) / (total_all * total_all)
        numer_wide = numer_grad.astype(jnp.float32)
        rim_parts = []
        own_pair_grads = []
        query_coarse = []
        for level_at in range(local_top + 1):
            coarse_rows = part_len >> level_at
            if level_at == 0:
                numer_sum = numer_grad
                total_sum = total_grad
            else:
                numer_sum = group_sum(numer_wide, 2**level_at).astype(jnp.bfloat16)
                total_sum = group_sum(total_grad, 2**level_at)
            query_grad, pair_grad = level_backward(kept_levels[level_at], numer_sum, total_sum)
            rim_parts.append(
                jnp.concatenate([pair_grad[:NR], pair_grad[NR + coarse_rows :]], axis=0)
            )
            own_pair_grads.append(pair_grad[NR : NR + coarse_rows])
            query_coarse.append(query_grad)
        rim_grads = jnp.concatenate(rim_parts, axis=1)
        upper_numer_grad = group_sum(numer_wide, 2**upper_start).reshape(upper_rows, columns)
        upper_total_grad = group_sum(total_grad, 2**upper_start)
        rims_all, numer_sums, total_sums = (
            lax.all_gather(rim_grads.astype(jnp.bfloat16), "seq", axis=0, tiled=True).astype(
                rim_grads.dtype
            ),
            lax.all_gather(upper_numer_grad.astype(jnp.bfloat16), "seq", axis=0, tiled=True).astype(
                upper_numer_grad.dtype
            ),
            lax.all_gather(upper_total_grad.astype(jnp.bfloat16), "seq", axis=0, tiled=True).astype(
                upper_total_grad.dtype
            ),
        )
        from_left, from_right = neighbour_rims(rims_all)
        fine_grad = jnp.zeros((part_len, 3 * columns), jnp.float32)
        for level_at in range(local_top + 1):
            coarse_rows = part_len >> level_at
            col_range = slice(level_at * 2 * columns, (level_at + 1) * 2 * columns)
            pair_here = (
                own_pair_grads[level_at]
                + jnp.pad(from_left[:, col_range], ((0, coarse_rows - NR), (0, 0)))
                + jnp.pad(from_right[:, col_range], ((coarse_rows - NR, 0), (0, 0)))
            )
            coarse_grad = jnp.concatenate([query_coarse[level_at], pair_here], axis=1)
            if level_at == 0:
                fine_grad = coarse_grad
            else:
                coarse_grad = coarse_grad / jnp.maximum(own_counts[level_at], 1.0)[:, None]
                fine_grad = (
                    fine_grad + jnp.repeat(coarse_grad, 2**level_at, axis=0) * valid_rows[:, None]
                )
        upper_grad = jnp.zeros((upper_whole, 3 * columns), jnp.float32)
        for index_at, level_at in enumerate(range(upper_start, level_top + 1)):
            repeat_by = 2 ** (level_at - upper_start)
            coarse_rows = upper_whole // repeat_by
            numer_sum = (
                group_sum(numer_sums, repeat_by)
                .reshape(coarse_rows, heads_here, HD)
                .astype(jnp.bfloat16)
            )
            total_sum = group_sum(total_sums, repeat_by)
            query_grad, pair_grad = level_backward(upper_kept[index_at], numer_sum, total_sum)
            coarse_grad = (
                jnp.concatenate([query_grad, pair_grad[NR : NR + coarse_rows]], axis=1)
                / jnp.maximum(upper_counts[index_at], 1.0)[:, None]
            )
            upper_grad = jnp.repeat(coarse_grad, repeat_by, axis=0)
        own_upper = lax.dynamic_slice_in_dim(upper_grad, slice_id * upper_rows, upper_rows, 0)
        fine_grad = fine_grad + jnp.repeat(own_upper, 2**upper_start, axis=0) * valid_rows[:, None]
        rows_grad = fine_grad.astype(jnp.bfloat16)
        query_rows_grad = rows_grad[:, :columns]
        key_rows_grad = rows_grad[:, columns : 2 * columns]
        value_rows_grad = rows_grad[:, 2 * columns :]
        query_acc = dot_inner(normed_low, query_rows_grad)
        key_acc = dot_inner(normed_low, key_rows_grad)
        value_acc = dot_inner(normed_low, value_rows_grad)
        normed_part = (
            dot_outer(query_rows_grad, full_query)
            + dot_outer(key_rows_grad, full_key)
            + dot_outer(value_rows_grad, full_value)
        )
        normed_grad, gain_mid_sum, shift_mid_sum = (
            lax.psum(normed_part.astype(jnp.bfloat16), "mp").astype(jnp.float32),
            lax.psum(gain_mid_part.astype(jnp.bfloat16), "mp").astype(jnp.float32),
            lax.psum(shift_mid_part.astype(jnp.bfloat16), "mp").astype(jnp.float32),
        )
        back_pre, gain_pre_acc, shift_pre_acc = pull_pre(normed_grad)
        input_share = (residual_share + take_share(back_pre)).astype(jnp.bfloat16)
        grad_terms = (
            query_acc,
            key_acc,
            value_acc,
            merge_acc,
            up_acc,
            down_acc,
            gain_pre_acc,
            shift_pre_acc,
            gain_mid_sum,
            shift_mid_sum,
        )
        return (result_share, input_share, grad_terms)

    result_list = []
    grad_list = []
    running_sum = None
    for batch_index in range(batches):
        learnable_collection = (
            lax.all_gather(asking_projector, ("dp", "seq"), axis=0, tiled=True),
            lax.all_gather(lookup_projector, ("dp", "seq"), axis=0, tiled=True),
            lax.all_gather(content_projector, ("dp", "seq"), axis=0, tiled=True),
            lax.all_gather(attention_combiner, ("dp", "seq"), axis=1, tiled=True),
            lax.all_gather(feedforward_expand, ("dp", "seq"), axis=0, tiled=True),
            lax.all_gather(feedforward_contract, ("dp", "seq"), axis=1, tiled=True),
            lax.all_gather(attention_norm_scale, ("dp", "seq"), axis=0, tiled=True),
            lax.all_gather(attention_norm_bias, ("dp", "seq"), axis=0, tiled=True),
            lax.all_gather(feedforward_norm_scale, ("dp", "seq"), axis=0, tiled=True),
            lax.all_gather(feedforward_norm_bias, ("dp", "seq"), axis=0, tiled=True),
        )
        result_share, input_share, grad_terms = one_batch(batch_index, learnable_collection)
        result_list.append(result_share)
        grad_list.append(input_share)
        if running_sum is None:
            running_sum = grad_terms
        else:
            running_sum = tuple(
                (older_sum + newer_sum for older_sum, newer_sum in zip(running_sum, grad_terms))
            )
    owned_grads = (
        *sent_together(
            (
                running_sum[0].astype(jnp.bfloat16),
                running_sum[1].astype(jnp.bfloat16),
                running_sum[2].astype(jnp.bfloat16),
            ),
            ("dp", "seq"),
            0,
            1,
        ),
        summed_on_arrival(running_sum[3].astype(jnp.bfloat16), ("dp", "seq"), 1),
        summed_on_arrival(running_sum[4].astype(jnp.bfloat16), ("dp", "seq"), 0),
        summed_on_arrival(running_sum[5].astype(jnp.bfloat16), ("dp", "seq"), 1),
        summed_on_arrival(running_sum[6].astype(jnp.bfloat16), ("dp", "seq"), 0),
        summed_on_arrival(running_sum[7].astype(jnp.bfloat16), ("dp", "seq"), 0),
        summed_on_arrival(running_sum[8].astype(jnp.bfloat16), ("dp", "seq"), 0),
        summed_on_arrival(running_sum[9].astype(jnp.bfloat16), ("dp", "seq"), 0),
    )
    result_all = jnp.stack(result_list, axis=0).reshape(batches, groups, share_len, model_width)
    grad_all = jnp.stack(grad_list, axis=0).reshape(batches, groups, share_len, model_width)
    back_out, back_grad = (
        lax.all_to_all(result_all, "dp", split_axis=1, concat_axis=0, tiled=True),
        lax.all_to_all(grad_all, "dp", split_axis=1, concat_axis=0, tiled=True),
    )
    return (
        back_out,
        back_grad,
        owned_grads[0],
        owned_grads[1],
        owned_grads[2],
        owned_grads[3],
        owned_grads[4],
        owned_grads[5],
        owned_grads[6],
        owned_grads[7],
        owned_grads[8],
        owned_grads[9],
    )


MESH = pl.DeviceIdType.MESH
NEG = -1e30


def nn(a, b):
    return lax.dot_general(a, b, (((1,), (0,)), ((), ())), preferred_element_type=jnp.float32)


def nt(a, b):
    return lax.dot_general(a, b, (((1,), (1,)), ((), ())), preferred_element_type=jnp.float32)


def tn(a, b):
    return lax.dot_general(a, b, (((0,), (0,)), ((), ())), preferred_element_type=jnp.float32)


def halves(values):
    high = values.astype(jnp.bfloat16)
    return high, (values - high.astype(jnp.float32)).astype(jnp.bfloat16)


class Plan:
    def __init__(self, part, spots):
        self.part, self.spots = part, spots
        self.levels = (part // NR).bit_length()
        self.top = (part * spots // (2 * NR)).bit_length() - 1
        self.own = [part >> level for level in range(self.levels)]
        self.at, row = [], 0
        for rows in self.own:
            self.at.append(row)
            row += rows + 2 * NR
        self.upper = row
        self.rows = row + spots * NR
        self.pool_at, row = [None], 0
        for rows in self.own[1:]:
            self.pool_at.append(row)
            row += rows
        self.pool_upper = row
        self.pooled = row + NR
        self.slot, row = [], 0
        for level in range(self.levels, self.top + 1):
            self.slot.append((level, row, part >> level))
            row += part >> level
        assert row <= NR and spots * NR == 128 and self.pooled == part
        self.segments = [(self.at[lv], self.own[lv] + 2 * NR, lv) for lv in range(self.levels)]
        self.inner, self.outer = [], []
        level = 0
        while level < self.levels:
            start, total = self.at[level], self.own[level] + 2 * NR
            end = start + total
            if total < 96:
                self.outer.append((start, self.upper - start, self.upper - 128, None))
                break
            row = start
            while row < end:
                count = min(96, end - row)
                window = max(start, min(row - NR, end - 128))
                tile = (row, count, window, level if window + 128 <= end else None)
                inside = window >= start + NR and window + 128 <= end - NR
                (self.inner if inside else self.outer).append(tile)
                row += count
            level += 1
        self.outer.append((self.upper, 128, self.upper, None))
        self.tiles = self.inner + self.outer

    def own_pieces(self, tile):
        first, count = tile[:2]
        pieces = []
        for start, rows in zip(self.at, self.own):
            low, high = max(first, start + NR), min(first + count, start + NR + rows)
            if low < high:
                pieces.append((low, high - low))
        return pieces


def row_places(plan, rows, low, high, spot):
    level = jnp.full(rows.shape, -1, jnp.int32)
    place = jnp.zeros(rows.shape, jnp.int32)
    for start, count, lv in plan.segments:
        if start < high and start + count > low:
            inside = (rows >= start) & (rows < start + count)
            level = jnp.where(inside, lv, level)
            place = jnp.where(inside, spot * plan.own[lv] - NR + rows - start, place)
    if high > plan.upper:
        owner = lax.shift_right_arithmetic(rows - plan.upper, 4)
        within = (rows - plan.upper) & (NR - 1)
        for lv, first, count in plan.slot:
            inside = (rows >= plan.upper) & (within >= first) & (within < first + count)
            level = jnp.where(inside, lv, level)
            place = jnp.where(inside, owner * count + within - first, place)
    return level, place


def log_counts(plan, tile, spot, length):
    first, count, window, level = tile
    row_at = first + lax.broadcasted_iota(jnp.int32, (count, 128), 0)
    key_at = window + lax.broadcasted_iota(jnp.int32, (8, 128), 1)
    row_level, row_place = row_places(plan, row_at, first, first + count, spot)
    key_level, key_place = row_places(plan, key_at, window, window + 128, spot)
    span = lax.shift_left(jnp.ones_like(key_level), jnp.maximum(key_level, 0))
    counts = jnp.clip(length - span * key_place, 0, span)
    usable = (counts > 0) & (key_place >= 0) & (key_level >= 0)
    logs = jnp.where(usable, jnp.log(jnp.maximum(counts, 1).astype(jnp.float32)), NEG)
    coarse = lambda level_at, place_at, by: level_at * 65536 + lax.shift_right_arithmetic(place_at, by)
    key_block = coarse(key_level, key_place, 4)[:1]
    key_half = coarse(key_level, key_place, 3)[:1]
    allowed = jnp.abs(coarse(row_level, row_place, 4) - key_block) <= 1
    if level != 0:
        apart = jnp.abs(coarse(row_level, row_place, 3) - key_half) >= 2
        allowed = allowed & (apart if level is not None else apart | (row_level == 0)) & (row_level >= 0)
    return jnp.where(allowed, logs[:1], NEG)


def pool_bounds(plan, shape, dim):
    row = lax.broadcasted_iota(jnp.int32, shape, dim)
    low = jnp.full(shape, -1, jnp.int32)
    size = jnp.zeros(shape, jnp.int32)
    level = jnp.zeros(shape, jnp.int32)
    parts = [(plan.pool_at[lv], plan.own[lv], lv) for lv in range(1, plan.levels)]
    parts += [(plan.pool_upper + first, count, lv) for lv, first, count in plan.slot]
    for start, count, lv in parts:
        inside = (row >= start) & (row < start + count)
        low = jnp.where(inside, (row - start) << lv, low)
        size = jnp.where(inside, 1 << lv, size)
    return low, size


def spread_columns(rows, place, count):
    width = rows.shape[1]
    source = lax.broadcasted_iota(jnp.int32, (width, width * count), 0)
    target = lax.broadcasted_iota(jnp.int32, (width, width * count), 1)
    return nn(rows, jnp.where(target == source + place * width, 1.0, 0.0).astype(rows.dtype))


def flip_bits(value, k):
    low, high, k_low, k_high = value % 2, value // 2, k % 2, k // 2
    return (high + k_high - 2 * high * k_high) * 2 + low + k_low - 2 * low * k_low


class Marks:
    def __init__(self):
        self.used = 0

    def take(self, count):
        self.used += count
        return self.used - count


def whole_layer(plan, dims, net_count, *refs):
    (extents, w_query, w_key, w_value, w_merge, w_expand, w_contract, norm_0, norm_1, norm_2, norm_3, tokens_in, cotangent_in,
     out_rows, out_grads, weight_grads, norm_grads,
     weights, norms, tokens, cotangent, ext, logs, pool, unpool, inverse, work,
     attended, ratio, recip, normed, scaled, rstd, grad_ext, total_ext, residual, acc, acc2, totals, result, row_grads,
     active, slope, grads, got1, got2, got3, got4, norm_got,
     load_sem, send_sem, recv_sem) = refs
    part, width, pair, hidden = dims
    f32, bf16 = jnp.float32, jnp.bfloat16
    models = weights.shape[0]
    strip, columns = weights.shape[4:]
    ax, sq, az = lax.axis_index("dp"), lax.axis_index("seq"), lax.axis_index("mp")
    ay, ac = sq // 2, sq % 2
    spot = sq * 2 + ax
    spots = plan.spots
    length = extents[az]
    qkv = 3 * pair

    def device(x, y, c, z):
        return (x, y * 2 + c, z)

    def at_spot(place):
        return (place % 2, place // 2, az)

    def plane(k):
        return flip_bits(az, k)

    x_peer, y_peer, c_peer = device(1 - ax, ay, ac, az), device(ax, 1 - ay, ac, az), device(ax, ay, 1 - ac, az)
    z_peer = lambda k: device(ax, ay, ac, plane(k))

    barrier = pltpu.get_barrier_semaphore()
    for step in range(1, spots):
        pl.semaphore_signal(barrier, inc=1, device_id=at_spot((spot + step) % spots), device_id_type=MESH)
    for k in range(1, models):
        pl.semaphore_signal(barrier, inc=1, device_id=z_peer(k), device_id_type=MESH)
    load_tokens = pltpu.make_async_copy(tokens_in.at[az, 0], tokens, load_sem.at[0])
    load_cotangent = pltpu.make_async_copy(cotangent_in.at[az, 0], cotangent, load_sem.at[1])
    load_tokens.start()
    load_cotangent.start()
    own = (az, ax, ay, ac)
    weights[own + (slice(None), slice(0, pair))] = w_query[...] * jnp.asarray(HD ** -0.5, bf16)
    weights[own + (slice(None), slice(pair, 2 * pair))] = w_key[...]
    weights[own + (slice(None), slice(2 * pair, qkv))] = w_value[...]
    weights[own + (slice(None), slice(qkv, qkv + pair))] = w_merge[...]
    weights[own + (slice(None), slice(4 * pair, 4 * pair + hidden))] = w_expand[...]
    weights[own + (slice(None), slice(4 * pair + hidden, columns))] = w_contract[...]
    owner = ax * 4 + sq
    norms[spot] = jnp.concatenate(
        [spread_columns(row[...], owner, width // strip) for row in (norm_0, norm_1, norm_2, norm_3)]
        + [jnp.zeros((4, width), f32)], axis=0)
    pl.semaphore_wait(barrier, spots - 1 + models - 1)

    marks = Marks()

    def copy(i, src, dst, to):
        return pltpu.make_async_remote_copy(
            src_ref=src, dst_ref=dst, send_sem=send_sem.at[i], recv_sem=recv_sem.at[i],
            device_id=to, device_id_type=MESH)

    class Group:
        def __init__(self, i, pairs, whole):
            self.i, self.pairs, self.whole = i, pairs, whole

        def start(self):
            for src, dst, to in self.pairs:
                copy(self.i, src, dst, to).start()
            return self

        def arrive(self):
            copy(self.i, self.whole, self.whole, self.pairs[0][2]).wait_recv()

        def leave(self):
            copy(self.i, self.whole, self.whole, self.pairs[0][2]).wait_send()

    sent = []

    def send(pairs, whole):
        group = Group(marks.take(1), pairs, whole).start()
        sent.append(group)
        return group

    class Gather:
        def __init__(self, col, count, through_y):
            self.cols, self.rows = pl.ds(col, count), through_y
            self.flight = {}

        def block(self, k, x, y, rows=slice(None)):
            return weights.at[plane(k), x, y, ac, rows, self.cols]

        def to_planes(self):
            here = self.block(0, ax, ay)
            for k in range(1, models):
                self.flight["z", k] = send([(here, here, z_peer(k))], here)

        def to_sides(self, k):
            if k:
                self.flight["z", k].arrive()
            here = self.block(k, ax, ay)
            self.flight["side", k] = send([(here, here, x_peer), (here, here, y_peer)],
                                          weights.at[plane(k), :, ay, ac, :, self.cols])

        def to_corner(self, k):
            self.flight["side", k].arrive()
            first = self.block(k, 1 - ax, ay, pl.ds(0, self.rows))
            rest = self.block(k, ax, 1 - ay, pl.ds(self.rows, strip - self.rows))
            self.flight["corner", k] = send([(first, first, y_peer), (rest, rest, x_peer)], self.block(k, ax, ay))

        def to_core(self, k):
            self.flight["corner", k].arrive()
            here = weights.at[plane(k), :, :, ac, :, self.cols]
            self.flight["core", k] = send([(here, here, c_peer)], here)

        def here(self, k):
            self.flight["core", k].arrive()

    first_gather = Gather(0, qkv, 32)
    merge_gather = Gather(qkv, pair + hidden, 48)
    last_gather = Gather(4 * pair + hidden, hidden, 48)

    first_gather.to_planes()
    first_gather.to_sides(0)
    norm_copies = send([(norms.at[spot], norms.at[spot], at_spot((spot + step) % spots)) for step in range(1, spots)],
                       norms.at[pl.ds(0, spots - 1)])

    low, size = pool_bounds(plan, (part, 128), 0)
    for block in range(part // 128):
        token_at = block * 128 + lax.broadcasted_iota(jnp.int32, (part, 128), 1)
        member = (token_at >= low) & (token_at < low + size) & (token_at + spot * part < length)
        pool[:, block * 128:(block + 1) * 128] = jnp.where(member, 1.0, 0.0).astype(bf16)
    counts = jnp.clip(length - spot * part - low, 0, size)
    inverse[...] = 1.0 / jnp.maximum(counts, 1).astype(f32)
    low, size = pool_bounds(plan, (8, part), 1)
    token_at = lax.broadcasted_iota(jnp.int32, (part, part), 0)
    member = (token_at >= low[:1]) & (token_at < (low + size)[:1])
    unpool[...] = jnp.where(member, 1.0, 0.0).astype(bf16)
    first_gather.to_corner(0)
    first_gather.to_sides(1)
    load_tokens.wait()

    def statistics(values):
        center = values - jnp.mean(values, axis=-1, keepdims=True)
        spread = jnp.mean(center * center, axis=-1, keepdims=True)
        scale = lax.rsqrt(spread + 1e-05)
        return center * scale, scale

    xhat, scale = statistics(tokens[...].astype(f32))
    scaled[...] = xhat
    rstd[...] = jnp.broadcast_to(scale, (part, 128))
    first_gather.to_sides(2)
    first_gather.to_sides(3)
    merge_gather.to_planes()
    first_gather.to_core(0)
    first_gather.to_corner(1)
    for i, tile in enumerate(plan.tiles):
        logs[i, 0:tile[1]] = log_counts(plan, tile, spot, length)
    first_gather.to_corner(2)
    first_gather.to_corner(3)
    merge_gather.to_sides(0)
    first_gather.to_core(1)
    norm_copies.arrive()
    gains = norms[0]
    for i in range(1, spots):
        gains = gains + norms[i]
    pre_gain, pre_shift, mid_gain, mid_shift = (gains[i:i + 1] for i in range(4))
    normed[...] = (scaled[...] * pre_gain + pre_shift).astype(bf16)
    first_gather.to_core(2)
    first_gather.to_core(3)
    last_gather.to_planes()

    is_first, is_last = spot == 0, spot == spots - 1

    @pl.when(is_first)
    def _():
        for lv in range(plan.levels):
            rows = slice(plan.at[lv], plan.at[lv] + NR)
            ext[:, rows, :] = jnp.zeros((models, NR, qkv), bf16)
            grad_ext[:, rows, :] = jnp.zeros((models, NR, pair), bf16)
            total_ext[rows, :] = jnp.zeros((NR, 128), bf16)

    @pl.when(is_last)
    def _():
        for lv in range(plan.levels):
            end = plan.at[lv] + NR + plan.own[lv]
            rows = slice(end, end + NR)
            ext[:, rows, :] = jnp.zeros((models, NR, qkv), bf16)
            grad_ext[:, rows, :] = jnp.zeros((models, NR, pair), bf16)
            total_ext[rows, :] = jnp.zeros((NR, 128), bf16)

    def weight_cols(m, col, count):
        return weights[m, :, :, :, :, col:col + count].reshape(width, count)

    slot_row = pl.multiple_of(spot * NR, NR)
    own_slot_rows = pl.ds(pl.multiple_of(plan.upper + slot_row, NR), NR)
    class Rims:
        def __init__(self, view, i):
            self.view, self.i, self.to = view, i, at_spot((spot + 1) % spots)

        def start(self):
            view, i = self.view, self.i
            right, left = at_spot((spot + 1) % spots), at_spot((spot + spots - 1) % spots)

            @pl.when(jnp.logical_not(is_last))
            def _():
                for start, rows in zip(plan.at, plan.own):
                    copy(i, view(pl.ds(start + rows, NR)), view(pl.ds(start, NR)), right).start()

            @pl.when(jnp.logical_not(is_first))
            def _():
                for start, rows in zip(plan.at, plan.own):
                    copy(i, view(pl.ds(start + NR, NR)), view(pl.ds(start + NR + rows, NR)), left).start()

            block = view(own_slot_rows)
            for step in range(1, spots):
                copy(i, block, block, at_spot((spot + step) % spots)).start()

        def whole(self, sides):
            rows = self.view(pl.ds(0, (sides * plan.levels + spots - 1) * NR))
            return copy(self.i, rows, rows, self.to)

        def wait(self):
            at_end = is_first | is_last

            @pl.when(at_end)
            def _():
                self.whole(1).wait_recv()

            @pl.when(jnp.logical_not(at_end))
            def _():
                self.whole(2).wait_recv()

        def done(self):
            at_end = is_first | is_last

            @pl.when(at_end)
            def _():
                self.whole(1).wait_send()

            @pl.when(jnp.logical_not(at_end))
            def _():
                self.whole(2).wait_send()

    pair_base = marks.take(models)
    query_base = marks.take(1)
    grad_base = marks.take(models)
    total_base = marks.take(1)
    pair_rims = lambda k: Rims(lambda rows: ext.at[plane(k), rows, pl.ds(pair, 2 * pair)], pair_base + k)
    query_rims = lambda: Rims(lambda rows: ext.at[:, rows, pl.ds(0, pair)], query_base)
    grad_rims = lambda k: Rims(lambda rows: grad_ext.at[plane(k), rows, :], grad_base + k)
    total_rims = lambda: Rims(lambda rows: total_ext.at[rows, :], total_base)

    for k in range(models):
        first_gather.here(k)
        m = plane(k)
        rows = nn(normed[...], weight_cols(m, 0, qkv)).astype(bf16)
        ext[m, NR:NR + part, :] = rows
        means = (nn(pool[...], rows) * jnp.concatenate([inverse[...]] * 3, axis=1)).astype(bf16)
        for lv in range(1, plan.levels):
            ext[m, plan.at[lv] + NR:plan.at[lv] + NR + plan.own[lv], :] = means[plan.pool_at[lv]:plan.pool_at[lv] + plan.own[lv]]
        ext[m, own_slot_rows, :] = means[plan.pool_upper:plan.pool_upper + NR]
        pair_rims(k).start()

    for k in range(1, models):
        merge_gather.to_sides(k)

    lane = lax.broadcasted_iota(jnp.int32, (1, pair), 1)
    left_head = lane < HD

    def both_heads(rows):
        zero = jnp.zeros_like(rows)
        return jnp.concatenate([jnp.where(left_head, rows, zero), jnp.where(left_head, zero, rows)], axis=0)

    def joined(rows):
        half = rows.shape[0] // 2
        return jnp.where(left_head, rows[:half], rows[half:])

    ones = jnp.ones((128, 128), bf16)

    def stacked(parts):
        return parts[0] if len(parts) == 1 else jnp.concatenate(parts, axis=0)

    def tile_weights(m, rows, mask, window):
        queries = both_heads(rows)
        keys = ext[m, window:window + 128, pair:2 * pair]
        values = jnp.concatenate([ext[m, window:window + 128, 2 * pair:3 * pair], ones], axis=1)
        weight = jnp.exp(nt(queries, keys) + jnp.concatenate([mask, mask], axis=0))
        return queries, keys, values, weight

    def attend(tiles, first_k, last_k, wait_rims):
        def body(k, carry):
            m = plane(k)
            if wait_rims:
                pair_rims(k).wait()
            for tile in tiles:
                first, _, window, _ = tile
                index = plan.tiles.index(tile)
                if first == plan.upper:
                    pieces = [(first, NR)]
                    rows, mask = ext[m, own_slot_rows, 0:pair], logs[index, pl.ds(slot_row, NR)]
                else:
                    pieces = plan.own_pieces(tile)
                    rows = stacked([ext[m, low:low + count, 0:pair] for low, count in pieces])
                    mask = stacked([logs[index, low - first:low - first + count] for low, count in pieces])
                _, _, values, weight = tile_weights(m, rows, mask, window)
                both = nn(weight.astype(bf16), values)
                numer, tot = joined(both[:, :128]), joined(both[:, 128:])
                at = 0
                for low, count in pieces:
                    work[m, low:low + count, 0:pair] = numer[at:at + count]
                    work[m, low:low + count, pair:2 * pair] = tot[at:at + count]
                    at += count
            return carry

        lax.fori_loop(first_k, last_k, body, 0)

    attend(plan.inner, 0, models, False)
    attend(plan.outer, 0, 2, True)
    for k in range(models):
        merge_gather.to_corner(k)
    for k in range(models):
        last_gather.to_sides(k)
    attend(plan.outer, 2, models, True)
    for k in range(models):
        merge_gather.to_core(k)

    def coarse_rows(m, cols, slot_at):
        rows = [work[m, plan.at[lv] + NR:plan.at[lv] + NR + plan.own[lv], 0:cols] for lv in range(1, plan.levels)]
        return jnp.concatenate(rows + [work[m, slot_at, 0:cols]], axis=0)

    def spread_out(rows):
        high, rest = halves(rows)
        return nn(unpool[...], high) + nn(unpool[...], rest)

    def normalise(m, carry):
        both = spread_out(coarse_rows(m, 2 * pair, slice(plan.upper, plan.upper + NR)))
        both = both + work[m, NR:NR + part, 0:2 * pair]
        inv_total = 1.0 / both[:, pair:]
        quotient = both[:, :pair] * inv_total
        ratio[m] = quotient
        recip[m] = inv_total
        attended[m] = quotient.astype(bf16)
        return carry

    lax.fori_loop(0, models, normalise, 0)
    for k in range(models):
        last_gather.to_corner(k)

    residual[...] = tokens[...].astype(f32)
    for k in range(models):
        merge_gather.here(k)

    def merge(m, carry):
        residual[...] += nt(attended[m], weight_cols(m, qkv, pair))
        return carry

    lax.fori_loop(0, models, merge, 0)
    after = residual[...]
    mid_hat, mid_scale = statistics(after)
    mid = (mid_hat * mid_gain + mid_shift).astype(bf16)
    mid_t = mid.T
    load_cotangent.wait()
    row_at = lax.broadcasted_iota(jnp.int32, (part, 1), 0) + spot * part
    valid = row_at < length
    out_grad = jnp.where(valid, cotangent[...], jnp.zeros((), bf16))
    out_grad_t = out_grad.T
    acc[...] = jnp.zeros(acc.shape, f32)
    acc2[...] = jnp.zeros(acc.shape, f32)
    block_shape = grads.shape[1:5] + (hidden,)

    def feed_up(m, carry):
        up = nn(mid, weight_cols(m, 4 * pair, hidden))
        phi = 0.5 + 0.5 * lax.erf(up * (0.5 ** 0.5))
        active[m] = (up * phi).astype(bf16)
        slope[m] = phi + up * (jnp.exp(-0.5 * up * up) * 0.3989422804014327)
        return carry

    lax.fori_loop(0, models, feed_up, 0)
    for k in range(models):
        last_gather.to_core(k)
    query_rims().start()

    class Reduce:
        def __init__(self, col, count):
            self.cols = pl.ds(col, count)
            self.first = marks.take(4 * models)

        def core(self, k):
            m = plane(k)
            landing = got1.at[m, :, :, :, self.cols]
            return Group(self.first + k, [(grads.at[m, :, :, 1 - ac, :, self.cols], landing, c_peer)], landing)

        def side(self, k):
            m = plane(k)
            top, bottom = pl.ds(0, 32), pl.ds(32, 32)
            return Group(self.first + models + k,
                         [(got1.at[m, 1 - ax, :, top, self.cols], got2.at[m, :, top, self.cols], x_peer),
                          (got1.at[m, :, 1 - ay, bottom, self.cols], got2.at[m, :, bottom, self.cols], y_peer)],
                         got2.at[m, :, :, self.cols])

        def corner(self, k):
            m = plane(k)
            top, bottom = pl.ds(0, 32), pl.ds(32, 32)
            return Group(self.first + 2 * models + k,
                         [(got2.at[m, 1 - ay, top, self.cols], got3.at[m, top, self.cols], y_peer),
                          (got2.at[m, 1 - ax, bottom, self.cols], got3.at[m, bottom, self.cols], x_peer)],
                         got3.at[m, :, self.cols])

        def home(self, k):
            block = got3.at[plane(k), :, self.cols]
            return Group(self.first + 3 * models + k, [(block, got4.at[k, :, self.cols], z_peer(k))], block)

        def start(self, k):
            self.core(k).start()

        def to_sides(self, k):
            m = plane(k)
            self.core(k).arrive()
            got1[m, :, :, :, self.cols] = got1[m, :, :, :, self.cols] + grads[m, :, :, ac, :, self.cols]
            self.side(k).start()

        def to_corner(self, k):
            m = plane(k)
            self.side(k).arrive()
            top, bottom = pl.ds(0, 32), pl.ds(32, 32)
            got2[m, :, top, self.cols] = got2[m, :, top, self.cols] + got1[m, ax, :, top, self.cols]
            got2[m, :, bottom, self.cols] = got2[m, :, bottom, self.cols] + got1[m, :, ay, bottom, self.cols]
            self.corner(k).start()

        def to_planes(self, k):
            m = plane(k)
            self.corner(k).arrive()
            top, bottom = pl.ds(0, 32), pl.ds(32, 32)
            got3[m, top, self.cols] = got3[m, top, self.cols] + got2[m, ay, top, self.cols]
            got3[m, bottom, self.cols] = got3[m, bottom, self.cols] + got2[m, ax, bottom, self.cols]

            @pl.when(k > 0)
            def _():
                self.home(k).start()

        def end(self):
            total = got3[az, :, self.cols].astype(f32)
            for k in range(1, models):
                self.home(k).arrive()
                total = total + got4[k, :, self.cols].astype(f32)
            weight_grads[:, self.cols] = total

        def done(self, k):
            for group in (self.core(k), self.side(k), self.corner(k)):
                group.leave()

            @pl.when(k > 0)
            def _():
                self.home(k).leave()

    feed_reduce = Reduce(4 * pair, 2 * hidden)
    attention_reduce = Reduce(0, 4 * pair)
    for k in range(models):
        last_gather.here(k)

    def feed_down(step, carry):
        k = models - 1 - step
        m = plane(k)
        contract_t = weight_cols(m, 4 * pair + hidden, hidden)
        acc[...] += nt(active[m], contract_t)
        hidden_grad = (nn(out_grad, contract_t) * slope[m]).astype(bf16)
        grads[m, :, :, :, :, 4 * pair:4 * pair + hidden] = nn(mid_t, hidden_grad).astype(bf16).reshape(block_shape)
        grads[m, :, :, :, :, 4 * pair + hidden:columns] = nn(out_grad_t, active[m]).astype(bf16).reshape(block_shape)
        feed_reduce.start(k)
        acc2[...] += nt(hidden_grad, weight_cols(m, 4 * pair, hidden))
        return carry

    lax.fori_loop(0, models, feed_down, 0)
    result[...] = jnp.where(valid, after + acc[...], 0.0).astype(bf16)
    mid_grad = acc2[...]

    def rows_home(source, target):
        share = part // models
        target[az] = source[pl.ds(pl.multiple_of(az * share, share), share), :]
        return send([(source.at[pl.ds(pl.multiple_of(plane(k) * share, share), share), :], target.at[az], z_peer(k))
                     for k in range(1, models)], target.at[pl.ds(0, models - 1)])

    def norm_back(grad, hat, scale_row, gain):
        scaled_grad = grad * gain
        mean_grad = jnp.mean(scaled_grad, axis=-1, keepdims=True)
        mean_along = jnp.mean(scaled_grad * hat, axis=-1, keepdims=True)
        return scale_row * (scaled_grad - mean_grad - hat * mean_along)

    through = out_grad.astype(f32) + norm_back(mid_grad, mid_hat, mid_scale, mid_gain)
    residual[...] = through
    branch = through.astype(bf16)
    branch_t = branch.T
    norm_sums = [jnp.sum(mid_grad * mid_hat, axis=0, keepdims=True), jnp.sum(mid_grad, axis=0, keepdims=True)]

    merge_shape = grads.shape[1:5] + (pair,)
    select_row = lax.broadcasted_iota(jnp.int32, (pair, 128), 0) // HD
    select_col = lax.broadcasted_iota(jnp.int32, (pair, 128), 1) // 2
    totals[...] = jnp.zeros(totals.shape, f32)

    def unmerge(step, carry):
        k = models - 1 - step
        m = plane(k)
        attended_grad = nn(branch, weight_cols(m, qkv, pair)) * recip[m]
        fine = attended_grad.astype(bf16)
        grad_ext[m, NR:NR + part, :] = fine
        sums = nn(pool[...], fine).astype(bf16)
        for lv in range(1, plan.levels):
            grad_ext[m, plan.at[lv] + NR:plan.at[lv] + NR + plan.own[lv], :] = sums[plan.pool_at[lv]:plan.pool_at[lv] + plan.own[lv]]
        grad_ext[m, own_slot_rows, :] = sums[plan.pool_upper:plan.pool_upper + NR]
        grad_rims(k).start()
        high, rest = halves(attended_grad * ratio[m])
        chosen = jnp.where(select_row + 2 * m == select_col, -1.0, 0.0).astype(bf16)
        totals[...] += nn(high, chosen) + nn(rest, chosen)
        grads[m, :, :, :, :, qkv:qkv + pair] = nn(branch_t, attended[m]).astype(bf16).reshape(merge_shape)
        return carry

    lax.fori_loop(0, models, unmerge, 0)
    even = lax.broadcasted_iota(jnp.int32, (1, 128), 1) % 2 == 0
    high, rest = halves(totals[...])
    total_ext[NR:NR + part, :] = jnp.where(even, high, rest)
    pooled_high, pooled_rest = halves(nn(pool[...], high) + nn(pool[...], rest))
    sums = jnp.where(even, pooled_high, pooled_rest)
    for lv in range(1, plan.levels):
        total_ext[plan.at[lv] + NR:plan.at[lv] + NR + plan.own[lv], :] = sums[plan.pool_at[lv]:plan.pool_at[lv] + plan.own[lv]]
    total_ext[own_slot_rows, :] = sums[plan.pool_upper:plan.pool_upper + NR]
    total_rims().start()
    rows_out = rows_home(result, out_rows)

    def advance(step, carry):
        feed_reduce.to_sides(models - 1 - step)
        return carry

    lax.fori_loop(0, models, advance, 0)

    head_of_lane = lax.broadcasted_iota(jnp.int32, (1, 128), 1) // 2

    def clear(m, carry):
        work[m] = jnp.zeros(work.shape[1:], f32)
        return carry

    lax.fori_loop(0, models, clear, 0)
    normed_t = normed[...].T
    acc[...] = jnp.zeros(acc.shape, f32)
    qkv_shape = grads.shape[1:5] + (qkv,)
    query_scale = jnp.where(lax.broadcasted_iota(jnp.int32, (1, qkv), 1) < pair, HD ** -0.5, 1.0)
    total_rims().wait()
    query_rims().wait()

    def back_tile(m, tile):
        first, count, window, _ = tile
        rows_at = slice(first, first + count)
        mask = logs[plan.tiles.index(tile), 0:count]
        queries, keys, values, weight = tile_weights(m, ext[m, rows_at, 0:pair], mask, window)
        numer = both_heads(grad_ext[m, rows_at, :])
        tot = total_ext[rows_at, :]
        zero = jnp.zeros_like(tot)
        tots = jnp.concatenate([jnp.where(head_of_lane == 2 * m, tot, zero),
                                jnp.where(head_of_lane == 2 * m + 1, tot, zero)], axis=0)
        score_grad = (weight * nt(jnp.concatenate([numer, tots], axis=1), values)).astype(bf16)
        work[m, rows_at, 0:pair] = joined(nn(score_grad, keys))
        key_rows = slice(window, window + 128)
        work[m, key_rows, pair:2 * pair] += tn(score_grad, queries)
        work[m, key_rows, 2 * pair:3 * pair] += tn(weight.astype(bf16), numer)

    def back(step, carry):
        k = models - 1 - step
        m = plane(k)
        grad_rims(k).wait()
        for tile in plan.tiles:
            back_tile(m, tile)
        coarse = coarse_rows(m, qkv, own_slot_rows)
        spread = spread_out(coarse * jnp.concatenate([inverse[...]] * 3, axis=1))
        rows = (work[m, NR:NR + part, :] + jnp.where(valid, spread, 0.0)).astype(bf16)
        grads[m, :, :, :, :, 0:qkv] = (nn(normed_t, rows) * query_scale).astype(bf16).reshape(qkv_shape)
        attention_reduce.start(k)
        acc[...] += nt(rows, weight_cols(m, 0, qkv))

        @pl.when(step >= 1)
        def _():
            attention_reduce.to_sides(k + 1)
            feed_reduce.to_planes(k + 1)

        feed_reduce.to_corner(k)

        @pl.when(step >= 2)
        def _():
            attention_reduce.to_corner(k + 2)

        @pl.when(step >= 3)
        def _():
            attention_reduce.to_planes(k + 3)

        return carry

    lax.fori_loop(0, models, back, 0)
    normed_grad = acc[...]
    hat = scaled[...]
    row_grads[...] = (residual[...] + norm_back(normed_grad, hat, rstd[:, 0:1], pre_gain)).astype(bf16)
    grads_out = rows_home(row_grads, out_grads)
    attention_reduce.to_sides(0)
    attention_reduce.to_corner(1)
    norm_sums = [jnp.sum(normed_grad * hat, axis=0, keepdims=True), jnp.sum(normed_grad, axis=0, keepdims=True)] + norm_sums
    norm_got[0] = jnp.concatenate(norm_sums + [jnp.zeros((4, width), f32)], axis=0)
    small = send([(norm_got.at[0], norm_got.at[step], at_spot((spot + step) % spots)) for step in range(1, spots)],
                 norm_got.at[pl.ds(0, spots - 1)])
    attention_reduce.to_planes(2)
    feed_reduce.to_planes(0)
    small.arrive()
    norm_total = norm_got[0]
    for step in range(1, spots):
        norm_total = norm_total + norm_got[step]
    norm_got[spots] = norm_total
    small = send([(norm_got.at[spots], norm_got.at[spots + k], z_peer(k)) for k in range(1, models)],
                 norm_got.at[pl.ds(0, models - 1)])
    attention_reduce.to_corner(0)
    attention_reduce.to_planes(1)
    feed_reduce.end()
    attention_reduce.to_planes(0)
    attention_reduce.end()
    small.arrive()
    for k in range(1, models):
        norm_total = norm_total + norm_got[spots + k]
    norm_grads[...] = norm_total
    rows_out.arrive()
    grads_out.arrive()
    assert marks.used == net_count, marks.used
    for group in sent:
        group.leave()

    def drain(k, carry):
        pair_rims(k).done()
        grad_rims(k).done()
        feed_reduce.done(k)
        attention_reduce.done(k)
        return carry

    lax.fori_loop(0, models, drain, 0)
    query_rims().done()
    total_rims().done()


def finish_outputs(dims, rows_ref, grads_ref, weights_ref, norms_ref,
                   out_rows, out_grads, query, key, value, merge, up, down, *norm_outs):
    part, width, pair, hidden = dims
    out_rows[...] = rows_ref[...].reshape(out_rows.shape)
    out_grads[...] = grads_ref[...].reshape(out_grads.shape)
    strip = query.shape[0]
    query[...] = weights_ref[:, 0:pair]
    key[...] = weights_ref[:, pair:2 * pair]
    value[...] = weights_ref[:, 2 * pair:3 * pair]
    up[...] = weights_ref[:, 4 * pair:4 * pair + hidden]
    merge[...] = weights_ref[:, 3 * pair:4 * pair]
    down[...] = weights_ref[:, 4 * pair + hidden:4 * pair + 2 * hidden]
    owner = lax.axis_index("dp") * 4 + lax.axis_index("seq")
    strips = width // strip
    mine = norms_ref[:, 0:strip] * (owner == 0).astype(jnp.float32)
    for i in range(1, strips):
        mine = jnp.where(owner == i, norms_ref[:, i * strip:(i + 1) * strip], mine)
    for i, out in enumerate(norm_outs):
        out[...] = mine[i].reshape(out.shape)


def fast_body(plan, incoming_embeddings, output_sensitivity, sequence_extents, asking_projector, lookup_projector,
              content_projector, attention_combiner, feedforward_expand, feedforward_contract,
              attention_norm_scale, attention_norm_bias, feedforward_norm_scale, feedforward_norm_bias):
    bf16, f32 = jnp.bfloat16, jnp.float32
    models = lax.axis_size("mp")
    seqs, _, part, width = incoming_embeddings.shape
    strip, pair = asking_projector.shape
    hidden = feedforward_expand.shape[1]
    columns = 4 * pair + 2 * hidden
    norm_parts = [row.reshape(1, strip) for row in (
        attention_norm_scale, attention_norm_bias, feedforward_norm_scale, feedforward_norm_bias)]
    share = part // models
    spots, rows = plan.spots, plan.rows
    deep = (2, 2, 2, strip, columns)
    net_count = 92
    vmem = pltpu.VMEM
    scratch = [
        vmem((models,) + deep, bf16), vmem((spots, 8, width), f32), vmem((part, width), bf16), vmem((part, width), bf16),
        vmem((models, rows, 3 * pair), bf16), vmem((len(plan.tiles), 128, 128), f32),
        vmem((part, part), bf16), vmem((part, part), bf16), vmem((part, 128), f32), vmem((models, rows, 3 * pair), f32),
        vmem((models, part, pair), bf16), vmem((models, part, pair), f32), vmem((models, part, pair), f32),
        vmem((part, width), bf16), vmem((part, width), f32), vmem((part, 128), f32),
        vmem((models, rows, pair), bf16), vmem((rows, 128), bf16), vmem((part, width), f32), vmem((part, width), f32),
        vmem((part, width), f32), vmem((part, 128), f32), vmem((part, width), bf16), vmem((part, width), bf16),
        vmem((models, part, hidden), bf16), vmem((models, part, hidden), f32),
        vmem((models,) + deep, bf16), vmem((models, 2, 2, strip, columns), bf16), vmem((models, 2, strip, columns), bf16),
        vmem((models, strip, columns), bf16), vmem((models, strip, columns), bf16), vmem((spots + models, 8, width), f32),
        pltpu.SemaphoreType.DMA((2,)), pltpu.SemaphoreType.DMA((net_count,)), pltpu.SemaphoreType.DMA((net_count,)),
    ]
    any_space, in_vmem = pl.BlockSpec(memory_space=pl.ANY), pl.BlockSpec(memory_space=pltpu.VMEM)
    out_rows, out_grads, weight_grads, norm_grads = pl.pallas_call(
        functools.partial(whole_layer, plan, (part, width, pair, hidden), net_count),
        out_shape=(jax.ShapeDtypeStruct((seqs, share, width), bf16), jax.ShapeDtypeStruct((seqs, share, width), bf16),
                   jax.ShapeDtypeStruct((strip, columns), f32), jax.ShapeDtypeStruct((8, width), f32)),
        in_specs=[pl.BlockSpec(memory_space=pltpu.SMEM)] + [in_vmem] * 10 + [any_space] * 2,
        out_specs=(in_vmem,) * 4,
        scratch_shapes=scratch,
        compiler_params=pltpu.CompilerParams(collective_id=0, has_side_effects=True, vmem_limit_bytes=60 * 2 ** 20),
        name="layer",
    )(sequence_extents, asking_projector, lookup_projector, content_projector, attention_combiner.T, feedforward_expand,
      feedforward_contract.T, *norm_parts, incoming_embeddings, output_sensitivity)
    flat = lambda *shape: jax.ShapeDtypeStruct(shape, f32)
    rows_type = jax.ShapeDtypeStruct((seqs, 1, share, width), bf16)
    finished = pl.pallas_call(
        functools.partial(finish_outputs, (part, width, pair, hidden)),
        out_shape=(rows_type, rows_type, flat(strip, pair), flat(strip, pair), flat(strip, pair), flat(strip, pair),
                   flat(strip, hidden), flat(strip, hidden)) + (flat(1, strip),) * 4,
        in_specs=[in_vmem] * 4,
        out_specs=(in_vmem,) * 12,
        name="outputs",
    )(out_rows, out_grads, weight_grads, norm_grads)
    rows_end, grads_end, query_grad, key_grad, value_grad, merge_t, up_grad, down_t = finished[:8]
    return (rows_end, grads_end, query_grad, key_grad, value_grad, merge_t.T, up_grad, down_t.T,
            *(row.reshape(strip) for row in finished[8:]))


def solution(mesh):
    in_specs = (
        P(None, "seq", "dp", None),
        P(None, "seq", "dp", None),
        P(),
        P(("dp", "seq"), "mp"),
        P(("dp", "seq"), "mp"),
        P(("dp", "seq"), "mp"),
        P("mp", ("dp", "seq")),
        P(("dp", "seq"), "mp"),
        P("mp", ("dp", "seq")),
        P(("dp", "seq")),
        P(("dp", "seq")),
        P(("dp", "seq")),
        P(("dp", "seq")),
    )
    out_specs = (
        P(None, "seq", ("dp", "mp"), None),
        P(None, "seq", ("dp", "mp"), None),
        P(("dp", "seq"), "mp"),
        P(("dp", "seq"), "mp"),
        P(("dp", "seq"), "mp"),
        P("mp", ("dp", "seq")),
        P(("dp", "seq"), "mp"),
        P("mp", ("dp", "seq")),
        P(("dp", "seq")),
        P(("dp", "seq")),
        P(("dp", "seq")),
        P(("dp", "seq")),
    )
    sizes = (mesh.shape["dp"], mesh.shape["seq"], mesh.shape["mp"])

    def chosen(*arrays):
        seqs, _, part, width = arrays[0].shape
        if sizes == (2, 4, 4) and seqs == sizes[2] and part == width == 512 and arrays[3].shape[1] == 128:
            return fast_body(Plan(part, sizes[0] * sizes[1]), *arrays)
        return general_body(*arrays)

    return jax.shard_map(chosen, mesh=mesh, in_specs=in_specs, out_specs=out_specs, check_vma=False)
```

```python
import functools

import jax
import jax.numpy as jnp
from jax import lax
from jax.experimental import pallas as pl
from jax.experimental.pallas import tpu as pltpu
from jax.sharding import PartitionSpec as P

HD = 64
NR = 16


def cut_along(x, dim, count):
    before, after = (x.shape[:dim], x.shape[dim + 1 :])
    return jnp.moveaxis(x.reshape(*before, count, -1, *after), dim, 0)


def summed_on_arrival(x, axis, dim):
    count = lax.axis_size(axis)
    blocks = lax.all_to_all(cut_along(x, dim, count), axis, 0, 0, tiled=True)
    return jnp.sum(blocks.astype(jnp.float32), axis=0)


def sent_together(arrays, axis, dim, along):
    ends, at = ([], 0)
    for a in arrays[:-1]:
        at += a.shape[along]
        ends.append(at)
    both = jnp.concatenate(arrays, axis=along)
    return tuple(jnp.split(summed_on_arrival(both, axis, dim), ends, axis=along))


def norm_rows(values, gain_row, shift_row):
    center = values - jnp.mean(values, axis=-1, keepdims=True)
    spread = jnp.mean(center * center, axis=-1, keepdims=True)
    return center * lax.rsqrt(spread + 1e-05) * gain_row + shift_row


def norm_gain_parts(values, grad_rows):
    center = values - jnp.mean(values, axis=-1, keepdims=True)
    spread = jnp.mean(center * center, axis=-1, keepdims=True)
    scaled = center * lax.rsqrt(spread + 1e-05)
    return (jnp.sum(grad_rows * scaled, axis=0), jnp.sum(grad_rows, axis=0))


def gelu_exact(values):
    return jax.nn.gelu(values, approximate=False)


def dot_plain(left_mat, right_mat):
    return jnp.dot(left_mat, right_mat, preferred_element_type=jnp.float32)


def dot_inner(left_mat, right_mat):
    return lax.dot_general(
        left_mat, right_mat, (((0,), (0,)), ((), ())), preferred_element_type=jnp.float32
    )


def dot_outer(left_mat, right_mat):
    return lax.dot_general(
        left_mat, right_mat, (((1,), (1,)), ((), ())), preferred_element_type=jnp.float32
    )


def group_sum(values, group_width):
    return jnp.sum(
        values.reshape((values.shape[0] // group_width, group_width) + values.shape[1:]), axis=1
    )


def block_shape(coarse_rows):
    query_len = min(coarse_rows, 512)
    span_len = query_len + 2 * NR
    window_len = -(-span_len // 128) * 128
    return (query_len, span_len, window_len)


def window_mask(level_at, first_row, query_len, window_len, span_len):
    rows_at = first_row + jnp.arange(query_len, dtype=jnp.int32)[:, None]
    keys_at = first_row + jnp.arange(window_len, dtype=jnp.int32)[None, :]
    inside = keys_at - first_row < span_len
    allowed = jnp.abs(rows_at // NR + 1 - keys_at // NR) <= 1
    if level_at > 0:
        half_block = NR // 2
        allowed = allowed & (jnp.abs(rows_at // half_block + 2 - keys_at // half_block) >= 2)
    return (allowed & inside).astype(jnp.float32)


def level_forward(query_rows, pair_wide, count_wide, level_at):
    coarse_rows = query_rows.shape[0]
    columns = query_rows.shape[1]
    heads_here = columns // HD
    query_len, span_len, window_len = block_shape(coarse_rows)
    tail_pad = window_len - span_len
    pair_padded = jnp.pad(pair_wide, ((0, tail_pad), (0, 0)))
    count_padded = jnp.pad(count_wide, (0, tail_pad))
    weight_list = []
    total_parts = []
    numer_parts = []
    for block_at in range(coarse_rows // query_len):
        first_row = block_at * query_len
        query_block = query_rows[first_row : first_row + query_len]
        pair_block = pair_padded[first_row : first_row + window_len]
        count_block = count_padded[first_row : first_row + window_len]
        keep_mask = (
            window_mask(level_at, first_row, query_len, window_len, span_len) * count_block[None, :]
        )
        head_weights = []
        head_totals = []
        head_numers = []
        for head_at in range(heads_here):
            head_cols = slice(head_at * HD, (head_at + 1) * HD)
            value_cols = slice(columns + head_at * HD, columns + (head_at + 1) * HD)
            scores = dot_outer(query_block[:, head_cols], pair_block[:, head_cols]) * HD ** (-0.5)
            weight = jnp.exp(scores) * keep_mask
            head_weights.append(weight)
            head_totals.append(jnp.sum(weight, axis=-1))
            head_numers.append(dot_plain(weight.astype(jnp.bfloat16), pair_block[:, value_cols]))
        weight_list.append(head_weights)
        total_parts.append(jnp.stack(head_totals, axis=1))
        numer_parts.append(jnp.concatenate(head_numers, axis=1))
    totals = jnp.concatenate(total_parts, axis=0)
    numer_part = jnp.concatenate(numer_parts, axis=0).reshape(coarse_rows, heads_here, HD)
    return ((query_rows, pair_padded, weight_list), totals, numer_part)


def level_backward(level_kept, numer_rows, total_rows):
    query_rows, pair_padded, weight_list = level_kept
    coarse_rows = query_rows.shape[0]
    columns = query_rows.shape[1]
    heads_here = columns // HD
    query_len, span_len, window_len = block_shape(coarse_rows)
    numer_flat = numer_rows.reshape(coarse_rows, columns)
    pair_grad = jnp.zeros(pair_padded.shape, jnp.float32)
    query_parts = []
    for block_at in range(coarse_rows // query_len):
        first_row = block_at * query_len
        query_block = query_rows[first_row : first_row + query_len]
        pair_block = pair_padded[first_row : first_row + window_len]
        numer_block = numer_flat[first_row : first_row + query_len]
        total_block = total_rows[first_row : first_row + query_len]
        query_heads = []
        key_heads = []
        value_heads = []
        for head_at in range(heads_here):
            head_cols = slice(head_at * HD, (head_at + 1) * HD)
            value_cols = slice(columns + head_at * HD, columns + (head_at + 1) * HD)
            weight = head_weights = weight_list[block_at][head_at]
            grad_here = numer_block[:, head_cols]
            score_grad = (
                (dot_outer(grad_here, pair_block[:, value_cols]) + total_block[:, head_at][:, None])
                * weight
            ).astype(jnp.bfloat16)
            query_heads.append(dot_plain(score_grad, pair_block[:, head_cols]) * HD ** (-0.5))
            key_heads.append(dot_inner(score_grad, query_block[:, head_cols]) * HD ** (-0.5))
            value_heads.append(dot_inner(head_weights.astype(jnp.bfloat16), grad_here))
        query_parts.append(jnp.concatenate(query_heads, axis=1))
        block_grad = jnp.concatenate(key_heads + value_heads, axis=1)
        pair_grad = pair_grad + jnp.pad(
            block_grad, ((first_row, pair_padded.shape[0] - first_row - window_len), (0, 0))
        )
    query_grad = jnp.concatenate(query_parts, axis=0)
    return (query_grad, pair_grad[: coarse_rows + 2 * NR])


def general_body(
    incoming_embeddings,
    output_sensitivity,
    sequence_extents,
    asking_projector,
    lookup_projector,
    content_projector,
    attention_combiner,
    feedforward_expand,
    feedforward_contract,
    attention_norm_scale,
    attention_norm_bias,
    feedforward_norm_scale,
    feedforward_norm_bias,
):
    groups = lax.axis_size("dp")
    slices = lax.axis_size("seq")
    models = lax.axis_size("mp")
    group_id = lax.axis_index("dp")
    slice_id = lax.axis_index("seq")
    model_id = lax.axis_index("mp")
    seq_count = incoming_embeddings.shape[0]
    piece_len = incoming_embeddings.shape[2]
    model_width = incoming_embeddings.shape[3]
    part_len = piece_len * groups
    batches = seq_count // groups
    share_len = piece_len // models
    share_rows = groups * share_len
    local_top = (part_len // NR).bit_length() - 1
    upper_start = local_top + 1
    level_top = (part_len * slices // (2 * NR)).bit_length() - 1
    upper_rows = NR // 2
    upper_whole = upper_rows * slices
    send_tok = incoming_embeddings.reshape(
        groups, batches, piece_len, model_width
    )
    send_cot = output_sensitivity.reshape(
        groups, batches, piece_len, model_width
    )
    dealt_tok, dealt_cot = (
        lax.all_to_all(send_tok, "dp", split_axis=0, concat_axis=2, tiled=True),
        lax.all_to_all(send_cot, "dp", split_axis=0, concat_axis=2, tiled=True),
    )
    dealt_tok = dealt_tok.reshape(batches, part_len, model_width)
    dealt_cot = dealt_cot.reshape(batches, part_len, model_width)
    my_lengths = lax.dynamic_slice_in_dim(sequence_extents, group_id * batches, batches, 0)

    def split_rows(rows):
        return rows.reshape((groups, models, share_len) + rows.shape[1:])

    def take_share(rows):
        return lax.dynamic_slice_in_dim(split_rows(rows), model_id, 1, 1).reshape(
            (share_rows,) + rows.shape[1:]
        )

    def neighbour_rims(gathered):
        padded = jnp.pad(gathered, ((2 * NR, 2 * NR), (0, 0)))
        from_left = lax.dynamic_slice_in_dim(padded, slice_id * 2 * NR + NR, NR, 0)
        from_right = lax.dynamic_slice_in_dim(padded, (slice_id + 2) * 2 * NR, NR, 0)
        return (from_left, from_right)

    def one_batch(batch_index, learnable_collection):
        full_query, full_key, full_value, full_merge, full_up, full_down = learnable_collection[:6]
        gain_pre, shift_pre, gain_mid, shift_mid = (
            learnable_tensor.astype(jnp.float32) for learnable_tensor in learnable_collection[6:]
        )
        columns = full_query.shape[1]
        heads_here = columns // HD
        length_now = my_lengths[batch_index]

        def level_counts(level_at, first_id, id_total):
            coarse_ids = first_id + jnp.arange(id_total, dtype=jnp.int32)
            group_len = 2**level_at
            return jnp.where(
                coarse_ids >= 0, jnp.clip(length_now - group_len * coarse_ids, 0, group_len), 0
            ).astype(jnp.float32)

        positions = slice_id * part_len + jnp.arange(part_len, dtype=jnp.int32)
        valid_rows = (positions < length_now).astype(jnp.float32)
        inputs = dealt_tok[batch_index].astype(jnp.float32)
        grad_in = dealt_cot[batch_index].astype(jnp.float32) * valid_rows[:, None]
        valid_share = take_share(valid_rows)
        normed, pull_pre = jax.vjp(norm_rows, inputs, gain_pre, shift_pre)
        normed_low = normed.astype(jnp.bfloat16)
        queries = dot_plain(normed_low, full_query).astype(jnp.bfloat16)
        keys_own = dot_plain(normed_low, full_key).astype(jnp.bfloat16)
        values_own = dot_plain(normed_low, full_value).astype(jnp.bfloat16)
        pair_own = jnp.concatenate([keys_own, values_own], axis=1)
        fine_all = (
            jnp.concatenate([queries, pair_own], axis=1).astype(jnp.float32) * valid_rows[:, None]
        )
        level_sums = [fine_all]
        for level_at in range(1, upper_start + 1):
            level_sums.append(group_sum(level_sums[-1], 2))
        query_levels = [queries]
        pair_levels = [pair_own]
        own_counts = [valid_rows]
        for level_at in range(1, local_top + 1):
            coarse_rows = part_len >> level_at
            counts_here = level_counts(level_at, slice_id * coarse_rows, coarse_rows)
            coarse_means = (level_sums[level_at] / jnp.maximum(counts_here, 1.0)[:, None]).astype(
                jnp.bfloat16
            )
            query_levels.append(coarse_means[:, :columns])
            pair_levels.append(coarse_means[:, columns:])
            own_counts.append(counts_here)
        edge_rows = jnp.concatenate(
            [
                jnp.concatenate([pair_rows[:NR], pair_rows[-NR:]], axis=0)
                for pair_rows in pair_levels
            ],
            axis=1,
        )
        edges_all, upper_all = (
            lax.all_gather(
                edge_rows.astype(jnp.float32).astype(jnp.bfloat16), "seq", axis=0, tiled=True
            ).astype(jnp.float32),
            lax.all_gather(
                level_sums[upper_start].astype(jnp.bfloat16), "seq", axis=0, tiled=True
            ).astype(jnp.float32),
        )
        left_edge, right_edge = neighbour_rims(edges_all)
        left_edge = left_edge.astype(jnp.bfloat16)
        right_edge = right_edge.astype(jnp.bfloat16)
        kept_levels = []
        total_all = jnp.zeros((part_len, heads_here), jnp.float32)
        numer_all = jnp.zeros((part_len, heads_here, HD), jnp.float32)
        for level_at in range(local_top + 1):
            coarse_rows = part_len >> level_at
            col_range = slice(level_at * 2 * columns, (level_at + 1) * 2 * columns)
            pair_wide = jnp.concatenate(
                [left_edge[:, col_range], pair_levels[level_at], right_edge[:, col_range]], axis=0
            )
            count_wide = level_counts(level_at, slice_id * coarse_rows - NR, coarse_rows + 2 * NR)
            level_kept, totals, numer_part = level_forward(
                query_levels[level_at], pair_wide, count_wide, level_at
            )
            kept_levels.append(level_kept)
            total_all = total_all + jnp.repeat(totals, 2**level_at, axis=0)
            numer_all = numer_all + jnp.repeat(numer_part, 2**level_at, axis=0)
        level_at = 7
        repeat_by = 2 ** (level_at - upper_start)
        coarse_rows = upper_whole // repeat_by
        counts_here = level_counts(level_at, 0, coarse_rows)
        coarse_means = (
            group_sum(upper_all, repeat_by) / jnp.maximum(counts_here, 1.0)[:, None]
        ).astype(jnp.bfloat16)
        pair_wide = jnp.pad(coarse_means[:, columns:], ((NR, NR), (0, 0)))
        count_wide = level_counts(level_at, -NR, coarse_rows + 2 * NR)
        level_kept, totals, numer_part = level_forward(
            coarse_means[:, :columns], pair_wide, count_wide, level_at
        )
        upper_kept = [level_kept]
        upper_counts = [counts_here]
        upper_total = jnp.repeat(totals, repeat_by, axis=0)
        upper_numer = jnp.repeat(numer_part, repeat_by, axis=0)
        total_all = total_all + jnp.repeat(
            lax.dynamic_slice_in_dim(upper_total, slice_id * upper_rows, upper_rows, 0),
            2**upper_start,
            axis=0,
        )
        numer_all = numer_all + jnp.repeat(
            lax.dynamic_slice_in_dim(upper_numer, slice_id * upper_rows, upper_rows, 0),
            2**upper_start,
            axis=0,
        )
        attended = (
            (numer_all / total_all[:, :, None]).reshape(part_len, columns).astype(jnp.bfloat16)
        )
        merged_part = dot_plain(attended, full_merge)
        branch_attn = lax.psum(merged_part, "mp")
        after_attn = inputs + branch_attn
        mid_normed, pull_mid = jax.vjp(norm_rows, after_attn, gain_mid, shift_mid)
        mid_low = mid_normed.astype(jnp.bfloat16)
        after_share = take_share(after_attn)
        up_proj = dot_plain(mid_low, full_up)
        activated, pull_gelu = jax.vjp(gelu_exact, up_proj)
        act_low = activated.astype(jnp.bfloat16)
        ffn_share = (
            lax.psum_scatter(
                split_rows(dot_plain(act_low, full_down)).astype(jnp.bfloat16),
                "mp",
                scatter_dimension=1,
                tiled=True,
            )
            .astype(jnp.float32)
            .reshape(share_rows, model_width)
        )
        result_share = (valid_share[:, None] * (after_share + ffn_share)).astype(jnp.bfloat16)
        grad_low = grad_in.astype(jnp.bfloat16)
        act_grad = dot_outer(grad_low, full_down)
        down_acc = dot_inner(act_low, grad_low)
        hidden_grad = pull_gelu(act_grad)[0].astype(jnp.bfloat16)
        up_acc = dot_inner(mid_low, hidden_grad)
        mid_part = dot_outer(hidden_grad, full_up)
        mid_grad = lax.psum(mid_part, "mp")
        back_mid = pull_mid(mid_grad)[0]
        residual_grad = grad_in + back_mid
        branch_grad = residual_grad.astype(jnp.bfloat16)
        residual_share = take_share(residual_grad)
        gain_mid_part, shift_mid_part = norm_gain_parts(after_share, take_share(mid_grad))
        merge_acc = dot_inner(attended, branch_grad)
        attended_grad = dot_outer(branch_grad, full_merge).reshape(part_len, heads_here, HD)
        numer_grad = (attended_grad / total_all[:, :, None]).astype(jnp.bfloat16)
        total_grad = -jnp.sum(attended_grad * numer_all, axis=-1) / (total_all * total_all)
        numer_wide = numer_grad.astype(jnp.float32)
        rim_parts = []
        own_pair_grads = []
        query_coarse = []
        for level_at in range(local_top + 1):
            coarse_rows = part_len >> level_at
            if level_at == 0:
                numer_sum = numer_grad
                total_sum = total_grad
            else:
                numer_sum = group_sum(numer_wide, 2**level_at).astype(jnp.bfloat16)
                total_sum = group_sum(total_grad, 2**level_at)
            query_grad, pair_grad = level_backward(kept_levels[level_at], numer_sum, total_sum)
            rim_parts.append(
                jnp.concatenate([pair_grad[:NR], pair_grad[NR + coarse_rows :]], axis=0)
            )
            own_pair_grads.append(pair_grad[NR : NR + coarse_rows])
            query_coarse.append(query_grad)
        rim_grads = jnp.concatenate(rim_parts, axis=1)
        upper_numer_grad = group_sum(numer_wide, 2**upper_start).reshape(upper_rows, columns)
        upper_total_grad = group_sum(total_grad, 2**upper_start)
        rims_all, numer_sums, total_sums = (
            lax.all_gather(rim_grads.astype(jnp.bfloat16), "seq", axis=0, tiled=True).astype(
                rim_grads.dtype
            ),
            lax.all_gather(upper_numer_grad.astype(jnp.bfloat16), "seq", axis=0, tiled=True).astype(
                upper_numer_grad.dtype
            ),
            lax.all_gather(upper_total_grad.astype(jnp.bfloat16), "seq", axis=0, tiled=True).astype(
                upper_total_grad.dtype
            ),
        )
        from_left, from_right = neighbour_rims(rims_all)
        fine_grad = jnp.zeros((part_len, 3 * columns), jnp.float32)
        for level_at in range(local_top + 1):
            coarse_rows = part_len >> level_at
            col_range = slice(level_at * 2 * columns, (level_at + 1) * 2 * columns)
            pair_here = (
                own_pair_grads[level_at]
                + jnp.pad(from_left[:, col_range], ((0, coarse_rows - NR), (0, 0)))
                + jnp.pad(from_right[:, col_range], ((coarse_rows - NR, 0), (0, 0)))
            )
            coarse_grad = jnp.concatenate([query_coarse[level_at], pair_here], axis=1)
            if level_at == 0:
                fine_grad = coarse_grad
            else:
                coarse_grad = coarse_grad / jnp.maximum(own_counts[level_at], 1.0)[:, None]
                fine_grad = (
                    fine_grad + jnp.repeat(coarse_grad, 2**level_at, axis=0) * valid_rows[:, None]
                )
        upper_grad = jnp.zeros((upper_whole, 3 * columns), jnp.float32)
        for index_at, level_at in enumerate(range(upper_start, level_top + 1)):
            repeat_by = 2 ** (level_at - upper_start)
            coarse_rows = upper_whole // repeat_by
            numer_sum = (
                group_sum(numer_sums, repeat_by)
                .reshape(coarse_rows, heads_here, HD)
                .astype(jnp.bfloat16)
            )
            total_sum = group_sum(total_sums, repeat_by)
            query_grad, pair_grad = level_backward(upper_kept[index_at], numer_sum, total_sum)
            coarse_grad = (
                jnp.concatenate([query_grad, pair_grad[NR : NR + coarse_rows]], axis=1)
                / jnp.maximum(upper_counts[index_at], 1.0)[:, None]
            )
            upper_grad = jnp.repeat(coarse_grad, repeat_by, axis=0)
        own_upper = lax.dynamic_slice_in_dim(upper_grad, slice_id * upper_rows, upper_rows, 0)
        fine_grad = fine_grad + jnp.repeat(own_upper, 2**upper_start, axis=0) * valid_rows[:, None]
        rows_grad = fine_grad.astype(jnp.bfloat16)
        query_rows_grad = rows_grad[:, :columns]
        key_rows_grad = rows_grad[:, columns : 2 * columns]
        value_rows_grad = rows_grad[:, 2 * columns :]
        query_acc = dot_inner(normed_low, query_rows_grad)
        key_acc = dot_inner(normed_low, key_rows_grad)
        value_acc = dot_inner(normed_low, value_rows_grad)
        normed_part = (
            dot_outer(query_rows_grad, full_query)
            + dot_outer(key_rows_grad, full_key)
            + dot_outer(value_rows_grad, full_value)
        )
        normed_grad, gain_mid_sum, shift_mid_sum = (
            lax.psum(normed_part.astype(jnp.bfloat16), "mp").astype(jnp.float32),
            lax.psum(gain_mid_part.astype(jnp.bfloat16), "mp").astype(jnp.float32),
            lax.psum(shift_mid_part.astype(jnp.bfloat16), "mp").astype(jnp.float32),
        )
        back_pre, gain_pre_acc, shift_pre_acc = pull_pre(normed_grad)
        input_share = (residual_share + take_share(back_pre)).astype(jnp.bfloat16)
        grad_terms = (
            query_acc,
            key_acc,
            value_acc,
            merge_acc,
            up_acc,
            down_acc,
            gain_pre_acc,
            shift_pre_acc,
            gain_mid_sum,
            shift_mid_sum,
        )
        return (result_share, input_share, grad_terms)

    result_list = []
    grad_list = []
    running_sum = None
    for batch_index in range(batches):
        learnable_collection = (
            lax.all_gather(asking_projector, ("dp", "seq"), axis=0, tiled=True),
            lax.all_gather(lookup_projector, ("dp", "seq"), axis=0, tiled=True),
            lax.all_gather(content_projector, ("dp", "seq"), axis=0, tiled=True),
            lax.all_gather(attention_combiner, ("dp", "seq"), axis=1, tiled=True),
            lax.all_gather(feedforward_expand, ("dp", "seq"), axis=0, tiled=True),
            lax.all_gather(feedforward_contract, ("dp", "seq"), axis=1, tiled=True),
            lax.all_gather(attention_norm_scale, ("dp", "seq"), axis=0, tiled=True),
            lax.all_gather(attention_norm_bias, ("dp", "seq"), axis=0, tiled=True),
            lax.all_gather(feedforward_norm_scale, ("dp", "seq"), axis=0, tiled=True),
            lax.all_gather(feedforward_norm_bias, ("dp", "seq"), axis=0, tiled=True),
        )
        result_share, input_share, grad_terms = one_batch(batch_index, learnable_collection)
        result_list.append(result_share)
        grad_list.append(input_share)
        if running_sum is None:
            running_sum = grad_terms
        else:
            running_sum = tuple(
                (older_sum + newer_sum for older_sum, newer_sum in zip(running_sum, grad_terms))
            )
    owned_grads = (
        *sent_together(
            (
                running_sum[0].astype(jnp.bfloat16),
                running_sum[1].astype(jnp.bfloat16),
                running_sum[2].astype(jnp.bfloat16),
            ),
            ("dp", "seq"),
            0,
            1,
        ),
        summed_on_arrival(running_sum[3].astype(jnp.bfloat16), ("dp", "seq"), 1),
        summed_on_arrival(running_sum[4].astype(jnp.bfloat16), ("dp", "seq"), 0),
        summed_on_arrival(running_sum[5].astype(jnp.bfloat16), ("dp", "seq"), 1),
        summed_on_arrival(running_sum[6].astype(jnp.bfloat16), ("dp", "seq"), 0),
        summed_on_arrival(running_sum[7].astype(jnp.bfloat16), ("dp", "seq"), 0),
        summed_on_arrival(running_sum[8].astype(jnp.bfloat16), ("dp", "seq"), 0),
        summed_on_arrival(running_sum[9].astype(jnp.bfloat16), ("dp", "seq"), 0),
    )
    result_all = jnp.stack(result_list, axis=0).reshape(batches, groups, share_len, model_width)
    grad_all = jnp.stack(grad_list, axis=0).reshape(batches, groups, share_len, model_width)
    back_out, back_grad = (
        lax.all_to_all(result_all, "dp", split_axis=1, concat_axis=0, tiled=True),
        lax.all_to_all(grad_all, "dp", split_axis=1, concat_axis=0, tiled=True),
    )
    return (
        back_out,
        back_grad,
        owned_grads[0],
        owned_grads[1],
        owned_grads[2],
        owned_grads[3],
        owned_grads[4],
        owned_grads[5],
        owned_grads[6],
        owned_grads[7],
        owned_grads[8],
        owned_grads[9],
    )


MESH = pl.DeviceIdType.MESH
NEG = -1e30
BACK_GROUP = 5
GROUP = 5


def nn(a, b):
    return lax.dot_general(a, b, (((1,), (0,)), ((), ())), preferred_element_type=jnp.float32)


def nt(a, b):
    return lax.dot_general(a, b, (((1,), (1,)), ((), ())), preferred_element_type=jnp.float32)


def tn(a, b):
    return lax.dot_general(a, b, (((0,), (0,)), ((), ())), preferred_element_type=jnp.float32)


def halves(values):
    high = values.astype(jnp.bfloat16)
    return high, (values - high.astype(jnp.float32)).astype(jnp.bfloat16)


class Plan:
    def __init__(self, part, spots):
        self.part, self.spots = part, spots
        self.levels = (part // NR).bit_length()
        self.top = (part * spots // (2 * NR)).bit_length() - 1
        self.own = [part >> level for level in range(self.levels)]
        self.at, row = [], 0
        for rows in self.own:
            self.at.append(row)
            row += rows + 2 * NR
        self.upper = row
        self.rows = row + spots * NR
        self.pool_at, row = [None], 0
        for rows in self.own[1:]:
            self.pool_at.append(row)
            row += rows
        self.pool_upper = row
        self.pooled = row + NR
        self.slot, row = [], 0
        for level in range(self.levels, self.top + 1):
            self.slot.append((level, row, part >> level))
            row += part >> level
        assert row <= NR and spots * NR == 128 and self.pooled == part
        self.segments = [(self.at[lv], self.own[lv] + 2 * NR, lv) for lv in range(self.levels)]
        self.inner, self.outer = [], []
        level = 0
        while level < self.levels:
            start, total = self.at[level], self.own[level] + 2 * NR
            end = start + total
            if total < 96:
                self.outer.append((start, self.upper - start, self.upper - 128, None))
                break
            row = start
            while row < end:
                count = min(96, end - row)
                window = max(start, min(row - NR, end - 128))
                tile = (row, count, window, level if window + 128 <= end else None)
                inside = window >= start + NR and window + 128 <= end - NR
                (self.inner if inside else self.outer).append(tile)
                row += count
            level += 1
        self.outer.append((self.upper, 128, self.upper, None))
        self.tiles = self.inner + self.outer

    def own_pieces(self, tile):
        first, count = tile[:2]
        pieces = []
        for start, rows in zip(self.at, self.own):
            low, high = max(first, start + NR), min(first + count, start + NR + rows)
            if low < high:
                pieces.append((low, high - low))
        return pieces


def row_places(plan, rows, low, high, spot):
    level = jnp.full(rows.shape, -1, jnp.int32)
    place = jnp.zeros(rows.shape, jnp.int32)
    for start, count, lv in plan.segments:
        if start < high and start + count > low:
            inside = (rows >= start) & (rows < start + count)
            level = jnp.where(inside, lv, level)
            place = jnp.where(inside, spot * plan.own[lv] - NR + rows - start, place)
    if high > plan.upper:
        owner = lax.shift_right_arithmetic(rows - plan.upper, 4)
        within = (rows - plan.upper) & (NR - 1)
        for lv, first, count in plan.slot:
            inside = (rows >= plan.upper) & (within >= first) & (within < first + count)
            level = jnp.where(inside, lv, level)
            place = jnp.where(inside, owner * count + within - first, place)
    return level, place


def log_counts(plan, tile, spot, length):
    first, count, window, level = tile
    row_at = first + lax.broadcasted_iota(jnp.int32, (count, 128), 0)
    key_at = window + lax.broadcasted_iota(jnp.int32, (8, 128), 1)
    row_level, row_place = row_places(plan, row_at, first, first + count, spot)
    key_level, key_place = row_places(plan, key_at, window, window + 128, spot)
    span = lax.shift_left(jnp.ones_like(key_level), jnp.maximum(key_level, 0))
    counts = jnp.clip(length - span * key_place, 0, span)
    usable = (counts > 0) & (key_place >= 0) & (key_level >= 0)
    logs = jnp.where(usable, jnp.log(jnp.maximum(counts, 1).astype(jnp.float32)), NEG)
    coarse = lambda level_at, place_at, by: level_at * 65536 + lax.shift_right_arithmetic(place_at, by)
    key_block = coarse(key_level, key_place, 4)[:1]
    key_half = coarse(key_level, key_place, 3)[:1]
    allowed = jnp.abs(coarse(row_level, row_place, 4) - key_block) <= 1
    if level != 0:
        apart = jnp.abs(coarse(row_level, row_place, 3) - key_half) >= 2
        allowed = allowed & (apart if level is not None else apart | (row_level == 0)) & (row_level >= 0)
    return jnp.where(allowed, logs[:1], NEG)


def pool_bounds(plan, shape, dim):
    row = lax.broadcasted_iota(jnp.int32, shape, dim)
    low = jnp.full(shape, -1, jnp.int32)
    size = jnp.zeros(shape, jnp.int32)
    level = jnp.zeros(shape, jnp.int32)
    parts = [(plan.pool_at[lv], plan.own[lv], lv) for lv in range(1, plan.levels)]
    parts += [(plan.pool_upper + first, count, lv) for lv, first, count in plan.slot]
    for start, count, lv in parts:
        inside = (row >= start) & (row < start + count)
        low = jnp.where(inside, (row - start) << lv, low)
        size = jnp.where(inside, 1 << lv, size)
    return low, size


def spread_columns(rows, place, count):
    width = rows.shape[1]
    source = lax.broadcasted_iota(jnp.int32, (width, width * count), 0)
    target = lax.broadcasted_iota(jnp.int32, (width, width * count), 1)
    return nn(rows, jnp.where(target == source + place * width, 1.0, 0.0).astype(rows.dtype))


def flip_bits(value, k):
    low, high, k_low, k_high = value % 2, value // 2, k % 2, k // 2
    return (high + k_high - 2 * high * k_high) * 2 + low + k_low - 2 * low * k_low


class Marks:
    def __init__(self):
        self.used = 0

    def take(self, count):
        self.used += count
        return self.used - count


def whole_layer(plan, dims, net_count, *refs):
    (extents, w_query, w_key, w_value, w_merge, w_expand, w_contract, norm_0, norm_1, norm_2, norm_3, tokens_in, cotangent_in,
     out_rows, out_grads, weight_grads, norm_grads,
     weights, norms, tokens, cotangent, ext, logs, pool, unpool, inverse, work,
     attended, ratio, recip, normed, scaled, rstd, grad_ext, total_ext, residual, acc, acc2, totals, result, row_grads,
     grads, got1, got2, got3, got4, norm_got,
     load_sem, send_sem, recv_sem) = refs
    part, width, pair, hidden = dims
    f32, bf16 = jnp.float32, jnp.bfloat16
    models = weights.shape[0]
    strip, columns = weights.shape[4:]
    ax, sq, az = lax.axis_index("dp"), lax.axis_index("seq"), lax.axis_index("mp")
    ay, ac = sq // 2, sq % 2
    spot = sq * 2 + ax
    spots = plan.spots
    length = extents[az]
    qkv = 3 * pair

    def device(x, y, c, z):
        return (x, y * 2 + c, z)

    def at_spot(place):
        return (place % 2, place // 2, az)

    def plane(k):
        return flip_bits(az, k)

    x_peer, y_peer, c_peer = device(1 - ax, ay, ac, az), device(ax, 1 - ay, ac, az), device(ax, ay, 1 - ac, az)
    z_peer = lambda k: device(ax, ay, ac, plane(k))

    barrier = pltpu.get_barrier_semaphore()
    for step in range(1, spots):
        pl.semaphore_signal(barrier, inc=1, device_id=at_spot((spot + step) % spots), device_id_type=MESH)
    for k in range(1, models):
        pl.semaphore_signal(barrier, inc=1, device_id=z_peer(k), device_id_type=MESH)
    load_tokens = pltpu.make_async_copy(tokens_in.at[az, 0], tokens, load_sem.at[0])
    load_cotangent = pltpu.make_async_copy(cotangent_in.at[az, 0], cotangent, load_sem.at[1])
    load_tokens.start()
    load_cotangent.start()
    own = (az, ax, ay, ac)
    weights[own + (slice(None), slice(0, pair))] = w_query[...] * jnp.asarray(HD ** -0.5, bf16)
    weights[own + (slice(None), slice(pair, 2 * pair))] = w_key[...]
    weights[own + (slice(None), slice(2 * pair, qkv))] = w_value[...]
    weights[own + (slice(None), slice(qkv, qkv + pair))] = w_merge[...]
    weights[own + (slice(None), slice(4 * pair, 4 * pair + hidden))] = w_expand[...]
    weights[own + (slice(None), slice(4 * pair + hidden, columns))] = w_contract[...]
    owner = ax * 4 + sq
    norms[spot] = jnp.concatenate(
        [spread_columns(row[...], owner, width // strip) for row in (norm_0, norm_1, norm_2, norm_3)]
        + [jnp.zeros((4, width), f32)], axis=0)
    pl.semaphore_wait(barrier, spots - 1 + models - 1)

    marks = Marks()

    def copy(i, src, dst, to):
        return pltpu.make_async_remote_copy(
            src_ref=src, dst_ref=dst, send_sem=send_sem.at[i], recv_sem=recv_sem.at[i],
            device_id=to, device_id_type=MESH)

    class Group:
        def __init__(self, i, pairs, whole):
            self.i, self.pairs, self.whole = i, pairs, whole

        def start(self):
            for src, dst, to in self.pairs:
                copy(self.i, src, dst, to).start()
            return self

        def arrive(self):
            copy(self.i, self.whole, self.whole, self.pairs[0][2]).wait_recv()

        def leave(self):
            copy(self.i, self.whole, self.whole, self.pairs[0][2]).wait_send()

    sent = []

    def send(pairs, whole):
        group = Group(marks.take(1), pairs, whole).start()
        sent.append(group)
        return group

    class Gather:
        def __init__(self, col, count, through_y):
            self.cols, self.rows = pl.ds(col, count), through_y
            self.flight = {}
            self.first = marks.take(models)

        def block(self, k, x, y, rows=slice(None)):
            return weights.at[plane(k), x, y, ac, rows, self.cols]

        def to_planes(self):
            here = self.block(0, ax, ay)
            for k in range(1, models):
                self.flight["z", k] = send([(here, here, z_peer(k))], here)

        def to_sides(self, k):
            if k:
                self.flight["z", k].arrive()
            here = self.block(k, ax, ay)
            self.flight["side", k] = send([(here, here, x_peer), (here, here, y_peer)],
                                          weights.at[plane(k), :, ay, ac, :, self.cols])

        def to_corner(self, k):
            self.flight["side", k].arrive()
            first = self.block(k, 1 - ax, ay, pl.ds(0, self.rows))
            rest = self.block(k, ax, 1 - ay, pl.ds(self.rows, strip - self.rows))
            self.flight["corner", k] = send([(first, first, y_peer), (rest, rest, x_peer)], self.block(k, ax, ay))

        def to_core(self, k):
            self.flight["corner", k].arrive()
            sent.append(self.last(k).start())

        def last(self, k):
            here = weights.at[plane(k), :, :, ac, :, self.cols]
            return Group(self.first + k, [(here, here, c_peer)], here)

        def here(self, k):
            self.last(k).arrive()

    first_gather = Gather(0, qkv, 32)
    merge_gather = Gather(qkv, pair, 48)
    feed_gather = Gather(4 * pair, 2 * hidden, 48)

    first_gather.to_planes()
    first_gather.to_sides(0)
    norm_copies = send([(norms.at[spot], norms.at[spot], at_spot((spot + step) % spots)) for step in range(1, spots)],
                       norms.at[pl.ds(0, spots - 1)])

    low, size = pool_bounds(plan, (part, 128), 0)
    for block in range(part // 128):
        token_at = block * 128 + lax.broadcasted_iota(jnp.int32, (part, 128), 1)
        member = (token_at >= low) & (token_at < low + size) & (token_at + spot * part < length)
        pool[:, block * 128:(block + 1) * 128] = jnp.where(member, 1.0, 0.0).astype(bf16)
    counts = jnp.clip(length - spot * part - low, 0, size)
    inverse[...] = 1.0 / jnp.maximum(counts, 1).astype(f32)
    low, size = pool_bounds(plan, (8, part), 1)
    token_at = lax.broadcasted_iota(jnp.int32, (part, part), 0)
    member = (token_at >= low[:1]) & (token_at < (low + size)[:1])
    unpool[...] = jnp.where(member, 1.0, 0.0).astype(bf16)
    first_gather.to_corner(0)
    first_gather.to_sides(1)
    load_tokens.wait()

    def statistics(values):
        center = values - jnp.mean(values, axis=-1, keepdims=True)
        spread = jnp.mean(center * center, axis=-1, keepdims=True)
        scale = lax.rsqrt(spread + 1e-05)
        return center * scale, scale

    xhat, scale = statistics(tokens[...].astype(f32))
    scaled[...] = xhat
    rstd[...] = jnp.broadcast_to(scale, (part, 128))
    first_gather.to_sides(2)
    first_gather.to_sides(3)
    merge_gather.to_planes()
    feed_gather.to_planes()
    first_gather.to_core(0)
    first_gather.to_corner(1)
    for i, tile in enumerate(plan.tiles):
        logs[i, 0:tile[1]] = log_counts(plan, tile, spot, length)
    first_gather.to_corner(2)
    first_gather.to_corner(3)
    merge_gather.to_sides(0)
    feed_gather.to_sides(0)
    first_gather.to_core(1)
    norm_copies.arrive()
    gains = norms[0]
    for i in range(1, spots):
        gains = gains + norms[i]
    pre_gain, pre_shift, mid_gain, mid_shift = (gains[i:i + 1] for i in range(4))
    normed[...] = (scaled[...] * pre_gain + pre_shift).astype(bf16)
    first_gather.to_core(2)
    first_gather.to_core(3)

    is_first, is_last = spot == 0, spot == spots - 1

    @pl.when(is_first)
    def _():
        for lv in range(plan.levels):
            rows = slice(plan.at[lv], plan.at[lv] + NR)
            ext[:, rows, :] = jnp.zeros((models, NR, qkv), bf16)
            grad_ext[:, rows, :] = jnp.zeros((models, NR, pair), bf16)
            total_ext[rows, :] = jnp.zeros((NR, 128), bf16)

    @pl.when(is_last)
    def _():
        for lv in range(plan.levels):
            end = plan.at[lv] + NR + plan.own[lv]
            rows = slice(end, end + NR)
            ext[:, rows, :] = jnp.zeros((models, NR, qkv), bf16)
            grad_ext[:, rows, :] = jnp.zeros((models, NR, pair), bf16)
            total_ext[rows, :] = jnp.zeros((NR, 128), bf16)

    def weight_cols(m, col, count):
        return weights[m, :, :, :, :, col:col + count].reshape(width, count)

    slot_row = pl.multiple_of(spot * NR, NR)
    own_slot_rows = pl.ds(pl.multiple_of(plan.upper + slot_row, NR), NR)
    class Rims:
        def __init__(self, view, i):
            self.view, self.i, self.to = view, i, at_spot((spot + 1) % spots)

        def start(self):
            view, i = self.view, self.i
            right, left = at_spot((spot + 1) % spots), at_spot((spot + spots - 1) % spots)

            @pl.when(jnp.logical_not(is_last))
            def _():
                for start, rows in zip(plan.at, plan.own):
                    copy(i, view(pl.ds(start + rows, NR)), view(pl.ds(start, NR)), right).start()

            @pl.when(jnp.logical_not(is_first))
            def _():
                for start, rows in zip(plan.at, plan.own):
                    copy(i, view(pl.ds(start + NR, NR)), view(pl.ds(start + NR + rows, NR)), left).start()

            block = view(own_slot_rows)
            for step in range(1, spots):
                copy(i, block, block, at_spot((spot + step) % spots)).start()

        def whole(self, sides):
            rows = self.view(pl.ds(0, (sides * plan.levels + spots - 1) * NR))
            return copy(self.i, rows, rows, self.to)

        def wait(self):
            at_end = is_first | is_last

            @pl.when(at_end)
            def _():
                self.whole(1).wait_recv()

            @pl.when(jnp.logical_not(at_end))
            def _():
                self.whole(2).wait_recv()

        def done(self):
            at_end = is_first | is_last

            @pl.when(at_end)
            def _():
                self.whole(1).wait_send()

            @pl.when(jnp.logical_not(at_end))
            def _():
                self.whole(2).wait_send()

    pair_base = marks.take(models)
    query_base = marks.take(1)
    grad_base = marks.take(models)
    total_base = marks.take(1)
    pair_rims = lambda k: Rims(lambda rows: ext.at[plane(k), rows, pl.ds(pair, 2 * pair)], pair_base + k)
    query_rims = lambda: Rims(lambda rows: ext.at[:, rows, pl.ds(0, pair)], query_base)
    grad_rims = lambda k: Rims(lambda rows: grad_ext.at[plane(k), rows, :], grad_base + k)
    total_rims = lambda: Rims(lambda rows: total_ext.at[rows, :], total_base)

    for k in range(models):
        first_gather.here(k)
        m = plane(k)
        rows = nn(normed[...], weight_cols(m, 0, qkv)).astype(bf16)
        ext[m, NR:NR + part, :] = rows
        means = (nn(pool[...], rows) * jnp.concatenate([inverse[...]] * 3, axis=1)).astype(bf16)
        for lv in range(1, plan.levels):
            ext[m, plan.at[lv] + NR:plan.at[lv] + NR + plan.own[lv], :] = means[plan.pool_at[lv]:plan.pool_at[lv] + plan.own[lv]]
        ext[m, own_slot_rows, :] = means[plan.pool_upper:plan.pool_upper + NR]
        pair_rims(k).start()

    lane = lax.broadcasted_iota(jnp.int32, (1, pair), 1)
    left_head = lane < HD

    def both_heads(rows):
        zero = jnp.zeros_like(rows)
        return jnp.concatenate([jnp.where(left_head, rows, zero), jnp.where(left_head, zero, rows)], axis=0)

    def joined(rows):
        half = rows.shape[0] // 2
        return jnp.where(left_head, rows[:half], rows[half:])

    ones = jnp.ones((128, 128), bf16)

    def stacked(parts):
        return parts[0] if len(parts) == 1 else jnp.concatenate(parts, axis=0)

    def tile_weights(m, rows, mask, window):
        queries = both_heads(rows)
        keys = ext[m, window:window + 128, pair:2 * pair]
        values = jnp.concatenate([ext[m, window:window + 128, 2 * pair:3 * pair], ones], axis=1)
        weight = jnp.exp(nt(queries, keys) + jnp.concatenate([mask, mask], axis=0))
        return queries, keys, values, weight

    def attend_tiles(m, tiles):
        pieces, weights_values = [], []
        for tile in tiles:
            first, _, window, _ = tile
            index = plan.tiles.index(tile)
            if first == plan.upper:
                pieces.append([(first, NR)])
                rows, mask = ext[m, own_slot_rows, 0:pair], logs[index, pl.ds(slot_row, NR)]
            else:
                pieces.append(plan.own_pieces(tile))
                rows = stacked([ext[m, low:low + count, 0:pair] for low, count in pieces[-1]])
                mask = stacked([logs[index, low - first:low - first + count] for low, count in pieces[-1]])
            _, _, values, weight = tile_weights(m, rows, mask, window)
            weights_values.append((weight.astype(bf16), values))
        both = [nn(weight, values) for weight, values in weights_values]
        sides = [(joined(product[:, :128]), joined(product[:, 128:])) for product in both]
        for rows, (numer, tot) in zip(pieces, sides):
            at = 0
            for low, count in rows:
                work[m, low:low + count, 0:pair] = numer[at:at + count]
                work[m, low:low + count, pair:2 * pair] = tot[at:at + count]
                at += count

    def attend(tiles, first_k, last_k, wait_rims):
        def body(k, carry):
            m = plane(k)
            if wait_rims:
                pair_rims(k).wait()
            for at in range(0, len(tiles), GROUP):
                attend_tiles(m, tiles[at:at + GROUP])
            return carry

        lax.fori_loop(first_k, last_k, body, 0)

    attend(plan.inner, 0, models, False)
    for k in range(1, models):
        merge_gather.to_sides(k)
    attend(plan.outer, 0, 2, True)
    feed_gather.to_corner(0)
    feed_gather.to_sides(1)
    attend(plan.outer, 2, models, True)
    for k in range(models):
        merge_gather.to_corner(k)
    feed_gather.to_sides(2)

    def coarse_rows(m, cols, slot_at):
        rows = [work[m, plan.at[lv] + NR:plan.at[lv] + NR + plan.own[lv], 0:cols] for lv in range(1, plan.levels)]
        return jnp.concatenate(rows + [work[m, slot_at, 0:cols]], axis=0)

    def spread_out(rows):
        high, rest = halves(rows)
        return nn(unpool[...], high) + nn(unpool[...], rest)

    def normalise(m, carry):
        both = spread_out(coarse_rows(m, 2 * pair, slice(plan.upper, plan.upper + NR)))
        both = both + work[m, NR:NR + part, 0:2 * pair]
        inv_total = 1.0 / both[:, pair:]
        quotient = both[:, :pair] * inv_total
        ratio[m] = quotient
        recip[m] = inv_total
        attended[m] = quotient.astype(bf16)
        return carry

    lax.fori_loop(0, models, normalise, 0)
    feed_gather.to_core(0)
    for k in range(models):
        merge_gather.to_core(k)
    feed_gather.to_corner(1)
    feed_gather.to_sides(3)

    residual[...] = tokens[...].astype(f32)
    for k in range(models):
        merge_gather.here(k)

    def merge(m, carry):
        residual[...] += nt(attended[m], weight_cols(m, qkv, pair))
        return carry

    lax.fori_loop(0, models, merge, 0)
    after = residual[...]
    mid_hat, mid_scale = statistics(after)
    mid = (mid_hat * mid_gain + mid_shift).astype(bf16)
    mid_t = mid.T
    load_cotangent.wait()
    row_at = lax.broadcasted_iota(jnp.int32, (part, 1), 0) + spot * part
    valid = row_at < length
    out_grad = jnp.where(valid, cotangent[...], jnp.zeros((), bf16))
    out_grad_t = out_grad.T
    acc[...] = jnp.zeros(acc.shape, f32)
    acc2[...] = jnp.zeros(acc.shape, f32)
    block_shape = grads.shape[1:5] + (hidden,)

    feed_gather.to_core(1)
    feed_gather.to_corner(2)

    class Reduce:
        def __init__(self, col, count):
            self.cols = pl.ds(col, count)
            self.first = marks.take(4 * models)

        def core(self, k):
            m = plane(k)
            landing = got1.at[m, :, :, :, self.cols]
            return Group(self.first + k, [(grads.at[m, :, :, 1 - ac, :, self.cols], landing, c_peer)], landing)

        def side(self, k):
            m = plane(k)
            top, bottom = pl.ds(0, 32), pl.ds(32, 32)
            return Group(self.first + models + k,
                         [(got1.at[m, 1 - ax, :, top, self.cols], got2.at[m, :, top, self.cols], x_peer),
                          (got1.at[m, :, 1 - ay, bottom, self.cols], got2.at[m, :, bottom, self.cols], y_peer)],
                         got2.at[m, :, :, self.cols])

        def corner(self, k):
            m = plane(k)
            top, bottom = pl.ds(0, 32), pl.ds(32, 32)
            return Group(self.first + 2 * models + k,
                         [(got2.at[m, 1 - ay, top, self.cols], got3.at[m, top, self.cols], y_peer),
                          (got2.at[m, 1 - ax, bottom, self.cols], got3.at[m, bottom, self.cols], x_peer)],
                         got3.at[m, :, self.cols])

        def home(self, k):
            block = got3.at[plane(k), :, self.cols]
            return Group(self.first + 3 * models + k, [(block, got4.at[k, :, self.cols], z_peer(1 + 2 * (k // 3)))], block)

        def start(self, k):
            self.core(k).start()

        def to_sides(self, k):
            m = plane(k)
            self.core(k).arrive()
            got1[m, :, :, :, self.cols] = got1[m, :, :, :, self.cols] + grads[m, :, :, ac, :, self.cols]
            self.side(k).start()

        def to_corner(self, k):
            m = plane(k)
            self.side(k).arrive()
            top, bottom = pl.ds(0, 32), pl.ds(32, 32)
            got2[m, :, top, self.cols] = got2[m, :, top, self.cols] + got1[m, ax, :, top, self.cols]
            got2[m, :, bottom, self.cols] = got2[m, :, bottom, self.cols] + got1[m, :, ay, bottom, self.cols]
            self.corner(k).start()

        def to_planes(self, k):
            m = plane(k)
            self.corner(k).arrive()
            top, bottom = pl.ds(0, 32), pl.ds(32, 32)
            got3[m, top, self.cols] = got3[m, top, self.cols] + got2[m, ay, top, self.cols]
            got3[m, bottom, self.cols] = got3[m, bottom, self.cols] + got2[m, ax, bottom, self.cols]

            @pl.when(k == 3)
            def _():
                self.home(2).arrive()
                got3[m, :, self.cols] = got3[m, :, self.cols] + got4[2, :, self.cols]

            @pl.when(k > 0)
            def _():
                self.home(k).start()

        def end(self):
            total = got3[az, :, self.cols].astype(f32)
            for k in (1, 3):
                self.home(k).arrive()
                total = total + got4[k, :, self.cols].astype(f32)
            weight_grads[:, self.cols] = total

        def done(self, k):
            for group in (self.core(k), self.side(k), self.corner(k)):
                group.leave()

            @pl.when(k > 0)
            def _():
                self.home(k).leave()

    feed_reduce = Reduce(4 * pair, 2 * hidden)
    attention_reduce = Reduce(0, 4 * pair)

    def feed(k, carry):
        m = plane(k)
        feed_gather.here(k)
        expand, contract_t = weight_cols(m, 4 * pair, hidden), weight_cols(m, 4 * pair + hidden, hidden)
        up = nn(mid, expand)
        act_grad = nn(out_grad, contract_t)
        phi = 0.5 + 0.5 * lax.erf(up * (0.5 ** 0.5))
        act = (up * phi).astype(bf16)
        slope = phi + up * (jnp.exp(-0.5 * up * up) * 0.3989422804014327)
        hidden_grad = (act_grad * slope).astype(bf16)
        grads[m, :, :, :, :, 4 * pair:4 * pair + hidden] = nn(mid_t, hidden_grad).astype(bf16).reshape(block_shape)
        grads[m, :, :, :, :, 4 * pair + hidden:columns] = nn(out_grad_t, act).astype(bf16).reshape(block_shape)
        feed_reduce.start(k)
        acc[...] += nt(act, contract_t)
        acc2[...] += nt(hidden_grad, expand)
        return carry

    lax.fori_loop(0, 1, feed, 0)
    feed_gather.to_core(2)
    feed_gather.to_corner(3)
    query_rims().start()
    lax.fori_loop(1, 2, feed, 0)
    feed_gather.to_core(3)
    feed_reduce.to_sides(0)
    lax.fori_loop(2, 3, feed, 0)
    feed_reduce.to_sides(1)
    lax.fori_loop(3, 4, feed, 0)
    result[...] = jnp.where(valid, after + acc[...], 0.0).astype(bf16)
    mid_grad = acc2[...]

    def rows_home(source, target):
        share = part // models
        target[az] = source[pl.ds(pl.multiple_of(az * share, share), share), :]
        return send([(source.at[pl.ds(pl.multiple_of(plane(k) * share, share), share), :], target.at[az], z_peer(k))
                     for k in range(1, models)], target.at[pl.ds(0, models - 1)])

    def norm_back(grad, hat, scale_row, gain):
        scaled_grad = grad * gain
        mean_grad = jnp.mean(scaled_grad, axis=-1, keepdims=True)
        mean_along = jnp.mean(scaled_grad * hat, axis=-1, keepdims=True)
        return scale_row * (scaled_grad - mean_grad - hat * mean_along)

    through = out_grad.astype(f32) + norm_back(mid_grad, mid_hat, mid_scale, mid_gain)
    residual[...] = through
    branch = through.astype(bf16)
    branch_t = branch.T
    norm_sums = [jnp.sum(mid_grad * mid_hat, axis=0, keepdims=True), jnp.sum(mid_grad, axis=0, keepdims=True)]

    merge_shape = grads.shape[1:5] + (pair,)
    select_row = lax.broadcasted_iota(jnp.int32, (pair, 128), 0) // HD
    select_col = lax.broadcasted_iota(jnp.int32, (pair, 128), 1) // 2
    totals[...] = jnp.zeros(totals.shape, f32)

    def unmerge(step, carry):
        k = models - 1 - step
        m = plane(k)
        attended_grad = nn(branch, weight_cols(m, qkv, pair)) * recip[m]
        fine = attended_grad.astype(bf16)
        grad_ext[m, NR:NR + part, :] = fine
        sums = nn(pool[...], fine).astype(bf16)
        for lv in range(1, plan.levels):
            grad_ext[m, plan.at[lv] + NR:plan.at[lv] + NR + plan.own[lv], :] = sums[plan.pool_at[lv]:plan.pool_at[lv] + plan.own[lv]]
        grad_ext[m, own_slot_rows, :] = sums[plan.pool_upper:plan.pool_upper + NR]
        grad_rims(k).start()
        high, rest = halves(attended_grad * ratio[m])
        chosen = jnp.where(select_row + 2 * m == select_col, -1.0, 0.0).astype(bf16)
        totals[...] += nn(high, chosen) + nn(rest, chosen)
        grads[m, :, :, :, :, qkv:qkv + pair] = nn(branch_t, attended[m]).astype(bf16).reshape(merge_shape)
        return carry

    lax.fori_loop(0, models, unmerge, 0)
    even = lax.broadcasted_iota(jnp.int32, (1, 128), 1) % 2 == 0
    high, rest = halves(totals[...])
    total_ext[NR:NR + part, :] = jnp.where(even, high, rest)
    pooled_high, pooled_rest = halves(nn(pool[...], high) + nn(pool[...], rest))
    sums = jnp.where(even, pooled_high, pooled_rest)
    for lv in range(1, plan.levels):
        total_ext[plan.at[lv] + NR:plan.at[lv] + NR + plan.own[lv], :] = sums[plan.pool_at[lv]:plan.pool_at[lv] + plan.own[lv]]
    total_ext[own_slot_rows, :] = sums[plan.pool_upper:plan.pool_upper + NR]
    total_rims().start()
    rows_out = rows_home(result, out_rows)

    feed_reduce.to_corner(0)
    feed_reduce.to_sides(2)
    feed_reduce.to_sides(3)

    head_of_lane = lax.broadcasted_iota(jnp.int32, (1, 128), 1) // 2

    def clear(m, carry):
        work[m] = jnp.zeros(work.shape[1:], f32)
        return carry

    lax.fori_loop(0, models, clear, 0)
    normed_t = normed[...].T
    acc[...] = jnp.zeros(acc.shape, f32)
    qkv_shape = grads.shape[1:5] + (qkv,)
    query_scale = jnp.where(lax.broadcasted_iota(jnp.int32, (1, qkv), 1) < pair, HD ** -0.5, 1.0)
    def back_tiles(m, tiles):
        rows_at = [slice(first, first + count) for first, count, _, _ in tiles]
        key_rows = [slice(window, window + 128) for _, _, window, _ in tiles]
        masks = [logs[plan.tiles.index(tile), 0:tile[1]] for tile in tiles]
        made = [tile_weights(m, ext[m, rows, 0:pair], mask, tile[2]) for tile, rows, mask in zip(tiles, rows_at, masks)]
        numers = [both_heads(grad_ext[m, rows, :]) for rows in rows_at]
        slopes = []
        for rows, numer, (_, _, values, _) in zip(rows_at, numers, made):
            tot = total_ext[rows, :]
            zero = jnp.zeros_like(tot)
            tots = jnp.concatenate([jnp.where(head_of_lane == 2 * m, tot, zero),
                                    jnp.where(head_of_lane == 2 * m + 1, tot, zero)], axis=0)
            slopes.append(nt(jnp.concatenate([numer, tots], axis=1), values))
        score_grads = [(weight * by).astype(bf16) for (_, _, _, weight), by in zip(made, slopes)]
        query_sides = [joined(nn(grad, keys)) for grad, (_, keys, _, _) in zip(score_grads, made)]
        key_sides = [tn(grad, queries) for grad, (queries, _, _, _) in zip(score_grads, made)]
        value_sides = [tn(weight.astype(bf16), numer) for (_, _, _, weight), numer in zip(made, numers)]
        for rows, side in zip(rows_at, query_sides):
            work[m, rows, 0:pair] = side
        for rows, key_side, value_side in zip(key_rows, key_sides, value_sides):
            work[m, rows, pair:2 * pair] += key_side
            work[m, rows, 2 * pair:3 * pair] += value_side

    def back_inner(m, carry):
        back_tiles(m, plan.inner)
        return carry

    lax.fori_loop(0, models, back_inner, 0)
    feed_reduce.to_corner(1)
    total_rims().wait()
    query_rims().wait()

    def turn(step):
        late = step // 2
        return (2 + step) * (1 - late) + (3 - step) * late

    def back(step, carry):
        k = turn(step)
        m = plane(k)
        grad_rims(k).wait()
        for at in range(0, len(plan.outer), BACK_GROUP):
            back_tiles(m, plan.outer[at:at + BACK_GROUP])
        coarse = coarse_rows(m, qkv, own_slot_rows)
        spread = spread_out(coarse * jnp.concatenate([inverse[...]] * 3, axis=1))
        rows = (work[m, NR:NR + part, :] + jnp.where(valid, spread, 0.0)).astype(bf16)
        grads[m, :, :, :, :, 0:qkv] = (nn(normed_t, rows) * query_scale).astype(bf16).reshape(qkv_shape)
        attention_reduce.start(k)
        acc[...] += nt(rows, weight_cols(m, 0, qkv))

        @pl.when(step == 0)
        def _():
            feed_reduce.to_corner(2)
            feed_reduce.to_planes(0)

        @pl.when(step == 1)
        def _():
            feed_reduce.to_corner(3)
            feed_reduce.to_planes(1)

        @pl.when(step == 2)
        def _():
            feed_reduce.to_planes(2)

        @pl.when(step == 3)
        def _():
            feed_reduce.to_planes(3)

        @pl.when(step >= 1)
        def _():
            attention_reduce.to_sides(turn(step - 1))

        @pl.when(step >= 2)
        def _():
            attention_reduce.to_corner(turn(step - 2))

        @pl.when(step >= 3)
        def _():
            attention_reduce.to_planes(turn(step - 3))

        return carry

    lax.fori_loop(0, models, back, 0)
    normed_grad = acc[...]
    hat = scaled[...]
    row_grads[...] = (residual[...] + norm_back(normed_grad, hat, rstd[:, 0:1], pre_gain)).astype(bf16)
    grads_out = rows_home(row_grads, out_grads)
    attention_reduce.to_sides(0)
    attention_reduce.to_corner(1)
    attention_reduce.to_planes(3)
    norm_sums = [jnp.sum(normed_grad * hat, axis=0, keepdims=True), jnp.sum(normed_grad, axis=0, keepdims=True)] + norm_sums
    norm_got[0] = jnp.concatenate(norm_sums + [jnp.zeros((4, width), f32)], axis=0)
    small = send([(norm_got.at[0], norm_got.at[step], at_spot((spot + step) % spots)) for step in range(1, spots)],
                 norm_got.at[pl.ds(0, spots - 1)])
    attention_reduce.to_corner(0)
    attention_reduce.to_planes(1)
    feed_reduce.end()
    attention_reduce.to_planes(0)
    small.arrive()
    norm_total = norm_got[0]
    for step in range(1, spots):
        norm_total = norm_total + norm_got[step]
    norm_got[spots] = norm_total
    small = send([(norm_got.at[spots], norm_got.at[spots + k], z_peer(k)) for k in range(1, models)],
                 norm_got.at[pl.ds(0, models - 1)])
    attention_reduce.end()
    small.arrive()
    for k in range(1, models):
        norm_total = norm_total + norm_got[spots + k]
    norm_grads[...] = norm_total
    rows_out.arrive()
    grads_out.arrive()
    assert marks.used == net_count, marks.used
    for group in sent:
        group.leave()

    def drain(k, carry):
        pair_rims(k).done()
        grad_rims(k).done()
        feed_reduce.done(k)
        attention_reduce.done(k)
        return carry

    lax.fori_loop(0, models, drain, 0)
    query_rims().done()
    total_rims().done()


def finish_outputs(dims, rows_ref, grads_ref, weights_ref, norms_ref,
                   out_rows, out_grads, query, key, value, merge, up, down, *norm_outs):
    part, width, pair, hidden = dims
    out_rows[...] = rows_ref[...].reshape(out_rows.shape)
    out_grads[...] = grads_ref[...].reshape(out_grads.shape)
    strip = query.shape[0]
    query[...] = weights_ref[:, 0:pair]
    key[...] = weights_ref[:, pair:2 * pair]
    value[...] = weights_ref[:, 2 * pair:3 * pair]
    up[...] = weights_ref[:, 4 * pair:4 * pair + hidden]
    merge[...] = weights_ref[:, 3 * pair:4 * pair]
    down[...] = weights_ref[:, 4 * pair + hidden:4 * pair + 2 * hidden]
    owner = lax.axis_index("dp") * 4 + lax.axis_index("seq")
    strips = width // strip
    mine = norms_ref[:, 0:strip] * (owner == 0).astype(jnp.float32)
    for i in range(1, strips):
        mine = jnp.where(owner == i, norms_ref[:, i * strip:(i + 1) * strip], mine)
    for i, out in enumerate(norm_outs):
        out[...] = mine[i].reshape(out.shape)


def fast_body(plan, incoming_embeddings, output_sensitivity, sequence_extents, asking_projector, lookup_projector,
              content_projector, attention_combiner, feedforward_expand, feedforward_contract,
              attention_norm_scale, attention_norm_bias, feedforward_norm_scale, feedforward_norm_bias):
    bf16, f32 = jnp.bfloat16, jnp.float32
    models = lax.axis_size("mp")
    seqs, _, part, width = incoming_embeddings.shape
    strip, pair = asking_projector.shape
    hidden = feedforward_expand.shape[1]
    columns = 4 * pair + 2 * hidden
    norm_parts = [row.reshape(1, strip) for row in (
        attention_norm_scale, attention_norm_bias, feedforward_norm_scale, feedforward_norm_bias)]
    share = part // models
    spots, rows = plan.spots, plan.rows
    deep = (2, 2, 2, strip, columns)
    net_count = 92
    vmem = pltpu.VMEM
    scratch = [
        vmem((models,) + deep, bf16), vmem((spots, 8, width), f32), vmem((part, width), bf16), vmem((part, width), bf16),
        vmem((models, rows, 3 * pair), bf16), vmem((len(plan.tiles), 128, 128), f32),
        vmem((part, part), bf16), vmem((part, part), bf16), vmem((part, 128), f32), vmem((models, rows, 3 * pair), f32),
        vmem((models, part, pair), bf16), vmem((models, part, pair), f32), vmem((models, part, pair), f32),
        vmem((part, width), bf16), vmem((part, width), f32), vmem((part, 128), f32),
        vmem((models, rows, pair), bf16), vmem((rows, 128), bf16), vmem((part, width), f32), vmem((part, width), f32),
        vmem((part, width), f32), vmem((part, 128), f32), vmem((part, width), bf16), vmem((part, width), bf16),
        vmem((models,) + deep, bf16), vmem((models, 2, 2, strip, columns), bf16), vmem((models, 2, strip, columns), bf16),
        vmem((models, strip, columns), bf16), vmem((models, strip, columns), bf16), vmem((spots + models, 8, width), f32),
        pltpu.SemaphoreType.DMA((2,)), pltpu.SemaphoreType.DMA((net_count,)), pltpu.SemaphoreType.DMA((net_count,)),
    ]
    any_space, in_vmem = pl.BlockSpec(memory_space=pl.ANY), pl.BlockSpec(memory_space=pltpu.VMEM)
    out_rows, out_grads, weight_grads, norm_grads = pl.pallas_call(
        functools.partial(whole_layer, plan, (part, width, pair, hidden), net_count),
        out_shape=(jax.ShapeDtypeStruct((seqs, share, width), bf16), jax.ShapeDtypeStruct((seqs, share, width), bf16),
                   jax.ShapeDtypeStruct((strip, columns), f32), jax.ShapeDtypeStruct((8, width), f32)),
        in_specs=[pl.BlockSpec(memory_space=pltpu.SMEM)] + [in_vmem] * 10 + [any_space] * 2,
        out_specs=(in_vmem,) * 4,
        scratch_shapes=scratch,
        compiler_params=pltpu.CompilerParams(collective_id=0, has_side_effects=True, vmem_limit_bytes=60 * 2 ** 20),
        name="layer",
    )(sequence_extents, asking_projector, lookup_projector, content_projector, attention_combiner.T, feedforward_expand,
      feedforward_contract.T, *norm_parts, incoming_embeddings, output_sensitivity)
    flat = lambda *shape: jax.ShapeDtypeStruct(shape, f32)
    rows_type = jax.ShapeDtypeStruct((seqs, 1, share, width), bf16)
    finished = pl.pallas_call(
        functools.partial(finish_outputs, (part, width, pair, hidden)),
        out_shape=(rows_type, rows_type, flat(strip, pair), flat(strip, pair), flat(strip, pair), flat(strip, pair),
                   flat(strip, hidden), flat(strip, hidden)) + (flat(1, strip),) * 4,
        in_specs=[in_vmem] * 4,
        out_specs=(in_vmem,) * 12,
        name="outputs",
    )(out_rows, out_grads, weight_grads, norm_grads)
    rows_end, grads_end, query_grad, key_grad, value_grad, merge_t, up_grad, down_t = finished[:8]
    return (rows_end, grads_end, query_grad, key_grad, value_grad, merge_t.T, up_grad, down_t.T,
            *(row.reshape(strip) for row in finished[8:]))


def solution(mesh):
    in_specs = (
        P(None, "seq", "dp", None),
        P(None, "seq", "dp", None),
        P(),
        P(("dp", "seq"), "mp"),
        P(("dp", "seq"), "mp"),
        P(("dp", "seq"), "mp"),
        P("mp", ("dp", "seq")),
        P(("dp", "seq"), "mp"),
        P("mp", ("dp", "seq")),
        P(("dp", "seq")),
        P(("dp", "seq")),
        P(("dp", "seq")),
        P(("dp", "seq")),
    )
    out_specs = (
        P(None, "seq", ("dp", "mp"), None),
        P(None, "seq", ("dp", "mp"), None),
        P(("dp", "seq"), "mp"),
        P(("dp", "seq"), "mp"),
        P(("dp", "seq"), "mp"),
        P("mp", ("dp", "seq")),
        P(("dp", "seq"), "mp"),
        P("mp", ("dp", "seq")),
        P(("dp", "seq")),
        P(("dp", "seq")),
        P(("dp", "seq")),
        P(("dp", "seq")),
    )
    sizes = (mesh.shape["dp"], mesh.shape["seq"], mesh.shape["mp"])

    def chosen(*arrays):
        seqs, _, part, width = arrays[0].shape
        if sizes == (2, 4, 4) and seqs == sizes[2] and part == width == 512 and arrays[3].shape[1] == 128:
            return fast_body(Plan(part, sizes[0] * sizes[1]), *arrays)
        return general_body(*arrays)

    return jax.shard_map(chosen, mesh=mesh, in_specs=in_specs, out_specs=out_specs, check_vma=False)
```

```python
import functools

import jax
import jax.numpy as jnp
from jax import lax
from jax.experimental import pallas as pl
from jax.experimental.pallas import tpu as pltpu
from jax.sharding import PartitionSpec as P

HD = 64
NR = 16


def cut_along(x, dim, count):
    before, after = (x.shape[:dim], x.shape[dim + 1 :])
    return jnp.moveaxis(x.reshape(*before, count, -1, *after), dim, 0)


def summed_on_arrival(x, axis, dim):
    count = lax.axis_size(axis)
    blocks = lax.all_to_all(cut_along(x, dim, count), axis, 0, 0, tiled=True)
    return jnp.sum(blocks.astype(jnp.float32), axis=0)


def sent_together(arrays, axis, dim, along):
    ends, at = ([], 0)
    for a in arrays[:-1]:
        at += a.shape[along]
        ends.append(at)
    both = jnp.concatenate(arrays, axis=along)
    return tuple(jnp.split(summed_on_arrival(both, axis, dim), ends, axis=along))


def norm_rows(values, gain_row, shift_row):
    center = values - jnp.mean(values, axis=-1, keepdims=True)
    spread = jnp.mean(center * center, axis=-1, keepdims=True)
    return center * lax.rsqrt(spread + 1e-05) * gain_row + shift_row


def norm_gain_parts(values, grad_rows):
    center = values - jnp.mean(values, axis=-1, keepdims=True)
    spread = jnp.mean(center * center, axis=-1, keepdims=True)
    scaled = center * lax.rsqrt(spread + 1e-05)
    return (jnp.sum(grad_rows * scaled, axis=0), jnp.sum(grad_rows, axis=0))


def gelu_exact(values):
    return jax.nn.gelu(values, approximate=False)


def dot_plain(left_mat, right_mat):
    return jnp.dot(left_mat, right_mat, preferred_element_type=jnp.float32)


def dot_inner(left_mat, right_mat):
    return lax.dot_general(
        left_mat, right_mat, (((0,), (0,)), ((), ())), preferred_element_type=jnp.float32
    )


def dot_outer(left_mat, right_mat):
    return lax.dot_general(
        left_mat, right_mat, (((1,), (1,)), ((), ())), preferred_element_type=jnp.float32
    )


def group_sum(values, group_width):
    return jnp.sum(
        values.reshape((values.shape[0] // group_width, group_width) + values.shape[1:]), axis=1
    )


def block_shape(coarse_rows):
    query_len = min(coarse_rows, 512)
    span_len = query_len + 2 * NR
    window_len = -(-span_len // 128) * 128
    return (query_len, span_len, window_len)


def window_mask(level_at, first_row, query_len, window_len, span_len):
    rows_at = first_row + jnp.arange(query_len, dtype=jnp.int32)[:, None]
    keys_at = first_row + jnp.arange(window_len, dtype=jnp.int32)[None, :]
    inside = keys_at - first_row < span_len
    allowed = jnp.abs(rows_at // NR + 1 - keys_at // NR) <= 1
    if level_at > 0:
        half_block = NR // 2
        allowed = allowed & (jnp.abs(rows_at // half_block + 2 - keys_at // half_block) >= 2)
    return (allowed & inside).astype(jnp.float32)


def level_forward(query_rows, pair_wide, count_wide, level_at):
    coarse_rows = query_rows.shape[0]
    columns = query_rows.shape[1]
    heads_here = columns // HD
    query_len, span_len, window_len = block_shape(coarse_rows)
    tail_pad = window_len - span_len
    pair_padded = jnp.pad(pair_wide, ((0, tail_pad), (0, 0)))
    count_padded = jnp.pad(count_wide, (0, tail_pad))
    weight_list = []
    total_parts = []
    numer_parts = []
    for block_at in range(coarse_rows // query_len):
        first_row = block_at * query_len
        query_block = query_rows[first_row : first_row + query_len]
        pair_block = pair_padded[first_row : first_row + window_len]
        count_block = count_padded[first_row : first_row + window_len]
        keep_mask = (
            window_mask(level_at, first_row, query_len, window_len, span_len) * count_block[None, :]
        )
        head_weights = []
        head_totals = []
        head_numers = []
        for head_at in range(heads_here):
            head_cols = slice(head_at * HD, (head_at + 1) * HD)
            value_cols = slice(columns + head_at * HD, columns + (head_at + 1) * HD)
            scores = dot_outer(query_block[:, head_cols], pair_block[:, head_cols]) * HD ** (-0.5)
            weight = jnp.exp(scores) * keep_mask
            head_weights.append(weight)
            head_totals.append(jnp.sum(weight, axis=-1))
            head_numers.append(dot_plain(weight.astype(jnp.bfloat16), pair_block[:, value_cols]))
        weight_list.append(head_weights)
        total_parts.append(jnp.stack(head_totals, axis=1))
        numer_parts.append(jnp.concatenate(head_numers, axis=1))
    totals = jnp.concatenate(total_parts, axis=0)
    numer_part = jnp.concatenate(numer_parts, axis=0).reshape(coarse_rows, heads_here, HD)
    return ((query_rows, pair_padded, weight_list), totals, numer_part)


def level_backward(level_kept, numer_rows, total_rows):
    query_rows, pair_padded, weight_list = level_kept
    coarse_rows = query_rows.shape[0]
    columns = query_rows.shape[1]
    heads_here = columns // HD
    query_len, span_len, window_len = block_shape(coarse_rows)
    numer_flat = numer_rows.reshape(coarse_rows, columns)
    pair_grad = jnp.zeros(pair_padded.shape, jnp.float32)
    query_parts = []
    for block_at in range(coarse_rows // query_len):
        first_row = block_at * query_len
        query_block = query_rows[first_row : first_row + query_len]
        pair_block = pair_padded[first_row : first_row + window_len]
        numer_block = numer_flat[first_row : first_row + query_len]
        total_block = total_rows[first_row : first_row + query_len]
        query_heads = []
        key_heads = []
        value_heads = []
        for head_at in range(heads_here):
            head_cols = slice(head_at * HD, (head_at + 1) * HD)
            value_cols = slice(columns + head_at * HD, columns + (head_at + 1) * HD)
            weight = head_weights = weight_list[block_at][head_at]
            grad_here = numer_block[:, head_cols]
            score_grad = (
                (dot_outer(grad_here, pair_block[:, value_cols]) + total_block[:, head_at][:, None])
                * weight
            ).astype(jnp.bfloat16)
            query_heads.append(dot_plain(score_grad, pair_block[:, head_cols]) * HD ** (-0.5))
            key_heads.append(dot_inner(score_grad, query_block[:, head_cols]) * HD ** (-0.5))
            value_heads.append(dot_inner(head_weights.astype(jnp.bfloat16), grad_here))
        query_parts.append(jnp.concatenate(query_heads, axis=1))
        block_grad = jnp.concatenate(key_heads + value_heads, axis=1)
        pair_grad = pair_grad + jnp.pad(
            block_grad, ((first_row, pair_padded.shape[0] - first_row - window_len), (0, 0))
        )
    query_grad = jnp.concatenate(query_parts, axis=0)
    return (query_grad, pair_grad[: coarse_rows + 2 * NR])


def general_body(
    incoming_embeddings,
    output_sensitivity,
    sequence_extents,
    asking_projector,
    lookup_projector,
    content_projector,
    attention_combiner,
    feedforward_expand,
    feedforward_contract,
    attention_norm_scale,
    attention_norm_bias,
    feedforward_norm_scale,
    feedforward_norm_bias,
):
    groups = lax.axis_size("dp")
    slices = lax.axis_size("seq")
    models = lax.axis_size("mp")
    group_id = lax.axis_index("dp")
    slice_id = lax.axis_index("seq")
    model_id = lax.axis_index("mp")
    seq_count = incoming_embeddings.shape[0]
    piece_len = incoming_embeddings.shape[2]
    model_width = incoming_embeddings.shape[3]
    part_len = piece_len * groups
    batches = seq_count // groups
    share_len = piece_len // models
    share_rows = groups * share_len
    local_top = (part_len // NR).bit_length() - 1
    upper_start = local_top + 1
    level_top = (part_len * slices // (2 * NR)).bit_length() - 1
    upper_rows = NR // 2
    upper_whole = upper_rows * slices
    send_tok = incoming_embeddings.reshape(
        groups, batches, piece_len, model_width
    )
    send_cot = output_sensitivity.reshape(
        groups, batches, piece_len, model_width
    )
    dealt_tok, dealt_cot = (
        lax.all_to_all(send_tok, "dp", split_axis=0, concat_axis=2, tiled=True),
        lax.all_to_all(send_cot, "dp", split_axis=0, concat_axis=2, tiled=True),
    )
    dealt_tok = dealt_tok.reshape(batches, part_len, model_width)
    dealt_cot = dealt_cot.reshape(batches, part_len, model_width)
    my_lengths = lax.dynamic_slice_in_dim(sequence_extents, group_id * batches, batches, 0)

    def split_rows(rows):
        return rows.reshape((groups, models, share_len) + rows.shape[1:])

    def take_share(rows):
        return lax.dynamic_slice_in_dim(split_rows(rows), model_id, 1, 1).reshape(
            (share_rows,) + rows.shape[1:]
        )

    def neighbour_rims(gathered):
        padded = jnp.pad(gathered, ((2 * NR, 2 * NR), (0, 0)))
        from_left = lax.dynamic_slice_in_dim(padded, slice_id * 2 * NR + NR, NR, 0)
        from_right = lax.dynamic_slice_in_dim(padded, (slice_id + 2) * 2 * NR, NR, 0)
        return (from_left, from_right)

    def one_batch(batch_index, learnable_collection):
        full_query, full_key, full_value, full_merge, full_up, full_down = learnable_collection[:6]
        gain_pre, shift_pre, gain_mid, shift_mid = (
            learnable_tensor.astype(jnp.float32) for learnable_tensor in learnable_collection[6:]
        )
        columns = full_query.shape[1]
        heads_here = columns // HD
        length_now = my_lengths[batch_index]

        def level_counts(level_at, first_id, id_total):
            coarse_ids = first_id + jnp.arange(id_total, dtype=jnp.int32)
            group_len = 2**level_at
            return jnp.where(
                coarse_ids >= 0, jnp.clip(length_now - group_len * coarse_ids, 0, group_len), 0
            ).astype(jnp.float32)

        positions = slice_id * part_len + jnp.arange(part_len, dtype=jnp.int32)
        valid_rows = (positions < length_now).astype(jnp.float32)
        inputs = dealt_tok[batch_index].astype(jnp.float32)
        grad_in = dealt_cot[batch_index].astype(jnp.float32) * valid_rows[:, None]
        valid_share = take_share(valid_rows)
        normed, pull_pre = jax.vjp(norm_rows, inputs, gain_pre, shift_pre)
        normed_low = normed.astype(jnp.bfloat16)
        queries = dot_plain(normed_low, full_query).astype(jnp.bfloat16)
        keys_own = dot_plain(normed_low, full_key).astype(jnp.bfloat16)
        values_own = dot_plain(normed_low, full_value).astype(jnp.bfloat16)
        pair_own = jnp.concatenate([keys_own, values_own], axis=1)
        fine_all = (
            jnp.concatenate([queries, pair_own], axis=1).astype(jnp.float32) * valid_rows[:, None]
        )
        level_sums = [fine_all]
        for level_at in range(1, upper_start + 1):
            level_sums.append(group_sum(level_sums[-1], 2))
        query_levels = [queries]
        pair_levels = [pair_own]
        own_counts = [valid_rows]
        for level_at in range(1, local_top + 1):
            coarse_rows = part_len >> level_at
            counts_here = level_counts(level_at, slice_id * coarse_rows, coarse_rows)
            coarse_means = (level_sums[level_at] / jnp.maximum(counts_here, 1.0)[:, None]).astype(
                jnp.bfloat16
            )
            query_levels.append(coarse_means[:, :columns])
            pair_levels.append(coarse_means[:, columns:])
            own_counts.append(counts_here)
        edge_rows = jnp.concatenate(
            [
                jnp.concatenate([pair_rows[:NR], pair_rows[-NR:]], axis=0)
                for pair_rows in pair_levels
            ],
            axis=1,
        )
        edges_all, upper_all = (
            lax.all_gather(
                edge_rows.astype(jnp.float32).astype(jnp.bfloat16), "seq", axis=0, tiled=True
            ).astype(jnp.float32),
            lax.all_gather(
                level_sums[upper_start].astype(jnp.bfloat16), "seq", axis=0, tiled=True
            ).astype(jnp.float32),
        )
        left_edge, right_edge = neighbour_rims(edges_all)
        left_edge = left_edge.astype(jnp.bfloat16)
        right_edge = right_edge.astype(jnp.bfloat16)
        kept_levels = []
        total_all = jnp.zeros((part_len, heads_here), jnp.float32)
        numer_all = jnp.zeros((part_len, heads_here, HD), jnp.float32)
        for level_at in range(local_top + 1):
            coarse_rows = part_len >> level_at
            col_range = slice(level_at * 2 * columns, (level_at + 1) * 2 * columns)
            pair_wide = jnp.concatenate(
                [left_edge[:, col_range], pair_levels[level_at], right_edge[:, col_range]], axis=0
            )
            count_wide = level_counts(level_at, slice_id * coarse_rows - NR, coarse_rows + 2 * NR)
            level_kept, totals, numer_part = level_forward(
                query_levels[level_at], pair_wide, count_wide, level_at
            )
            kept_levels.append(level_kept)
            total_all = total_all + jnp.repeat(totals, 2**level_at, axis=0)
            numer_all = numer_all + jnp.repeat(numer_part, 2**level_at, axis=0)
        level_at = 7
        repeat_by = 2 ** (level_at - upper_start)
        coarse_rows = upper_whole // repeat_by
        counts_here = level_counts(level_at, 0, coarse_rows)
        coarse_means = (
            group_sum(upper_all, repeat_by) / jnp.maximum(counts_here, 1.0)[:, None]
        ).astype(jnp.bfloat16)
        pair_wide = jnp.pad(coarse_means[:, columns:], ((NR, NR), (0, 0)))
        count_wide = level_counts(level_at, -NR, coarse_rows + 2 * NR)
        level_kept, totals, numer_part = level_forward(
            coarse_means[:, :columns], pair_wide, count_wide, level_at
        )
        upper_kept = [level_kept]
        upper_counts = [counts_here]
        upper_total = jnp.repeat(totals, repeat_by, axis=0)
        upper_numer = jnp.repeat(numer_part, repeat_by, axis=0)
        total_all = total_all + jnp.repeat(
            lax.dynamic_slice_in_dim(upper_total, slice_id * upper_rows, upper_rows, 0),
            2**upper_start,
            axis=0,
        )
        numer_all = numer_all + jnp.repeat(
            lax.dynamic_slice_in_dim(upper_numer, slice_id * upper_rows, upper_rows, 0),
            2**upper_start,
            axis=0,
        )
        attended = (
            (numer_all / total_all[:, :, None]).reshape(part_len, columns).astype(jnp.bfloat16)
        )
        merged_part = dot_plain(attended, full_merge)
        branch_attn = lax.psum(merged_part, "mp")
        after_attn = inputs + branch_attn
        mid_normed, pull_mid = jax.vjp(norm_rows, after_attn, gain_mid, shift_mid)
        mid_low = mid_normed.astype(jnp.bfloat16)
        after_share = take_share(after_attn)
        up_proj = dot_plain(mid_low, full_up)
        activated, pull_gelu = jax.vjp(gelu_exact, up_proj)
        act_low = activated.astype(jnp.bfloat16)
        ffn_share = (
            lax.psum_scatter(
                split_rows(dot_plain(act_low, full_down)).astype(jnp.bfloat16),
                "mp",
                scatter_dimension=1,
                tiled=True,
            )
            .astype(jnp.float32)
            .reshape(share_rows, model_width)
        )
        result_share = (valid_share[:, None] * (after_share + ffn_share)).astype(jnp.bfloat16)
        grad_low = grad_in.astype(jnp.bfloat16)
        act_grad = dot_outer(grad_low, full_down)
        down_acc = dot_inner(act_low, grad_low)
        hidden_grad = pull_gelu(act_grad)[0].astype(jnp.bfloat16)
        up_acc = dot_inner(mid_low, hidden_grad)
        mid_part = dot_outer(hidden_grad, full_up)
        mid_grad = lax.psum(mid_part, "mp")
        back_mid = pull_mid(mid_grad)[0]
        residual_grad = grad_in + back_mid
        branch_grad = residual_grad.astype(jnp.bfloat16)
        residual_share = take_share(residual_grad)
        gain_mid_part, shift_mid_part = norm_gain_parts(after_share, take_share(mid_grad))
        merge_acc = dot_inner(attended, branch_grad)
        attended_grad = dot_outer(branch_grad, full_merge).reshape(part_len, heads_here, HD)
        numer_grad = (attended_grad / total_all[:, :, None]).astype(jnp.bfloat16)
        total_grad = -jnp.sum(attended_grad * numer_all, axis=-1) / (total_all * total_all)
        numer_wide = numer_grad.astype(jnp.float32)
        rim_parts = []
        own_pair_grads = []
        query_coarse = []
        for level_at in range(local_top + 1):
            coarse_rows = part_len >> level_at
            if level_at == 0:
                numer_sum = numer_grad
                total_sum = total_grad
            else:
                numer_sum = group_sum(numer_wide, 2**level_at).astype(jnp.bfloat16)
                total_sum = group_sum(total_grad, 2**level_at)
            query_grad, pair_grad = level_backward(kept_levels[level_at], numer_sum, total_sum)
            rim_parts.append(
                jnp.concatenate([pair_grad[:NR], pair_grad[NR + coarse_rows :]], axis=0)
            )
            own_pair_grads.append(pair_grad[NR : NR + coarse_rows])
            query_coarse.append(query_grad)
        rim_grads = jnp.concatenate(rim_parts, axis=1)
        upper_numer_grad = group_sum(numer_wide, 2**upper_start).reshape(upper_rows, columns)
        upper_total_grad = group_sum(total_grad, 2**upper_start)
        rims_all, numer_sums, total_sums = (
            lax.all_gather(rim_grads.astype(jnp.bfloat16), "seq", axis=0, tiled=True).astype(
                rim_grads.dtype
            ),
            lax.all_gather(upper_numer_grad.astype(jnp.bfloat16), "seq", axis=0, tiled=True).astype(
                upper_numer_grad.dtype
            ),
            lax.all_gather(upper_total_grad.astype(jnp.bfloat16), "seq", axis=0, tiled=True).astype(
                upper_total_grad.dtype
            ),
        )
        from_left, from_right = neighbour_rims(rims_all)
        fine_grad = jnp.zeros((part_len, 3 * columns), jnp.float32)
        for level_at in range(local_top + 1):
            coarse_rows = part_len >> level_at
            col_range = slice(level_at * 2 * columns, (level_at + 1) * 2 * columns)
            pair_here = (
                own_pair_grads[level_at]
                + jnp.pad(from_left[:, col_range], ((0, coarse_rows - NR), (0, 0)))
                + jnp.pad(from_right[:, col_range], ((coarse_rows - NR, 0), (0, 0)))
            )
            coarse_grad = jnp.concatenate([query_coarse[level_at], pair_here], axis=1)
            if level_at == 0:
                fine_grad = coarse_grad
            else:
                coarse_grad = coarse_grad / jnp.maximum(own_counts[level_at], 1.0)[:, None]
                fine_grad = (
                    fine_grad + jnp.repeat(coarse_grad, 2**level_at, axis=0) * valid_rows[:, None]
                )
        upper_grad = jnp.zeros((upper_whole, 3 * columns), jnp.float32)
        for index_at, level_at in enumerate(range(upper_start, level_top + 1)):
            repeat_by = 2 ** (level_at - upper_start)
            coarse_rows = upper_whole // repeat_by
            numer_sum = (
                group_sum(numer_sums, repeat_by)
                .reshape(coarse_rows, heads_here, HD)
                .astype(jnp.bfloat16)
            )
            total_sum = group_sum(total_sums, repeat_by)
            query_grad, pair_grad = level_backward(upper_kept[index_at], numer_sum, total_sum)
            coarse_grad = (
                jnp.concatenate([query_grad, pair_grad[NR : NR + coarse_rows]], axis=1)
                / jnp.maximum(upper_counts[index_at], 1.0)[:, None]
            )
            upper_grad = jnp.repeat(coarse_grad, repeat_by, axis=0)
        own_upper = lax.dynamic_slice_in_dim(upper_grad, slice_id * upper_rows, upper_rows, 0)
        fine_grad = fine_grad + jnp.repeat(own_upper, 2**upper_start, axis=0) * valid_rows[:, None]
        rows_grad = fine_grad.astype(jnp.bfloat16)
        query_rows_grad = rows_grad[:, :columns]
        key_rows_grad = rows_grad[:, columns : 2 * columns]
        value_rows_grad = rows_grad[:, 2 * columns :]
        query_acc = dot_inner(normed_low, query_rows_grad)
        key_acc = dot_inner(normed_low, key_rows_grad)
        value_acc = dot_inner(normed_low, value_rows_grad)
        normed_part = (
            dot_outer(query_rows_grad, full_query)
            + dot_outer(key_rows_grad, full_key)
            + dot_outer(value_rows_grad, full_value)
        )
        normed_grad, gain_mid_sum, shift_mid_sum = (
            lax.psum(normed_part.astype(jnp.bfloat16), "mp").astype(jnp.float32),
            lax.psum(gain_mid_part.astype(jnp.bfloat16), "mp").astype(jnp.float32),
            lax.psum(shift_mid_part.astype(jnp.bfloat16), "mp").astype(jnp.float32),
        )
        back_pre, gain_pre_acc, shift_pre_acc = pull_pre(normed_grad)
        input_share = (residual_share + take_share(back_pre)).astype(jnp.bfloat16)
        grad_terms = (
            query_acc,
            key_acc,
            value_acc,
            merge_acc,
            up_acc,
            down_acc,
            gain_pre_acc,
            shift_pre_acc,
            gain_mid_sum,
            shift_mid_sum,
        )
        return (result_share, input_share, grad_terms)

    result_list = []
    grad_list = []
    running_sum = None
    for batch_index in range(batches):
        learnable_collection = (
            lax.all_gather(asking_projector, ("dp", "seq"), axis=0, tiled=True),
            lax.all_gather(lookup_projector, ("dp", "seq"), axis=0, tiled=True),
            lax.all_gather(content_projector, ("dp", "seq"), axis=0, tiled=True),
            lax.all_gather(attention_combiner, ("dp", "seq"), axis=1, tiled=True),
            lax.all_gather(feedforward_expand, ("dp", "seq"), axis=0, tiled=True),
            lax.all_gather(feedforward_contract, ("dp", "seq"), axis=1, tiled=True),
            lax.all_gather(attention_norm_scale, ("dp", "seq"), axis=0, tiled=True),
            lax.all_gather(attention_norm_bias, ("dp", "seq"), axis=0, tiled=True),
            lax.all_gather(feedforward_norm_scale, ("dp", "seq"), axis=0, tiled=True),
            lax.all_gather(feedforward_norm_bias, ("dp", "seq"), axis=0, tiled=True),
        )
        result_share, input_share, grad_terms = one_batch(batch_index, learnable_collection)
        result_list.append(result_share)
        grad_list.append(input_share)
        if running_sum is None:
            running_sum = grad_terms
        else:
            running_sum = tuple(
                (older_sum + newer_sum for older_sum, newer_sum in zip(running_sum, grad_terms))
            )
    owned_grads = (
        *sent_together(
            (
                running_sum[0].astype(jnp.bfloat16),
                running_sum[1].astype(jnp.bfloat16),
                running_sum[2].astype(jnp.bfloat16),
            ),
            ("dp", "seq"),
            0,
            1,
        ),
        summed_on_arrival(running_sum[3].astype(jnp.bfloat16), ("dp", "seq"), 1),
        summed_on_arrival(running_sum[4].astype(jnp.bfloat16), ("dp", "seq"), 0),
        summed_on_arrival(running_sum[5].astype(jnp.bfloat16), ("dp", "seq"), 1),
        summed_on_arrival(running_sum[6].astype(jnp.bfloat16), ("dp", "seq"), 0),
        summed_on_arrival(running_sum[7].astype(jnp.bfloat16), ("dp", "seq"), 0),
        summed_on_arrival(running_sum[8].astype(jnp.bfloat16), ("dp", "seq"), 0),
        summed_on_arrival(running_sum[9].astype(jnp.bfloat16), ("dp", "seq"), 0),
    )
    result_all = jnp.stack(result_list, axis=0).reshape(batches, groups, share_len, model_width)
    grad_all = jnp.stack(grad_list, axis=0).reshape(batches, groups, share_len, model_width)
    back_out, back_grad = (
        lax.all_to_all(result_all, "dp", split_axis=1, concat_axis=0, tiled=True),
        lax.all_to_all(grad_all, "dp", split_axis=1, concat_axis=0, tiled=True),
    )
    return (
        back_out,
        back_grad,
        owned_grads[0],
        owned_grads[1],
        owned_grads[2],
        owned_grads[3],
        owned_grads[4],
        owned_grads[5],
        owned_grads[6],
        owned_grads[7],
        owned_grads[8],
        owned_grads[9],
    )


MESH = pl.DeviceIdType.MESH
NEG = -1e30
BACK_GROUP = 5
FIRST = 32
THROUGH_Y = 32
TOP = 16
TOP_LAST = 32
GROUP = 5


def nn(a, b):
    return lax.dot_general(a, b, (((1,), (0,)), ((), ())), preferred_element_type=jnp.float32)


def nt(a, b):
    return lax.dot_general(a, b, (((1,), (1,)), ((), ())), preferred_element_type=jnp.float32)


def tn(a, b):
    return lax.dot_general(a, b, (((0,), (0,)), ((), ())), preferred_element_type=jnp.float32)


def halves(values):
    high = values.astype(jnp.bfloat16)
    return high, (values - high.astype(jnp.float32)).astype(jnp.bfloat16)


class Plan:
    def __init__(self, part, spots):
        self.part, self.spots = part, spots
        self.levels = (part // NR).bit_length()
        self.top = (part * spots // (2 * NR)).bit_length() - 1
        self.own = [part >> level for level in range(self.levels)]
        self.at, row = [], 0
        for rows in self.own:
            self.at.append(row)
            row += rows + 2 * NR
        self.upper = row
        self.rows = row + spots * NR
        self.pool_at, row = [None], 0
        for rows in self.own[1:]:
            self.pool_at.append(row)
            row += rows
        self.pool_upper = row
        self.pooled = row + NR
        self.slot, row = [], 0
        for level in range(self.levels, self.top + 1):
            self.slot.append((level, row, part >> level))
            row += part >> level
        assert row <= NR and spots * NR == 128 and self.pooled == part
        self.segments = [(self.at[lv], self.own[lv] + 2 * NR, lv) for lv in range(self.levels)]
        self.inner, self.outer = [], []
        level = 0
        while level < self.levels:
            start, total = self.at[level], self.own[level] + 2 * NR
            end = start + total
            if total < 96:
                self.outer.append((start, self.upper - start, self.upper - 128, None))
                break
            row = start
            while row < end:
                count = min(96, end - row)
                window = max(start, min(row - NR, end - 128))
                tile = (row, count, window, level if window + 128 <= end else None)
                inside = window >= start + NR and window + 128 <= end - NR
                (self.inner if inside else self.outer).append(tile)
                row += count
            level += 1
        self.outer.append((self.upper, 128, self.upper, None))
        self.tiles = self.inner + self.outer

    def own_pieces(self, tile):
        first, count = tile[:2]
        pieces = []
        for start, rows in zip(self.at, self.own):
            low, high = max(first, start + NR), min(first + count, start + NR + rows)
            if low < high:
                pieces.append((low, high - low))
        return pieces


def row_places(plan, rows, low, high, spot):
    level = jnp.full(rows.shape, -1, jnp.int32)
    place = jnp.zeros(rows.shape, jnp.int32)
    for start, count, lv in plan.segments:
        if start < high and start + count > low:
            inside = (rows >= start) & (rows < start + count)
            level = jnp.where(inside, lv, level)
            place = jnp.where(inside, spot * plan.own[lv] - NR + rows - start, place)
    if high > plan.upper:
        owner = lax.shift_right_arithmetic(rows - plan.upper, 4)
        within = (rows - plan.upper) & (NR - 1)
        for lv, first, count in plan.slot:
            inside = (rows >= plan.upper) & (within >= first) & (within < first + count)
            level = jnp.where(inside, lv, level)
            place = jnp.where(inside, owner * count + within - first, place)
    return level, place


def log_counts(plan, tile, spot, length):
    first, count, window, level = tile
    row_at = first + lax.broadcasted_iota(jnp.int32, (count, 128), 0)
    key_at = window + lax.broadcasted_iota(jnp.int32, (8, 128), 1)
    row_level, row_place = row_places(plan, row_at, first, first + count, spot)
    key_level, key_place = row_places(plan, key_at, window, window + 128, spot)
    span = lax.shift_left(jnp.ones_like(key_level), jnp.maximum(key_level, 0))
    counts = jnp.clip(length - span * key_place, 0, span)
    usable = (counts > 0) & (key_place >= 0) & (key_level >= 0)
    logs = jnp.where(usable, jnp.log(jnp.maximum(counts, 1).astype(jnp.float32)), NEG)
    coarse = lambda level_at, place_at, by: level_at * 65536 + lax.shift_right_arithmetic(place_at, by)
    key_block = coarse(key_level, key_place, 4)[:1]
    key_half = coarse(key_level, key_place, 3)[:1]
    allowed = jnp.abs(coarse(row_level, row_place, 4) - key_block) <= 1
    if level != 0:
        apart = jnp.abs(coarse(row_level, row_place, 3) - key_half) >= 2
        allowed = allowed & (apart if level is not None else apart | (row_level == 0)) & (row_level >= 0)
    return jnp.where(allowed, logs[:1], NEG)


def pool_bounds(plan, shape, dim):
    row = lax.broadcasted_iota(jnp.int32, shape, dim)
    low = jnp.full(shape, -1, jnp.int32)
    size = jnp.zeros(shape, jnp.int32)
    level = jnp.zeros(shape, jnp.int32)
    parts = [(plan.pool_at[lv], plan.own[lv], lv) for lv in range(1, plan.levels)]
    parts += [(plan.pool_upper + first, count, lv) for lv, first, count in plan.slot]
    for start, count, lv in parts:
        inside = (row >= start) & (row < start + count)
        low = jnp.where(inside, (row - start) << lv, low)
        size = jnp.where(inside, 1 << lv, size)
    return low, size


def spread_columns(rows, place, count):
    width = rows.shape[1]
    source = lax.broadcasted_iota(jnp.int32, (width, width * count), 0)
    target = lax.broadcasted_iota(jnp.int32, (width, width * count), 1)
    return nn(rows, jnp.where(target == source + place * width, 1.0, 0.0).astype(rows.dtype))


def flip_bits(value, k):
    low, high, k_low, k_high = value % 2, value // 2, k % 2, k // 2
    return (high + k_high - 2 * high * k_high) * 2 + low + k_low - 2 * low * k_low


class Marks:
    def __init__(self):
        self.used = 0

    def take(self, count):
        self.used += count
        return self.used - count


def whole_layer(plan, dims, net_count, *refs):
    (extents, w_query, w_key, w_value, w_merge, w_expand, w_contract, norm_0, norm_1, norm_2, norm_3, tokens_in, cotangent_in,
     out_rows, out_grads, weight_grads, norm_grads,
     weights, norms, tokens, cotangent, ext, logs, pool, unpool, inverse, work,
     attended, ratio, recip, normed, scaled, rstd, grad_ext, total_ext, residual, acc, acc2, totals, result, row_grads,
     grads, got1, got2, got3, got4, norm_got,
     load_sem, send_sem, recv_sem) = refs
    part, width, pair, hidden = dims
    f32, bf16 = jnp.float32, jnp.bfloat16
    models = weights.shape[0]
    strip, columns = weights.shape[4:]
    ax, sq, az = lax.axis_index("dp"), lax.axis_index("seq"), lax.axis_index("mp")
    ay, ac = sq // 2, sq % 2
    spot = sq * 2 + ax
    spots = plan.spots
    length = extents[az]
    qkv = 3 * pair

    def device(x, y, c, z):
        return (x, y * 2 + c, z)

    def at_spot(place):
        return (place % 2, place // 2, az)

    def plane(k):
        return flip_bits(az, k)

    x_peer, y_peer, c_peer = device(1 - ax, ay, ac, az), device(ax, 1 - ay, ac, az), device(ax, ay, 1 - ac, az)
    xy_peer = device(1 - ax, 1 - ay, ac, az)
    z_peer = lambda k: device(ax, ay, ac, plane(k))

    barrier = pltpu.get_barrier_semaphore()
    for step in range(1, spots):
        pl.semaphore_signal(barrier, inc=1, device_id=at_spot((spot + step) % spots), device_id_type=MESH)
    for k in range(1, models):
        pl.semaphore_signal(barrier, inc=1, device_id=z_peer(k), device_id_type=MESH)
    load_tokens = pltpu.make_async_copy(tokens_in.at[az, 0], tokens, load_sem.at[0])
    load_cotangent = pltpu.make_async_copy(cotangent_in.at[az, 0], cotangent, load_sem.at[1])
    load_tokens.start()
    load_cotangent.start()
    own = (az, ax, ay, ac)
    weights[own + (slice(None), slice(0, pair))] = w_query[...] * jnp.asarray(HD ** -0.5, bf16)
    weights[own + (slice(None), slice(pair, 2 * pair))] = w_key[...]
    weights[own + (slice(None), slice(2 * pair, qkv))] = w_value[...]
    weights[own + (slice(None), slice(qkv, qkv + pair))] = w_merge[...]
    weights[own + (slice(None), slice(4 * pair, 4 * pair + hidden))] = w_expand[...]
    weights[own + (slice(None), slice(4 * pair + hidden, columns))] = w_contract[...]
    owner = ax * 4 + sq
    norms[spot] = jnp.concatenate(
        [spread_columns(row[...], owner, width // strip) for row in (norm_0, norm_1, norm_2, norm_3)]
        + [jnp.zeros((4, width), f32)], axis=0)
    pl.semaphore_wait(barrier, spots - 1 + models - 1)

    marks = Marks()

    def copy(i, src, dst, to):
        return pltpu.make_async_remote_copy(
            src_ref=src, dst_ref=dst, send_sem=send_sem.at[i], recv_sem=recv_sem.at[i],
            device_id=to, device_id_type=MESH)

    class Group:
        def __init__(self, i, pairs, whole):
            self.i, self.pairs, self.whole = i, pairs, whole

        def start(self):
            for src, dst, to in self.pairs:
                copy(self.i, src, dst, to).start()
            return self

        def arrive(self):
            copy(self.i, self.whole, self.whole, self.pairs[0][2]).wait_recv()

        def leave(self):
            copy(self.i, self.whole, self.whole, self.pairs[0][2]).wait_send()

    sent = []
    kept = []

    def send(pairs, whole):
        group = Group(marks.take(1), pairs, whole).start()
        sent.append(group)
        return group

    class Gather:
        def __init__(self, col, count, through_y):
            self.cols, self.rows = pl.ds(col, count), through_y
            self.flight = {}
            self.first = marks.take(models)

        def block(self, k, x, y, rows=slice(None)):
            return weights.at[plane(k), x, y, ac, rows, self.cols]

        def to_planes(self):
            here = self.block(0, ax, ay)
            for k in range(1, models):
                self.flight["z", k] = send([(here, here, z_peer(k))], here)

        def to_sides(self, k):
            if k:
                self.flight["z", k].arrive()
            here = self.block(k, ax, ay)
            if self.rows == 0:
                self.flight["corner", k] = send([(here, here, x_peer), (here, here, y_peer), (here, here, xy_peer)],
                                                weights.at[pl.ds(0, 3), ax, ay, ac, :, self.cols])
                return
            self.flight["side", k] = send([(here, here, x_peer), (here, here, y_peer)],
                                          weights.at[plane(k), :, ay, ac, :, self.cols])

        def to_corner(self, k):
            if self.rows == 0:
                return
            self.flight["side", k].arrive()
            pairs = []
            if self.rows > 0:
                first = self.block(k, 1 - ax, ay, pl.ds(0, self.rows))
                pairs.append((first, first, y_peer))
            if self.rows < strip:
                rest = self.block(k, ax, 1 - ay, pl.ds(self.rows, strip - self.rows))
                pairs.append((rest, rest, x_peer))
            self.flight["corner", k] = send(pairs, self.block(k, ax, ay))

        def to_core(self, k):
            self.flight["corner", k].arrive()
            sent.append(self.last(k).start())

        def last(self, k):
            here = weights.at[plane(k), :, :, ac, :, self.cols]
            return Group(self.first + k, [(here, here, c_peer)], here)

        def here(self, k):
            self.last(k).arrive()

    first_gather = Gather(0, qkv, FIRST)
    merge_gather = Gather(qkv, pair, 48)
    feed_gather = Gather(4 * pair, 2 * hidden, THROUGH_Y)

    first_gather.to_planes()
    first_gather.to_sides(0)
    norm_copies = send([(norms.at[spot], norms.at[spot], at_spot((spot + step) % spots)) for step in range(1, spots)],
                       norms.at[pl.ds(0, spots - 1)])
    merge_gather.to_planes()
    feed_gather.to_planes()
    merge_gather.to_sides(0)
    feed_gather.to_sides(0)

    low, size = pool_bounds(plan, (part, 128), 0)
    for block in range(part // 128):
        token_at = block * 128 + lax.broadcasted_iota(jnp.int32, (part, 128), 1)
        member = (token_at >= low) & (token_at < low + size) & (token_at + spot * part < length)
        pool[:, block * 128:(block + 1) * 128] = jnp.where(member, 1.0, 0.0).astype(bf16)
    counts = jnp.clip(length - spot * part - low, 0, size)
    inverse[...] = 1.0 / jnp.maximum(counts, 1).astype(f32)
    low, size = pool_bounds(plan, (8, part), 1)
    token_at = lax.broadcasted_iota(jnp.int32, (part, part), 0)
    member = (token_at >= low[:1]) & (token_at < (low + size)[:1])
    unpool[...] = jnp.where(member, 1.0, 0.0).astype(bf16)
    first_gather.to_corner(0)
    first_gather.to_sides(1)
    load_tokens.wait()

    def statistics(values):
        center = values - jnp.mean(values, axis=-1, keepdims=True)
        spread = jnp.mean(center * center, axis=-1, keepdims=True)
        scale = lax.rsqrt(spread + 1e-05)
        return center * scale, scale

    xhat, scale = statistics(tokens[...].astype(f32))
    scaled[...] = xhat
    rstd[...] = jnp.broadcast_to(scale, (part, 128))
    first_gather.to_sides(2)
    first_gather.to_sides(3)
    first_gather.to_core(0)
    first_gather.to_corner(1)
    for i, tile in enumerate(plan.tiles):
        logs[i, 0:tile[1]] = log_counts(plan, tile, spot, length)
    first_gather.to_corner(2)
    first_gather.to_corner(3)
    feed_gather.to_corner(0)
    first_gather.to_core(1)
    norm_copies.arrive()
    gains = norms[0]
    for i in range(1, spots):
        gains = gains + norms[i]
    pre_gain, pre_shift, mid_gain, mid_shift = (gains[i:i + 1] for i in range(4))
    normed[...] = (scaled[...] * pre_gain + pre_shift).astype(bf16)

    is_first, is_last = spot == 0, spot == spots - 1

    @pl.when(is_first)
    def _():
        for lv in range(plan.levels):
            rows = slice(plan.at[lv], plan.at[lv] + NR)
            ext[:, rows, :] = jnp.zeros((models, NR, qkv), bf16)
            grad_ext[:, rows, :] = jnp.zeros((models, NR, pair), bf16)
            total_ext[rows, :] = jnp.zeros((NR, 128), bf16)

    @pl.when(is_last)
    def _():
        for lv in range(plan.levels):
            end = plan.at[lv] + NR + plan.own[lv]
            rows = slice(end, end + NR)
            ext[:, rows, :] = jnp.zeros((models, NR, qkv), bf16)
            grad_ext[:, rows, :] = jnp.zeros((models, NR, pair), bf16)
            total_ext[rows, :] = jnp.zeros((NR, 128), bf16)

    def weight_cols(m, col, count):
        return weights[m, :, :, :, :, col:col + count].reshape(width, count)

    slot_row = pl.multiple_of(spot * NR, NR)
    own_slot_rows = pl.ds(pl.multiple_of(plan.upper + slot_row, NR), NR)
    class Rims:
        def __init__(self, view, i):
            self.view, self.i, self.to = view, i, at_spot((spot + 1) % spots)

        def start(self):
            view, i = self.view, self.i
            right, left = at_spot((spot + 1) % spots), at_spot((spot + spots - 1) % spots)

            @pl.when(jnp.logical_not(is_last))
            def _():
                for start, rows in zip(plan.at, plan.own):
                    copy(i, view(pl.ds(start + rows, NR)), view(pl.ds(start, NR)), right).start()

            @pl.when(jnp.logical_not(is_first))
            def _():
                for start, rows in zip(plan.at, plan.own):
                    copy(i, view(pl.ds(start + NR, NR)), view(pl.ds(start + NR + rows, NR)), left).start()

            block = view(own_slot_rows)
            for step in range(1, spots):
                copy(i, block, block, at_spot((spot + step) % spots)).start()

        def whole(self, sides):
            rows = self.view(pl.ds(0, (sides * plan.levels + spots - 1) * NR))
            return copy(self.i, rows, rows, self.to)

        def wait(self):
            at_end = is_first | is_last

            @pl.when(at_end)
            def _():
                self.whole(1).wait_recv()

            @pl.when(jnp.logical_not(at_end))
            def _():
                self.whole(2).wait_recv()

        def done(self):
            at_end = is_first | is_last

            @pl.when(at_end)
            def _():
                self.whole(1).wait_send()

            @pl.when(jnp.logical_not(at_end))
            def _():
                self.whole(2).wait_send()

    pair_base = marks.take(models)
    query_base = marks.take(1)
    grad_base = marks.take(models)
    total_base = marks.take(1)
    pair_rims = lambda k: Rims(lambda rows: ext.at[plane(k), rows, pl.ds(pair, 2 * pair)], pair_base + k)
    query_rims = lambda: Rims(lambda rows: ext.at[:, rows, pl.ds(0, pair)], query_base)
    grad_rims = lambda k: Rims(lambda rows: grad_ext.at[plane(k), rows, :], grad_base + k)
    total_rims = lambda: Rims(lambda rows: total_ext.at[rows, :], total_base)

    for k in range(models):
        if k >= 1 and k + 1 < models:
            first_gather.to_core(k + 1)
        first_gather.here(k)
        m = plane(k)
        rows = nn(normed[...], weight_cols(m, 0, qkv)).astype(bf16)
        ext[m, NR:NR + part, :] = rows
        means = (nn(pool[...], rows) * jnp.concatenate([inverse[...]] * 3, axis=1)).astype(bf16)
        for lv in range(1, plan.levels):
            ext[m, plan.at[lv] + NR:plan.at[lv] + NR + plan.own[lv], :] = means[plan.pool_at[lv]:plan.pool_at[lv] + plan.own[lv]]
        ext[m, own_slot_rows, :] = means[plan.pool_upper:plan.pool_upper + NR]
        pair_rims(k).start()

    lane = lax.broadcasted_iota(jnp.int32, (1, pair), 1)
    left_head = lane < HD

    def both_heads(rows):
        zero = jnp.zeros_like(rows)
        return jnp.concatenate([jnp.where(left_head, rows, zero), jnp.where(left_head, zero, rows)], axis=0)

    def joined(rows):
        half = rows.shape[0] // 2
        return jnp.where(left_head, rows[:half], rows[half:])

    ones = jnp.ones((128, 128), bf16)

    def stacked(parts):
        return parts[0] if len(parts) == 1 else jnp.concatenate(parts, axis=0)

    def tile_weights(m, rows, mask, window):
        queries = both_heads(rows)
        keys = ext[m, window:window + 128, pair:2 * pair]
        values = jnp.concatenate([ext[m, window:window + 128, 2 * pair:3 * pair], ones], axis=1)
        weight = jnp.exp(nt(queries, keys) + jnp.concatenate([mask, mask], axis=0))
        return queries, keys, values, weight

    def attend_tiles(m, tiles):
        pieces, weights_values = [], []
        for tile in tiles:
            first, _, window, _ = tile
            index = plan.tiles.index(tile)
            if first == plan.upper:
                pieces.append([(first, NR)])
                rows, mask = ext[m, own_slot_rows, 0:pair], logs[index, pl.ds(slot_row, NR)]
            else:
                pieces.append(plan.own_pieces(tile))
                rows = stacked([ext[m, low:low + count, 0:pair] for low, count in pieces[-1]])
                mask = stacked([logs[index, low - first:low - first + count] for low, count in pieces[-1]])
            _, _, values, weight = tile_weights(m, rows, mask, window)
            weights_values.append((weight.astype(bf16), values))
        both = [nn(weight, values) for weight, values in weights_values]
        sides = [(joined(product[:, :128]), joined(product[:, 128:])) for product in both]
        for rows, (numer, tot) in zip(pieces, sides):
            at = 0
            for low, count in rows:
                work[m, low:low + count, 0:pair] = numer[at:at + count]
                work[m, low:low + count, pair:2 * pair] = tot[at:at + count]
                at += count

    def attend(tiles, first_k, last_k, wait_rims):
        def body(k, carry):
            m = plane(k)
            if wait_rims:
                pair_rims(k).wait()
            for at in range(0, len(tiles), GROUP):
                attend_tiles(m, tiles[at:at + GROUP])
            return carry

        lax.fori_loop(first_k, last_k, body, 0)

    attend(plan.inner, 0, models, False)
    for k in range(1, models):
        merge_gather.to_sides(k)
    attend(plan.outer, 0, 2, True)
    feed_gather.to_sides(1)
    attend(plan.outer, 2, models, True)
    for k in range(models):
        merge_gather.to_corner(k)
    feed_gather.to_sides(2)

    def coarse_rows(m, cols, slot_at):
        rows = [work[m, plan.at[lv] + NR:plan.at[lv] + NR + plan.own[lv], 0:cols] for lv in range(1, plan.levels)]
        return jnp.concatenate(rows + [work[m, slot_at, 0:cols]], axis=0)

    def spread_out(rows):
        high, rest = halves(rows)
        return nn(unpool[...], high) + nn(unpool[...], rest)

    def normalise(m, carry):
        both = spread_out(coarse_rows(m, 2 * pair, slice(plan.upper, plan.upper + NR)))
        both = both + work[m, NR:NR + part, 0:2 * pair]
        inv_total = 1.0 / both[:, pair:]
        quotient = both[:, :pair] * inv_total
        ratio[m] = quotient
        recip[m] = inv_total
        attended[m] = quotient.astype(bf16)
        return carry

    lax.fori_loop(0, models, normalise, 0)
    feed_gather.to_core(0)
    for k in range(models):
        merge_gather.to_core(k)
    feed_gather.to_corner(1)
    feed_gather.to_sides(3)

    residual[...] = tokens[...].astype(f32)
    for k in range(models):
        merge_gather.here(k)

    def merge(m, carry):
        residual[...] += nt(attended[m], weight_cols(m, qkv, pair))
        return carry

    lax.fori_loop(0, models, merge, 0)
    after = residual[...]
    mid_hat, mid_scale = statistics(after)
    mid = (mid_hat * mid_gain + mid_shift).astype(bf16)
    mid_t = mid.T
    load_cotangent.wait()
    row_at = lax.broadcasted_iota(jnp.int32, (part, 1), 0) + spot * part
    valid = row_at < length
    out_grad = jnp.where(valid, cotangent[...], jnp.zeros((), bf16))
    out_grad_t = out_grad.T
    acc[...] = jnp.zeros(acc.shape, f32)
    acc2[...] = jnp.zeros(acc.shape, f32)
    block_shape = grads.shape[1:5] + (hidden,)

    feed_gather.to_core(1)
    feed_gather.to_corner(2)

    class Reduce:
        def __init__(self, col, count, top):
            self.cols = pl.ds(col, count)
            self.top, self.bottom = pl.ds(0, top), pl.ds(top, strip - top)
            self.first = marks.take(4 * models)

        def core(self, k):
            m = plane(k)
            landing = got1.at[m, :, :, :, self.cols]
            return Group(self.first + k, [(grads.at[m, :, :, 1 - ac, :, self.cols], landing, c_peer)], landing)

        def side(self, k):
            m = plane(k)
            top, bottom = self.top, self.bottom
            return Group(self.first + models + k,
                         [(got1.at[m, 1 - ax, :, top, self.cols], got2.at[m, :, top, self.cols], x_peer),
                          (got1.at[m, :, 1 - ay, bottom, self.cols], got2.at[m, :, bottom, self.cols], y_peer)],
                         got2.at[m, :, :, self.cols])

        def corner(self, k):
            m = plane(k)
            top, bottom = self.top, self.bottom
            return Group(self.first + 2 * models + k,
                         [(got2.at[m, 1 - ay, top, self.cols], got3.at[m, top, self.cols], y_peer),
                          (got2.at[m, 1 - ax, bottom, self.cols], got3.at[m, bottom, self.cols], x_peer)],
                         got3.at[m, :, self.cols])

        def home(self, k):
            block = got3.at[plane(k), :, self.cols]
            return Group(self.first + 3 * models + k, [(block, got4.at[k, :, self.cols], z_peer(1 + 2 * (k // 3)))], block)

        def start(self, k):
            self.core(k).start()

        def to_sides(self, k):
            m = plane(k)
            self.core(k).arrive()
            got1[m, :, :, :, self.cols] = got1[m, :, :, :, self.cols] + grads[m, :, :, ac, :, self.cols]
            self.side(k).start()

        def to_corner(self, k):
            m = plane(k)
            self.side(k).arrive()
            top, bottom = self.top, self.bottom
            got2[m, :, top, self.cols] = got2[m, :, top, self.cols] + got1[m, ax, :, top, self.cols]
            got2[m, :, bottom, self.cols] = got2[m, :, bottom, self.cols] + got1[m, :, ay, bottom, self.cols]
            self.corner(k).start()

        def to_planes(self, k):
            m = plane(k)
            self.corner(k).arrive()
            top, bottom = self.top, self.bottom
            got3[m, top, self.cols] = got3[m, top, self.cols] + got2[m, ay, top, self.cols]
            got3[m, bottom, self.cols] = got3[m, bottom, self.cols] + got2[m, ax, bottom, self.cols]

            @pl.when(k == 3)
            def _():
                self.home(2).arrive()
                got3[m, :, self.cols] = got3[m, :, self.cols] + got4[2, :, self.cols]

            @pl.when(k > 0)
            def _():
                self.home(k).start()

        def end(self):
            total = got3[az, :, self.cols].astype(f32)
            for k in (1, 3):
                self.home(k).arrive()
                total = total + got4[k, :, self.cols].astype(f32)
            weight_grads[:, self.cols] = total

        def done(self, k):
            for group in (self.core(k), self.side(k), self.corner(k)):
                group.leave()

            @pl.when(k > 0)
            def _():
                self.home(k).leave()

    feed_reduce = Reduce(4 * pair, 2 * hidden, TOP)
    attention_reduce = Reduce(0, 4 * pair, TOP_LAST)

    def feed(k, carry):
        m = plane(k)
        feed_gather.here(k)
        expand, contract_t = weight_cols(m, 4 * pair, hidden), weight_cols(m, 4 * pair + hidden, hidden)
        up = nn(mid, expand)
        act_grad = nn(out_grad, contract_t)
        phi = 0.5 + 0.5 * lax.erf(up * (0.5 ** 0.5))
        act = (up * phi).astype(bf16)
        slope = phi + up * (jnp.exp(-0.5 * up * up) * 0.3989422804014327)
        hidden_grad = (act_grad * slope).astype(bf16)
        grads[m, :, :, :, :, 4 * pair:4 * pair + hidden] = nn(mid_t, hidden_grad).astype(bf16).reshape(block_shape)
        grads[m, :, :, :, :, 4 * pair + hidden:columns] = nn(out_grad_t, act).astype(bf16).reshape(block_shape)
        feed_reduce.start(k)
        acc[...] += nt(act, contract_t)
        acc2[...] += nt(hidden_grad, expand)
        return carry

    lax.fori_loop(0, 1, feed, 0)
    feed_gather.to_core(2)
    feed_gather.to_corner(3)
    query_rims().start()
    lax.fori_loop(1, 2, feed, 0)
    feed_gather.to_core(3)
    feed_reduce.to_sides(0)
    lax.fori_loop(2, 3, feed, 0)
    feed_reduce.to_sides(1)
    lax.fori_loop(3, 4, feed, 0)
    result[...] = jnp.where(valid, after + acc[...], 0.0).astype(bf16)
    mid_grad = acc2[...]

    def rows_home(source, target, i):
        share = part // models
        mine = pltpu.make_async_copy(
            source.at[pl.ds(pl.multiple_of(az * share, share), share), :], target.at[az], load_sem.at[i])
        mine.start()
        kept.append(mine)
        return send([(source.at[pl.ds(pl.multiple_of(plane(k) * share, share), share), :], target.at[az], z_peer(k))
                     for k in range(1, models)], target.at[pl.ds(0, models - 1)])

    def norm_back(grad, hat, scale_row, gain):
        scaled_grad = grad * gain
        mean_grad = jnp.mean(scaled_grad, axis=-1, keepdims=True)
        mean_along = jnp.mean(scaled_grad * hat, axis=-1, keepdims=True)
        return scale_row * (scaled_grad - mean_grad - hat * mean_along)

    through = out_grad.astype(f32) + norm_back(mid_grad, mid_hat, mid_scale, mid_gain)
    residual[...] = through
    branch = through.astype(bf16)
    branch_t = branch.T
    norm_sums = [jnp.sum(mid_grad * mid_hat, axis=0, keepdims=True), jnp.sum(mid_grad, axis=0, keepdims=True)]

    merge_shape = grads.shape[1:5] + (pair,)
    select_row = lax.broadcasted_iota(jnp.int32, (pair, 128), 0) // HD
    select_col = lax.broadcasted_iota(jnp.int32, (pair, 128), 1) // 2
    totals[...] = jnp.zeros(totals.shape, f32)

    def unmerge(step, carry):
        k = models - 1 - step
        m = plane(k)
        attended_grad = nn(branch, weight_cols(m, qkv, pair)) * recip[m]
        fine = attended_grad.astype(bf16)
        grad_ext[m, NR:NR + part, :] = fine
        sums = nn(pool[...], fine).astype(bf16)
        for lv in range(1, plan.levels):
            grad_ext[m, plan.at[lv] + NR:plan.at[lv] + NR + plan.own[lv], :] = sums[plan.pool_at[lv]:plan.pool_at[lv] + plan.own[lv]]
        grad_ext[m, own_slot_rows, :] = sums[plan.pool_upper:plan.pool_upper + NR]
        grad_rims(k).start()
        high, rest = halves(attended_grad * ratio[m])
        chosen = jnp.where(select_row + 2 * m == select_col, -1.0, 0.0).astype(bf16)
        totals[...] += nn(high, chosen) + nn(rest, chosen)
        grads[m, :, :, :, :, qkv:qkv + pair] = nn(branch_t, attended[m]).astype(bf16).reshape(merge_shape)
        return carry

    lax.fori_loop(0, models, unmerge, 0)
    even = lax.broadcasted_iota(jnp.int32, (1, 128), 1) % 2 == 0
    high, rest = halves(totals[...])
    total_ext[NR:NR + part, :] = jnp.where(even, high, rest)
    pooled_high, pooled_rest = halves(nn(pool[...], high) + nn(pool[...], rest))
    sums = jnp.where(even, pooled_high, pooled_rest)
    for lv in range(1, plan.levels):
        total_ext[plan.at[lv] + NR:plan.at[lv] + NR + plan.own[lv], :] = sums[plan.pool_at[lv]:plan.pool_at[lv] + plan.own[lv]]
    total_ext[own_slot_rows, :] = sums[plan.pool_upper:plan.pool_upper + NR]
    total_rims().start()
    rows_out = rows_home(result, out_rows, 2)

    feed_reduce.to_corner(0)
    feed_reduce.to_sides(2)
    feed_reduce.to_sides(3)

    head_of_lane = lax.broadcasted_iota(jnp.int32, (1, 128), 1) // 2

    def clear(m, carry):
        work[m] = jnp.zeros(work.shape[1:], f32)
        return carry

    lax.fori_loop(0, models, clear, 0)
    normed_t = normed[...].T
    acc[...] = jnp.zeros(acc.shape, f32)
    qkv_shape = grads.shape[1:5] + (qkv,)
    query_scale = jnp.where(lax.broadcasted_iota(jnp.int32, (1, qkv), 1) < pair, HD ** -0.5, 1.0)
    def back_tiles(m, tiles):
        rows_at = [slice(first, first + count) for first, count, _, _ in tiles]
        key_rows = [slice(window, window + 128) for _, _, window, _ in tiles]
        masks = [logs[plan.tiles.index(tile), 0:tile[1]] for tile in tiles]
        made = [tile_weights(m, ext[m, rows, 0:pair], mask, tile[2]) for tile, rows, mask in zip(tiles, rows_at, masks)]
        numers = [both_heads(grad_ext[m, rows, :]) for rows in rows_at]
        slopes = []
        for rows, numer, (_, _, values, _) in zip(rows_at, numers, made):
            tot = total_ext[rows, :]
            zero = jnp.zeros_like(tot)
            tots = jnp.concatenate([jnp.where(head_of_lane == 2 * m, tot, zero),
                                    jnp.where(head_of_lane == 2 * m + 1, tot, zero)], axis=0)
            slopes.append(nt(jnp.concatenate([numer, tots], axis=1), values))
        score_grads = [(weight * by).astype(bf16) for (_, _, _, weight), by in zip(made, slopes)]
        query_sides = [joined(nn(grad, keys)) for grad, (_, keys, _, _) in zip(score_grads, made)]
        key_sides = [tn(grad, queries) for grad, (queries, _, _, _) in zip(score_grads, made)]
        value_sides = [tn(weight.astype(bf16), numer) for (_, _, _, weight), numer in zip(made, numers)]
        for rows, side in zip(rows_at, query_sides):
            work[m, rows, 0:pair] = side
        for rows, key_side, value_side in zip(key_rows, key_sides, value_sides):
            work[m, rows, pair:2 * pair] += key_side
            work[m, rows, 2 * pair:3 * pair] += value_side

    def back_inner(m, carry):
        back_tiles(m, plan.inner)
        return carry

    lax.fori_loop(0, models, back_inner, 0)
    feed_reduce.to_corner(1)
    total_rims().wait()
    query_rims().wait()

    def turn(step):
        late = step // 2
        return (2 + step) * (1 - late) + (3 - step) * late

    def back(step, carry):
        k = turn(step)
        m = plane(k)
        grad_rims(k).wait()
        for at in range(0, len(plan.outer), BACK_GROUP):
            back_tiles(m, plan.outer[at:at + BACK_GROUP])
        coarse = coarse_rows(m, qkv, own_slot_rows)
        spread = spread_out(coarse * jnp.concatenate([inverse[...]] * 3, axis=1))
        rows = (work[m, NR:NR + part, :] + jnp.where(valid, spread, 0.0)).astype(bf16)
        grads[m, :, :, :, :, 0:qkv] = (nn(normed_t, rows) * query_scale).astype(bf16).reshape(qkv_shape)
        attention_reduce.start(k)
        acc[...] += nt(rows, weight_cols(m, 0, qkv))

        @pl.when(step == 0)
        def _():
            feed_reduce.to_corner(2)
            feed_reduce.to_planes(0)

        @pl.when(step == 1)
        def _():
            feed_reduce.to_corner(3)
            feed_reduce.to_planes(1)

        @pl.when(step == 2)
        def _():
            feed_reduce.to_planes(2)

        @pl.when(step == 3)
        def _():
            feed_reduce.to_planes(3)

        @pl.when(step >= 1)
        def _():
            attention_reduce.to_sides(turn(step - 1))

        @pl.when(step >= 2)
        def _():
            attention_reduce.to_corner(turn(step - 2))

        @pl.when(step >= 3)
        def _():
            attention_reduce.to_planes(turn(step - 3))

        return carry

    lax.fori_loop(0, models, back, 0)
    normed_grad = acc[...]
    hat = scaled[...]
    norm_sums = [jnp.sum(normed_grad * hat, axis=0, keepdims=True), jnp.sum(normed_grad, axis=0, keepdims=True)] + norm_sums
    norm_got[0] = jnp.concatenate(norm_sums + [jnp.zeros((4, width), f32)], axis=0)
    small = send([(norm_got.at[0], norm_got.at[k], z_peer(k)) for k in range(1, models)], norm_got.at[pl.ds(0, models - 1)])
    row_grads[...] = (residual[...] + norm_back(normed_grad, hat, rstd[:, 0:1], pre_gain)).astype(bf16)
    grads_out = rows_home(row_grads, out_grads, 3)
    attention_reduce.to_sides(0)
    attention_reduce.to_corner(1)
    attention_reduce.to_planes(3)
    small.arrive()
    norm_total = norm_got[0]
    for k in range(1, models):
        norm_total = norm_total + norm_got[k]
    norm_got[models] = norm_total
    small = send([(norm_got.at[models], norm_got.at[models + step], at_spot((spot + step) % spots)) for step in range(1, spots)],
                 norm_got.at[pl.ds(0, spots - 1)])
    attention_reduce.to_corner(0)
    attention_reduce.to_planes(1)
    feed_reduce.end()
    attention_reduce.to_planes(0)
    small.arrive()
    for step in range(1, spots):
        norm_total = norm_total + norm_got[models + step]
    norm_grads[...] = norm_total
    attention_reduce.end()
    rows_out.arrive()
    grads_out.arrive()
    assert marks.used <= net_count, marks.used
    for group in sent:
        group.leave()
    for c in kept:
        c.wait()

    def drain(k, carry):
        pair_rims(k).done()
        grad_rims(k).done()
        feed_reduce.done(k)
        attention_reduce.done(k)
        return carry

    lax.fori_loop(0, models, drain, 0)
    query_rims().done()
    total_rims().done()


def finish_outputs(dims, rows_ref, grads_ref, weights_ref, norms_ref,
                   out_rows, out_grads, query, key, value, merge, up, down, *rest):
    norm_outs, sem = rest[:4], rest[4]
    part, width, pair, hidden = dims
    copies = [pltpu.make_async_copy(rows_ref, out_rows.at[:, 0], sem.at[0]),
              pltpu.make_async_copy(grads_ref, out_grads.at[:, 0], sem.at[1])]
    for c in copies:
        c.start()
    strip = query.shape[0]
    query[...] = weights_ref[:, 0:pair]
    key[...] = weights_ref[:, pair:2 * pair]
    value[...] = weights_ref[:, 2 * pair:3 * pair]
    up[...] = weights_ref[:, 4 * pair:4 * pair + hidden]
    merge[...] = weights_ref[:, 3 * pair:4 * pair]
    down[...] = weights_ref[:, 4 * pair + hidden:4 * pair + 2 * hidden]
    owner = lax.axis_index("dp") * 4 + lax.axis_index("seq")
    strips = width // strip
    mine = norms_ref[:, 0:strip] * (owner == 0).astype(jnp.float32)
    for i in range(1, strips):
        mine = jnp.where(owner == i, norms_ref[:, i * strip:(i + 1) * strip], mine)
    for i, out in enumerate(norm_outs):
        out[...] = mine[i].reshape(out.shape)
    for c in copies:
        c.wait()


def fast_body(plan, incoming_embeddings, output_sensitivity, sequence_extents, asking_projector, lookup_projector,
              content_projector, attention_combiner, feedforward_expand, feedforward_contract,
              attention_norm_scale, attention_norm_bias, feedforward_norm_scale, feedforward_norm_bias):
    bf16, f32 = jnp.bfloat16, jnp.float32
    models = lax.axis_size("mp")
    seqs, _, part, width = incoming_embeddings.shape
    strip, pair = asking_projector.shape
    hidden = feedforward_expand.shape[1]
    columns = 4 * pair + 2 * hidden
    norm_parts = [row.reshape(1, strip) for row in (
        attention_norm_scale, attention_norm_bias, feedforward_norm_scale, feedforward_norm_bias)]
    share = part // models
    spots, rows = plan.spots, plan.rows
    deep = (2, 2, 2, strip, columns)
    net_count = 92
    vmem = pltpu.VMEM
    scratch = [
        vmem((models,) + deep, bf16), vmem((spots, 8, width), f32), vmem((part, width), bf16), vmem((part, width), bf16),
        vmem((models, rows, 3 * pair), bf16), vmem((len(plan.tiles), 128, 128), f32),
        vmem((part, part), bf16), vmem((part, part), bf16), vmem((part, 128), f32), vmem((models, rows, 3 * pair), f32),
        vmem((models, part, pair), bf16), vmem((models, part, pair), f32), vmem((models, part, pair), f32),
        vmem((part, width), bf16), vmem((part, width), f32), vmem((part, 128), f32),
        vmem((models, rows, pair), bf16), vmem((rows, 128), bf16), vmem((part, width), f32), vmem((part, width), f32),
        vmem((part, width), f32), vmem((part, 128), f32), vmem((part, width), bf16), vmem((part, width), bf16),
        vmem((models,) + deep, bf16), vmem((models, 2, 2, strip, columns), bf16), vmem((models, 2, strip, columns), bf16),
        vmem((models, strip, columns), bf16), vmem((models, strip, columns), bf16), vmem((spots + models, 8, width), f32),
        pltpu.SemaphoreType.DMA((4,)), pltpu.SemaphoreType.DMA((net_count,)), pltpu.SemaphoreType.DMA((net_count,)),
    ]
    any_space, in_vmem = pl.BlockSpec(memory_space=pl.ANY), pl.BlockSpec(memory_space=pltpu.VMEM)
    out_rows, out_grads, weight_grads, norm_grads = pl.pallas_call(
        functools.partial(whole_layer, plan, (part, width, pair, hidden), net_count),
        out_shape=(jax.ShapeDtypeStruct((seqs, share, width), bf16), jax.ShapeDtypeStruct((seqs, share, width), bf16),
                   jax.ShapeDtypeStruct((strip, columns), f32), jax.ShapeDtypeStruct((8, width), f32)),
        in_specs=[pl.BlockSpec(memory_space=pltpu.SMEM)] + [in_vmem] * 10 + [any_space] * 2,
        out_specs=(any_space,) * 2 + (in_vmem,) * 2,
        scratch_shapes=scratch,
        compiler_params=pltpu.CompilerParams(collective_id=0, has_side_effects=True, vmem_limit_bytes=60 * 2 ** 20),
        name="layer",
    )(sequence_extents, asking_projector, lookup_projector, content_projector, attention_combiner.T, feedforward_expand,
      feedforward_contract.T, *norm_parts, incoming_embeddings, output_sensitivity)
    flat = lambda *shape: jax.ShapeDtypeStruct(shape, f32)
    rows_type = jax.ShapeDtypeStruct((seqs, 1, share, width), bf16)
    finished = pl.pallas_call(
        functools.partial(finish_outputs, (part, width, pair, hidden)),
        out_shape=(rows_type, rows_type, flat(strip, pair), flat(strip, pair), flat(strip, pair), flat(strip, pair),
                   flat(strip, hidden), flat(strip, hidden)) + (flat(1, strip),) * 4,
        in_specs=[in_vmem] * 4,
        out_specs=(any_space,) * 2 + (in_vmem,) * 10,
        scratch_shapes=[pltpu.SemaphoreType.DMA((2,))],
        name="outputs",
    )(out_rows, out_grads, weight_grads, norm_grads)
    rows_end, grads_end, query_grad, key_grad, value_grad, merge_t, up_grad, down_t = finished[:8]
    return (rows_end, grads_end, query_grad, key_grad, value_grad, merge_t.T, up_grad, down_t.T,
            *(row.reshape(strip) for row in finished[8:]))


def solution(mesh):
    in_specs = (
        P(None, "seq", "dp", None),
        P(None, "seq", "dp", None),
        P(),
        P(("dp", "seq"), "mp"),
        P(("dp", "seq"), "mp"),
        P(("dp", "seq"), "mp"),
        P("mp", ("dp", "seq")),
        P(("dp", "seq"), "mp"),
        P("mp", ("dp", "seq")),
        P(("dp", "seq")),
        P(("dp", "seq")),
        P(("dp", "seq")),
        P(("dp", "seq")),
    )
    out_specs = (
        P(None, "seq", ("dp", "mp"), None),
        P(None, "seq", ("dp", "mp"), None),
        P(("dp", "seq"), "mp"),
        P(("dp", "seq"), "mp"),
        P(("dp", "seq"), "mp"),
        P("mp", ("dp", "seq")),
        P(("dp", "seq"), "mp"),
        P("mp", ("dp", "seq")),
        P(("dp", "seq")),
        P(("dp", "seq")),
        P(("dp", "seq")),
        P(("dp", "seq")),
    )
    sizes = (mesh.shape["dp"], mesh.shape["seq"], mesh.shape["mp"])

    def chosen(*arrays):
        seqs, _, part, width = arrays[0].shape
        if sizes == (2, 4, 4) and seqs == sizes[2] and part == width == 512 and arrays[3].shape[1] == 128:
            return fast_body(Plan(part, sizes[0] * sizes[1]), *arrays)
        return general_body(*arrays)

    return jax.shard_map(chosen, mesh=mesh, in_specs=in_specs, out_specs=out_specs, check_vma=False)
```

```python
import functools

import jax
import jax.numpy as jnp
from jax import lax
from jax.experimental import pallas as pl
from jax.experimental.pallas import tpu as pltpu
from jax.sharding import PartitionSpec as P

HD = 64
NR = 16


def cut_along(x, dim, count):
    before, after = (x.shape[:dim], x.shape[dim + 1 :])
    return jnp.moveaxis(x.reshape(*before, count, -1, *after), dim, 0)


def summed_on_arrival(x, axis, dim):
    count = lax.axis_size(axis)
    blocks = lax.all_to_all(cut_along(x, dim, count), axis, 0, 0, tiled=True)
    return jnp.sum(blocks.astype(jnp.float32), axis=0)


def sent_together(arrays, axis, dim, along):
    ends, at = ([], 0)
    for a in arrays[:-1]:
        at += a.shape[along]
        ends.append(at)
    both = jnp.concatenate(arrays, axis=along)
    return tuple(jnp.split(summed_on_arrival(both, axis, dim), ends, axis=along))


def norm_rows(values, gain_row, shift_row):
    center = values - jnp.mean(values, axis=-1, keepdims=True)
    spread = jnp.mean(center * center, axis=-1, keepdims=True)
    return center * lax.rsqrt(spread + 1e-05) * gain_row + shift_row


def norm_gain_parts(values, grad_rows):
    center = values - jnp.mean(values, axis=-1, keepdims=True)
    spread = jnp.mean(center * center, axis=-1, keepdims=True)
    scaled = center * lax.rsqrt(spread + 1e-05)
    return (jnp.sum(grad_rows * scaled, axis=0), jnp.sum(grad_rows, axis=0))


def gelu_exact(values):
    return jax.nn.gelu(values, approximate=False)


def dot_plain(left_mat, right_mat):
    return jnp.dot(left_mat, right_mat, preferred_element_type=jnp.float32)


def dot_inner(left_mat, right_mat):
    return lax.dot_general(
        left_mat, right_mat, (((0,), (0,)), ((), ())), preferred_element_type=jnp.float32
    )


def dot_outer(left_mat, right_mat):
    return lax.dot_general(
        left_mat, right_mat, (((1,), (1,)), ((), ())), preferred_element_type=jnp.float32
    )


def group_sum(values, group_width):
    return jnp.sum(
        values.reshape((values.shape[0] // group_width, group_width) + values.shape[1:]), axis=1
    )


def block_shape(coarse_rows):
    query_len = min(coarse_rows, 512)
    span_len = query_len + 2 * NR
    window_len = -(-span_len // 128) * 128
    return (query_len, span_len, window_len)


def window_mask(level_at, first_row, query_len, window_len, span_len):
    rows_at = first_row + jnp.arange(query_len, dtype=jnp.int32)[:, None]
    keys_at = first_row + jnp.arange(window_len, dtype=jnp.int32)[None, :]
    inside = keys_at - first_row < span_len
    allowed = jnp.abs(rows_at // NR + 1 - keys_at // NR) <= 1
    if level_at > 0:
        half_block = NR // 2
        allowed = allowed & (jnp.abs(rows_at // half_block + 2 - keys_at // half_block) >= 2)
    return (allowed & inside).astype(jnp.float32)


def level_forward(query_rows, pair_wide, count_wide, level_at):
    coarse_rows = query_rows.shape[0]
    columns = query_rows.shape[1]
    heads_here = columns // HD
    query_len, span_len, window_len = block_shape(coarse_rows)
    tail_pad = window_len - span_len
    pair_padded = jnp.pad(pair_wide, ((0, tail_pad), (0, 0)))
    count_padded = jnp.pad(count_wide, (0, tail_pad))
    weight_list = []
    total_parts = []
    numer_parts = []
    for block_at in range(coarse_rows // query_len):
        first_row = block_at * query_len
        query_block = query_rows[first_row : first_row + query_len]
        pair_block = pair_padded[first_row : first_row + window_len]
        count_block = count_padded[first_row : first_row + window_len]
        keep_mask = (
            window_mask(level_at, first_row, query_len, window_len, span_len) * count_block[None, :]
        )
        head_weights = []
        head_totals = []
        head_numers = []
        for head_at in range(heads_here):
            head_cols = slice(head_at * HD, (head_at + 1) * HD)
            value_cols = slice(columns + head_at * HD, columns + (head_at + 1) * HD)
            scores = dot_outer(query_block[:, head_cols], pair_block[:, head_cols]) * HD ** (-0.5)
            weight = jnp.exp(scores) * keep_mask
            head_weights.append(weight)
            head_totals.append(jnp.sum(weight, axis=-1))
            head_numers.append(dot_plain(weight.astype(jnp.bfloat16), pair_block[:, value_cols]))
        weight_list.append(head_weights)
        total_parts.append(jnp.stack(head_totals, axis=1))
        numer_parts.append(jnp.concatenate(head_numers, axis=1))
    totals = jnp.concatenate(total_parts, axis=0)
    numer_part = jnp.concatenate(numer_parts, axis=0).reshape(coarse_rows, heads_here, HD)
    return ((query_rows, pair_padded, weight_list), totals, numer_part)


def level_backward(level_kept, numer_rows, total_rows):
    query_rows, pair_padded, weight_list = level_kept
    coarse_rows = query_rows.shape[0]
    columns = query_rows.shape[1]
    heads_here = columns // HD
    query_len, span_len, window_len = block_shape(coarse_rows)
    numer_flat = numer_rows.reshape(coarse_rows, columns)
    pair_grad = jnp.zeros(pair_padded.shape, jnp.float32)
    query_parts = []
    for block_at in range(coarse_rows // query_len):
        first_row = block_at * query_len
        query_block = query_rows[first_row : first_row + query_len]
        pair_block = pair_padded[first_row : first_row + window_len]
        numer_block = numer_flat[first_row : first_row + query_len]
        total_block = total_rows[first_row : first_row + query_len]
        query_heads = []
        key_heads = []
        value_heads = []
        for head_at in range(heads_here):
            head_cols = slice(head_at * HD, (head_at + 1) * HD)
            value_cols = slice(columns + head_at * HD, columns + (head_at + 1) * HD)
            weight = head_weights = weight_list[block_at][head_at]
            grad_here = numer_block[:, head_cols]
            score_grad = (
                (dot_outer(grad_here, pair_block[:, value_cols]) + total_block[:, head_at][:, None])
                * weight
            ).astype(jnp.bfloat16)
            query_heads.append(dot_plain(score_grad, pair_block[:, head_cols]) * HD ** (-0.5))
            key_heads.append(dot_inner(score_grad, query_block[:, head_cols]) * HD ** (-0.5))
            value_heads.append(dot_inner(head_weights.astype(jnp.bfloat16), grad_here))
        query_parts.append(jnp.concatenate(query_heads, axis=1))
        block_grad = jnp.concatenate(key_heads + value_heads, axis=1)
        pair_grad = pair_grad + jnp.pad(
            block_grad, ((first_row, pair_padded.shape[0] - first_row - window_len), (0, 0))
        )
    query_grad = jnp.concatenate(query_parts, axis=0)
    return (query_grad, pair_grad[: coarse_rows + 2 * NR])


def general_body(
    incoming_embeddings,
    output_sensitivity,
    sequence_extents,
    asking_projector,
    lookup_projector,
    content_projector,
    attention_combiner,
    feedforward_expand,
    feedforward_contract,
    attention_norm_scale,
    attention_norm_bias,
    feedforward_norm_scale,
    feedforward_norm_bias,
):
    groups = lax.axis_size("dp")
    slices = lax.axis_size("seq")
    models = lax.axis_size("mp")
    group_id = lax.axis_index("dp")
    slice_id = lax.axis_index("seq")
    model_id = lax.axis_index("mp")
    seq_count = incoming_embeddings.shape[0]
    piece_len = incoming_embeddings.shape[2]
    model_width = incoming_embeddings.shape[3]
    part_len = piece_len * groups
    batches = seq_count // groups
    share_len = piece_len // models
    share_rows = groups * share_len
    local_top = (part_len // NR).bit_length() - 1
    upper_start = local_top + 1
    level_top = (part_len * slices // (2 * NR)).bit_length() - 1
    upper_rows = NR // 2
    upper_whole = upper_rows * slices
    send_tok = incoming_embeddings.reshape(
        groups, batches, piece_len, model_width
    )
    send_cot = output_sensitivity.reshape(
        groups, batches, piece_len, model_width
    )
    dealt_tok, dealt_cot = (
        lax.all_to_all(send_tok, "dp", split_axis=0, concat_axis=2, tiled=True),
        lax.all_to_all(send_cot, "dp", split_axis=0, concat_axis=2, tiled=True),
    )
    dealt_tok = dealt_tok.reshape(batches, part_len, model_width)
    dealt_cot = dealt_cot.reshape(batches, part_len, model_width)
    my_lengths = lax.dynamic_slice_in_dim(sequence_extents, group_id * batches, batches, 0)

    def split_rows(rows):
        return rows.reshape((groups, models, share_len) + rows.shape[1:])

    def take_share(rows):
        return lax.dynamic_slice_in_dim(split_rows(rows), model_id, 1, 1).reshape(
            (share_rows,) + rows.shape[1:]
        )

    def neighbour_rims(gathered):
        padded = jnp.pad(gathered, ((2 * NR, 2 * NR), (0, 0)))
        from_left = lax.dynamic_slice_in_dim(padded, slice_id * 2 * NR + NR, NR, 0)
        from_right = lax.dynamic_slice_in_dim(padded, (slice_id + 2) * 2 * NR, NR, 0)
        return (from_left, from_right)

    def one_batch(batch_index, learnable_collection):
        full_query, full_key, full_value, full_merge, full_up, full_down = learnable_collection[:6]
        gain_pre, shift_pre, gain_mid, shift_mid = (
            learnable_tensor.astype(jnp.float32) for learnable_tensor in learnable_collection[6:]
        )
        columns = full_query.shape[1]
        heads_here = columns // HD
        length_now = my_lengths[batch_index]

        def level_counts(level_at, first_id, id_total):
            coarse_ids = first_id + jnp.arange(id_total, dtype=jnp.int32)
            group_len = 2**level_at
            return jnp.where(
                coarse_ids >= 0, jnp.clip(length_now - group_len * coarse_ids, 0, group_len), 0
            ).astype(jnp.float32)

        positions = slice_id * part_len + jnp.arange(part_len, dtype=jnp.int32)
        valid_rows = (positions < length_now).astype(jnp.float32)
        inputs = dealt_tok[batch_index].astype(jnp.float32)
        grad_in = dealt_cot[batch_index].astype(jnp.float32) * valid_rows[:, None]
        valid_share = take_share(valid_rows)
        normed, pull_pre = jax.vjp(norm_rows, inputs, gain_pre, shift_pre)
        normed_low = normed.astype(jnp.bfloat16)
        queries = dot_plain(normed_low, full_query).astype(jnp.bfloat16)
        keys_own = dot_plain(normed_low, full_key).astype(jnp.bfloat16)
        values_own = dot_plain(normed_low, full_value).astype(jnp.bfloat16)
        pair_own = jnp.concatenate([keys_own, values_own], axis=1)
        fine_all = (
            jnp.concatenate([queries, pair_own], axis=1).astype(jnp.float32) * valid_rows[:, None]
        )
        level_sums = [fine_all]
        for level_at in range(1, upper_start + 1):
            level_sums.append(group_sum(level_sums[-1], 2))
        query_levels = [queries]
        pair_levels = [pair_own]
        own_counts = [valid_rows]
        for level_at in range(1, local_top + 1):
            coarse_rows = part_len >> level_at
            counts_here = level_counts(level_at, slice_id * coarse_rows, coarse_rows)
            coarse_means = (level_sums[level_at] / jnp.maximum(counts_here, 1.0)[:, None]).astype(
                jnp.bfloat16
            )
            query_levels.append(coarse_means[:, :columns])
            pair_levels.append(coarse_means[:, columns:])
            own_counts.append(counts_here)
        edge_rows = jnp.concatenate(
            [
                jnp.concatenate([pair_rows[:NR], pair_rows[-NR:]], axis=0)
                for pair_rows in pair_levels
            ],
            axis=1,
        )
        edges_all, upper_all = (
            lax.all_gather(
                edge_rows.astype(jnp.float32).astype(jnp.bfloat16), "seq", axis=0, tiled=True
            ).astype(jnp.float32),
            lax.all_gather(
                level_sums[upper_start].astype(jnp.bfloat16), "seq", axis=0, tiled=True
            ).astype(jnp.float32),
        )
        left_edge, right_edge = neighbour_rims(edges_all)
        left_edge = left_edge.astype(jnp.bfloat16)
        right_edge = right_edge.astype(jnp.bfloat16)
        kept_levels = []
        total_all = jnp.zeros((part_len, heads_here), jnp.float32)
        numer_all = jnp.zeros((part_len, heads_here, HD), jnp.float32)
        for level_at in range(local_top + 1):
            coarse_rows = part_len >> level_at
            col_range = slice(level_at * 2 * columns, (level_at + 1) * 2 * columns)
            pair_wide = jnp.concatenate(
                [left_edge[:, col_range], pair_levels[level_at], right_edge[:, col_range]], axis=0
            )
            count_wide = level_counts(level_at, slice_id * coarse_rows - NR, coarse_rows + 2 * NR)
            level_kept, totals, numer_part = level_forward(
                query_levels[level_at], pair_wide, count_wide, level_at
            )
            kept_levels.append(level_kept)
            total_all = total_all + jnp.repeat(totals, 2**level_at, axis=0)
            numer_all = numer_all + jnp.repeat(numer_part, 2**level_at, axis=0)
        level_at = 7
        repeat_by = 2 ** (level_at - upper_start)
        coarse_rows = upper_whole // repeat_by
        counts_here = level_counts(level_at, 0, coarse_rows)
        coarse_means = (
            group_sum(upper_all, repeat_by) / jnp.maximum(counts_here, 1.0)[:, None]
        ).astype(jnp.bfloat16)
        pair_wide = jnp.pad(coarse_means[:, columns:], ((NR, NR), (0, 0)))
        count_wide = level_counts(level_at, -NR, coarse_rows + 2 * NR)
        level_kept, totals, numer_part = level_forward(
            coarse_means[:, :columns], pair_wide, count_wide, level_at
        )
        upper_kept = [level_kept]
        upper_counts = [counts_here]
        upper_total = jnp.repeat(totals, repeat_by, axis=0)
        upper_numer = jnp.repeat(numer_part, repeat_by, axis=0)
        total_all = total_all + jnp.repeat(
            lax.dynamic_slice_in_dim(upper_total, slice_id * upper_rows, upper_rows, 0),
            2**upper_start,
            axis=0,
        )
        numer_all = numer_all + jnp.repeat(
            lax.dynamic_slice_in_dim(upper_numer, slice_id * upper_rows, upper_rows, 0),
            2**upper_start,
            axis=0,
        )
        attended = (
            (numer_all / total_all[:, :, None]).reshape(part_len, columns).astype(jnp.bfloat16)
        )
        merged_part = dot_plain(attended, full_merge)
        branch_attn = lax.psum(merged_part, "mp")
        after_attn = inputs + branch_attn
        mid_normed, pull_mid = jax.vjp(norm_rows, after_attn, gain_mid, shift_mid)
        mid_low = mid_normed.astype(jnp.bfloat16)
        after_share = take_share(after_attn)
        up_proj = dot_plain(mid_low, full_up)
        activated, pull_gelu = jax.vjp(gelu_exact, up_proj)
        act_low = activated.astype(jnp.bfloat16)
        ffn_share = (
            lax.psum_scatter(
                split_rows(dot_plain(act_low, full_down)).astype(jnp.bfloat16),
                "mp",
                scatter_dimension=1,
                tiled=True,
            )
            .astype(jnp.float32)
            .reshape(share_rows, model_width)
        )
        result_share = (valid_share[:, None] * (after_share + ffn_share)).astype(jnp.bfloat16)
        grad_low = grad_in.astype(jnp.bfloat16)
        act_grad = dot_outer(grad_low, full_down)
        down_acc = dot_inner(act_low, grad_low)
        hidden_grad = pull_gelu(act_grad)[0].astype(jnp.bfloat16)
        up_acc = dot_inner(mid_low, hidden_grad)
        mid_part = dot_outer(hidden_grad, full_up)
        mid_grad = lax.psum(mid_part, "mp")
        back_mid = pull_mid(mid_grad)[0]
        residual_grad = grad_in + back_mid
        branch_grad = residual_grad.astype(jnp.bfloat16)
        residual_share = take_share(residual_grad)
        gain_mid_part, shift_mid_part = norm_gain_parts(after_share, take_share(mid_grad))
        merge_acc = dot_inner(attended, branch_grad)
        attended_grad = dot_outer(branch_grad, full_merge).reshape(part_len, heads_here, HD)
        numer_grad = (attended_grad / total_all[:, :, None]).astype(jnp.bfloat16)
        total_grad = -jnp.sum(attended_grad * numer_all, axis=-1) / (total_all * total_all)
        numer_wide = numer_grad.astype(jnp.float32)
        rim_parts = []
        own_pair_grads = []
        query_coarse = []
        for level_at in range(local_top + 1):
            coarse_rows = part_len >> level_at
            if level_at == 0:
                numer_sum = numer_grad
                total_sum = total_grad
            else:
                numer_sum = group_sum(numer_wide, 2**level_at).astype(jnp.bfloat16)
                total_sum = group_sum(total_grad, 2**level_at)
            query_grad, pair_grad = level_backward(kept_levels[level_at], numer_sum, total_sum)
            rim_parts.append(
                jnp.concatenate([pair_grad[:NR], pair_grad[NR + coarse_rows :]], axis=0)
            )
            own_pair_grads.append(pair_grad[NR : NR + coarse_rows])
            query_coarse.append(query_grad)
        rim_grads = jnp.concatenate(rim_parts, axis=1)
        upper_numer_grad = group_sum(numer_wide, 2**upper_start).reshape(upper_rows, columns)
        upper_total_grad = group_sum(total_grad, 2**upper_start)
        rims_all, numer_sums, total_sums = (
            lax.all_gather(rim_grads.astype(jnp.bfloat16), "seq", axis=0, tiled=True).astype(
                rim_grads.dtype
            ),
            lax.all_gather(upper_numer_grad.astype(jnp.bfloat16), "seq", axis=0, tiled=True).astype(
                upper_numer_grad.dtype
            ),
            lax.all_gather(upper_total_grad.astype(jnp.bfloat16), "seq", axis=0, tiled=True).astype(
                upper_total_grad.dtype
            ),
        )
        from_left, from_right = neighbour_rims(rims_all)
        fine_grad = jnp.zeros((part_len, 3 * columns), jnp.float32)
        for level_at in range(local_top + 1):
            coarse_rows = part_len >> level_at
            col_range = slice(level_at * 2 * columns, (level_at + 1) * 2 * columns)
            pair_here = (
                own_pair_grads[level_at]
                + jnp.pad(from_left[:, col_range], ((0, coarse_rows - NR), (0, 0)))
                + jnp.pad(from_right[:, col_range], ((coarse_rows - NR, 0), (0, 0)))
            )
            coarse_grad = jnp.concatenate([query_coarse[level_at], pair_here], axis=1)
            if level_at == 0:
                fine_grad = coarse_grad
            else:
                coarse_grad = coarse_grad / jnp.maximum(own_counts[level_at], 1.0)[:, None]
                fine_grad = (
                    fine_grad + jnp.repeat(coarse_grad, 2**level_at, axis=0) * valid_rows[:, None]
                )
        upper_grad = jnp.zeros((upper_whole, 3 * columns), jnp.float32)
        for index_at, level_at in enumerate(range(upper_start, level_top + 1)):
            repeat_by = 2 ** (level_at - upper_start)
            coarse_rows = upper_whole // repeat_by
            numer_sum = (
                group_sum(numer_sums, repeat_by)
                .reshape(coarse_rows, heads_here, HD)
                .astype(jnp.bfloat16)
            )
            total_sum = group_sum(total_sums, repeat_by)
            query_grad, pair_grad = level_backward(upper_kept[index_at], numer_sum, total_sum)
            coarse_grad = (
                jnp.concatenate([query_grad, pair_grad[NR : NR + coarse_rows]], axis=1)
                / jnp.maximum(upper_counts[index_at], 1.0)[:, None]
            )
            upper_grad = jnp.repeat(coarse_grad, repeat_by, axis=0)
        own_upper = lax.dynamic_slice_in_dim(upper_grad, slice_id * upper_rows, upper_rows, 0)
        fine_grad = fine_grad + jnp.repeat(own_upper, 2**upper_start, axis=0) * valid_rows[:, None]
        rows_grad = fine_grad.astype(jnp.bfloat16)
        query_rows_grad = rows_grad[:, :columns]
        key_rows_grad = rows_grad[:, columns : 2 * columns]
        value_rows_grad = rows_grad[:, 2 * columns :]
        query_acc = dot_inner(normed_low, query_rows_grad)
        key_acc = dot_inner(normed_low, key_rows_grad)
        value_acc = dot_inner(normed_low, value_rows_grad)
        normed_part = (
            dot_outer(query_rows_grad, full_query)
            + dot_outer(key_rows_grad, full_key)
            + dot_outer(value_rows_grad, full_value)
        )
        normed_grad, gain_mid_sum, shift_mid_sum = (
            lax.psum(normed_part.astype(jnp.bfloat16), "mp").astype(jnp.float32),
            lax.psum(gain_mid_part.astype(jnp.bfloat16), "mp").astype(jnp.float32),
            lax.psum(shift_mid_part.astype(jnp.bfloat16), "mp").astype(jnp.float32),
        )
        back_pre, gain_pre_acc, shift_pre_acc = pull_pre(normed_grad)
        input_share = (residual_share + take_share(back_pre)).astype(jnp.bfloat16)
        grad_terms = (
            query_acc,
            key_acc,
            value_acc,
            merge_acc,
            up_acc,
            down_acc,
            gain_pre_acc,
            shift_pre_acc,
            gain_mid_sum,
            shift_mid_sum,
        )
        return (result_share, input_share, grad_terms)

    result_list = []
    grad_list = []
    running_sum = None
    for batch_index in range(batches):
        learnable_collection = (
            lax.all_gather(asking_projector, ("dp", "seq"), axis=0, tiled=True),
            lax.all_gather(lookup_projector, ("dp", "seq"), axis=0, tiled=True),
            lax.all_gather(content_projector, ("dp", "seq"), axis=0, tiled=True),
            lax.all_gather(attention_combiner, ("dp", "seq"), axis=1, tiled=True),
            lax.all_gather(feedforward_expand, ("dp", "seq"), axis=0, tiled=True),
            lax.all_gather(feedforward_contract, ("dp", "seq"), axis=1, tiled=True),
            lax.all_gather(attention_norm_scale, ("dp", "seq"), axis=0, tiled=True),
            lax.all_gather(attention_norm_bias, ("dp", "seq"), axis=0, tiled=True),
            lax.all_gather(feedforward_norm_scale, ("dp", "seq"), axis=0, tiled=True),
            lax.all_gather(feedforward_norm_bias, ("dp", "seq"), axis=0, tiled=True),
        )
        result_share, input_share, grad_terms = one_batch(batch_index, learnable_collection)
        result_list.append(result_share)
        grad_list.append(input_share)
        if running_sum is None:
            running_sum = grad_terms
        else:
            running_sum = tuple(
                (older_sum + newer_sum for older_sum, newer_sum in zip(running_sum, grad_terms))
            )
    owned_grads = (
        *sent_together(
            (
                running_sum[0].astype(jnp.bfloat16),
                running_sum[1].astype(jnp.bfloat16),
                running_sum[2].astype(jnp.bfloat16),
            ),
            ("dp", "seq"),
            0,
            1,
        ),
        summed_on_arrival(running_sum[3].astype(jnp.bfloat16), ("dp", "seq"), 1),
        summed_on_arrival(running_sum[4].astype(jnp.bfloat16), ("dp", "seq"), 0),
        summed_on_arrival(running_sum[5].astype(jnp.bfloat16), ("dp", "seq"), 1),
        summed_on_arrival(running_sum[6].astype(jnp.bfloat16), ("dp", "seq"), 0),
        summed_on_arrival(running_sum[7].astype(jnp.bfloat16), ("dp", "seq"), 0),
        summed_on_arrival(running_sum[8].astype(jnp.bfloat16), ("dp", "seq"), 0),
        summed_on_arrival(running_sum[9].astype(jnp.bfloat16), ("dp", "seq"), 0),
    )
    result_all = jnp.stack(result_list, axis=0).reshape(batches, groups, share_len, model_width)
    grad_all = jnp.stack(grad_list, axis=0).reshape(batches, groups, share_len, model_width)
    back_out, back_grad = (
        lax.all_to_all(result_all, "dp", split_axis=1, concat_axis=0, tiled=True),
        lax.all_to_all(grad_all, "dp", split_axis=1, concat_axis=0, tiled=True),
    )
    return (
        back_out,
        back_grad,
        owned_grads[0],
        owned_grads[1],
        owned_grads[2],
        owned_grads[3],
        owned_grads[4],
        owned_grads[5],
        owned_grads[6],
        owned_grads[7],
        owned_grads[8],
        owned_grads[9],
    )


MESH = pl.DeviceIdType.MESH
NEG = -1e30
BACK_GROUP = 5
FIRST = 32
THROUGH_Y = 32
TOP = 16
TOP_LAST = 32
GROUP = 5


def nn(a, b):
    return lax.dot_general(a, b, (((1,), (0,)), ((), ())), preferred_element_type=jnp.float32)


def nt(a, b):
    return lax.dot_general(a, b, (((1,), (1,)), ((), ())), preferred_element_type=jnp.float32)


def tn(a, b):
    return lax.dot_general(a, b, (((0,), (0,)), ((), ())), preferred_element_type=jnp.float32)


def halves(values):
    high = values.astype(jnp.bfloat16)
    return high, (values - high.astype(jnp.float32)).astype(jnp.bfloat16)


class Plan:
    def __init__(self, part, spots):
        self.part, self.spots = part, spots
        self.levels = (part // NR).bit_length()
        self.top = (part * spots // (2 * NR)).bit_length() - 1
        self.own = [part >> level for level in range(self.levels)]
        self.at, row = [], 0
        for rows in self.own:
            self.at.append(row)
            row += rows + 2 * NR
        self.upper = row
        self.rows = row + spots * NR
        self.pool_at, row = [None], 0
        for rows in self.own[1:]:
            self.pool_at.append(row)
            row += rows
        self.pool_upper = row
        self.pooled = row + NR
        self.slot, row = [], 0
        for level in range(self.levels, self.top + 1):
            self.slot.append((level, row, part >> level))
            row += part >> level
        assert row <= NR and spots * NR == 128 and self.pooled == part
        self.segments = [(self.at[lv], self.own[lv] + 2 * NR, lv) for lv in range(self.levels)]
        self.inner, self.outer = [], []
        level = 0
        while level < self.levels:
            start, total = self.at[level], self.own[level] + 2 * NR
            end = start + total
            if total < 96:
                self.outer.append((start, self.upper - start, self.upper - 128, None))
                break
            row = start
            while row < end:
                count = min(96, end - row)
                window = max(start, min(row - NR, end - 128))
                tile = (row, count, window, level if window + 128 <= end else None)
                inside = window >= start + NR and window + 128 <= end - NR
                (self.inner if inside else self.outer).append(tile)
                row += count
            level += 1
        self.outer.append((self.upper, 128, self.upper, None))
        self.tiles = self.inner + self.outer

    def own_pieces(self, tile):
        first, count = tile[:2]
        pieces = []
        for start, rows in zip(self.at, self.own):
            low, high = max(first, start + NR), min(first + count, start + NR + rows)
            if low < high:
                pieces.append((low, high - low))
        return pieces


def row_places(plan, rows, low, high, spot):
    level = jnp.full(rows.shape, -1, jnp.int32)
    place = jnp.zeros(rows.shape, jnp.int32)
    for start, count, lv in plan.segments:
        if start < high and start + count > low:
            inside = (rows >= start) & (rows < start + count)
            level = jnp.where(inside, lv, level)
            place = jnp.where(inside, spot * plan.own[lv] - NR + rows - start, place)
    if high > plan.upper:
        owner = lax.shift_right_arithmetic(rows - plan.upper, 4)
        within = (rows - plan.upper) & (NR - 1)
        for lv, first, count in plan.slot:
            inside = (rows >= plan.upper) & (within >= first) & (within < first + count)
            level = jnp.where(inside, lv, level)
            place = jnp.where(inside, owner * count + within - first, place)
    return level, place


def log_counts(plan, tile, spot, length):
    first, count, window, level = tile
    row_at = first + lax.broadcasted_iota(jnp.int32, (count, 128), 0)
    key_at = window + lax.broadcasted_iota(jnp.int32, (8, 128), 1)
    row_level, row_place = row_places(plan, row_at, first, first + count, spot)
    key_level, key_place = row_places(plan, key_at, window, window + 128, spot)
    span = lax.shift_left(jnp.ones_like(key_level), jnp.maximum(key_level, 0))
    counts = jnp.clip(length - span * key_place, 0, span)
    usable = (counts > 0) & (key_place >= 0) & (key_level >= 0)
    logs = jnp.where(usable, jnp.log(jnp.maximum(counts, 1).astype(jnp.float32)), NEG)
    coarse = lambda level_at, place_at, by: level_at * 65536 + lax.shift_right_arithmetic(place_at, by)
    key_block = coarse(key_level, key_place, 4)[:1]
    key_half = coarse(key_level, key_place, 3)[:1]
    allowed = jnp.abs(coarse(row_level, row_place, 4) - key_block) <= 1
    if level != 0:
        apart = jnp.abs(coarse(row_level, row_place, 3) - key_half) >= 2
        allowed = allowed & (apart if level is not None else apart | (row_level == 0)) & (row_level >= 0)
    return jnp.where(allowed, logs[:1], NEG)


def pool_bounds(plan, shape, dim):
    row = lax.broadcasted_iota(jnp.int32, shape, dim)
    low = jnp.full(shape, -1, jnp.int32)
    size = jnp.zeros(shape, jnp.int32)
    level = jnp.zeros(shape, jnp.int32)
    parts = [(plan.pool_at[lv], plan.own[lv], lv) for lv in range(1, plan.levels)]
    parts += [(plan.pool_upper + first, count, lv) for lv, first, count in plan.slot]
    for start, count, lv in parts:
        inside = (row >= start) & (row < start + count)
        low = jnp.where(inside, (row - start) << lv, low)
        size = jnp.where(inside, 1 << lv, size)
    return low, size


def spread_columns(rows, place, count):
    width = rows.shape[1]
    source = lax.broadcasted_iota(jnp.int32, (width, width * count), 0)
    target = lax.broadcasted_iota(jnp.int32, (width, width * count), 1)
    return nn(rows, jnp.where(target == source + place * width, 1.0, 0.0).astype(rows.dtype))


def flip_bits(value, k):
    low, high, k_low, k_high = value % 2, value // 2, k % 2, k // 2
    return (high + k_high - 2 * high * k_high) * 2 + low + k_low - 2 * low * k_low


class Marks:
    def __init__(self):
        self.used = 0

    def take(self, count):
        self.used += count
        return self.used - count


def whole_layer(plan, dims, net_count, *refs):
    (extents, w_query, w_key, w_value, w_merge, w_expand, w_contract, norm_0, norm_1, norm_2, norm_3, tokens_in, cotangent_in,
     out_rows, out_grads, weight_grads, norm_grads,
     weights, norms, tokens, cotangent, ext, logs, pool, unpool, inverse, work,
     attended, ratio, recip, normed, scaled, rstd, grad_ext, total_ext, residual, acc, acc2, totals, result, row_grads,
     grads, got1, got2, got3, got4, norm_got,
     load_sem, send_sem, recv_sem) = refs
    part, width, pair, hidden = dims
    f32, bf16 = jnp.float32, jnp.bfloat16
    models = weights.shape[0]
    strip, columns = weights.shape[4:]
    ax, sq, az = lax.axis_index("dp"), lax.axis_index("seq"), lax.axis_index("mp")
    ay, ac = sq // 2, sq % 2
    spot = sq * 2 + ax
    spots = plan.spots
    length = extents[az]
    qkv = 3 * pair

    def device(x, y, c, z):
        return (x, y * 2 + c, z)

    def at_spot(place):
        return (place % 2, place // 2, az)

    def plane(k):
        return flip_bits(az, k)

    x_peer, y_peer, c_peer = device(1 - ax, ay, ac, az), device(ax, 1 - ay, ac, az), device(ax, ay, 1 - ac, az)
    xy_peer = device(1 - ax, 1 - ay, ac, az)
    z_peer = lambda k: device(ax, ay, ac, plane(k))

    barrier = pltpu.get_barrier_semaphore()
    for step in range(1, spots):
        pl.semaphore_signal(barrier, inc=1, device_id=at_spot((spot + step) % spots), device_id_type=MESH)
    for k in range(1, models):
        pl.semaphore_signal(barrier, inc=1, device_id=z_peer(k), device_id_type=MESH)
    load_tokens = pltpu.make_async_copy(tokens_in.at[az, 0], tokens, load_sem.at[0])
    load_cotangent = pltpu.make_async_copy(cotangent_in.at[az, 0], cotangent, load_sem.at[1])
    load_tokens.start()
    load_cotangent.start()
    own = (az, ax, ay, ac)
    weights[own + (slice(None), slice(0, pair))] = w_query[...] * jnp.asarray(HD ** -0.5, bf16)
    weights[own + (slice(None), slice(pair, 2 * pair))] = w_key[...]
    weights[own + (slice(None), slice(2 * pair, qkv))] = w_value[...]
    weights[own + (slice(None), slice(qkv, qkv + pair))] = w_merge[...]
    weights[own + (slice(None), slice(4 * pair, 4 * pair + hidden))] = w_expand[...]
    weights[own + (slice(None), slice(4 * pair + hidden, columns))] = w_contract[...]
    owner = ax * 4 + sq
    norms[spot] = jnp.concatenate(
        [spread_columns(row[...], owner, width // strip) for row in (norm_0, norm_1, norm_2, norm_3)]
        + [jnp.zeros((4, width), f32)], axis=0)
    pl.semaphore_wait(barrier, spots - 1 + models - 1)

    marks = Marks()

    def copy(i, src, dst, to):
        return pltpu.make_async_remote_copy(
            src_ref=src, dst_ref=dst, send_sem=send_sem.at[i], recv_sem=recv_sem.at[i],
            device_id=to, device_id_type=MESH)

    class Group:
        def __init__(self, i, pairs, whole):
            self.i, self.pairs, self.whole = i, pairs, whole

        def start(self):
            for src, dst, to in self.pairs:
                copy(self.i, src, dst, to).start()
            return self

        def arrive(self):
            copy(self.i, self.whole, self.whole, self.pairs[0][2]).wait_recv()

        def leave(self):
            copy(self.i, self.whole, self.whole, self.pairs[0][2]).wait_send()

    sent = []
    kept = []

    def send(pairs, whole):
        group = Group(marks.take(1), pairs, whole).start()
        sent.append(group)
        return group

    class Gather:
        def __init__(self, col, count, through_y):
            self.cols, self.rows = pl.ds(col, count), through_y
            self.flight = {}
            self.first = marks.take(models)

        def block(self, k, x, y, rows=slice(None)):
            return weights.at[plane(k), x, y, ac, rows, self.cols]

        def to_planes(self):
            here = self.block(0, ax, ay)
            for k in range(1, models):
                self.flight["z", k] = send([(here, here, z_peer(k))], here)

        def to_sides(self, k):
            if k:
                self.flight["z", k].arrive()
            here = self.block(k, ax, ay)
            if self.rows == 0:
                self.flight["corner", k] = send([(here, here, x_peer), (here, here, y_peer), (here, here, xy_peer)],
                                                weights.at[pl.ds(0, 3), ax, ay, ac, :, self.cols])
                return
            self.flight["side", k] = send([(here, here, x_peer), (here, here, y_peer)],
                                          weights.at[plane(k), :, ay, ac, :, self.cols])

        def to_corner(self, k):
            if self.rows == 0:
                return
            self.flight["side", k].arrive()
            pairs = []
            if self.rows > 0:
                first = self.block(k, 1 - ax, ay, pl.ds(0, self.rows))
                pairs.append((first, first, y_peer))
            if self.rows < strip:
                rest = self.block(k, ax, 1 - ay, pl.ds(self.rows, strip - self.rows))
                pairs.append((rest, rest, x_peer))
            self.flight["corner", k] = send(pairs, self.block(k, ax, ay))

        def to_core(self, k):
            self.flight["corner", k].arrive()
            sent.append(self.last(k).start())

        def last(self, k):
            here = weights.at[plane(k), :, :, ac, :, self.cols]
            return Group(self.first + k, [(here, here, c_peer)], here)

        def here(self, k):
            self.last(k).arrive()

    first_gather = Gather(0, qkv, FIRST)
    merge_gather = Gather(qkv, pair, 32)
    feed_gather = Gather(4 * pair, 2 * hidden, THROUGH_Y)

    first_gather.to_planes()
    first_gather.to_sides(0)
    norm_copies = send([(norms.at[spot], norms.at[spot], at_spot((spot + step) % spots)) for step in range(1, spots)],
                       norms.at[pl.ds(0, spots - 1)])
    merge_gather.to_planes()
    feed_gather.to_planes()
    merge_gather.to_sides(0)
    feed_gather.to_sides(0)

    low, size = pool_bounds(plan, (part, 128), 0)
    for block in range(part // 128):
        token_at = block * 128 + lax.broadcasted_iota(jnp.int32, (part, 128), 1)
        member = (token_at >= low) & (token_at < low + size) & (token_at + spot * part < length)
        pool[:, block * 128:(block + 1) * 128] = jnp.where(member, 1.0, 0.0).astype(bf16)
    counts = jnp.clip(length - spot * part - low, 0, size)
    inverse[...] = 1.0 / jnp.maximum(counts, 1).astype(f32)
    low, size = pool_bounds(plan, (8, part), 1)
    token_at = lax.broadcasted_iota(jnp.int32, (part, part), 0)
    member = (token_at >= low[:1]) & (token_at < (low + size)[:1])
    unpool[...] = jnp.where(member, 1.0, 0.0).astype(bf16)
    first_gather.to_corner(0)
    first_gather.to_sides(1)
    load_tokens.wait()

    def statistics(values):
        center = values - jnp.mean(values, axis=-1, keepdims=True)
        spread = jnp.mean(center * center, axis=-1, keepdims=True)
        scale = lax.rsqrt(spread + 1e-05)
        return center * scale, scale

    xhat, scale = statistics(tokens[...].astype(f32))
    scaled[...] = xhat
    rstd[...] = jnp.broadcast_to(scale, (part, 128))
    first_gather.to_sides(2)
    first_gather.to_sides(3)
    first_gather.to_core(0)
    first_gather.to_corner(1)
    for i, tile in enumerate(plan.tiles):
        logs[i, 0:tile[1]] = log_counts(plan, tile, spot, length)
    first_gather.to_corner(2)
    first_gather.to_corner(3)
    feed_gather.to_corner(0)
    first_gather.to_core(1)
    norm_copies.arrive()
    gains = norms[0]
    for i in range(1, spots):
        gains = gains + norms[i]
    pre_gain, pre_shift, mid_gain, mid_shift = (gains[i:i + 1] for i in range(4))
    normed[...] = (scaled[...] * pre_gain + pre_shift).astype(bf16)

    is_first, is_last = spot == 0, spot == spots - 1

    @pl.when(is_first)
    def _():
        for lv in range(plan.levels):
            rows = slice(plan.at[lv], plan.at[lv] + NR)
            ext[:, rows, :] = jnp.zeros((models, NR, qkv), bf16)
            grad_ext[:, rows, :] = jnp.zeros((models, NR, pair), bf16)
            total_ext[rows, :] = jnp.zeros((NR, 128), bf16)

    @pl.when(is_last)
    def _():
        for lv in range(plan.levels):
            end = plan.at[lv] + NR + plan.own[lv]
            rows = slice(end, end + NR)
            ext[:, rows, :] = jnp.zeros((models, NR, qkv), bf16)
            grad_ext[:, rows, :] = jnp.zeros((models, NR, pair), bf16)
            total_ext[rows, :] = jnp.zeros((NR, 128), bf16)

    def weight_cols(m, col, count):
        return weights[m, :, :, :, :, col:col + count].reshape(width, count)

    slot_row = pl.multiple_of(spot * NR, NR)
    own_slot_rows = pl.ds(pl.multiple_of(plan.upper + slot_row, NR), NR)
    class Rims:
        def __init__(self, view, i):
            self.view, self.i, self.to = view, i, at_spot((spot + 1) % spots)

        def start(self):
            view, i = self.view, self.i
            right, left = at_spot((spot + 1) % spots), at_spot((spot + spots - 1) % spots)

            @pl.when(jnp.logical_not(is_last))
            def _():
                for start, rows in zip(plan.at, plan.own):
                    copy(i, view(pl.ds(start + rows, NR)), view(pl.ds(start, NR)), right).start()

            @pl.when(jnp.logical_not(is_first))
            def _():
                for start, rows in zip(plan.at, plan.own):
                    copy(i, view(pl.ds(start + NR, NR)), view(pl.ds(start + NR + rows, NR)), left).start()

            block = view(own_slot_rows)
            for step in range(1, spots):
                copy(i, block, block, at_spot((spot + step) % spots)).start()

        def whole(self, sides):
            rows = self.view(pl.ds(0, (sides * plan.levels + spots - 1) * NR))
            return copy(self.i, rows, rows, self.to)

        def wait(self):
            at_end = is_first | is_last

            @pl.when(at_end)
            def _():
                self.whole(1).wait_recv()

            @pl.when(jnp.logical_not(at_end))
            def _():
                self.whole(2).wait_recv()

        def done(self):
            at_end = is_first | is_last

            @pl.when(at_end)
            def _():
                self.whole(1).wait_send()

            @pl.when(jnp.logical_not(at_end))
            def _():
                self.whole(2).wait_send()

    pair_base = marks.take(models)
    query_base = marks.take(1)
    grad_base = marks.take(models)
    total_base = marks.take(1)
    pair_rims = lambda k: Rims(lambda rows: ext.at[plane(k), rows, pl.ds(pair, 2 * pair)], pair_base + k)
    query_rims = lambda: Rims(lambda rows: ext.at[:, rows, pl.ds(0, pair)], query_base)
    grad_rims = lambda k: Rims(lambda rows: grad_ext.at[plane(k), rows, :], grad_base + k)
    total_rims = lambda: Rims(lambda rows: total_ext.at[rows, :], total_base)

    for k in range(models):
        if k >= 1 and k + 1 < models:
            first_gather.to_core(k + 1)
        first_gather.here(k)
        m = plane(k)
        rows = nn(normed[...], weight_cols(m, 0, qkv)).astype(bf16)
        ext[m, NR:NR + part, :] = rows
        means = (nn(pool[...], rows) * jnp.concatenate([inverse[...]] * 3, axis=1)).astype(bf16)
        for lv in range(1, plan.levels):
            ext[m, plan.at[lv] + NR:plan.at[lv] + NR + plan.own[lv], :] = means[plan.pool_at[lv]:plan.pool_at[lv] + plan.own[lv]]
        ext[m, own_slot_rows, :] = means[plan.pool_upper:plan.pool_upper + NR]
        pair_rims(k).start()

    lane = lax.broadcasted_iota(jnp.int32, (1, pair), 1)
    left_head = lane < HD

    def both_heads(rows):
        zero = jnp.zeros_like(rows)
        return jnp.concatenate([jnp.where(left_head, rows, zero), jnp.where(left_head, zero, rows)], axis=0)

    def joined(rows):
        half = rows.shape[0] // 2
        return jnp.where(left_head, rows[:half], rows[half:])

    ones = jnp.ones((128, 128), bf16)

    def stacked(parts):
        return parts[0] if len(parts) == 1 else jnp.concatenate(parts, axis=0)

    def tile_weights(m, rows, mask, window):
        queries = both_heads(rows)
        keys = ext[m, window:window + 128, pair:2 * pair]
        values = jnp.concatenate([ext[m, window:window + 128, 2 * pair:3 * pair], ones], axis=1)
        weight = jnp.exp(nt(queries, keys) + jnp.concatenate([mask, mask], axis=0))
        return queries, keys, values, weight

    def attend_tiles(m, tiles):
        pieces, weights_values = [], []
        for tile in tiles:
            first, _, window, _ = tile
            index = plan.tiles.index(tile)
            if first == plan.upper:
                pieces.append([(first, NR)])
                rows, mask = ext[m, own_slot_rows, 0:pair], logs[index, pl.ds(slot_row, NR)]
            else:
                pieces.append(plan.own_pieces(tile))
                rows = stacked([ext[m, low:low + count, 0:pair] for low, count in pieces[-1]])
                mask = stacked([logs[index, low - first:low - first + count] for low, count in pieces[-1]])
            _, _, values, weight = tile_weights(m, rows, mask, window)
            weights_values.append((weight.astype(bf16), values))
        both = [nn(weight, values) for weight, values in weights_values]
        sides = [(joined(product[:, :128]), joined(product[:, 128:])) for product in both]
        for rows, (numer, tot) in zip(pieces, sides):
            at = 0
            for low, count in rows:
                work[m, low:low + count, 0:pair] = numer[at:at + count]
                work[m, low:low + count, pair:2 * pair] = tot[at:at + count]
                at += count

    def attend(tiles, first_k, last_k, wait_rims):
        def body(k, carry):
            m = plane(k)
            if wait_rims:
                pair_rims(k).wait()
            for at in range(0, len(tiles), GROUP):
                attend_tiles(m, tiles[at:at + GROUP])
            return carry

        lax.fori_loop(first_k, last_k, body, 0)

    attend(plan.inner, 0, models, False)
    for k in range(1, models):
        merge_gather.to_sides(k)
    attend(plan.outer, 0, 2, True)
    feed_gather.to_sides(1)
    attend(plan.outer, 2, models, True)
    for k in range(models):
        merge_gather.to_corner(k)
    feed_gather.to_sides(2)

    def coarse_rows(m, cols, slot_at):
        rows = [work[m, plan.at[lv] + NR:plan.at[lv] + NR + plan.own[lv], 0:cols] for lv in range(1, plan.levels)]
        return jnp.concatenate(rows + [work[m, slot_at, 0:cols]], axis=0)

    def spread_out(rows):
        high, rest = halves(rows)
        return nn(unpool[...], high) + nn(unpool[...], rest)

    def normalise(m, carry):
        both = spread_out(coarse_rows(m, 2 * pair, slice(plan.upper, plan.upper + NR)))
        both = both + work[m, NR:NR + part, 0:2 * pair]
        inv_total = 1.0 / both[:, pair:]
        quotient = both[:, :pair] * inv_total
        ratio[m] = quotient
        recip[m] = inv_total
        attended[m] = quotient.astype(bf16)
        return carry

    lax.fori_loop(0, models, normalise, 0)
    feed_gather.to_core(0)
    for k in range(models):
        merge_gather.to_core(k)
    feed_gather.to_corner(1)
    feed_gather.to_sides(3)

    def clear(m, carry):
        work[m, :, pair:qkv] = jnp.zeros((work.shape[1], 2 * pair), f32)
        return carry

    lax.fori_loop(0, models, clear, 0)
    residual[...] = tokens[...].astype(f32)
    for k in range(models):
        merge_gather.here(k)

    def merge(m, carry):
        residual[...] += nt(attended[m], weight_cols(m, qkv, pair))
        return carry

    lax.fori_loop(0, models, merge, 0)
    after = residual[...]
    mid_hat, mid_scale = statistics(after)
    mid = (mid_hat * mid_gain + mid_shift).astype(bf16)
    mid_t = mid.T
    load_cotangent.wait()
    row_at = lax.broadcasted_iota(jnp.int32, (part, 1), 0) + spot * part
    valid = row_at < length
    out_grad = jnp.where(valid, cotangent[...], jnp.zeros((), bf16))
    out_grad_t = out_grad.T
    acc[...] = jnp.zeros(acc.shape, f32)
    acc2[...] = jnp.zeros(acc.shape, f32)
    block_shape = grads.shape[1:5] + (hidden,)

    feed_gather.to_core(1)
    feed_gather.to_corner(2)

    class Reduce:
        def __init__(self, col, count, top):
            self.cols = pl.ds(col, count)
            self.top, self.bottom = pl.ds(0, top), pl.ds(top, strip - top)
            self.first = marks.take(4 * models)

        def core(self, k):
            m = plane(k)
            landing = got1.at[m, :, :, :, self.cols]
            return Group(self.first + k, [(grads.at[m, :, :, 1 - ac, :, self.cols], landing, c_peer)], landing)

        def side(self, k):
            m = plane(k)
            top, bottom = self.top, self.bottom
            return Group(self.first + models + k,
                         [(got1.at[m, 1 - ax, :, top, self.cols], got2.at[m, :, top, self.cols], x_peer),
                          (got1.at[m, :, 1 - ay, bottom, self.cols], got2.at[m, :, bottom, self.cols], y_peer)],
                         got2.at[m, :, :, self.cols])

        def corner(self, k):
            m = plane(k)
            top, bottom = self.top, self.bottom
            return Group(self.first + 2 * models + k,
                         [(got2.at[m, 1 - ay, top, self.cols], got3.at[m, top, self.cols], y_peer),
                          (got2.at[m, 1 - ax, bottom, self.cols], got3.at[m, bottom, self.cols], x_peer)],
                         got3.at[m, :, self.cols])

        def home(self, k):
            block = got3.at[plane(k), :, self.cols]
            return Group(self.first + 3 * models + k, [(block, got4.at[k, :, self.cols], z_peer(1 + 2 * (k // 3)))], block)

        def start(self, k):
            self.core(k).start()

        def to_sides(self, k):
            m = plane(k)
            self.core(k).arrive()
            got1[m, :, :, :, self.cols] = got1[m, :, :, :, self.cols] + grads[m, :, :, ac, :, self.cols]
            self.side(k).start()

        def to_corner(self, k):
            m = plane(k)
            self.side(k).arrive()
            top, bottom = self.top, self.bottom
            got2[m, :, top, self.cols] = got2[m, :, top, self.cols] + got1[m, ax, :, top, self.cols]
            got2[m, :, bottom, self.cols] = got2[m, :, bottom, self.cols] + got1[m, :, ay, bottom, self.cols]
            self.corner(k).start()

        def to_planes(self, k):
            m = plane(k)
            self.corner(k).arrive()
            top, bottom = self.top, self.bottom
            got3[m, top, self.cols] = got3[m, top, self.cols] + got2[m, ay, top, self.cols]
            got3[m, bottom, self.cols] = got3[m, bottom, self.cols] + got2[m, ax, bottom, self.cols]

            @pl.when(k == 3)
            def _():
                self.home(2).arrive()
                got3[m, :, self.cols] = got3[m, :, self.cols] + got4[2, :, self.cols]

            @pl.when(k > 0)
            def _():
                self.home(k).start()

        def end(self):
            total = got3[az, :, self.cols].astype(f32)
            for k in (1, 3):
                self.home(k).arrive()
                total = total + got4[k, :, self.cols].astype(f32)
            weight_grads[:, self.cols] = total

        def done(self, k):
            for group in (self.core(k), self.side(k), self.corner(k)):
                group.leave()

            @pl.when(k > 0)
            def _():
                self.home(k).leave()

    feed_reduce = Reduce(4 * pair, 2 * hidden, TOP)
    attention_reduce = Reduce(0, 4 * pair, TOP_LAST)

    def feed(k, carry):
        m = plane(k)
        feed_gather.here(k)
        expand, contract_t = weight_cols(m, 4 * pair, hidden), weight_cols(m, 4 * pair + hidden, hidden)
        up = nn(mid, expand)
        act_grad = nn(out_grad, contract_t)
        phi = 0.5 + 0.5 * lax.erf(up * (0.5 ** 0.5))
        act = (up * phi).astype(bf16)
        slope = phi + up * (jnp.exp(-0.5 * up * up) * 0.3989422804014327)
        hidden_grad = (act_grad * slope).astype(bf16)
        grads[m, :, :, :, :, 4 * pair:4 * pair + hidden] = nn(mid_t, hidden_grad).astype(bf16).reshape(block_shape)
        grads[m, :, :, :, :, 4 * pair + hidden:columns] = nn(out_grad_t, act).astype(bf16).reshape(block_shape)
        feed_reduce.start(k)
        acc[...] += nt(act, contract_t)
        acc2[...] += nt(hidden_grad, expand)
        return carry

    lax.fori_loop(0, 1, feed, 0)
    feed_gather.to_core(2)
    feed_gather.to_corner(3)
    query_rims().start()
    lax.fori_loop(1, 2, feed, 0)
    feed_gather.to_core(3)
    feed_reduce.to_sides(0)
    lax.fori_loop(2, 3, feed, 0)
    feed_reduce.to_sides(1)
    lax.fori_loop(3, 4, feed, 0)
    result[...] = jnp.where(valid, after + acc[...], 0.0).astype(bf16)
    mid_grad = acc2[...]

    def rows_home(source, target, i):
        share = part // models
        mine = pltpu.make_async_copy(
            source.at[pl.ds(pl.multiple_of(az * share, share), share), :], target.at[az], load_sem.at[i])
        mine.start()
        kept.append(mine)
        return send([(source.at[pl.ds(pl.multiple_of(plane(k) * share, share), share), :], target.at[az], z_peer(k))
                     for k in range(1, models)], target.at[pl.ds(0, models - 1)])

    def norm_back(grad, hat, scale_row, gain):
        scaled_grad = grad * gain
        mean_grad = jnp.mean(scaled_grad, axis=-1, keepdims=True)
        mean_along = jnp.mean(scaled_grad * hat, axis=-1, keepdims=True)
        return scale_row * (scaled_grad - mean_grad - hat * mean_along)

    through = out_grad.astype(f32) + norm_back(mid_grad, mid_hat, mid_scale, mid_gain)
    residual[...] = through
    branch = through.astype(bf16)
    branch_t = branch.T
    norm_sums = [jnp.sum(mid_grad * mid_hat, axis=0, keepdims=True), jnp.sum(mid_grad, axis=0, keepdims=True)]

    merge_shape = grads.shape[1:5] + (pair,)
    select_row = lax.broadcasted_iota(jnp.int32, (pair, 128), 0) // HD
    select_col = lax.broadcasted_iota(jnp.int32, (pair, 128), 1) // 2
    totals[...] = jnp.zeros(totals.shape, f32)

    def unmerge(step, carry):
        k = models - 1 - step
        m = plane(k)
        attended_grad = nn(branch, weight_cols(m, qkv, pair)) * recip[m]
        fine = attended_grad.astype(bf16)
        grad_ext[m, NR:NR + part, :] = fine
        sums = nn(pool[...], fine).astype(bf16)
        for lv in range(1, plan.levels):
            grad_ext[m, plan.at[lv] + NR:plan.at[lv] + NR + plan.own[lv], :] = sums[plan.pool_at[lv]:plan.pool_at[lv] + plan.own[lv]]
        grad_ext[m, own_slot_rows, :] = sums[plan.pool_upper:plan.pool_upper + NR]
        grad_rims(k).start()
        high, rest = halves(attended_grad * ratio[m])
        chosen = jnp.where(select_row + 2 * m == select_col, -1.0, 0.0).astype(bf16)
        totals[...] += nn(high, chosen) + nn(rest, chosen)
        grads[m, :, :, :, :, qkv:qkv + pair] = nn(branch_t, attended[m]).astype(bf16).reshape(merge_shape)
        return carry

    lax.fori_loop(0, models, unmerge, 0)
    even = lax.broadcasted_iota(jnp.int32, (1, 128), 1) % 2 == 0
    high, rest = halves(totals[...])
    total_ext[NR:NR + part, :] = jnp.where(even, high, rest)
    pooled_high, pooled_rest = halves(nn(pool[...], high) + nn(pool[...], rest))
    sums = jnp.where(even, pooled_high, pooled_rest)
    for lv in range(1, plan.levels):
        total_ext[plan.at[lv] + NR:plan.at[lv] + NR + plan.own[lv], :] = sums[plan.pool_at[lv]:plan.pool_at[lv] + plan.own[lv]]
    total_ext[own_slot_rows, :] = sums[plan.pool_upper:plan.pool_upper + NR]
    total_rims().start()
    rows_out = rows_home(result, out_rows, 2)

    feed_reduce.to_corner(0)
    feed_reduce.to_sides(2)
    feed_reduce.to_sides(3)

    head_of_lane = lax.broadcasted_iota(jnp.int32, (1, 128), 1) // 2

    normed_t = normed[...].T
    acc[...] = jnp.zeros(acc.shape, f32)
    qkv_shape = grads.shape[1:5] + (qkv,)
    query_scale = jnp.where(lax.broadcasted_iota(jnp.int32, (1, qkv), 1) < pair, HD ** -0.5, 1.0)
    def back_tiles(m, tiles):
        rows_at = [slice(first, first + count) for first, count, _, _ in tiles]
        key_rows = [slice(window, window + 128) for _, _, window, _ in tiles]
        masks = [logs[plan.tiles.index(tile), 0:tile[1]] for tile in tiles]
        made = [tile_weights(m, ext[m, rows, 0:pair], mask, tile[2]) for tile, rows, mask in zip(tiles, rows_at, masks)]
        numers = [both_heads(grad_ext[m, rows, :]) for rows in rows_at]
        slopes = []
        for rows, numer, (_, _, values, _) in zip(rows_at, numers, made):
            tot = total_ext[rows, :]
            zero = jnp.zeros_like(tot)
            tots = jnp.concatenate([jnp.where(head_of_lane == 2 * m, tot, zero),
                                    jnp.where(head_of_lane == 2 * m + 1, tot, zero)], axis=0)
            slopes.append(nt(jnp.concatenate([numer, tots], axis=1), values))
        score_grads = [(weight * by).astype(bf16) for (_, _, _, weight), by in zip(made, slopes)]
        query_sides = [joined(nn(grad, keys)) for grad, (_, keys, _, _) in zip(score_grads, made)]
        key_sides = [tn(grad, queries) for grad, (queries, _, _, _) in zip(score_grads, made)]
        value_sides = [tn(weight.astype(bf16), numer) for (_, _, _, weight), numer in zip(made, numers)]
        for rows, side in zip(rows_at, query_sides):
            work[m, rows, 0:pair] = side
        for rows, key_side, value_side in zip(key_rows, key_sides, value_sides):
            work[m, rows, pair:2 * pair] += key_side
            work[m, rows, 2 * pair:3 * pair] += value_side

    def back_inner(m, carry):
        back_tiles(m, plan.inner)
        return carry

    lax.fori_loop(0, models, back_inner, 0)
    feed_reduce.to_corner(1)
    total_rims().wait()
    query_rims().wait()

    def turn(step):
        late = step // 2
        return (2 + step) * (1 - late) + (3 - step) * late

    def back(step, carry):
        k = turn(step)
        m = plane(k)
        grad_rims(k).wait()
        for at in range(0, len(plan.outer), BACK_GROUP):
            back_tiles(m, plan.outer[at:at + BACK_GROUP])
        coarse = coarse_rows(m, qkv, own_slot_rows)
        spread = spread_out(coarse * jnp.concatenate([inverse[...]] * 3, axis=1))
        rows = (work[m, NR:NR + part, :] + jnp.where(valid, spread, 0.0)).astype(bf16)
        grads[m, :, :, :, :, 0:qkv] = (nn(normed_t, rows) * query_scale).astype(bf16).reshape(qkv_shape)
        attention_reduce.start(k)
        acc[...] += nt(rows, weight_cols(m, 0, qkv))

        @pl.when(step == 0)
        def _():
            feed_reduce.to_planes(0)
            feed_reduce.to_corner(2)

        @pl.when(step == 1)
        def _():
            feed_reduce.to_planes(1)
            feed_reduce.to_corner(3)
            feed_reduce.to_planes(2)

        @pl.when(step == 2)
        def _():
            feed_reduce.to_planes(3)

        @pl.when(step >= 1)
        def _():
            attention_reduce.to_sides(turn(step - 1))

        @pl.when(step >= 2)
        def _():
            attention_reduce.to_corner(turn(step - 2))

        @pl.when(step >= 3)
        def _():
            attention_reduce.to_planes(turn(step - 3))

        return carry

    lax.fori_loop(0, models, back, 0)
    normed_grad = acc[...]
    hat = scaled[...]
    norm_sums = [jnp.sum(normed_grad * hat, axis=0, keepdims=True), jnp.sum(normed_grad, axis=0, keepdims=True)] + norm_sums
    norm_got[0] = jnp.concatenate(norm_sums + [jnp.zeros((4, width), f32)], axis=0)
    small = send([(norm_got.at[0], norm_got.at[k], z_peer(k)) for k in range(1, models)], norm_got.at[pl.ds(0, models - 1)])
    row_grads[...] = (residual[...] + norm_back(normed_grad, hat, rstd[:, 0:1], pre_gain)).astype(bf16)
    grads_out = rows_home(row_grads, out_grads, 3)
    attention_reduce.to_sides(0)
    attention_reduce.to_corner(1)
    attention_reduce.to_planes(3)
    small.arrive()
    norm_total = norm_got[0]
    for k in range(1, models):
        norm_total = norm_total + norm_got[k]
    norm_got[models] = norm_total
    small = send([(norm_got.at[models], norm_got.at[models + step], at_spot((spot + step) % spots)) for step in range(1, spots)],
                 norm_got.at[pl.ds(0, spots - 1)])
    attention_reduce.to_corner(0)
    attention_reduce.to_planes(1)
    feed_reduce.end()
    attention_reduce.to_planes(0)
    small.arrive()
    for step in range(1, spots):
        norm_total = norm_total + norm_got[models + step]
    norm_grads[...] = norm_total
    attention_reduce.end()
    rows_out.arrive()
    grads_out.arrive()
    assert marks.used <= net_count, marks.used
    for group in sent:
        group.leave()
    for c in kept:
        c.wait()

    def drain(k, carry):
        pair_rims(k).done()
        grad_rims(k).done()
        feed_reduce.done(k)
        attention_reduce.done(k)
        return carry

    lax.fori_loop(0, models, drain, 0)
    query_rims().done()
    total_rims().done()


def finish_outputs(dims, rows_ref, grads_ref, weights_ref, norms_ref,
                   out_rows, out_grads, query, key, value, merge, up, down, *rest):
    norm_outs, sem = rest[:4], rest[4]
    part, width, pair, hidden = dims
    copies = [pltpu.make_async_copy(rows_ref, out_rows.at[:, 0], sem.at[0]),
              pltpu.make_async_copy(grads_ref, out_grads.at[:, 0], sem.at[1])]
    for c in copies:
        c.start()
    strip = query.shape[0]
    query[...] = weights_ref[:, 0:pair]
    key[...] = weights_ref[:, pair:2 * pair]
    value[...] = weights_ref[:, 2 * pair:3 * pair]
    up[...] = weights_ref[:, 4 * pair:4 * pair + hidden]
    merge[...] = weights_ref[:, 3 * pair:4 * pair]
    down[...] = weights_ref[:, 4 * pair + hidden:4 * pair + 2 * hidden]
    owner = lax.axis_index("dp") * 4 + lax.axis_index("seq")
    strips = width // strip
    mine = norms_ref[:, 0:strip] * (owner == 0).astype(jnp.float32)
    for i in range(1, strips):
        mine = jnp.where(owner == i, norms_ref[:, i * strip:(i + 1) * strip], mine)
    for i, out in enumerate(norm_outs):
        out[...] = mine[i].reshape(out.shape)
    for c in copies:
        c.wait()


def fast_body(plan, incoming_embeddings, output_sensitivity, sequence_extents, asking_projector, lookup_projector,
              content_projector, attention_combiner, feedforward_expand, feedforward_contract,
              attention_norm_scale, attention_norm_bias, feedforward_norm_scale, feedforward_norm_bias):
    bf16, f32 = jnp.bfloat16, jnp.float32
    models = lax.axis_size("mp")
    seqs, _, part, width = incoming_embeddings.shape
    strip, pair = asking_projector.shape
    hidden = feedforward_expand.shape[1]
    columns = 4 * pair + 2 * hidden
    norm_parts = [row.reshape(1, strip) for row in (
        attention_norm_scale, attention_norm_bias, feedforward_norm_scale, feedforward_norm_bias)]
    share = part // models
    spots, rows = plan.spots, plan.rows
    deep = (2, 2, 2, strip, columns)
    net_count = 92
    vmem = pltpu.VMEM
    scratch = [
        vmem((models,) + deep, bf16), vmem((spots, 8, width), f32), vmem((part, width), bf16), vmem((part, width), bf16),
        vmem((models, rows, 3 * pair), bf16), vmem((len(plan.tiles), 128, 128), f32),
        vmem((part, part), bf16), vmem((part, part), bf16), vmem((part, 128), f32), vmem((models, rows, 3 * pair), f32),
        vmem((models, part, pair), bf16), vmem((models, part, pair), f32), vmem((models, part, pair), f32),
        vmem((part, width), bf16), vmem((part, width), f32), vmem((part, 128), f32),
        vmem((models, rows, pair), bf16), vmem((rows, 128), bf16), vmem((part, width), f32), vmem((part, width), f32),
        vmem((part, width), f32), vmem((part, 128), f32), vmem((part, width), bf16), vmem((part, width), bf16),
        vmem((models,) + deep, bf16), vmem((models, 2, 2, strip, columns), bf16), vmem((models, 2, strip, columns), bf16),
        vmem((models, strip, columns), bf16), vmem((models, strip, columns), bf16), vmem((spots + models, 8, width), f32),
        pltpu.SemaphoreType.DMA((4,)), pltpu.SemaphoreType.DMA((net_count,)), pltpu.SemaphoreType.DMA((net_count,)),
    ]
    any_space, in_vmem = pl.BlockSpec(memory_space=pl.ANY), pl.BlockSpec(memory_space=pltpu.VMEM)
    out_rows, out_grads, weight_grads, norm_grads = pl.pallas_call(
        functools.partial(whole_layer, plan, (part, width, pair, hidden), net_count),
        out_shape=(jax.ShapeDtypeStruct((seqs, share, width), bf16), jax.ShapeDtypeStruct((seqs, share, width), bf16),
                   jax.ShapeDtypeStruct((strip, columns), f32), jax.ShapeDtypeStruct((8, width), f32)),
        in_specs=[pl.BlockSpec(memory_space=pltpu.SMEM)] + [in_vmem] * 10 + [any_space] * 2,
        out_specs=(any_space,) * 2 + (in_vmem,) * 2,
        scratch_shapes=scratch,
        compiler_params=pltpu.CompilerParams(collective_id=0, has_side_effects=True, vmem_limit_bytes=60 * 2 ** 20),
        name="layer",
    )(sequence_extents, asking_projector, lookup_projector, content_projector, attention_combiner.T, feedforward_expand,
      feedforward_contract.T, *norm_parts, incoming_embeddings, output_sensitivity)
    flat = lambda *shape: jax.ShapeDtypeStruct(shape, f32)
    rows_type = jax.ShapeDtypeStruct((seqs, 1, share, width), bf16)
    finished = pl.pallas_call(
        functools.partial(finish_outputs, (part, width, pair, hidden)),
        out_shape=(rows_type, rows_type, flat(strip, pair), flat(strip, pair), flat(strip, pair), flat(strip, pair),
                   flat(strip, hidden), flat(strip, hidden)) + (flat(1, strip),) * 4,
        in_specs=[in_vmem] * 4,
        out_specs=(any_space,) * 2 + (in_vmem,) * 10,
        scratch_shapes=[pltpu.SemaphoreType.DMA((2,))],
        name="outputs",
    )(out_rows, out_grads, weight_grads, norm_grads)
    rows_end, grads_end, query_grad, key_grad, value_grad, merge_t, up_grad, down_t = finished[:8]
    return (rows_end, grads_end, query_grad, key_grad, value_grad, merge_t.T, up_grad, down_t.T,
            *(row.reshape(strip) for row in finished[8:]))


def solution(mesh):
    in_specs = (
        P(None, "seq", "dp", None),
        P(None, "seq", "dp", None),
        P(),
        P(("dp", "seq"), "mp"),
        P(("dp", "seq"), "mp"),
        P(("dp", "seq"), "mp"),
        P("mp", ("dp", "seq")),
        P(("dp", "seq"), "mp"),
        P("mp", ("dp", "seq")),
        P(("dp", "seq")),
        P(("dp", "seq")),
        P(("dp", "seq")),
        P(("dp", "seq")),
    )
    out_specs = (
        P(None, "seq", ("dp", "mp"), None),
        P(None, "seq", ("dp", "mp"), None),
        P(("dp", "seq"), "mp"),
        P(("dp", "seq"), "mp"),
        P(("dp", "seq"), "mp"),
        P("mp", ("dp", "seq")),
        P(("dp", "seq"), "mp"),
        P("mp", ("dp", "seq")),
        P(("dp", "seq")),
        P(("dp", "seq")),
        P(("dp", "seq")),
        P(("dp", "seq")),
    )
    sizes = (mesh.shape["dp"], mesh.shape["seq"], mesh.shape["mp"])

    def chosen(*arrays):
        seqs, _, part, width = arrays[0].shape
        if sizes == (2, 4, 4) and seqs == sizes[2] and part == width == 512 and arrays[3].shape[1] == 128:
            return fast_body(Plan(part, sizes[0] * sizes[1]), *arrays)
        return general_body(*arrays)

    return jax.shard_map(chosen, mesh=mesh, in_specs=in_specs, out_specs=out_specs, check_vma=False)
```
